32 devices in a mesh: batch: 4 (over x, core), seq: 8 (over z, y).
Axes of the slice: x: 2, y: 2, z: 4, core: 2. Of those that a mesh axis runs over, the one named last changes fastest.
Arguments:
- tokens: bfloat16 [8, 1024, 768], P('batch', 'seq'), may hold values from -6 to 6
- in_proj: bfloat16 [768, 3072], P(('batch', 'seq')), may hold values from -0.21875 to 0.21875
- conv_weight: bfloat16 [4, 1536], P(None, ('batch', 'seq')), may hold values from -3 to 3
- conv_bias: bfloat16 [1536], P(('batch', 'seq')), may hold values from -1.5 to 1.5
- state_proj: bfloat16 [1536, 80], P(('batch', 'seq')), may hold values from -0.15625 to 0.15625
- step_proj: bfloat16 [48, 1536], P(None, ('batch', 'seq')), may hold values from -0.875 to 0.875
- step_bias: bfloat16 [1536], P(('batch', 'seq')), may hold values from -3 to -1
- decay_log: bfloat16 [16, 1536], P(None, ('batch', 'seq'))
- skip_gain: bfloat16 [1536], P(('batch', 'seq')), may hold values from 0.5 to 1.5
- out_proj: bfloat16 [1536, 768], P(('batch', 'seq')), may hold values from -0.0390625 to 0.0390625
- norm_gain: bfloat16 [768], P(('batch', 'seq')), may hold values from 0.5 to 1.5
- moe_gain: bfloat16 [768], P(('batch', 'seq')), may hold values from 0.5 to 1.5
- router_proj: bfloat16 [768, 8], P(('batch', 'seq')), may hold values from -0.14941406 to 0.14941406
- expert_up: bfloat16 [8, 768, 3072], P('seq', None, 'batch'), may hold values from -0.21875 to 0.21875
- expert_down: bfloat16 [8, 3072, 768], P('seq', 'batch'), may hold values from -0.21875 to 0.21875
- routes: int32 [8, 1024], P('batch', 'seq'), may hold values from 0 to 7, as said below
- slot_index: int32 [8, 1024], P('batch', 'seq'), may hold values from 0 to 79, as said below
- cotangent: bfloat16 [8, 1024, 768], P('batch', 'seq'), may hold values from -6 to 6
Outputs:
- block_out: bfloat16 [8, 1024, 768], P('batch', 'seq')
- d_tokens: float32 [8, 1024, 768], P('batch', 'seq')
- d_in_proj: float32 [768, 3072], P(('batch', 'seq'))
- d_conv_weight: float32 [4, 1536], P(None, ('batch', 'seq'))
- d_conv_bias: float32 [1536], P(('batch', 'seq'))
- d_state_proj: float32 [1536, 80], P(('batch', 'seq'))
- d_step_proj: float32 [48, 1536], P(None, ('batch', 'seq'))
- d_step_bias: float32 [1536], P(('batch', 'seq'))
- d_decay_log: float32 [16, 1536], P(None, ('batch', 'seq'))
- d_skip_gain: float32 [1536], P(('batch', 'seq'))
- d_out_proj: float32 [1536, 768], P(('batch', 'seq'))
- d_norm_gain: float32 [768], P(('batch', 'seq'))
- d_moe_gain: float32 [768], P(('batch', 'seq'))
- d_router_proj: float32 [768, 8], P(('batch', 'seq'))
- d_expert_up: float32 [8, 768, 3072], P('seq', None, 'batch')
- d_expert_down: float32 [8, 3072, 768], P('seq', 'batch')
The draws below stay inside these ranges and needn't reach their ends.
Inputs may be any that keep to these rules, and one draw needn't show every extreme that they name: `routes`: each token's expert; among the tokens of one device, one expert is named by exactly min(256, 80) of them and every other expert by fewer. `slot_index`: the number of earlier tokens with the same expert among the 256 tokens of the same device, counted over its sequences in order and positions in order within each.
All inputs are finite; a program needn't handle non-finite values.
Results may differ from the reference program's by a relative error of at most 0.018.
Values may be sent and summed in bfloat16 or wider, within the bound.
A program may use at most 192 MiB of HBM per device.

```python
import math
from functools import partial
import jax
import jax.numpy as jnp
from jax import lax

D = 768
DI = 1536
DSTATE = 16
R = 48
KCONV = 4
FF = 3072
SEQ_DEV = 2
SEG = 128
E = 8
SEQS = 8
LEN = 1024
CAP = 40


def route_table(key):
    base_key = jax.random.fold_in(key, 11)
    groups = SEQS // SEQ_DEV
    pieces = LEN // SEG
    block_rows = SEQ_DEV * SEG
    block_count = groups * pieces
    busy_rows = min(block_rows, 2 * CAP)
    positions = jnp.arange(block_rows, dtype=jnp.int32)
    labels = jnp.where(positions < busy_rows, 0, 1 + (positions - busy_rows) % (E - 1)).astype(jnp.int32)

    def one_block(index):
        block_key = jax.random.fold_in(base_key, index)
        place_key, order_key = jax.random.split(block_key)
        placed = jax.random.permutation(place_key, block_rows)
        expert_order = jax.random.permutation(order_key, E).astype(jnp.int32)
        return expert_order[labels[placed]]
    blocks = jax.vmap(one_block)(jnp.arange(block_count, dtype=jnp.int32))
    onehot = (blocks[:, :, None] == jnp.arange(E, dtype=jnp.int32)[None, None, :]).astype(jnp.int32)
    rank_table = jnp.sum((jnp.cumsum(onehot, axis=1) - onehot) * onehot, axis=2)
    chosen = jnp.swapaxes(blocks.reshape(groups, pieces, SEQ_DEV, SEG), 1, 2).reshape(SEQS, LEN)
    slot_table = jnp.swapaxes(rank_table.reshape(groups, pieces, SEQ_DEV, SEG), 1, 2).reshape(SEQS, LEN)
    return (chosen.astype(jnp.int32), slot_table.astype(jnp.int32))


def draw_routes(key, part):
    return route_table(key)[0]


def draw_slot_index(key, part):
    return route_table(key)[1]


def draw_decay_log(key, part):
    lower_end = math.log(1.0 / LEN)
    upper_end = math.log(0.3)
    return jax.random.uniform(key, (DSTATE, DI), jnp.float32, lower_end, upper_end).astype(jnp.bfloat16)


def block_scale(rng, dims, shards, least, top_value):
    def one(axis_at, blocks):
        draws = jax.random.uniform(jax.random.fold_in(jax.random.fold_in(rng, 6), axis_at), (blocks,), jnp.float32, least / len(shards), top_value / len(shards))
        return jnp.repeat(jnp.exp(draws), dims[axis_at] // blocks).reshape((-1,) + (1,) * (len(dims) - axis_at - 1))

    gain = one(*shards[0])
    for cut in shards[1:]:
        gain = gain * one(*cut)
    return gain


def scatter_about(own_key, extent, spread, most, cuts=(), held_as=jnp.bfloat16):
    drawn = spread * jax.random.normal(own_key, extent, jnp.float32)
    if cuts:
        drawn = drawn * block_scale(own_key, extent, cuts, -0.22, 0.18)
    return jnp.clip(drawn, -most, most).astype(held_as)


def setup_inputs(seed: int = 0) -> dict:
    key_of = jax.random.split(jax.random.key(seed), 19)
    tokens = scatter_about(key_of[0], (SEQS, LEN, D), 1.0, 6.0, ((0, 4), (1, 8)))
    in_proj = scatter_about(key_of[1], (D, 2 * DI), D ** -0.5, 0.21875, ((0, 32),))
    conv_weight = scatter_about(key_of[2], (KCONV, DI), KCONV ** -0.5, 3.0, ((1, 32),))
    conv_bias = scatter_about(key_of[3], (DI,), 0.3, 1.5, ((0, 32),))
    state_proj = scatter_about(key_of[4], (DI, R + 2 * DSTATE), DI ** -0.5, 0.15625, ((0, 32),))
    step_proj = scatter_about(key_of[5], (R, DI), R ** -0.5, 0.875, ((1, 32),))
    step_bias = jnp.clip(-3.0 + 2.0 * jax.random.uniform(key_of[6], (DI,), jnp.float32) ** block_scale(key_of[6], (DI,), ((0, 32),), -0.2, 0.2), -3.0, -1.0).astype(jnp.bfloat16)
    decay_log = draw_decay_log(jax.random.fold_in(key_of[18], 71), 0)
    skip_gain = jnp.clip(1.0 + 0.1 * jax.random.normal(key_of[8], (DI,), jnp.float32), 0.5, 1.5).astype(jnp.bfloat16)
    out_proj = scatter_about(key_of[9], (DI, D), (16 * DI) ** -0.5, 0.0390625, ((0, 32),))
    norm_gain = jnp.clip(1.0 + 0.1 * jax.random.normal(key_of[10], (D,), jnp.float32), 0.5, 1.5).astype(jnp.bfloat16)
    moe_gain = jnp.clip(1.0 + 0.1 * jax.random.normal(key_of[11], (D,), jnp.float32), 0.5, 1.5).astype(jnp.bfloat16)
    router_proj = scatter_about(key_of[12], (D, E), 0.025, 0.14941406, ((0, 32),))
    expert_up = scatter_about(key_of[13], (E, D, FF), D ** -0.5, 0.21875, ((0, 8), (2, 4)))
    expert_down = scatter_about(key_of[14], (E, FF, D), (FF // 4) ** -0.5, 0.21875, ((0, 8), (1, 4)))
    routes = draw_routes(jax.random.fold_in(key_of[18], 71), 0)
    slot_index = draw_slot_index(jax.random.fold_in(key_of[18], 71), 0)
    cotangent = scatter_about(key_of[17], (SEQS, LEN, D), 1.0, 6.0, ((0, 4), (1, 8)))
    return {"tokens": tokens, "in_proj": in_proj, "conv_weight": conv_weight, "conv_bias": conv_bias, "state_proj": state_proj, "step_proj": step_proj, "step_bias": step_bias, "decay_log": decay_log, "skip_gain": skip_gain, "out_proj": out_proj, "norm_gain": norm_gain, "moe_gain": moe_gain, "router_proj": router_proj, "expert_up": expert_up, "expert_down": expert_down, "routes": routes, "slot_index": slot_index, "cotangent": cotangent}


epsilon = 1e-05
highest = lax.Precision.HIGHEST

@jax.custom_vjp
def low(v):
    return lax.optimization_barrier(v.astype(jnp.bfloat16)).astype(jnp.float32)

@jax.custom_vjp
def low_back(v):
    return v

def low_keep(v):
    return (low(v), None)

def low_pass(kept, grad):
    return (grad,)

def back_keep(v):
    return (v, None)

def back_low(kept, grad):
    return (low(grad),)
low.defvjp(low_keep, low_pass)
low_back.defvjp(back_keep, back_low)

def product(left, right):
    return jnp.dot(left, right, precision=highest)

def advance(decay_rates, running, inputs):
    now_dt, now_u, now_b, now_c = inputs
    decay_now = jnp.exp(now_dt[None, :] * decay_rates)
    running = decay_now * running + now_b[:, None] * (now_dt * now_u)[None, :]
    return (running, lax.optimization_barrier(jnp.sum(running * now_c[:, None], axis=0)))

def mamba_sequence(weights, sequence):
    in_weight, conv_kernel, conv_shift, state_weight, step_weight, step_shift, decay_value, skip_value, out_weight, first_gain = weights
    inner_width = skip_value.shape[0]
    state_count = decay_value.shape[0]
    rank_count = step_weight.shape[0]
    kernel_len = conv_kernel.shape[0]
    row_count = sequence.shape[0]
    rms_one = lax.rsqrt(lax.optimization_barrier(jnp.mean(sequence * sequence, axis=-1, keepdims=True)) + epsilon)
    normed = low(sequence * rms_one * first_gain)
    mixed = low_back(product(normed, in_weight))
    inner_x = mixed[:, :inner_width]
    gate_z = mixed[:, inner_width:]
    padded = jnp.concatenate([jnp.zeros((kernel_len - 1, inner_width), jnp.float32), inner_x], axis=0)
    conv_total = conv_shift + jnp.zeros_like(inner_x)
    for offset in range(kernel_len):
        conv_total = conv_total + conv_kernel[offset] * padded[offset:offset + row_count]
    activated_input = jax.nn.silu(conv_total)
    projected = low_back(product(low(activated_input), state_weight))
    rank_low = low(projected[:, :rank_count])
    input_matrix_b = projected[:, rank_count:rank_count + state_count]
    input_matrix_c = projected[:, rank_count + state_count:]
    step_delta = jax.nn.softplus(low_back(product(rank_low, step_weight)) + step_shift)
    decay_rates = -jnp.exp(decay_value)
    block_count = row_count // SEG
    blocks = (step_delta.reshape(block_count, SEG, inner_width), activated_input.reshape(block_count, SEG, inner_width), input_matrix_b.reshape(block_count, SEG, state_count), input_matrix_c.reshape(block_count, SEG, state_count))

    def through_block(running, block):
        return lax.scan(partial(advance, decay_rates), running, block)
    end_state, outputs = lax.scan(jax.checkpoint(through_block), jnp.zeros((state_count, inner_width), jnp.float32), blocks)
    mamba_y = outputs.reshape(row_count, inner_width) + skip_value * activated_input
    gated = low(mamba_y * jax.nn.silu(gate_z))
    return sequence + low_back(product(gated, out_weight))

def moe_block(weights, block_rows, block_route, block_slot):
    second_gain, router_weight, up_weight, down_weight = weights
    rms_two = lax.rsqrt(lax.optimization_barrier(jnp.mean(block_rows * block_rows, axis=-1, keepdims=True)) + epsilon)
    moe_in = low(block_rows * rms_two * second_gain)
    logits = low_back(product(moe_in, router_weight))
    picked = (block_route[:, None] == jnp.arange(E, dtype=jnp.int32)[None, :]).astype(jnp.float32)
    gate_prob = jax.nn.sigmoid(lax.optimization_barrier(jnp.sum(logits * picked, axis=1)))
    kept = (block_slot < CAP).astype(jnp.float32)
    clipped = jnp.minimum(block_slot, CAP - 1)
    sent = low_back(moe_in)
    buffer = jnp.zeros((E, CAP, D), jnp.float32).at[block_route, block_slot].set(sent, mode='drop')
    hidden = low_back(jnp.einsum('ecd,edf->ecf', buffer, up_weight, precision=highest))
    activated = low(jax.nn.gelu(hidden, approximate=False))
    outputs = low(low_back(jnp.einsum('ecf,efd->ecd', activated, down_weight, precision=highest)))
    expert_rows = outputs[block_route, clipped] * kept[:, None]
    return block_rows + gate_prob[:, None] * expert_rows

def to_blocks(value_entries):
    groups = SEQS // SEQ_DEV
    pieces = LEN // SEG
    shaped = value_entries.reshape((groups, SEQ_DEV, pieces, SEG) + value_entries.shape[2:])
    return jnp.swapaxes(shaped, 1, 2).reshape((groups * pieces, SEQ_DEV * SEG) + value_entries.shape[2:])

def from_blocks(value_entries):
    groups = SEQS // SEQ_DEV
    pieces = LEN // SEG
    shaped = value_entries.reshape((groups, pieces, SEQ_DEV, SEG) + value_entries.shape[2:])
    return jnp.swapaxes(shaped, 1, 2).reshape((SEQS, LEN) + value_entries.shape[2:])

def reference(tokens, in_proj, conv_weight, conv_bias, state_proj, step_proj, step_bias, decay_log, skip_gain, out_proj, norm_gain, moe_gain, router_proj, expert_up, expert_down, routes, slot_index, cotangent):
    route_blocks = to_blocks(routes)
    slot_blocks = to_blocks(slot_index)

    def forward(tokens_all, in_weight, conv_kernel, conv_shift, state_weight, step_weight, step_shift, decay_value, skip_value, out_weight, first_gain, second_gain, router_weight, up_weight, down_weight):
        mamba_weights = (in_weight, conv_kernel, conv_shift, state_weight, step_weight, step_shift, decay_value, skip_value, out_weight, first_gain)
        moe_weights = (second_gain, router_weight, up_weight, down_weight)

        def per_sequence(running, sequence):
            return (running, jax.checkpoint(mamba_sequence)(mamba_weights, sequence))
        running, hidden_one = lax.scan(per_sequence, jnp.zeros((), jnp.float32), tokens_all)

        def per_block(running, items):
            return (running, jax.checkpoint(moe_block)(moe_weights, items[0], items[1], items[2]))
        running, out_blocks = lax.scan(per_block, running, (to_blocks(hidden_one), route_blocks, slot_blocks))
        return from_blocks(out_blocks)
    block_out, pullback = jax.vjp(forward, tokens.astype(jnp.float32), in_proj.astype(jnp.float32), conv_weight.astype(jnp.float32), conv_bias.astype(jnp.float32), state_proj.astype(jnp.float32), step_proj.astype(jnp.float32), step_bias.astype(jnp.float32), decay_log.astype(jnp.float32), skip_gain.astype(jnp.float32), out_proj.astype(jnp.float32), norm_gain.astype(jnp.float32), moe_gain.astype(jnp.float32), router_proj.astype(jnp.float32), expert_up.astype(jnp.float32), expert_down.astype(jnp.float32))
    grads = pullback(cotangent.astype(jnp.float32))
    return (block_out.astype(jnp.bfloat16), grads[0], grads[1], grads[2], grads[3], grads[4], grads[5], grads[6], grads[7], grads[8], grads[9], grads[10], grads[11], grads[12], grads[13], grads[14])
```

```python
from functools import partial
import functools
import math

import jax
import jax.numpy as jnp
from jax import lax
from jax.experimental import pallas as pl
from jax.experimental.pallas import tpu as pltpu
from jax.sharding import PartitionSpec as P

epsilon = 1e-05
MESH = pl.DeviceIdType.MESH
HBM = pl.BlockSpec(memory_space=pl.ANY)
VM = pl.BlockSpec(memory_space=pltpu.VMEM)
bf16, f32 = jnp.bfloat16, jnp.float32


class Place:
    def __init__(self, batch, seq, ydim=2):
        self.batch, self.seq, self.Y = batch, seq, ydim
        self.Z = seq // ydim
        b, s = lax.axis_index("batch"), lax.axis_index("seq")
        self.x, self.c = b // 2, b % 2
        self.z, self.y = s // ydim, s % ydim

    def at(self, x=None, c=None, y=None, z=None):
        pick = lambda v, own: own if v is None else v
        x, c, y, z = pick(x, self.x), pick(c, self.c), pick(y, self.y), pick(z, self.z)
        return (x * 2 + c, z * self.Y + y)

    def index(self, dev):
        return dev[0] * self.seq + dev[1]


def greet(devices):
    barrier = pltpu.get_barrier_semaphore()
    count = 0
    for pred, dev in devices:
        if pred is None:
            pl.semaphore_signal(barrier, inc=1, device_id=dev, device_id_type=MESH)
            count = count + 1
        else:
            @pl.when(pred)
            def _(dev=dev):
                pl.semaphore_signal(barrier, inc=1, device_id=dev, device_id_type=MESH)
            count = count + jnp.where(pred, 1, 0)
    pl.semaphore_wait(barrier, count)


def gather_kernel(batch, seq, n_arrays, *refs):
    ins, outs = refs[:n_arrays], refs[n_arrays : 2 * n_arrays]
    local_sem, send_sem, recv_sem = refs[2 * n_arrays :]
    me = Place(batch, seq)
    Z, z = me.Z, me.z
    rows = [r.shape[0] for r in ins]
    sib = me.at(c=1 - me.c)
    up_ok, down_ok = z < Z - 1, z > 0
    up, down = me.at(z=z + 1), me.at(z=z - 1)
    nx, ny = me.at(x=1 - me.x), me.at(y=1 - me.y)
    first = me.c == 0
    nb2 = tuple(jnp.where(first, a, b) for a, b in zip(ny, nx))
    nb3 = tuple(jnp.where(first, a, b) for a, b in zip(nx, ny))
    x2, y2 = jnp.where(first, me.x, 1 - me.x), jnp.where(first, 1 - me.y, me.y)
    x3, y3 = jnp.where(first, 1 - me.x, me.x), jnp.where(first, me.y, 1 - me.y)
    greet([(None, sib), (None, nx), (None, ny), (up_ok, up), (down_ok, down)])
    own = me.index(me.at())

    def part(a, index):
        return outs[a].at[pl.ds(pl.multiple_of(index * rows[a], 8), rows[a])]

    sends = []

    def send(pred, index, dev, mine=False):
        slot = len(sends)
        copies = []
        for a in range(n_arrays):
            copies.append(
                pltpu.make_async_remote_copy(
                    src_ref=ins[a] if mine else part(a, index),
                    dst_ref=part(a, index),
                    send_sem=send_sem.at[slot, a],
                    recv_sem=recv_sem.at[index, a],
                    device_id=dev,
                    device_id_type=MESH,
                )
            )

        def go():
            for cp in copies:
                cp.start()
        if pred is None:
            go()
        else:
            pl.when(pred)(go)
        sends.append((pred, copies))

    def arrive(pred, index, targets):
        def wait():
            for a in range(n_arrays):
                pltpu.make_async_remote_copy(
                    src_ref=part(a, index), dst_ref=part(a, index),
                    send_sem=send_sem.at[0, a], recv_sem=recv_sem.at[index, a],
                    device_id=sib, device_id_type=MESH,
                ).wait_recv()
        if pred is None:
            wait()
        else:
            pl.when(pred)(wait)
        for extra, dev in targets:
            p = pred if extra is None else (extra if pred is None else jnp.logical_and(pred, extra))
            send(p, index, dev)

    for dev, pred in ((up, up_ok), (down, down_ok), (nb2, None), (nb3, None), (sib, None)):
        send(pred, own, dev, mine=True)
    local = [pltpu.make_async_copy(ins[a], part(a, own), local_sem.at[a]) for a in range(n_arrays)]
    for cp in local:
        cp.start()

    def offsets(k):
        return [(None, 0)] if k == 0 else [(z >= k, -k), (z + k < Z, k)]

    def col(k):
        for pred, off in offsets(k):
            fwd = (up_ok, up) if off < 0 else (down_ok, down)
            arrive(pred, me.index(me.at(z=z + off)), [fwd, (None, nb2), (None, nb3), (None, sib)])

    def second(k):
        for pred, off in offsets(k):
            arrive(pred, me.index(me.at(x=x2, y=y2, z=z + off)), [(None, nb3), (None, sib)])

    def third(k):
        for pred, off in offsets(k):
            arrive(pred, me.index(me.at(x=x3, y=y3, z=z + off)), [(None, sib)])

    def fourth(k):
        for pred, off in offsets(k):
            arrive(pred, me.index(me.at(x=1 - me.x, y=1 - me.y, z=z + off)), [(None, sib)])

    for h in range(1, Z + 3):
        if h < Z:
            col(h)
        if 0 <= h - 1 < Z:
            second(h - 1)
        if 0 <= h - 2 < Z:
            third(h - 2)
        if 0 <= h - 3 < Z:
            fourth(h - 3)
    for h in range(Z):
        for xx in (0, 1):
            for yy in (0, 1):
                for pred, off in offsets(h):
                    arrive(pred, me.index(me.at(x=xx, y=yy, c=1 - me.c, z=z + off)), [])
    for cp in local:
        cp.wait()
    for pred, copies in sends:
        def done(copies=copies):
            for cp in copies:
                cp.wait_send()
        if pred is None:
            done()
        else:
            pl.when(pred)(done)


def n_sends(Z):
    return 5 + (Z - 1) * 8 + (2 * Z - 1) * 2 + (2 * Z - 1) * 2


def gather_all(batch, seq, *shards):
    n, count = len(shards), batch * seq
    return pl.pallas_call(
        functools.partial(gather_kernel, batch, seq, n),
        out_shape=[jax.ShapeDtypeStruct((count * a.shape[0],) + a.shape[1:], a.dtype) for a in shards],
        in_specs=[HBM] * n,
        out_specs=[HBM] * n,
        scratch_shapes=[
            pltpu.SemaphoreType.DMA((n,)),
            pltpu.SemaphoreType.DMA((n_sends(seq // 2), n)),
            pltpu.SemaphoreType.DMA((count, n)),
        ],
        compiler_params=pltpu.CompilerParams(collective_id=0, has_side_effects=True),
        name="gather_weights",
    )(*shards)


def reduce_kernel(batch, seq, n_arrays, *refs):
    n = n_arrays
    ins, outs = refs[:n], refs[n : 2 * n]
    work, sib_buf, far_buf, near_buf, line_buf = (refs[(2 + i) * n : (3 + i) * n] for i in range(5))
    load_sem, send_sem, sib_sem, far_sem, near_sem, line_sem = refs[7 * n :]
    me = Place(batch, seq)
    Z, z = me.Z, me.z
    rows = [r.shape[0] for r in outs]
    sib = me.at(c=1 - me.c)
    up, down = me.at(z=z + 1), me.at(z=z - 1)
    nx, ny = me.at(x=1 - me.x), me.at(y=1 - me.y)
    first = me.c == 0
    pick = lambda flag, a, b: jnp.where(flag, a, b)
    near = tuple(pick(first, a, b) for a, b in zip(ny, nx))
    far = tuple(pick(first, a, b) for a, b in zip(nx, ny))
    greet([(None, sib), (None, nx), (None, ny), (z < Z - 1, up), (z > 0, down)])

    def groups(c):
        f = c == 0
        ox, oy = 1 - me.x, 1 - me.y
        return [
            (ox, oy),
            (pick(f, ox, me.x), pick(f, me.y, oy)),
            (pick(f, me.x, ox), pick(f, oy, me.y)),
            (me.x, me.y),
        ]

    def slot(xy, zz):
        return (xy[0] * 2 + xy[1]) * Z + zz

    def turn(k):
        return (z + 1 + k) % Z

    sends = []

    def send(pred, srcs, dsts, recv, dev):
        copies = [
            pltpu.make_async_remote_copy(
                src_ref=srcs[a], dst_ref=dsts[a], send_sem=send_sem.at[len(sends), a],
                recv_sem=recv(a), device_id=dev, device_id_type=MESH)
            for a in range(n)
        ]

        def go():
            for cp in copies:
                cp.start()
        if pred is None:
            go()
        else:
            pl.when(pred)(go)
        sends.append((pred, copies))

    def take(bufs, recv):
        for a in range(n):
            pltpu.make_async_remote_copy(
                src_ref=bufs[a], dst_ref=bufs[a], send_sem=send_sem.at[0, a],
                recv_sem=recv(a), device_id=sib, device_id_type=MESH).wait_recv()

    def source(a, c, xy, zz):
        index = me.index((xy[0] * 2 + c, zz * me.Y + xy[1]))
        return ins[a].at[pl.ds(pl.multiple_of(index * rows[a], 8), rows[a])]

    other = 1 - me.c
    for xy in groups(other):
        for k in range(Z):
            s = slot(xy, turn(k))
            send(None, [source(a, other, xy, turn(k)) for a in range(n)],
                 [sib_buf[a].at[s] for a in range(n)], lambda a, s=s: sib_sem.at[s, a], sib)
    mine = groups(me.c)
    loads = []
    for xy in mine:
        for k in range(Z):
            s = slot(xy, turn(k))
            cps = [pltpu.make_async_copy(source(a, me.c, xy, turn(k)), work[a].at[s], load_sem.at[s, a])
                   for a in range(n)]
            for cp in cps:
                cp.start()
            loads.append(cps)

    def total(bufs):
        t = bufs[0][...].astype(jnp.float32)
        for b in bufs[1:]:
            t = t + b[...].astype(jnp.float32)
        return t

    for g, xy in enumerate(mine):
        for k in range(Z):
            zz = turn(k)
            s = slot(xy, zz)
            for cp in loads[g * Z + k]:
                cp.wait()
            take([sib_buf[a].at[s] for a in range(n)], lambda a: sib_sem.at[s, a])
            parts = [[work[a].at[s], sib_buf[a].at[s]] for a in range(n)]
            if g >= 2:
                fs = (g - 2) * Z + zz
                take([far_buf[a].at[fs] for a in range(n)], lambda a: far_sem.at[fs, a])
                for a in range(n):
                    parts[a].append(far_buf[a].at[fs])
            if g == 3:
                take([near_buf[a].at[zz] for a in range(n)], lambda a: near_sem.at[zz, a])
                for a in range(n):
                    parts[a].append(near_buf[a].at[zz])
            if g < 3:
                for a in range(n):
                    work[a][s] = total(parts[a]).astype(jnp.bfloat16)
                srcs = [work[a].at[s] for a in range(n)]
                if g < 2:
                    fs = g * Z + zz
                    send(None, srcs, [far_buf[a].at[fs] for a in range(n)],
                         lambda a: far_sem.at[fs, a], far)
                else:
                    send(None, srcs, [near_buf[a].at[zz] for a in range(n)],
                         lambda a: near_sem.at[zz, a], near)
                continue
            if k < Z - 1:
                rising = zz > z
                side = jnp.where(rising, 0, 1)
                more = jnp.where(rising, z, Z - 1 - z) > 0
                line = [line_buf[a].at[side, zz] for a in range(n)]
                for a in range(n):
                    work[a][s] = total(parts[a]).astype(jnp.bfloat16)

                @pl.when(more)
                def _():
                    take(line, lambda a: line_sem.at[side, zz, a])
                    for a in range(n):
                        work[a][s] = total([work[a].at[s], line[a]]).astype(jnp.bfloat16)
                dev = (me.at()[0], jnp.where(rising, up[1], down[1]))
                send(None, [work[a].at[s] for a in range(n)], line,
                     lambda a: line_sem.at[side, zz, a], dev)
            else:
                for a in range(n):
                    outs[a][...] = total(parts[a])
                for side, pred in ((0, z > 0), (1, z < Z - 1)):
                    @pl.when(pred)
                    def _(side=side):
                        line = [line_buf[a].at[side, zz] for a in range(n)]
                        take(line, lambda a: line_sem.at[side, zz, a])
                        for a in range(n):
                            outs[a][...] = outs[a][...] + line[a][...].astype(jnp.float32)
    for pred, copies in sends:
        for cp in copies:
            cp.wait_send()


def reduce_all(batch, seq, *sums):
    n, count, Z = len(sums), batch * seq, seq // 2
    shapes = [(a.shape[0] // count,) + a.shape[1:] for a in sums]
    half = count // 2
    scratch = []
    for lead in ((half,), (half,), (2 * Z,), (Z,), (2, Z)):
        scratch += [pltpu.VMEM(lead + s, jnp.bfloat16) for s in shapes]
    n_send = half + 2 * Z + Z + Z
    scratch += [
        pltpu.SemaphoreType.DMA((half, n)),
        pltpu.SemaphoreType.DMA((n_send, n)),
        pltpu.SemaphoreType.DMA((half, n)),
        pltpu.SemaphoreType.DMA((2 * Z, n)),
        pltpu.SemaphoreType.DMA((Z, n)),
        pltpu.SemaphoreType.DMA((2, Z, n)),
    ]
    return pl.pallas_call(
        functools.partial(reduce_kernel, batch, seq, n),
        out_shape=[jax.ShapeDtypeStruct(s, jnp.float32) for s in shapes],
        in_specs=[HBM] * n,
        out_specs=[pl.BlockSpec(memory_space=pltpu.VMEM)] * n,
        scratch_shapes=scratch,
        compiler_params=pltpu.CompilerParams(
            collective_id=1, has_side_effects=True, vmem_limit_bytes=40 << 20),
        name="reduce_grads",
    )(*sums)


def spread_kernel(batch, seq, rows_ref, out_ref, local_sem, send_sem, recv_sem):
    me = Place(batch, seq)
    b, s = me.at()
    sib, nx = me.at(c=1 - me.c), me.at(x=1 - me.x)
    greet([(None, sib), (None, nx)] + [(None, (b, (s + k) % seq)) for k in range(1, seq)])
    sends = []

    def send(src, dst, recv, dev):
        cp = pltpu.make_async_remote_copy(
            src_ref=src, dst_ref=dst, send_sem=send_sem.at[len(sends)], recv_sem=recv,
            device_id=dev, device_id_type=MESH)
        cp.start()
        sends.append(cp)

    def arrived(bb, ss):
        pltpu.make_async_remote_copy(
            src_ref=out_ref.at[bb, ss], dst_ref=out_ref.at[bb, ss], send_sem=send_sem.at[0],
            recv_sem=recv_sem.at[bb, ss], device_id=sib, device_id_type=MESH).wait_recv()

    for k in range(seq - 1, 0, -1):
        there = (s + k) % seq
        send(rows_ref.at[there], out_ref.at[b, s], recv_sem.at[b, s], (b, there))
    for dev in (nx, sib):
        send(rows_ref.at[s], out_ref.at[b, s], recv_sem.at[b, s], dev)
    local = pltpu.make_async_copy(rows_ref.at[s], out_ref.at[b, s], local_sem)
    local.start()
    near = nx[0]
    for k in range(1, seq):
        there = (s + k) % seq
        arrived(b, there)
        for dev in (nx, sib):
            send(out_ref.at[b, there], out_ref.at[b, there], recv_sem.at[b, there], dev)
        there = (s + k - 1) % seq
        arrived(near, there)
        send(out_ref.at[near, there], out_ref.at[near, there], recv_sem.at[near, there], sib)
    there = (s + seq - 1) % seq
    arrived(near, there)
    send(out_ref.at[near, there], out_ref.at[near, there], recv_sem.at[near, there], sib)
    for k in range(seq):
        there = (s + k) % seq
        arrived(sib[0], there)
        arrived((1 - me.x) * 2 + 1 - me.c, there)
    local.wait()
    for cp in sends:
        cp.wait_send()


def spread_rows(batch, seq, rows):
    if not tuned(batch, seq):
        mine = lax.all_to_all(rows, "seq", split_axis=0, concat_axis=0, tiled=True)
        return lax.all_gather(mine, "batch", axis=0)
    return pl.pallas_call(
        functools.partial(spread_kernel, batch, seq),
        out_shape=jax.ShapeDtypeStruct((batch,) + rows.shape, rows.dtype),
        in_specs=[HBM],
        out_specs=HBM,
        scratch_shapes=[
            pltpu.SemaphoreType.DMA,
            pltpu.SemaphoreType.DMA((seq - 1 + 2 * seq + seq,)),
            pltpu.SemaphoreType.DMA((batch, seq)),
        ],
        compiler_params=pltpu.CompilerParams(collective_id=2, has_side_effects=True),
        name="spread_rows",
    )(rows)


def tuned(batch, seq):
    return batch == 4 and seq == 8


def collect_kernel(batch, seq, part_ref, out_ref, held, total, sib_buf, near_buf,
                   load_sem, send_sem, sib_sem, near_sem, out_sem, local_sem):
    me = Place(batch, seq)
    b, s = me.at()
    sib, nx = me.at(c=1 - me.c), me.at(x=1 - me.x)
    greet([(None, sib), (None, nx)] + [(None, (b, (s + k) % seq)) for k in range(1, seq)])
    sends = []

    def send(src, dst, recv, dev):
        cp = pltpu.make_async_remote_copy(
            src_ref=src, dst_ref=dst, send_sem=send_sem.at[len(sends)], recv_sem=recv,
            device_id=dev, device_id_type=MESH)
        cp.start()
        sends.append(cp)

    def arrived(ref, recv):
        pltpu.make_async_remote_copy(
            src_ref=ref, dst_ref=ref, send_sem=send_sem.at[0],
            recv_sem=recv, device_id=sib, device_id_type=MESH).wait_recv()

    f32 = lambda ref: ref[...].astype(jnp.float32)
    far_x = 1 - me.x
    turn = lambda k: (s + 1 + k) % seq
    loads = []
    for k in range(seq):
        t = turn(k)
        for g, xx in enumerate((far_x, me.x)):
            send(part_ref.at[xx * 2 + 1 - me.c, t], sib_buf.at[g, t], sib_sem.at[g, t], sib)
            cp = pltpu.make_async_copy(part_ref.at[xx * 2 + me.c, t], held.at[g, t], load_sem.at[g, t])
            cp.start()
            loads.append(cp)

    def first(k):
        t = turn(k)
        loads[2 * k].wait()
        arrived(sib_buf.at[0, t], sib_sem.at[0, t])
        total[0, t] = (f32(held.at[0, t]) + f32(sib_buf.at[0, t])).astype(jnp.bfloat16)
        send(total.at[0, t], near_buf.at[t], near_sem.at[t], nx)

    def second(k):
        t = turn(k)
        loads[2 * k + 1].wait()
        arrived(sib_buf.at[1, t], sib_sem.at[1, t])
        arrived(near_buf.at[t], near_sem.at[t])
        total[1, t] = (f32(held.at[1, t]) + f32(sib_buf.at[1, t]) + f32(near_buf.at[t])).astype(jnp.bfloat16)
        if k < seq - 1:
            send(total.at[1, t], out_ref.at[s], out_sem.at[s], (b, t))
        else:
            cp = pltpu.make_async_copy(total.at[1, t], out_ref.at[s], local_sem)
            cp.start()
            return cp

    first(0)
    first(1)
    for k in range(seq):
        if k + 2 < seq:
            first(k + 2)
        own = second(k)
    for k in range(1, seq):
        t = (s + k) % seq
        arrived(out_ref.at[t], out_sem.at[t])
    own.wait()
    for cp in sends:
        cp.wait_send()


def collect_rows(batch, seq, part):
    if not tuned(batch, seq):
        mine = lax.psum_scatter(part, "batch", scatter_dimension=0, tiled=False)
        return lax.all_to_all(mine, "seq", split_axis=0, concat_axis=0, tiled=True)
    slab = part.shape[2:]
    return pl.pallas_call(
        functools.partial(collect_kernel, batch, seq),
        out_shape=jax.ShapeDtypeStruct((seq,) + slab, part.dtype),
        in_specs=[HBM],
        out_specs=HBM,
        scratch_shapes=[
            pltpu.VMEM((2, seq) + slab, part.dtype),
            pltpu.VMEM((2, seq) + slab, part.dtype),
            pltpu.VMEM((2, seq) + slab, part.dtype),
            pltpu.VMEM((seq,) + slab, part.dtype),
            pltpu.SemaphoreType.DMA((2, seq)),
            pltpu.SemaphoreType.DMA((4 * seq - 1,)),
            pltpu.SemaphoreType.DMA((2, seq)),
            pltpu.SemaphoreType.DMA((seq,)),
            pltpu.SemaphoreType.DMA((seq,)),
            pltpu.SemaphoreType.DMA,
        ],
        compiler_params=pltpu.CompilerParams(
            collective_id=3, has_side_effects=True, vmem_limit_bytes=32 << 20),
        name="collect_rows",
    )(part)


def chain_kernel(seq, forward, dsum_ref, rates_ref, end_ref, out_ref, held, outgoing, send_sem, recv_sem):
    s = lax.axis_index("seq")
    b = lax.axis_index("batch")
    step = 1 if forward else -1
    has_before = s > 0 if forward else s < seq - 1
    has_after = s < seq - 1 if forward else s > 0
    before, after = (b, s - step), (b, s + step)
    barrier = pltpu.get_barrier_semaphore()
    for pred, dev in ((has_before, before), (has_after, after)):
        @pl.when(pred)
        def _(dev=dev):
            pl.semaphore_signal(barrier, inc=1, device_id=dev, device_id_type=MESH)
    pl.semaphore_wait(barrier, jnp.where(has_before, 1, 0) + jnp.where(has_after, 1, 0))
    count = end_ref.shape[0]

    def copy(i):
        return pltpu.make_async_remote_copy(
            src_ref=outgoing.at[i], dst_ref=held.at[i], send_sem=send_sem.at[i],
            recv_sem=recv_sem.at[i], device_id=after, device_id_type=MESH)

    for i in range(count):
        @pl.when(has_before)
        def _(i=i):
            copy(i).wait_recv()
            out_ref[i] = held[i].astype(jnp.float32)
            decay = jnp.exp(rates_ref[...] * dsum_ref[i])
            outgoing[i] = (end_ref[i] + decay * out_ref[i]).astype(jnp.bfloat16)

        @pl.when(jnp.logical_not(has_before))
        def _(i=i):
            out_ref[i] = jnp.zeros_like(out_ref[i])
            outgoing[i] = end_ref[i].astype(jnp.bfloat16)

        @pl.when(has_after)
        def _(i=i):
            copy(i).start()
    for i in range(count):
        @pl.when(has_after)
        def _(i=i):
            copy(i).wait_send()


def chain_states(seq, forward, dsum, rates, end):
    vm = pl.BlockSpec(memory_space=pltpu.VMEM)
    return pl.pallas_call(
        functools.partial(chain_kernel, seq, forward),
        out_shape=jax.ShapeDtypeStruct(end.shape, jnp.float32),
        in_specs=[vm] * 3,
        out_specs=vm,
        scratch_shapes=[
            pltpu.VMEM(end.shape, jnp.bfloat16),
            pltpu.VMEM(end.shape, jnp.bfloat16),
            pltpu.SemaphoreType.DMA((end.shape[0],)),
            pltpu.SemaphoreType.DMA((end.shape[0],)),
        ],
        compiler_params=pltpu.CompilerParams(
            collective_id=4 if forward else 5, has_side_effects=True),
        name="chain_forward" if forward else "chain_backward",
    )(dsum, rates, end)


def dot(a, b):
    return jnp.dot(a, b, preferred_element_type=jnp.float32)


def dot_nt(a, b):
    return lax.dot_general(a, b, (((1,), (1,)), ((), ())), preferred_element_type=jnp.float32)


def dot_tn(a, b):
    return lax.dot_general(a, b, (((0,), (0,)), ((), ())), preferred_element_type=jnp.float32)


def sigmoid(v):
    return 1.0 / (1.0 + jnp.exp(-v))


def lanes(shape):
    return lax.broadcasted_iota(jnp.int32, shape, 1)


def subs(shape):
    return lax.broadcasted_iota(jnp.int32, shape, 0)


def column(row, base, states):
    shape = (states, row.shape[1])
    only = jnp.where(lanes(shape) == subs(shape) + base, jnp.broadcast_to(row, shape), 0.0)
    return jnp.broadcast_to(jnp.sum(only, axis=1, keepdims=True), shape)


def block_diagonal(rows, base, states):
    t = rows.shape[0]
    pick = (rows.shape[1], t * states)
    spread = (subs(pick) == lanes(pick) % states + base).astype(jnp.bfloat16)
    wide = dot(rows.astype(jnp.bfloat16), spread)
    own = lanes(wide.shape) // states == subs(wide.shape)
    return jnp.where(own, wide, 0.0).astype(jnp.bfloat16)


WIDE = 256
GROUP = 16
LOG2E = math.log2(math.e)


def conv_sum(ext_ref, s, cols, vec_ref, states, taps, rows):
    first = ext_ref.shape[1] - rows - taps + 1
    total = vec_ref[states + taps : states + taps + 1, cols]
    for k in range(taps):
        total = total + vec_ref[states + k : states + k + 1, cols] * ext_ref[s, first + k : first + k + rows, cols]
    return total


def normalize(x):
    return lax.rsqrt(jnp.mean(x * x, axis=-1, keepdims=True) + epsilon)


def enter_kernel(dims, tok_ref, halo_ref, win_ref, small_ref, vec_ref, gain_ref,
                 ext_ref, z_ref, u_ref, dt_ref, proj_ref, end_ref, dsum_ref, xn):
    seqs, rows, inner, states, rank, taps = dims
    count = seqs * rows
    for ref, at in ((tok_ref, 0), (halo_ref, count)):
        x = ref[...].astype(jnp.float32)
        xn[at : at + x.shape[0]] = (x * normalize(x) * gain_ref[0:1]).astype(jnp.bfloat16)
    proj = jnp.zeros((count, small_ref.shape[1]), jnp.float32)
    for j in range(inner // WIDE):
        cols = slice(j * WIDE, (j + 1) * WIDE)
        part = dot(xn[...], win_ref[:, cols])
        z_ref[:, cols] = dot(xn[:count], win_ref[:, inner + j * WIDE : inner + (j + 1) * WIDE])
        for s in range(seqs):
            ext_ref[s, 0:8, cols] = part[count + 8 * s : count + 8 * s + 8]
            ext_ref[s, 8:, cols] = part[s * rows : (s + 1) * rows]
            pre = conv_sum(ext_ref, s, cols, vec_ref, states, taps, rows)
            u_ref[s * rows : (s + 1) * rows, cols] = pre * sigmoid(pre)
        proj = proj + dot(u_ref[:, cols].astype(jnp.bfloat16), small_ref[cols, :])
    proj_ref[...] = proj
    low = rank_lanes(proj, rank, states)
    for j in range(inner // WIDE):
        cols = slice(j * WIDE, (j + 1) * WIDE)
        pre = dot_nt(low, small_ref[cols, :]) + vec_ref[states + taps + 1 : states + taps + 2, cols]
        dt = jnp.maximum(pre, 0.0) + jnp.log1p(jnp.exp(-jnp.abs(pre)))
        dt_ref[:, cols] = dt
        for s in range(seqs):
            dsum_ref[s, 0:1, cols] = jnp.sum(dt[s * rows : (s + 1) * rows], axis=0, keepdims=True)
    a2 = -jnp.exp(vec_ref[0:states]) * LOG2E
    blocks = inner // 128
    for s in range(seqs):
        def eight(i, hs):
            hs = list(hs)
            at = pl.multiple_of(s * rows + i * 8, 8)
            small = proj_ref[pl.ds(at, 8), :]
            bs = [column(small[j : j + 1], rank, states) for j in range(8)]
            for k in range(blocks):
                sl = slice(k * 128, (k + 1) * 128)
                d8 = dt_ref[pl.ds(at, 8), sl]
                w8 = d8 * u_ref[pl.ds(at, 8), sl]
                for j in range(8):
                    hs[k] = jnp.exp2(d8[j : j + 1] * a2[:, sl]) * hs[k] + bs[j] * w8[j : j + 1]
            return tuple(hs)
        zero = jnp.zeros((states, 128), jnp.float32)
        hs = lax.fori_loop(0, rows // 8, eight, (zero,) * blocks)
        for k in range(blocks):
            end_ref[s, :, k * 128 : (k + 1) * 128] = hs[k]


def rank_lanes(proj, rank, states):
    at = rank + 2 * states
    moved = pltpu.roll(proj, at, axis=1)
    return jnp.where(lanes(proj.shape) >= at, moved, 0.0).astype(jnp.bfloat16)


def leave_kernel(dims, capacity, tok_ref, cot_ref, h0_ref, dt_ref, u_ref, z_ref, proj_ref, vec_ref, out_ref,
                 gain_ref, router_ref, route_ref, slot_ref, place_ref,
                 hist_ref, y_ref, hid_ref, gated_ref, moe_ref, gate_ref, rows_ref,
                 hbuf, hcur, sem, sem0):
    seqs, rows, inner, states, rank, taps = dims
    count = seqs * rows
    a2 = -jnp.exp(vec_ref[0:states]) * LOG2E
    blocks = inner // 128
    groups = rows // GROUP
    size = GROUP * states
    firsts = []
    for s in range(seqs):
        hcur[s] = h0_ref[s].astype(jnp.bfloat16)
        cp = pltpu.make_async_copy(hcur.at[s], hist_ref.at[s, pl.ds(0, states)], sem0.at[s])
        cp.start()
        firsts.append(cp)

    def out_copy(s, g, slot):
        at = pl.multiple_of(states + g * size, states)
        return pltpu.make_async_copy(hbuf.at[slot], hist_ref.at[s, pl.ds(at, size)], sem.at[slot])

    for s in range(seqs):
        def group(g, hs):
            hs = list(hs)
            slot = g % 2

            @pl.when(g >= 2)
            def _():
                out_copy(s, g - 2, slot).wait()
            for half in range(GROUP // 8):
                at = pl.multiple_of(s * rows + g * GROUP + half * 8, 8)
                small = proj_ref[pl.ds(at, 8), :]
                bs = [column(small[j : j + 1], rank, states) for j in range(8)]
                for k in range(blocks):
                    sl = slice(k * 128, (k + 1) * 128)
                    d8 = dt_ref[pl.ds(at, 8), sl]
                    w8 = d8 * u_ref[pl.ds(at, 8), sl]
                    for j in range(8):
                        t = half * 8 + j
                        hs[k] = jnp.exp2(d8[j : j + 1] * a2[:, sl]) * hs[k] + bs[j] * w8[j : j + 1]
                        hbuf[slot, t * states : (t + 1) * states, sl] = hs[k].astype(jnp.bfloat16)
            at = pl.multiple_of(s * rows + g * GROUP, GROUP)
            mix = block_diagonal(proj_ref[pl.ds(at, GROUP), :], rank + states, states)
            y_ref[pl.ds(at, GROUP), :] = dot(mix, hbuf[slot])
            out_copy(s, g, slot).start()
            return tuple(hs)
        hs = tuple(h0_ref[s, :, k * 128 : (k + 1) * 128] for k in range(blocks))
        lax.fori_loop(0, groups, group, hs)
        for g in (groups - 2, groups - 1):
            out_copy(s, g, g % 2).wait()
    for cp in firsts:
        cp.wait()
    hid = tok_ref[...].astype(jnp.float32)
    for j in range(inner // WIDE):
        cols = slice(j * WIDE, (j + 1) * WIDE)
        y = y_ref[:, cols] + vec_ref[states + taps + 2 : states + taps + 3, cols] * u_ref[:, cols]
        y_ref[:, cols] = y
        z = z_ref[:, cols]
        gated = (y * (z * sigmoid(z))).astype(jnp.bfloat16)
        gated_ref[:, cols] = gated
        hid = hid + dot(gated, out_ref[cols, :])
    hid_ref[...] = hid
    moe_in = (hid * normalize(hid) * gain_ref[1:2]).astype(jnp.bfloat16)
    moe_ref[...] = moe_in
    logits = dot(moe_in, router_ref[...])
    chosen = lanes(logits.shape) == route_ref[...]
    gate = sigmoid(jnp.sum(jnp.where(chosen, logits, 0.0), axis=1, keepdims=True))
    gate_ref[...] = gate
    kept = (slot_ref[...] < capacity).astype(jnp.float32)
    grad_rows = (cot_ref[...].astype(jnp.float32) * (gate * kept)).astype(jnp.bfloat16)
    total = rows_ref.shape[0]
    pick = (subs((total, count)) == place_ref[...]).astype(jnp.bfloat16)
    width = moe_in.shape[1]
    rows_ref[:, :width] = dot(pick, moe_in).astype(jnp.bfloat16)
    rows_ref[:, width:] = dot(pick, grad_rows).astype(jnp.bfloat16)


def erf(x):
    x = jnp.clip(x, -4.0, 4.0)
    x2 = x * x
    top = (-2.72614225801306e-10, 2.77068142495902e-08, -2.10102402082508e-06, -5.69250639462346e-05,
           -7.34990630326855e-04, -2.95459980854025e-03, -1.60960333262415e-02)
    low = (-1.45660718464996e-05, -2.13374055278905e-04, -1.68282697438203e-03, -7.37332916720468e-03,
           -1.42647390514189e-02)
    p = jnp.full_like(x2, top[0])
    for c in top[1:]:
        p = p * x2 + c
    q = jnp.full_like(x2, low[0])
    for c in low[1:]:
        q = q * x2 + c
    return x * p / q


def expert_kernel(rows_ref, up_ref, down_ref, part_ref, dup_ref, ddown_ref):
    width = up_ref.shape[0]
    x, g = rows_ref[:, :width], rows_ref[:, width:]
    hidden = dot(x, up_ref[...])
    half = 0.5 * (1.0 + erf(hidden * math.sqrt(0.5)))
    act = (hidden * half).astype(jnp.bfloat16)
    slope = half + hidden * (jnp.exp(-0.5 * hidden * hidden) * (1.0 / math.sqrt(2.0 * math.pi)))
    part_ref[:, :width] = dot(act, down_ref[...]).astype(jnp.bfloat16)
    grad_hidden = (dot_nt(g, down_ref[...]) * slope).astype(jnp.bfloat16)
    part_ref[:, width:] = dot_nt(grad_hidden, up_ref[...]).astype(jnp.bfloat16)
    ddown, dup = dot_tn(act, g), dot_tn(x, grad_hidden)

    @pl.when(pl.program_id(0) == 0)
    def _():
        dup_ref[...] = dup
        ddown_ref[...] = ddown

    @pl.when(pl.program_id(0) > 0)
    def _():
        dup_ref[...] += dup
        ddown_ref[...] += ddown


def return_kernel(dims, ret_ref, cot_ref, hid_ref, moe_ref, gate_ref, gated_ref, y_ref, u_ref, z_ref, dt_ref,
                  proj_ref, vec_ref, out_ref, gain_ref, router_ref, route_ref, place_ref,
                  block_ref, ghid_ref, gy_ref, gz_ref, dout_ref, drouter_ref, dskip_ref, dgain_ref, adj_ref):
    seqs, rows, inner, states, rank, taps = dims
    count = seqs * rows
    total, width = ret_ref.shape[0], hid_ref.shape[1]
    pick = (lanes((count, total)) == place_ref[...]).astype(jnp.bfloat16)
    result = dot(pick, ret_ref[:, :width])
    hid, gate = hid_ref[...], gate_ref[...]
    block_ref[...] = (hid + gate * result).astype(jnp.bfloat16)
    cot = cot_ref[...].astype(jnp.float32)
    grad_gate = jnp.sum(cot * result, axis=1, keepdims=True)
    wide = (count, router_ref.shape[1])
    grad_logits = jnp.where(lanes(wide) == route_ref[...], grad_gate * gate * (1.0 - gate), 0.0).astype(jnp.bfloat16)
    grad_in = dot(pick, ret_ref[:, width:]) + dot_nt(grad_logits, router_ref[...])
    drouter_ref[...] = dot_tn(moe_ref[...], grad_logits)
    r2 = normalize(hid)
    dgain_ref[...] = jnp.sum(grad_in * (hid * r2), axis=0, keepdims=True)
    scaled = grad_in * gain_ref[1:2]
    grad_hid = cot + r2 * scaled - hid * (r2 * r2 * r2) * jnp.mean(scaled * hid, axis=1, keepdims=True)
    ghid_ref[...] = grad_hid
    branch = grad_hid.astype(jnp.bfloat16)
    for j in range(inner // WIDE):
        cols = slice(j * WIDE, (j + 1) * WIDE)
        dout_ref[cols, :] = dot_tn(gated_ref[:, cols], branch).astype(jnp.bfloat16)
        grad = dot_nt(branch, out_ref[cols, :])
        z = z_ref[:, cols]
        sig = sigmoid(z)
        gy = grad * (z * sig)
        gy_ref[:, cols] = gy
        gz_ref[:, cols] = (grad * y_ref[:, cols] * (sig + z * sig * (1.0 - sig))).astype(jnp.bfloat16)
        dskip_ref[:, cols] = jnp.sum(gy * u_ref[:, cols], axis=0, keepdims=True)
    a2 = -jnp.exp(vec_ref[0:states]) * LOG2E
    blocks = inner // 128
    for s in range(seqs):
        def eight(i, ms):
            ms = list(ms)
            at = pl.multiple_of((s + 1) * rows - 8 - i * 8, 8)
            small = proj_ref[pl.ds(at, 8), :]
            cs = [column(small[j : j + 1], rank + states, states) for j in range(8)]
            for k in range(blocks):
                sl = slice(k * 128, (k + 1) * 128)
                d8, g8 = dt_ref[pl.ds(at, 8), sl], gy_ref[pl.ds(at, 8), sl]
                for j in reversed(range(8)):
                    ms[k] = jnp.exp2(d8[j : j + 1] * a2[:, sl]) * (ms[k] + cs[j] * g8[j : j + 1])
            return tuple(ms)
        zero = jnp.zeros((states, 128), jnp.float32)
        ms = lax.fori_loop(0, rows // 8, eight, (zero,) * blocks)
        for k in range(blocks):
            adj_ref[s, :, k * 128 : (k + 1) * 128] = ms[k]


def back_kernel(dims, tok_ref, halo_ref, ext_ref, hist_ref, later_ref, gy_ref, gz_ref, ghid_ref, u_ref, dt_ref,
                proj_ref, win_ref, small_ref, vec_ref, gain_ref,
                dtok_ref, dhalo_ref, din_ref, dsmall_ref, dvec_ref, dgain_ref,
                hbuf, abuf, rbuf, ccol, adj, gdt, gu, gproj, gpad, gm, xn, gpre, sem):
    seqs, rows, inner, states, rank, taps = dims
    count = seqs * rows
    groups = rows // GROUP
    size = GROUP * states
    steps = seqs * groups

    def fetch(i, slot):
        s, g = i // groups, groups - 1 - i % groups
        at = pl.multiple_of(g * size, size)
        return pltpu.make_async_copy(hist_ref.at[s, pl.ds(at, size + states)], hbuf.at[slot], sem.at[slot])

    fetch(0, 0).start()
    dvec_ref[...] = jnp.zeros_like(dvec_ref)
    ones = (lanes((GROUP, size)) // states == subs((GROUP, size))).astype(jnp.bfloat16)

    def group(i, carry):
        slot = i % 2
        s, g = i // groups, groups - 1 - i % groups

        @pl.when(i + 1 < steps)
        def _():
            fetch(i + 1, 1 - slot).start()

        @pl.when(g == groups - 1)
        def _():
            adj[...] = later_ref[s]
        fetch(i, slot).wait()
        at = pl.multiple_of(s * rows + g * GROUP, GROUP)
        small = proj_ref[pl.ds(at, GROUP), :]
        bmix = block_diagonal(small, rank, states)
        for t in range(GROUP):
            cbuf_t = column(small[t : t + 1], rank + states, states)
            ccol[t] = cbuf_t

        def pair(c, carry2):
            gb, gc = carry2
            c0 = pl.multiple_of(c * WIDE, WIDE)
            for half in range(WIDE // 128):
                sl = pl.ds(pl.multiple_of(c0 + half * 128, 128), 128)
                hl = slice(half * 128, (half + 1) * 128)
                rates = -jnp.exp(vec_ref[0:states, sl])
                a2 = rates * LOG2E
                m = adj[:, sl]
                dd = dvec_ref[0:states, sl]
                for h8 in reversed(range(GROUP // 8)):
                    a8 = pl.multiple_of(at + h8 * 8, 8)
                    d8, g8 = dt_ref[pl.ds(a8, 8), sl], gy_ref[pl.ds(a8, 8), sl]
                    for j in reversed(range(8)):
                        t = h8 * 8 + j
                        a = m + ccol[t] * g8[j : j + 1]
                        m = jnp.exp2(d8[j : j + 1] * a2) * a
                        p = m * hbuf[slot, t * states : (t + 1) * states, sl].astype(jnp.float32) * rates
                        dd = dd + p * d8[j : j + 1]
                        abuf[t * states : (t + 1) * states, hl] = a.astype(jnp.bfloat16)
                        rbuf[t * states : (t + 1) * states, hl] = p.astype(jnp.bfloat16)
                adj[:, sl] = m
                dvec_ref[0:states, sl] = dd
            sl = pl.ds(c0, WIDE)
            d, g_, u = dt_ref[pl.ds(at, GROUP), sl], gy_ref[pl.ds(at, GROUP), sl], u_ref[pl.ds(at, GROUP), sl]
            w1, w2 = dot(ones, rbuf[...]), dot(bmix, abuf[...])
            gdt[pl.ds(at, GROUP), sl] = w1 + u * w2
            gu[pl.ds(at, GROUP), sl] = d * w2
            gb = gb + dot_nt((d * u).astype(jnp.bfloat16), abuf[...])
            gc = gc + dot_nt(g_.astype(jnp.bfloat16), hbuf[slot, states:, sl])
            return gb, gc
        zero = jnp.zeros((GROUP, size), jnp.float32)
        gb, gc = lax.fori_loop(0, inner // WIDE, pair, (zero, zero))
        place = (size, small.shape[1])
        own = subs(place) % states
        put = lambda base: (lanes(place) == own + base).astype(jnp.bfloat16)
        only = lambda v: jnp.where(ones > 0, v, 0.0).astype(jnp.bfloat16)
        gproj[pl.ds(at, GROUP), :] = dot(only(gb), put(rank)) + dot(only(gc), put(rank + states))
        return carry
    lax.fori_loop(0, steps, group, 0)

    low = rank_lanes(proj_ref[...], rank, states)
    at = rank + 2 * states
    row = states + taps
    grad_rank = jnp.zeros(proj_ref.shape, jnp.float32)
    for j in range(inner // WIDE):
        cols = slice(j * WIDE, (j + 1) * WIDE)
        pre = dot_nt(low, small_ref[cols, :]) + vec_ref[row + 1 : row + 2, cols]
        grad_pre = gdt[:, cols] * sigmoid(pre)
        dvec_ref[row + 1 : row + 2, cols] = jnp.sum(grad_pre, axis=0, keepdims=True)
        grad_pre = grad_pre.astype(jnp.bfloat16)
        gpre[:, cols] = grad_pre
        grad_rank = grad_rank + dot(grad_pre, small_ref[cols, :])
    where = lanes(grad_rank.shape)
    grad_rank = pltpu.roll(grad_rank, small_ref.shape[1] - at, axis=1)
    grad_proj = jnp.where(where < rank, grad_rank, jnp.where(where < at, gproj[...], 0.0)).astype(jnp.bfloat16)
    for ref, to in ((tok_ref, 0), (halo_ref, count)):
        x = ref[...].astype(jnp.float32)
        xn[to : to + x.shape[0]] = (x * normalize(x) * gain_ref[0:1]).astype(jnp.bfloat16)
    grad_normed = jnp.zeros((gm.shape[0], xn.shape[1]), jnp.float32)
    first = ext_ref.shape[1] - rows - taps + 1
    for j in range(inner // WIDE):
        cols = slice(j * WIDE, (j + 1) * WIDE)
        dsmall_ref[cols, :] = (
            dot_tn(u_ref[:, cols].astype(jnp.bfloat16), grad_proj) + dot_tn(gpre[:, cols], low)
        ).astype(jnp.bfloat16)
        grad_u = dot_nt(grad_proj, small_ref[cols, :]) + gy_ref[:, cols] * vec_ref[row + 2 : row + 3, cols] + gu[:, cols]
        taps_sum = [0.0] * taps
        bias_sum = 0.0
        heads = []
        for s in range(seqs):
            pre = conv_sum(ext_ref, s, cols, vec_ref, states, taps, rows)
            sig = sigmoid(pre)
            grad_conv = grad_u[s * rows : (s + 1) * rows] * (sig + pre * sig * (1.0 - sig))
            bias_sum = bias_sum + jnp.sum(grad_conv, axis=0, keepdims=True)
            for k in range(taps):
                taps_sum[k] = taps_sum[k] + jnp.sum(
                    grad_conv * ext_ref[s, first + k : first + k + rows, cols], axis=0, keepdims=True)
            gpad[0:8] = jnp.zeros((8, WIDE), jnp.float32)
            gpad[8 : 8 + rows] = grad_conv
            gpad[8 + rows :] = jnp.zeros((8, WIDE), jnp.float32)
            grad = 0.0
            for k in range(taps):
                grad = grad + vec_ref[states + k : states + k + 1, cols] * gpad[taps - 1 - k : taps + 7 - k + rows]
            heads.append(grad[0:8])
            gm[s * rows : (s + 1) * rows, cols] = grad[8:].astype(jnp.bfloat16)
        gm[count:, cols] = jnp.concatenate(heads).astype(jnp.bfloat16)
        dvec_ref[row : row + 1, cols] = bias_sum
        for k in range(taps):
            dvec_ref[states + k : states + k + 1, cols] = taps_sum[k]
        zcols = slice(inner + j * WIDE, inner + (j + 1) * WIDE)
        din_ref[:, cols] = dot_tn(xn[...], gm[:, cols]).astype(jnp.bfloat16)
        din_ref[:, zcols] = dot_tn(xn[:count], gz_ref[:, cols]).astype(jnp.bfloat16)
        gz = jnp.concatenate([gz_ref[:, cols], jnp.zeros((gm.shape[0] - count, WIDE), jnp.bfloat16)])
        grad_normed = grad_normed + dot_nt(gm[:, cols], win_ref[:, cols]) + dot_nt(gz, win_ref[:, zcols])
    gain_sum = 0.0
    for ref, to, base, out in ((tok_ref, 0, ghid_ref, dtok_ref), (halo_ref, count, None, dhalo_ref)):
        x = ref[...].astype(jnp.float32)
        r1 = normalize(x)
        grad = grad_normed[to : to + x.shape[0]]
        gain_sum = gain_sum + jnp.sum(grad * (x * r1), axis=0, keepdims=True)
        grad = grad * gain_ref[0:1]
        grad = r1 * grad - x * (r1 * r1 * r1) * jnp.mean(grad * x, axis=1, keepdims=True)
        out[...] = grad if base is None else grad + base[...]
    dgain_ref[...] = gain_sum


def like(*shape, dtype=f32):
    return jax.ShapeDtypeStruct(shape, dtype)


def params(mib=56):
    return pltpu.CompilerParams(vmem_limit_bytes=mib << 20)


def body(
    tokens,
    in_proj,
    conv_weight,
    conv_bias,
    state_proj,
    step_proj,
    step_bias,
    decay_log,
    skip_gain,
    out_proj,
    norm_gain,
    moe_gain,
    router_proj,
    expert_up,
    expert_down,
    routes,
    slot_index,
    cotangent,
):
    batch, seq = lax.axis_size("batch"), lax.axis_size("seq")
    both = ("batch", "seq")
    seqs, rows, width = tokens.shape
    count = seqs * rows
    devices = batch * seq
    taps, share = conv_weight.shape
    inner = share * devices
    states, rank = decay_log.shape[0], step_proj.shape[0]
    low_share = norm_gain.shape[0]
    experts = router_proj.shape[1]
    capacity = max(2, 5 * count // (4 * experts))
    dims = (seqs, rows, inner, states, rank, taps)
    tile = 128

    vectors = jnp.concatenate([decay_log, conv_weight, conv_bias[None], step_bias[None], skip_gain[None]])
    features = jnp.concatenate([router_proj, norm_gain[:, None], moe_gain[:, None]], axis=1)
    used = vectors.shape[0]
    room = -(-used // 8) * 8
    tail = jnp.concatenate(
        [
            state_proj,
            step_proj.T,
            jnp.pad(vectors, ((0, room - used), (0, 0))).T,
            jnp.pad(features, ((0, share - low_share), (0, tile - room - features.shape[1]))),
        ],
        axis=1,
    )
    halo = lax.ppermute(tokens[:, rows - taps + 1 :], "seq", [(i, i + 1) for i in range(seq - 1)])
    halo = jnp.pad(halo, ((0, 0), (8 - taps + 1, 0), (0, 0))).reshape(seqs * 8, width)
    if tuned(batch, seq):
        in_full, out_full, tail_full = gather_all(batch, seq, in_proj, out_proj, tail)
    else:
        in_full, out_full, tail_full = (
            lax.all_gather(a, both, axis=0, tiled=True) for a in (in_proj, out_proj, tail)
        )
    small = tail_full[:, :tile]
    vec = tail_full[:, tile : tile + room].T.astype(f32)
    model = tail_full[:, tile + room : tile + room + experts + 2]
    model = model.reshape(devices, share, experts + 2)[:, :low_share].reshape(width, experts + 2)
    gain = model[:, experts:].T.astype(f32)
    router = jnp.pad(model[:, :experts], ((0, 0), (0, tile - experts)))
    tok, cot = tokens.reshape(count, width), cotangent.reshape(count, width)
    route, slot = routes.reshape(count, 1), slot_index.reshape(count, 1)
    place = jnp.where(slot < capacity, route * capacity + slot, -1)

    ext, z, u, dt, proj, end, dsum = pl.pallas_call(
        partial(enter_kernel, dims),
        out_shape=[
            like(seqs, rows + 8, inner),
            like(count, inner),
            like(count, inner),
            like(count, inner),
            like(count, tile),
            like(seqs, states, inner),
            like(seqs, 1, inner),
        ],
        in_specs=[VM] * 6,
        out_specs=[VM] * 7,
        scratch_shapes=[pltpu.VMEM((count + seqs * 8, width), bf16)],
        compiler_params=params(),
        name="enter",
    )(tok, halo, in_full, small, vec, gain)
    rates = -jnp.exp(vec[:states])
    before = chain_states(seq, True, dsum, rates, end)
    size = GROUP * states
    total = experts * capacity
    hist, y, hid, gated, moe_in, gate, sent = pl.pallas_call(
        partial(leave_kernel, dims, capacity),
        out_shape=[
            like(seqs, (rows + 1) * states, inner, dtype=bf16),
            like(count, inner),
            like(count, width),
            like(count, inner, dtype=bf16),
            like(count, width, dtype=bf16),
            like(count, 1),
            like(total, 2 * width, dtype=bf16),
        ],
        in_specs=[VM] * 14,
        out_specs=[HBM] + [VM] * 6,
        scratch_shapes=[
            pltpu.VMEM((2, size, inner), bf16),
            pltpu.VMEM((seqs, states, inner), bf16),
            pltpu.SemaphoreType.DMA((2,)),
            pltpu.SemaphoreType.DMA((seqs,)),
        ],
        compiler_params=params(),
        name="leave",
    )(tok, cot, before, dt, u, z, proj, vec, out_full, gain, router, route, slot, place.reshape(1, count))

    spread = spread_rows(batch, seq, sent.reshape(experts, capacity, 2 * width))
    block = seq * capacity
    hidden_share = expert_up.shape[2]
    part, d_up, d_down = pl.pallas_call(
        expert_kernel,
        out_shape=[
            like(batch * block, 2 * width, dtype=bf16),
            like(width, hidden_share),
            like(hidden_share, width),
        ],
        grid=(batch,),
        in_specs=[
            pl.BlockSpec((block, 2 * width), lambda i: (i, 0)),
            pl.BlockSpec((width, hidden_share), lambda i: (0, 0)),
            pl.BlockSpec((hidden_share, width), lambda i: (0, 0)),
        ],
        out_specs=[
            pl.BlockSpec((block, 2 * width), lambda i: (i, 0)),
            pl.BlockSpec((width, hidden_share), lambda i: (0, 0)),
            pl.BlockSpec((hidden_share, width), lambda i: (0, 0)),
        ],
        compiler_params=params(),
        name="experts",
    )(spread.reshape(batch * block, 2 * width), expert_up[0], expert_down[0])
    back = collect_rows(batch, seq, part.reshape(batch, seq, capacity, 2 * width)).reshape(total, 2 * width)

    block_out, ghid, gy, gz, d_out, d_router, d_skip, d_moe, adj = pl.pallas_call(
        partial(return_kernel, dims),
        out_shape=[
            like(count, width, dtype=bf16),
            like(count, width),
            like(count, inner),
            like(count, inner, dtype=bf16),
            like(inner, width, dtype=bf16),
            like(width, tile),
            like(1, inner),
            like(1, width),
            like(seqs, states, inner),
        ],
        in_specs=[VM] * 17,
        out_specs=[VM] * 9,
        compiler_params=params(),
        name="back_experts",
    )(back, cot, hid, moe_in, gate, gated, y, u, z, dt, proj, vec, out_full, gain, router, route, place)
    later = chain_states(seq, False, dsum, rates, adj)
    d_tok, d_halo, d_in, d_small, d_vec, d_norm = pl.pallas_call(
        partial(back_kernel, dims),
        out_shape=[
            like(count, width),
            like(seqs * 8, width),
            like(width, 2 * inner, dtype=bf16),
            like(inner, tile, dtype=bf16),
            like(room, inner),
            like(1, width),
        ],
        in_specs=[VM] * 3 + [HBM] + [VM] * 11,
        out_specs=[VM] * 6,
        scratch_shapes=[
            pltpu.VMEM((2, size + states, inner), bf16),
            pltpu.VMEM((size, WIDE), bf16),
            pltpu.VMEM((size, WIDE), bf16),
            pltpu.VMEM((GROUP, states, tile), f32),
            pltpu.VMEM((states, inner), f32),
            pltpu.VMEM((count, inner), f32),
            pltpu.VMEM((count, inner), f32),
            pltpu.VMEM((count, tile), f32),
            pltpu.VMEM((rows + 16, WIDE), f32),
            pltpu.VMEM((count + seqs * 8, inner), bf16),
            pltpu.VMEM((count + seqs * 8, width), bf16),
            pltpu.VMEM((count, inner), bf16),
            pltpu.SemaphoreType.DMA((2,)),
        ],
        compiler_params=params(),
        name="back_mixer",
    )(tok, halo, ext, hist, later, gy, gz, ghid, u, dt, proj, in_full, small, vec, gain)

    d_model = jnp.concatenate([d_router[:, :experts], d_norm.T, d_moe.T], axis=1)
    d_model = jnp.pad(
        d_model.reshape(devices, low_share, experts + 2),
        ((0, 0), (0, share - low_share), (0, tile - room - experts - 2)),
    ).reshape(inner, tile - room)
    skip_row = states + taps + 2
    d_vec = d_vec.at[skip_row].set(d_skip[0])
    d_tail = jnp.concatenate([d_small, d_vec.T.astype(bf16), d_model.astype(bf16)], axis=1)
    if tuned(batch, seq):
        s_in, s_out, s_tail = reduce_all(batch, seq, d_in, d_out, d_tail)
    else:
        s_in, s_out, s_tail = (
            lax.psum_scatter(a.astype(f32), both, scatter_dimension=0, tiled=True) for a in (d_in, d_out, d_tail)
        )
    from_next = lax.ppermute(
        d_halo.reshape(seqs, 8, width)[:, 8 - taps + 1 :], "seq", [(i + 1, i) for i in range(seq - 1)]
    )
    d_tok = d_tok.reshape(tokens.shape).at[:, rows - taps + 1 :].add(from_next)
    s_vec = s_tail[:, tile : tile + room].T
    s_model = s_tail[:low_share, tile + room :]
    return (
        block_out.reshape(tokens.shape),
        d_tok,
        s_in,
        s_vec[states : states + taps],
        s_vec[states + taps],
        s_tail[:, : rank + 2 * states],
        s_tail[:, rank + 2 * states : tile].T,
        s_vec[states + taps + 1],
        s_vec[:states],
        s_vec[states + taps + 2],
        s_out,
        s_model[:, experts],
        s_model[:, experts + 1],
        s_model[:, :experts],
        d_up[None],
        d_down[None],
    )


def solution(mesh):
    in_specs = (
        P("batch", "seq", None),
        P(("batch", "seq"), None),
        P(None, ("batch", "seq")),
        P(("batch", "seq")),
        P(("batch", "seq"), None),
        P(None, ("batch", "seq")),
        P(("batch", "seq")),
        P(None, ("batch", "seq")),
        P(("batch", "seq")),
        P(("batch", "seq"), None),
        P(("batch", "seq")),
        P(("batch", "seq")),
        P(("batch", "seq"), None),
        P("seq", None, "batch"),
        P("seq", "batch", None),
        P("batch", "seq"),
        P("batch", "seq"),
        P("batch", "seq", None),
    )
    out_specs = (
        P("batch", "seq", None),
        P("batch", "seq", None),
        P(("batch", "seq"), None),
        P(None, ("batch", "seq")),
        P(("batch", "seq")),
        P(("batch", "seq"), None),
        P(None, ("batch", "seq")),
        P(("batch", "seq")),
        P(None, ("batch", "seq")),
        P(("batch", "seq")),
        P(("batch", "seq"), None),
        P(("batch", "seq")),
        P(("batch", "seq")),
        P(("batch", "seq"), None),
        P("seq", None, "batch"),
        P("seq", "batch", None),
    )
    return jax.shard_map(body, mesh=mesh, in_specs=in_specs, out_specs=out_specs, check_vma=False)
```

```python
from functools import partial
import functools
import math

import jax
import jax.numpy as jnp
from jax import lax
from jax.experimental import pallas as pl
from jax.experimental.pallas import tpu as pltpu
from jax.sharding import PartitionSpec as P

epsilon = 1e-05
MESH = pl.DeviceIdType.MESH
HBM = pl.BlockSpec(memory_space=pl.ANY)
VM = pl.BlockSpec(memory_space=pltpu.VMEM)
bf16, f32 = jnp.bfloat16, jnp.float32


class Place:
    def __init__(self, batch, seq, ydim=2):
        self.batch, self.seq, self.Y = batch, seq, ydim
        self.Z = seq // ydim
        b, s = lax.axis_index("batch"), lax.axis_index("seq")
        self.x, self.c = b // 2, b % 2
        self.z, self.y = s // ydim, s % ydim

    def at(self, x=None, c=None, y=None, z=None):
        pick = lambda v, own: own if v is None else v
        x, c, y, z = pick(x, self.x), pick(c, self.c), pick(y, self.y), pick(z, self.z)
        return (x * 2 + c, z * self.Y + y)

    def index(self, dev):
        return dev[0] * self.seq + dev[1]


def greet(devices):
    barrier = pltpu.get_barrier_semaphore()
    count = 0
    for pred, dev in devices:
        if pred is None:
            pl.semaphore_signal(barrier, inc=1, device_id=dev, device_id_type=MESH)
            count = count + 1
        else:
            @pl.when(pred)
            def _(dev=dev):
                pl.semaphore_signal(barrier, inc=1, device_id=dev, device_id_type=MESH)
            count = count + jnp.where(pred, 1, 0)
    pl.semaphore_wait(barrier, count)


def gather_kernel(batch, seq, n_arrays, *refs):
    ins, outs = refs[:n_arrays], refs[n_arrays : 2 * n_arrays]
    local_sem, send_sem, recv_sem = refs[2 * n_arrays :]
    me = Place(batch, seq)
    Z, z = me.Z, me.z
    rows = [r.shape[0] for r in ins]
    sib = me.at(c=1 - me.c)
    up_ok, down_ok = z < Z - 1, z > 0
    up, down = me.at(z=z + 1), me.at(z=z - 1)
    nx, ny = me.at(x=1 - me.x), me.at(y=1 - me.y)
    first = me.c == 0
    nb2 = tuple(jnp.where(first, a, b) for a, b in zip(ny, nx))
    nb3 = tuple(jnp.where(first, a, b) for a, b in zip(nx, ny))
    x2, y2 = jnp.where(first, me.x, 1 - me.x), jnp.where(first, 1 - me.y, me.y)
    x3, y3 = jnp.where(first, 1 - me.x, me.x), jnp.where(first, me.y, 1 - me.y)
    greet([(None, sib), (None, nx), (None, ny), (up_ok, up), (down_ok, down)])
    own = me.index(me.at())

    def part(a, index):
        return outs[a].at[pl.ds(pl.multiple_of(index * rows[a], 8), rows[a])]

    sends = []

    def send(pred, index, dev, mine=False):
        slot = len(sends)
        copies = []
        for a in range(n_arrays):
            copies.append(
                pltpu.make_async_remote_copy(
                    src_ref=ins[a] if mine else part(a, index),
                    dst_ref=part(a, index),
                    send_sem=send_sem.at[slot, a],
                    recv_sem=recv_sem.at[index, a],
                    device_id=dev,
                    device_id_type=MESH,
                )
            )

        def go():
            for cp in copies:
                cp.start()
        if pred is None:
            go()
        else:
            pl.when(pred)(go)
        sends.append((pred, copies))

    def arrive(pred, index, targets):
        def wait():
            for a in range(n_arrays):
                pltpu.make_async_remote_copy(
                    src_ref=part(a, index), dst_ref=part(a, index),
                    send_sem=send_sem.at[0, a], recv_sem=recv_sem.at[index, a],
                    device_id=sib, device_id_type=MESH,
                ).wait_recv()
        if pred is None:
            wait()
        else:
            pl.when(pred)(wait)
        for extra, dev in targets:
            p = pred if extra is None else (extra if pred is None else jnp.logical_and(pred, extra))
            send(p, index, dev)

    for dev, pred in ((up, up_ok), (down, down_ok), (nb2, None), (nb3, None), (sib, None)):
        send(pred, own, dev, mine=True)
    local = [pltpu.make_async_copy(ins[a], part(a, own), local_sem.at[a]) for a in range(n_arrays)]
    for cp in local:
        cp.start()

    def offsets(k):
        return [(None, 0)] if k == 0 else [(z >= k, -k), (z + k < Z, k)]

    def col(k):
        for pred, off in offsets(k):
            fwd = (up_ok, up) if off < 0 else (down_ok, down)
            arrive(pred, me.index(me.at(z=z + off)), [fwd, (None, nb2), (None, nb3), (None, sib)])

    def second(k):
        for pred, off in offsets(k):
            arrive(pred, me.index(me.at(x=x2, y=y2, z=z + off)), [(None, nb3), (None, sib)])

    def third(k):
        for pred, off in offsets(k):
            arrive(pred, me.index(me.at(x=x3, y=y3, z=z + off)), [(None, sib)])

    def fourth(k):
        for pred, off in offsets(k):
            arrive(pred, me.index(me.at(x=1 - me.x, y=1 - me.y, z=z + off)), [(None, sib)])

    for h in range(1, Z + 3):
        if h < Z:
            col(h)
        if 0 <= h - 1 < Z:
            second(h - 1)
        if 0 <= h - 2 < Z:
            third(h - 2)
        if 0 <= h - 3 < Z:
            fourth(h - 3)
    for h in range(Z):
        for xx in (0, 1):
            for yy in (0, 1):
                for pred, off in offsets(h):
                    arrive(pred, me.index(me.at(x=xx, y=yy, c=1 - me.c, z=z + off)), [])
    for cp in local:
        cp.wait()
    for pred, copies in sends:
        def done(copies=copies):
            for cp in copies:
                cp.wait_send()
        if pred is None:
            done()
        else:
            pl.when(pred)(done)


def n_sends(Z):
    return 5 + (Z - 1) * 8 + (2 * Z - 1) * 2 + (2 * Z - 1) * 2


def gather_all(batch, seq, *shards):
    n, count = len(shards), batch * seq
    return pl.pallas_call(
        functools.partial(gather_kernel, batch, seq, n),
        out_shape=[jax.ShapeDtypeStruct((count * a.shape[0],) + a.shape[1:], a.dtype) for a in shards],
        in_specs=[HBM] * n,
        out_specs=[HBM] * n,
        scratch_shapes=[
            pltpu.SemaphoreType.DMA((n,)),
            pltpu.SemaphoreType.DMA((n_sends(seq // 2), n)),
            pltpu.SemaphoreType.DMA((count, n)),
        ],
        compiler_params=pltpu.CompilerParams(collective_id=0, has_side_effects=True),
        name="gather_weights",
    )(*shards)


def reduce_kernel(batch, seq, n_arrays, *refs):
    n = n_arrays
    ins, outs = refs[:n], refs[n : 2 * n]
    work, sib_buf, far_buf, near_buf, line_buf = (refs[(2 + i) * n : (3 + i) * n] for i in range(5))
    load_sem, send_sem, sib_sem, far_sem, near_sem, line_sem = refs[7 * n :]
    me = Place(batch, seq)
    Z, z = me.Z, me.z
    rows = [r.shape[0] for r in outs]
    sib = me.at(c=1 - me.c)
    up, down = me.at(z=z + 1), me.at(z=z - 1)
    nx, ny = me.at(x=1 - me.x), me.at(y=1 - me.y)
    first = me.c == 0
    pick = lambda flag, a, b: jnp.where(flag, a, b)
    near = tuple(pick(first, a, b) for a, b in zip(ny, nx))
    far = tuple(pick(first, a, b) for a, b in zip(nx, ny))
    greet([(None, sib), (None, nx), (None, ny), (z < Z - 1, up), (z > 0, down)])

    def groups(c):
        f = c == 0
        ox, oy = 1 - me.x, 1 - me.y
        return [
            (ox, oy),
            (pick(f, ox, me.x), pick(f, me.y, oy)),
            (pick(f, me.x, ox), pick(f, oy, me.y)),
            (me.x, me.y),
        ]

    def slot(xy, zz):
        return (xy[0] * 2 + xy[1]) * Z + zz

    def turn(k):
        return (z + 1 + k) % Z

    sends = []

    def send(pred, srcs, dsts, recv, dev):
        copies = [
            pltpu.make_async_remote_copy(
                src_ref=srcs[a], dst_ref=dsts[a], send_sem=send_sem.at[len(sends), a],
                recv_sem=recv(a), device_id=dev, device_id_type=MESH)
            for a in range(n)
        ]

        def go():
            for cp in copies:
                cp.start()
        if pred is None:
            go()
        else:
            pl.when(pred)(go)
        sends.append((pred, copies))

    def take(bufs, recv):
        for a in range(n):
            pltpu.make_async_remote_copy(
                src_ref=bufs[a], dst_ref=bufs[a], send_sem=send_sem.at[0, a],
                recv_sem=recv(a), device_id=sib, device_id_type=MESH).wait_recv()

    def source(a, c, xy, zz):
        index = me.index((xy[0] * 2 + c, zz * me.Y + xy[1]))
        return ins[a].at[pl.ds(pl.multiple_of(index * rows[a], 8), rows[a])]

    other = 1 - me.c
    for xy in groups(other):
        for k in range(Z):
            s = slot(xy, turn(k))
            send(None, [source(a, other, xy, turn(k)) for a in range(n)],
                 [sib_buf[a].at[s] for a in range(n)], lambda a, s=s: sib_sem.at[s, a], sib)
    mine = groups(me.c)
    loads = []
    for xy in mine:
        for k in range(Z):
            s = slot(xy, turn(k))
            cps = [pltpu.make_async_copy(source(a, me.c, xy, turn(k)), work[a].at[s], load_sem.at[s, a])
                   for a in range(n)]
            for cp in cps:
                cp.start()
            loads.append(cps)

    def total(bufs):
        t = bufs[0][...].astype(jnp.float32)
        for b in bufs[1:]:
            t = t + b[...].astype(jnp.float32)
        return t

    for g, xy in enumerate(mine):
        for k in range(Z):
            zz = turn(k)
            s = slot(xy, zz)
            for cp in loads[g * Z + k]:
                cp.wait()
            take([sib_buf[a].at[s] for a in range(n)], lambda a: sib_sem.at[s, a])
            parts = [[work[a].at[s], sib_buf[a].at[s]] for a in range(n)]
            if g >= 2:
                fs = (g - 2) * Z + zz
                take([far_buf[a].at[fs] for a in range(n)], lambda a: far_sem.at[fs, a])
                for a in range(n):
                    parts[a].append(far_buf[a].at[fs])
            if g == 3:
                take([near_buf[a].at[zz] for a in range(n)], lambda a: near_sem.at[zz, a])
                for a in range(n):
                    parts[a].append(near_buf[a].at[zz])
            if g < 3:
                for a in range(n):
                    work[a][s] = total(parts[a]).astype(jnp.bfloat16)
                srcs = [work[a].at[s] for a in range(n)]
                if g < 2:
                    fs = g * Z + zz
                    send(None, srcs, [far_buf[a].at[fs] for a in range(n)],
                         lambda a: far_sem.at[fs, a], far)
                else:
                    send(None, srcs, [near_buf[a].at[zz] for a in range(n)],
                         lambda a: near_sem.at[zz, a], near)
                continue
            if k < Z - 1:
                rising = zz > z
                side = jnp.where(rising, 0, 1)
                more = jnp.where(rising, z, Z - 1 - z) > 0
                line = [line_buf[a].at[side, zz] for a in range(n)]
                for a in range(n):
                    work[a][s] = total(parts[a]).astype(jnp.bfloat16)

                @pl.when(more)
                def _():
                    take(line, lambda a: line_sem.at[side, zz, a])
                    for a in range(n):
                        work[a][s] = total([work[a].at[s], line[a]]).astype(jnp.bfloat16)
                dev = (me.at()[0], jnp.where(rising, up[1], down[1]))
                send(None, [work[a].at[s] for a in range(n)], line,
                     lambda a: line_sem.at[side, zz, a], dev)
            else:
                for a in range(n):
                    outs[a][...] = total(parts[a])
                for side, pred in ((0, z > 0), (1, z < Z - 1)):
                    @pl.when(pred)
                    def _(side=side):
                        line = [line_buf[a].at[side, zz] for a in range(n)]
                        take(line, lambda a: line_sem.at[side, zz, a])
                        for a in range(n):
                            outs[a][...] = outs[a][...] + line[a][...].astype(jnp.float32)
    for pred, copies in sends:
        for cp in copies:
            cp.wait_send()


def reduce_all(batch, seq, *sums):
    n, count, Z = len(sums), batch * seq, seq // 2
    shapes = [(a.shape[0] // count,) + a.shape[1:] for a in sums]
    half = count // 2
    scratch = []
    for lead in ((half,), (half,), (2 * Z,), (Z,), (2, Z)):
        scratch += [pltpu.VMEM(lead + s, jnp.bfloat16) for s in shapes]
    n_send = half + 2 * Z + Z + Z
    scratch += [
        pltpu.SemaphoreType.DMA((half, n)),
        pltpu.SemaphoreType.DMA((n_send, n)),
        pltpu.SemaphoreType.DMA((half, n)),
        pltpu.SemaphoreType.DMA((2 * Z, n)),
        pltpu.SemaphoreType.DMA((Z, n)),
        pltpu.SemaphoreType.DMA((2, Z, n)),
    ]
    return pl.pallas_call(
        functools.partial(reduce_kernel, batch, seq, n),
        out_shape=[jax.ShapeDtypeStruct(s, jnp.float32) for s in shapes],
        in_specs=[HBM] * n,
        out_specs=[pl.BlockSpec(memory_space=pltpu.VMEM)] * n,
        scratch_shapes=scratch,
        compiler_params=pltpu.CompilerParams(
            collective_id=1, has_side_effects=True, vmem_limit_bytes=40 << 20),
        name="reduce_grads",
    )(*sums)


def tuned(batch, seq):
    return batch == 4 and seq == 8


def chain_kernel(seq, forward, dsum_ref, rates_ref, end_ref, out_ref, held, outgoing, send_sem, recv_sem):
    s = lax.axis_index("seq")
    b = lax.axis_index("batch")
    step = 1 if forward else -1
    has_before = s > 0 if forward else s < seq - 1
    has_after = s < seq - 1 if forward else s > 0
    before, after = (b, s - step), (b, s + step)
    barrier = pltpu.get_barrier_semaphore()
    for pred, dev in ((has_before, before), (has_after, after)):
        @pl.when(pred)
        def _(dev=dev):
            pl.semaphore_signal(barrier, inc=1, device_id=dev, device_id_type=MESH)
    pl.semaphore_wait(barrier, jnp.where(has_before, 1, 0) + jnp.where(has_after, 1, 0))
    count = end_ref.shape[0]

    def copy(i):
        return pltpu.make_async_remote_copy(
            src_ref=outgoing.at[i], dst_ref=held.at[i], send_sem=send_sem.at[i],
            recv_sem=recv_sem.at[i], device_id=after, device_id_type=MESH)

    for i in range(count):
        @pl.when(has_before)
        def _(i=i):
            copy(i).wait_recv()
            out_ref[i] = held[i].astype(jnp.float32)
            decay = jnp.exp(rates_ref[...] * dsum_ref[i])
            outgoing[i] = (end_ref[i] + decay * out_ref[i]).astype(jnp.bfloat16)

        @pl.when(jnp.logical_not(has_before))
        def _(i=i):
            out_ref[i] = jnp.zeros_like(out_ref[i])
            outgoing[i] = end_ref[i].astype(jnp.bfloat16)

        @pl.when(has_after)
        def _(i=i):
            copy(i).start()
    for i in range(count):
        @pl.when(has_after)
        def _(i=i):
            copy(i).wait_send()


def chain_states(seq, forward, dsum, rates, end):
    vm = pl.BlockSpec(memory_space=pltpu.VMEM)
    return pl.pallas_call(
        functools.partial(chain_kernel, seq, forward),
        out_shape=jax.ShapeDtypeStruct(end.shape, jnp.float32),
        in_specs=[vm] * 3,
        out_specs=vm,
        scratch_shapes=[
            pltpu.VMEM(end.shape, jnp.bfloat16),
            pltpu.VMEM(end.shape, jnp.bfloat16),
            pltpu.SemaphoreType.DMA((end.shape[0],)),
            pltpu.SemaphoreType.DMA((end.shape[0],)),
        ],
        compiler_params=pltpu.CompilerParams(
            collective_id=4 if forward else 5, has_side_effects=True),
        name="chain_forward" if forward else "chain_backward",
    )(dsum, rates, end)


def relay_kernel(seq, forward, states, dsum_ref, vec_ref, end_ref, out_ref, mine, theirs, their_sum, held, outgoing,
                 pair_send, pair_recv, line_send, line_recv):
    me = Place(4, seq)
    y, z, last = me.y, me.z, me.Z - 1
    step = 1 if forward else -1
    first = y == (0 if forward else 1)
    has_before = z > 0 if forward else z < last
    has_after = z < last if forward else z > 0
    pair, before, after = me.at(y=1 - y), me.at(z=z - step), me.at(z=z + step)
    greet([(None, pair), (has_before, before), (has_after, after)])
    count = end_ref.shape[0]
    rates = -jnp.exp(vec_ref[0:states])

    def swaps(i):
        return [
            pltpu.make_async_remote_copy(
                src_ref=src, dst_ref=dst, send_sem=pair_send.at[i, k], recv_sem=pair_recv.at[i, k],
                device_id=pair, device_id_type=MESH)
            for k, (src, dst) in enumerate(((mine.at[i], theirs.at[i]), (dsum_ref.at[i], their_sum.at[i])))
        ]

    def onward(i):
        return pltpu.make_async_remote_copy(
            src_ref=outgoing.at[i], dst_ref=held.at[i], send_sem=line_send.at[i],
            recv_sem=line_recv.at[i], device_id=after, device_id_type=MESH)

    for i in range(count):
        mine[i] = end_ref[i].astype(bf16)
        for cp in swaps(i):
            cp.start()
    for i in range(count):
        for cp in swaps(i):
            cp.wait_recv()
        own, other = end_ref[i], theirs[i].astype(f32)
        own_sum, other_sum = dsum_ref[i], their_sum[i]
        early, late = jnp.where(first, own, other), jnp.where(first, other, own)
        early_sum, late_sum = jnp.where(first, own_sum, other_sum), jnp.where(first, other_sum, own_sum)
        both = late + jnp.exp(rates * late_sum) * early

        @pl.when(has_before)
        def _():
            onward(i).wait_recv()
            arrived = held[i].astype(f32)
            outgoing[i] = (both + jnp.exp(rates * (early_sum + late_sum)) * arrived).astype(bf16)

        @pl.when(jnp.logical_not(has_before))
        def _():
            outgoing[i] = both.astype(bf16)

        @pl.when(has_after)
        def _():
            onward(i).start()

        @pl.when(has_before)
        def _():
            arrived = held[i].astype(f32)
            out_ref[i] = jnp.where(first, arrived, early + jnp.exp(rates * early_sum) * arrived)

        @pl.when(jnp.logical_not(has_before))
        def _():
            out_ref[i] = jnp.where(first, jnp.zeros_like(early), early)
    for i in range(count):
        for cp in swaps(i):
            cp.wait_send()

        @pl.when(has_after)
        def _():
            onward(i).wait_send()


def relay_states(batch, seq, forward, states, dsum, vec, end):
    if not tuned(batch, seq):
        return chain_states(seq, forward, dsum, -jnp.exp(vec[:states]), end)
    n = end.shape[0]
    return pl.pallas_call(
        functools.partial(relay_kernel, seq, forward, states),
        out_shape=jax.ShapeDtypeStruct(end.shape, f32),
        in_specs=[VM] * 3,
        out_specs=VM,
        scratch_shapes=[
            pltpu.VMEM(end.shape, bf16),
            pltpu.VMEM(end.shape, bf16),
            pltpu.VMEM(dsum.shape, f32),
            pltpu.VMEM(end.shape, bf16),
            pltpu.VMEM(end.shape, bf16),
            pltpu.SemaphoreType.DMA((n, 2)),
            pltpu.SemaphoreType.DMA((n, 2)),
            pltpu.SemaphoreType.DMA((n,)),
            pltpu.SemaphoreType.DMA((n,)),
        ],
        compiler_params=pltpu.CompilerParams(
            collective_id=6 if forward else 7, has_side_effects=True),
        name="relay_forward" if forward else "relay_backward",
    )(dsum, vec, end)


def dot(a, b):
    return jnp.dot(a, b, preferred_element_type=jnp.float32)


def dot_nt(a, b):
    return lax.dot_general(a, b, (((1,), (1,)), ((), ())), preferred_element_type=jnp.float32)


def dot_tn(a, b):
    return lax.dot_general(a, b, (((0,), (0,)), ((), ())), preferred_element_type=jnp.float32)


def sigmoid(v):
    return 1.0 / (1.0 + jnp.exp(-v))


def lanes(shape):
    return lax.broadcasted_iota(jnp.int32, shape, 1)


def subs(shape):
    return lax.broadcasted_iota(jnp.int32, shape, 0)


def column(row, base, states):
    shape = (states, row.shape[1])
    only = jnp.where(lanes(shape) == subs(shape) + base, jnp.broadcast_to(row, shape), 0.0)
    return jnp.broadcast_to(jnp.sum(only, axis=1, keepdims=True), shape)


def row_sums(parts):
    row = subs(parts[0].shape)
    four, two, one = row < 4, (row // 2) % 2 == 0, row % 2 == 0
    turn = lambda v, by: pltpu.roll(v, by, axis=0)
    a = [
        jnp.where(four, parts[j], parts[j + 4]) + turn(jnp.where(four, parts[j + 4], parts[j]), 4)
        for j in range(4)
    ]
    b = [jnp.where(two, a[j] + turn(a[j], 6), a[j + 2] + turn(a[j + 2], 2)) for j in range(2)]
    return jnp.where(one, b[0] + turn(b[0], 7), b[1] + turn(b[1], 1))


def fold(v):
    return sum(v[i : i + 8] for i in range(8, v.shape[0], 8)) + v[:8]


WIDE = 256
GROUP = 16
LOG2E = math.log2(math.e)


def conv_sum(ext_ref, s, cols, vec_ref, states, taps, rows):
    first = ext_ref.shape[1] - rows - taps + 1
    total = vec_ref[states + taps : states + taps + 1, cols]
    for k in range(taps):
        total = total + vec_ref[states + k : states + k + 1, cols] * ext_ref[s, first + k : first + k + rows, cols]
    return total


def normalize(x):
    return lax.rsqrt(jnp.mean(x * x, axis=-1, keepdims=True) + epsilon)


def enter_kernel(dims, tok_ref, halo_ref, win_ref, small_ref, vec_ref, gain_ref,
                 ext_ref, z_ref, u_ref, dt_ref, proj_ref, end_ref, dsum_ref, xn):
    seqs, rows, inner, states, rank, taps = dims
    count = seqs * rows
    for ref, at in ((tok_ref, 0), (halo_ref, count)):
        x = ref[...].astype(jnp.float32)
        xn[at : at + x.shape[0]] = (x * normalize(x) * gain_ref[0:1]).astype(jnp.bfloat16)
    proj = jnp.zeros((count, small_ref.shape[1]), jnp.float32)
    for j in range(inner // WIDE):
        cols = slice(j * WIDE, (j + 1) * WIDE)
        part = dot(xn[...], win_ref[:, cols])
        z_ref[:, cols] = dot(xn[:count], win_ref[:, inner + j * WIDE : inner + (j + 1) * WIDE])
        for s in range(seqs):
            ext_ref[s, 0:8, cols] = part[count + 8 * s : count + 8 * s + 8]
            ext_ref[s, 8:, cols] = part[s * rows : (s + 1) * rows]
            pre = conv_sum(ext_ref, s, cols, vec_ref, states, taps, rows)
            u_ref[s * rows : (s + 1) * rows, cols] = pre * sigmoid(pre)
        proj = proj + dot(u_ref[:, cols].astype(jnp.bfloat16), small_ref[cols, :])
    proj_ref[...] = proj
    low = rank_lanes(proj, rank, states)
    for j in range(inner // WIDE):
        cols = slice(j * WIDE, (j + 1) * WIDE)
        pre = dot_nt(low, small_ref[cols, :]) + vec_ref[states + taps + 1 : states + taps + 2, cols]
        dt = jnp.maximum(pre, 0.0) + jnp.log1p(jnp.exp(-jnp.abs(pre)))
        dt_ref[:, cols] = dt
        for s in range(seqs):
            dsum_ref[s, 0:1, cols] = jnp.sum(dt[s * rows : (s + 1) * rows], axis=0, keepdims=True)
    a2 = -jnp.exp(vec_ref[0:states]) * LOG2E
    blocks = inner // 128
    for s in range(seqs):
        def eight(i, hs):
            hs = list(hs)
            at = pl.multiple_of(s * rows + i * 8, 8)
            small = proj_ref[pl.ds(at, 8), :]
            bs = [column(small[j : j + 1], rank, states) for j in range(8)]
            for k in range(blocks):
                sl = slice(k * 128, (k + 1) * 128)
                d8 = dt_ref[pl.ds(at, 8), sl]
                w8 = d8 * u_ref[pl.ds(at, 8), sl]
                for j in range(8):
                    hs[k] = jnp.exp2(d8[j : j + 1] * a2[:, sl]) * hs[k] + bs[j] * w8[j : j + 1]
            return tuple(hs)
        zero = jnp.zeros((states, 128), jnp.float32)
        hs = lax.fori_loop(0, rows // 8, eight, (zero,) * blocks)
        for k in range(blocks):
            end_ref[s, :, k * 128 : (k + 1) * 128] = hs[k]


def rank_lanes(proj, rank, states):
    at = rank + 2 * states
    moved = pltpu.roll(proj, at, axis=1)
    return jnp.where(lanes(proj.shape) >= at, moved, 0.0).astype(jnp.bfloat16)


def leave_kernel(dims, capacity, tok_ref, cot_ref, h0_ref, dt_ref, u_ref, z_ref, proj_ref, vec_ref, out_ref,
                 gain_ref, router_ref, route_ref, slot_ref, place_ref,
                 hist_ref, y_ref, hid_ref, gated_ref, moe_ref, gate_ref, rows_ref,
                 hbuf, hcur, sem, sem0):
    seqs, rows, inner, states, rank, taps = dims
    count = seqs * rows
    a2 = -jnp.exp(vec_ref[0:states]) * LOG2E
    blocks = inner // 128
    groups = rows // GROUP
    size = GROUP * states
    firsts = []
    for s in range(seqs):
        hcur[s] = h0_ref[s].astype(jnp.bfloat16)
        cp = pltpu.make_async_copy(hcur.at[s], hist_ref.at[s, pl.ds(0, states)], sem0.at[s])
        cp.start()
        firsts.append(cp)

    def out_copy(s, g, slot):
        at = pl.multiple_of(states + g * size, states)
        return pltpu.make_async_copy(hbuf.at[slot], hist_ref.at[s, pl.ds(at, size)], sem.at[slot])

    for s in range(seqs):
        def group(g, hs):
            hs = list(hs)
            slot = g % 2

            @pl.when(g >= 2)
            def _():
                out_copy(s, g - 2, slot).wait()
            for half in range(GROUP // 8):
                at = pl.multiple_of(s * rows + g * GROUP + half * 8, 8)
                small = proj_ref[pl.ds(at, 8), :]
                bs = [column(small[j : j + 1], rank, states) for j in range(8)]
                cs = [column(small[j : j + 1], rank + states, states) for j in range(8)]
                for k in range(blocks):
                    sl = slice(k * 128, (k + 1) * 128)
                    d8 = dt_ref[pl.ds(at, 8), sl]
                    w8 = d8 * u_ref[pl.ds(at, 8), sl]
                    parts = []
                    for j in range(8):
                        t = half * 8 + j
                        hs[k] = jnp.exp2(d8[j : j + 1] * a2[:, sl]) * hs[k] + bs[j] * w8[j : j + 1]
                        hbuf[slot, t * states : (t + 1) * states, sl] = hs[k].astype(jnp.bfloat16)
                        parts.append(fold(cs[j] * hs[k]))
                    y_ref[pl.ds(at, 8), sl] = row_sums(parts)
            out_copy(s, g, slot).start()
            return tuple(hs)
        hs = tuple(h0_ref[s, :, k * 128 : (k + 1) * 128] for k in range(blocks))
        lax.fori_loop(0, groups, group, hs)
        for g in (groups - 2, groups - 1):
            out_copy(s, g, g % 2).wait()
    for cp in firsts:
        cp.wait()
    hid = tok_ref[...].astype(jnp.float32)
    for j in range(inner // WIDE):
        cols = slice(j * WIDE, (j + 1) * WIDE)
        y = y_ref[:, cols] + vec_ref[states + taps + 2 : states + taps + 3, cols] * u_ref[:, cols]
        y_ref[:, cols] = y
        z = z_ref[:, cols]
        gated = (y * (z * sigmoid(z))).astype(jnp.bfloat16)
        gated_ref[:, cols] = gated
        hid = hid + dot(gated, out_ref[cols, :])
    hid_ref[...] = hid
    moe_in = (hid * normalize(hid) * gain_ref[1:2]).astype(jnp.bfloat16)
    moe_ref[...] = moe_in
    logits = dot(moe_in, router_ref[...])
    chosen = lanes(logits.shape) == route_ref[...]
    gate = sigmoid(jnp.sum(jnp.where(chosen, logits, 0.0), axis=1, keepdims=True))
    gate_ref[...] = gate
    kept = (slot_ref[...] < capacity).astype(jnp.float32)
    grad_rows = (cot_ref[...].astype(jnp.float32) * (gate * kept)).astype(jnp.bfloat16)
    total = rows_ref.shape[0]
    pick = (subs((total, count)) == place_ref[...]).astype(jnp.bfloat16)
    width = moe_in.shape[1]
    rows_ref[:, :width] = dot(pick, moe_in).astype(jnp.bfloat16)
    rows_ref[:, width:] = dot(pick, grad_rows).astype(jnp.bfloat16)


def erf(x):
    x = jnp.clip(x, -4.0, 4.0)
    x2 = x * x
    top = (-2.72614225801306e-10, 2.77068142495902e-08, -2.10102402082508e-06, -5.69250639462346e-05,
           -7.34990630326855e-04, -2.95459980854025e-03, -1.60960333262415e-02)
    low = (-1.45660718464996e-05, -2.13374055278905e-04, -1.68282697438203e-03, -7.37332916720468e-03,
           -1.42647390514189e-02)
    p = jnp.full_like(x2, top[0])
    for c in top[1:]:
        p = p * x2 + c
    q = jnp.full_like(x2, low[0])
    for c in low[1:]:
        q = q * x2 + c
    return x * p / q


def expert_kernel(rows_ref, up_ref, down_ref, part_ref, dup_ref, ddown_ref):
    width = up_ref.shape[0]
    x, g = rows_ref[:, :width], rows_ref[:, width:]
    hidden = dot(x, up_ref[...])
    half = 0.5 * (1.0 + erf(hidden * math.sqrt(0.5)))
    act = (hidden * half).astype(jnp.bfloat16)
    slope = half + hidden * (jnp.exp(-0.5 * hidden * hidden) * (1.0 / math.sqrt(2.0 * math.pi)))
    part_ref[:, :width] = dot(act, down_ref[...]).astype(jnp.bfloat16)
    grad_hidden = (dot_nt(g, down_ref[...]) * slope).astype(jnp.bfloat16)
    part_ref[:, width:] = dot_nt(grad_hidden, up_ref[...]).astype(jnp.bfloat16)
    ddown, dup = dot_tn(act, g), dot_tn(x, grad_hidden)

    @pl.when(pl.program_id(0) == 0)
    def _():
        dup_ref[...] = dup
        ddown_ref[...] = ddown

    @pl.when(pl.program_id(0) > 0)
    def _():
        dup_ref[...] += dup
        ddown_ref[...] += ddown


def return_kernel(dims, ret_ref, cot_ref, hid_ref, moe_ref, gate_ref, gated_ref, y_ref, u_ref, z_ref, dt_ref,
                  proj_ref, vec_ref, out_ref, gain_ref, router_ref, route_ref, place_ref,
                  block_ref, ghid_ref, gy_ref, gz_ref, dout_ref, drouter_ref, dskip_ref, dgain_ref, adj_ref):
    seqs, rows, inner, states, rank, taps = dims
    count = seqs * rows
    total, width = ret_ref.shape[0], hid_ref.shape[1]
    pick = (lanes((count, total)) == place_ref[...]).astype(jnp.bfloat16)
    result = dot(pick, ret_ref[:, :width])
    hid, gate = hid_ref[...], gate_ref[...]
    block_ref[...] = (hid + gate * result).astype(jnp.bfloat16)
    cot = cot_ref[...].astype(jnp.float32)
    grad_gate = jnp.sum(cot * result, axis=1, keepdims=True)
    wide = (count, router_ref.shape[1])
    grad_logits = jnp.where(lanes(wide) == route_ref[...], grad_gate * gate * (1.0 - gate), 0.0).astype(jnp.bfloat16)
    grad_in = dot(pick, ret_ref[:, width:]) + dot_nt(grad_logits, router_ref[...])
    drouter_ref[...] = dot_tn(moe_ref[...], grad_logits)
    r2 = normalize(hid)
    dgain_ref[...] = jnp.sum(grad_in * (hid * r2), axis=0, keepdims=True)
    scaled = grad_in * gain_ref[1:2]
    grad_hid = cot + r2 * scaled - hid * (r2 * r2 * r2) * jnp.mean(scaled * hid, axis=1, keepdims=True)
    ghid_ref[...] = grad_hid
    branch = grad_hid.astype(jnp.bfloat16)
    for j in range(inner // WIDE):
        cols = slice(j * WIDE, (j + 1) * WIDE)
        dout_ref[cols, :] = dot_tn(gated_ref[:, cols], branch).astype(jnp.bfloat16)
        grad = dot_nt(branch, out_ref[cols, :])
        z = z_ref[:, cols]
        sig = sigmoid(z)
        gy = grad * (z * sig)
        gy_ref[:, cols] = gy
        gz_ref[:, cols] = (grad * y_ref[:, cols] * (sig + z * sig * (1.0 - sig))).astype(jnp.bfloat16)
        dskip_ref[:, cols] = jnp.sum(gy * u_ref[:, cols], axis=0, keepdims=True)
    a2 = -jnp.exp(vec_ref[0:states]) * LOG2E
    blocks = inner // 128
    for s in range(seqs):
        def eight(i, ms):
            ms = list(ms)
            at = pl.multiple_of((s + 1) * rows - 8 - i * 8, 8)
            small = proj_ref[pl.ds(at, 8), :]
            cs = [column(small[j : j + 1], rank + states, states) for j in range(8)]
            for k in range(blocks):
                sl = slice(k * 128, (k + 1) * 128)
                d8, g8 = dt_ref[pl.ds(at, 8), sl], gy_ref[pl.ds(at, 8), sl]
                for j in reversed(range(8)):
                    ms[k] = jnp.exp2(d8[j : j + 1] * a2[:, sl]) * (ms[k] + cs[j] * g8[j : j + 1])
            return tuple(ms)
        zero = jnp.zeros((states, 128), jnp.float32)
        ms = lax.fori_loop(0, rows // 8, eight, (zero,) * blocks)
        for k in range(blocks):
            adj_ref[s, :, k * 128 : (k + 1) * 128] = ms[k]


def back_kernel(dims, tok_ref, halo_ref, ext_ref, hist_ref, later_ref, gy_ref, gz_ref, ghid_ref, u_ref, dt_ref,
                proj_ref, win_ref, small_ref, vec_ref, gain_ref,
                dtok_ref, dhalo_ref, din_ref, dsmall_ref, dvec_ref, dgain_ref,
                hbuf, ccol, bcol, gbsum, gcsum, adj, gdt, gu, gproj, gpad, gm, xn, gpre, sem):
    seqs, rows, inner, states, rank, taps = dims
    count = seqs * rows
    groups = rows // GROUP
    size = GROUP * states
    steps = seqs * groups

    def fetch(i, slot):
        s, g = i // groups, groups - 1 - i % groups
        at = pl.multiple_of(g * size, size)
        return pltpu.make_async_copy(hist_ref.at[s, pl.ds(at, size + states)], hbuf.at[slot], sem.at[slot])

    fetch(0, 0).start()
    dvec_ref[...] = jnp.zeros_like(dvec_ref)
    strip = 512

    def group(i, carry):
        slot = i % 2
        s, g = i // groups, groups - 1 - i % groups

        @pl.when(i + 1 < steps)
        def _():
            fetch(i + 1, 1 - slot).start()

        @pl.when(g == groups - 1)
        def _():
            adj[...] = later_ref[s]
        at = pl.multiple_of(s * rows + g * GROUP, GROUP)
        small = proj_ref[pl.ds(at, GROUP), :]
        for t in range(GROUP):
            ccol[t] = column(small[t : t + 1], rank + states, states)
            bcol[t] = column(small[t : t + 1], rank, states)
            gbsum[t] = jnp.zeros((states, 128), f32)
            gcsum[t] = jnp.zeros((states, 128), f32)
        fetch(i, slot).wait()
        for c0 in range(0, inner, strip):
            sls = [slice(c0 + k, c0 + k + 128) for k in range(0, strip, 128)]
            rates = [-jnp.exp(vec_ref[0:states, sl]) for sl in sls]
            m = [adj[:, sl] for sl in sls]
            dd = [dvec_ref[0:states, sl] for sl in sls]
            for half in reversed(range(GROUP // 8)):
                a8 = pl.multiple_of(at + half * 8, 8)
                d8 = [dt_ref[pl.ds(a8, 8), sl] for sl in sls]
                g8 = [gy_ref[pl.ds(a8, 8), sl] for sl in sls]
                u8 = [u_ref[pl.ds(a8, 8), sl] for sl in sls]
                w8 = [d * u for d, u in zip(d8, u8)]
                r1, r2 = [[None] * 8 for _ in sls], [[None] * 8 for _ in sls]
                for j in reversed(range(8)):
                    t = half * 8 + j
                    gb = gc = 0.0
                    for k, sl in enumerate(sls):
                        d, gy = d8[k][j : j + 1], g8[k][j : j + 1]
                        a = m[k] + ccol[t] * gy
                        m[k] = jnp.exp2(d * (rates[k] * LOG2E)) * a
                        p = m[k] * hbuf[slot, t * states : (t + 1) * states, sl].astype(f32) * rates[k]
                        dd[k] = dd[k] + p * d
                        gb = gb + a * w8[k][j : j + 1]
                        gc = gc + gy * hbuf[slot, (t + 1) * states : (t + 2) * states, sl].astype(f32)
                        r1[k][j], r2[k][j] = fold(p), fold(a * bcol[t])
                    gbsum[t] += gb
                    gcsum[t] += gc
                for k, sl in enumerate(sls):
                    w1, w2 = row_sums(r1[k]), row_sums(r2[k])
                    gdt[pl.ds(a8, 8), sl] = w1 + u8[k] * w2
                    gu[pl.ds(a8, 8), sl] = d8[k] * w2
            for k, sl in enumerate(sls):
                adj[:, sl] = m[k]
                dvec_ref[0:states, sl] = dd[k]
        square = (states, small.shape[1])
        where, entry = lanes(square), subs(square)
        line = subs((GROUP, small.shape[1]))
        out = jnp.zeros(small.shape, f32)
        for t in range(GROUP):
            gb = jnp.broadcast_to(jnp.sum(gbsum[t], axis=1, keepdims=True), square)
            gc = jnp.broadcast_to(jnp.sum(gcsum[t], axis=1, keepdims=True), square)
            put = jnp.where(where == entry + rank, gb, jnp.where(where == entry + rank + states, gc, 0.0))
            out = jnp.where(line == t, jnp.sum(put, axis=0, keepdims=True), out)
        gproj[pl.ds(at, GROUP), :] = out
        return carry
    lax.fori_loop(0, steps, group, 0)

    low = rank_lanes(proj_ref[...], rank, states)
    at = rank + 2 * states
    row = states + taps
    grad_rank = jnp.zeros(proj_ref.shape, jnp.float32)
    for j in range(inner // WIDE):
        cols = slice(j * WIDE, (j + 1) * WIDE)
        pre = dot_nt(low, small_ref[cols, :]) + vec_ref[row + 1 : row + 2, cols]
        grad_pre = gdt[:, cols] * sigmoid(pre)
        dvec_ref[row + 1 : row + 2, cols] = jnp.sum(grad_pre, axis=0, keepdims=True)
        grad_pre = grad_pre.astype(jnp.bfloat16)
        gpre[:, cols] = grad_pre
        grad_rank = grad_rank + dot(grad_pre, small_ref[cols, :])
    where = lanes(grad_rank.shape)
    grad_rank = pltpu.roll(grad_rank, small_ref.shape[1] - at, axis=1)
    grad_proj = jnp.where(where < rank, grad_rank, jnp.where(where < at, gproj[...], 0.0)).astype(jnp.bfloat16)
    for ref, to in ((tok_ref, 0), (halo_ref, count)):
        x = ref[...].astype(jnp.float32)
        xn[to : to + x.shape[0]] = (x * normalize(x) * gain_ref[0:1]).astype(jnp.bfloat16)
    grad_normed = jnp.zeros((gm.shape[0], xn.shape[1]), jnp.float32)
    first = ext_ref.shape[1] - rows - taps + 1
    for j in range(inner // WIDE):
        cols = slice(j * WIDE, (j + 1) * WIDE)
        dsmall_ref[cols, :] = (
            dot_tn(u_ref[:, cols].astype(jnp.bfloat16), grad_proj) + dot_tn(gpre[:, cols], low)
        ).astype(jnp.bfloat16)
        grad_u = dot_nt(grad_proj, small_ref[cols, :]) + gy_ref[:, cols] * vec_ref[row + 2 : row + 3, cols] + gu[:, cols]
        taps_sum = [0.0] * taps
        bias_sum = 0.0
        heads = []
        for s in range(seqs):
            pre = conv_sum(ext_ref, s, cols, vec_ref, states, taps, rows)
            sig = sigmoid(pre)
            grad_conv = grad_u[s * rows : (s + 1) * rows] * (sig + pre * sig * (1.0 - sig))
            bias_sum = bias_sum + jnp.sum(grad_conv, axis=0, keepdims=True)
            for k in range(taps):
                taps_sum[k] = taps_sum[k] + jnp.sum(
                    grad_conv * ext_ref[s, first + k : first + k + rows, cols], axis=0, keepdims=True)
            gpad[0:8] = jnp.zeros((8, WIDE), jnp.float32)
            gpad[8 : 8 + rows] = grad_conv
            gpad[8 + rows :] = jnp.zeros((8, WIDE), jnp.float32)
            grad = 0.0
            for k in range(taps):
                grad = grad + vec_ref[states + k : states + k + 1, cols] * gpad[taps - 1 - k : taps + 7 - k + rows]
            heads.append(grad[0:8])
            gm[s * rows : (s + 1) * rows, cols] = grad[8:].astype(jnp.bfloat16)
        gm[count:, cols] = jnp.concatenate(heads).astype(jnp.bfloat16)
        dvec_ref[row : row + 1, cols] = bias_sum
        for k in range(taps):
            dvec_ref[states + k : states + k + 1, cols] = taps_sum[k]
        zcols = slice(inner + j * WIDE, inner + (j + 1) * WIDE)
        din_ref[:, cols] = dot_tn(xn[...], gm[:, cols]).astype(jnp.bfloat16)
        din_ref[:, zcols] = dot_tn(xn[:count], gz_ref[:, cols]).astype(jnp.bfloat16)
        gz = jnp.concatenate([gz_ref[:, cols], jnp.zeros((gm.shape[0] - count, WIDE), jnp.bfloat16)])
        grad_normed = grad_normed + dot_nt(gm[:, cols], win_ref[:, cols]) + dot_nt(gz, win_ref[:, zcols])
    gain_sum = 0.0
    for ref, to, base, out in ((tok_ref, 0, ghid_ref, dtok_ref), (halo_ref, count, None, dhalo_ref)):
        x = ref[...].astype(jnp.float32)
        r1 = normalize(x)
        grad = grad_normed[to : to + x.shape[0]]
        gain_sum = gain_sum + jnp.sum(grad * (x * r1), axis=0, keepdims=True)
        grad = grad * gain_ref[0:1]
        grad = r1 * grad - x * (r1 * r1 * r1) * jnp.mean(grad * x, axis=1, keepdims=True)
        out[...] = grad if base is None else grad + base[...]
    dgain_ref[...] = gain_sum


def like(*shape, dtype=f32):
    return jax.ShapeDtypeStruct(shape, dtype)


def params(mib=56):
    return pltpu.CompilerParams(vmem_limit_bytes=mib << 20)


def moe_kernel(seq, rows_ref, up_ref, down_ref, back_ref, land_ref, dup_ref, ddown_ref,
               xbuf, part, act, ghid, hid, gact, sib_buf, near_buf, far_sum, own_sum,
               local_sem, disp_sem, pass_sem, recv_sem, load_sem, sib_send, sib_recv, near_send, near_recv,
               final_send, final_recv, final_local):
    me = Place(4, seq)
    b, s = me.at()
    y, z, Z = me.y, me.z, me.Z
    cap, wide = rows_ref.shape[1], rows_ref.shape[2]
    width = wide // 2
    two = 2 * cap
    block = 4 * two
    sib, nx = me.at(c=1 - me.c), me.at(x=1 - me.x)
    near, beside, across = nx[0], sib[0], (1 - me.x) * 2 + 1 - me.c
    greet([(None, sib), (None, nx)] + [(None, (b, (s + k) % seq)) for k in range(1, seq)])

    def remote(src, dst, send, recv, dev):
        return pltpu.make_async_remote_copy(
            src_ref=src, dst_ref=dst, send_sem=send, recv_sem=recv, device_id=dev, device_id_type=MESH)

    def slab(bb, ss):
        return land_ref.at[bb, pl.ds(pl.multiple_of(ss * cap, 8), cap)]

    def there(k, j):
        return ((z + k) % Z) * 2 + j

    def arrived(bb, ss):
        remote(slab(bb, ss), slab(bb, ss), disp_sem.at[0], recv_sem.at[bb, ss], sib).wait_recv()

    def hand_own(ss):
        arrived(b, ss)
        remote(slab(b, ss), slab(b, ss), pass_sem.at[ss, 0], recv_sem.at[b, ss], nx).start()
        remote(slab(b, ss), slab(b, ss), pass_sem.at[ss, 1], recv_sem.at[b, ss], sib).start()

    def hand_near(ss):
        arrived(near, ss)
        remote(slab(near, ss), slab(near, ss), pass_sem.at[ss, 2], recv_sem.at[near, ss], sib).start()

    def load(k, bb):
        zz = (z + k) % Z
        return pltpu.make_async_copy(
            land_ref.at[bb, pl.ds(pl.multiple_of(zz * two, 8), two)],
            xbuf.at[k, pl.ds(pl.multiple_of(bb * two, 16), two)], load_sem.at[k, bb])

    def dispatch(k, j):
        to = ((z + Z - k) % Z) * 2 + j
        return remote(rows_ref.at[to], slab(b, s), disp_sem.at[2 * k + j], recv_sem.at[b, s], (b, to))

    dispatch(0, 1 - y).start()
    own = [remote(rows_ref.at[s], slab(b, s), pass_sem.at[s, i], recv_sem.at[b, s], dev)
           for i, dev in enumerate((nx, sib))]
    for cp in own:
        cp.start()
    local = pltpu.make_async_copy(rows_ref.at[s], slab(b, s), local_sem)
    local.start()
    for k in range(1, Z):
        for j in range(2):
            dispatch(k, j).start()

    hand_own(z * 2 + 1 - y)
    local.wait()
    load(0, b).start()
    for j in range(2):
        hand_near(z * 2 + j)
    load(0, near).start()
    for bb in (beside, across):
        for j in range(2):
            arrived(bb, z * 2 + j)
        load(0, bb).start()

    def compute(k):
        for n in range(0, width, WIDE):
            cols = slice(n, n + WIDE)
            hid[:, cols] = dot(xbuf[k, :, :width], up_ref[:, cols])
            gact[:, cols] = dot_nt(xbuf[k, :, width:], down_ref[cols, :])

        def sixteen(r, carry):
            at = pl.ds(pl.multiple_of(r * 16, 16), 16)
            to = pl.ds(pl.multiple_of(k * block + r * 16, 16), 16)
            h = hid[at, :]
            half = 0.5 * (1.0 + erf(h * math.sqrt(0.5)))
            act[to, :] = (h * half).astype(bf16)
            slope = half + h * (jnp.exp(-0.5 * h * h) * (1.0 / math.sqrt(2.0 * math.pi)))
            ghid[to, :] = (gact[at, :] * slope).astype(bf16)
            return carry
        lax.fori_loop(0, block // 16, sixteen, 0)
        mine = pl.ds(pl.multiple_of(k * block, 16), block)
        for n in range(0, width, WIDE):
            part[k, :, n : n + WIDE] = dot(act[mine, :], down_ref[:, n : n + WIDE]).astype(bf16)
            part[k, :, width + n : width + n + WIDE] = dot_nt(ghid[mine, :], up_ref[n : n + WIDE, :]).astype(bf16)

    def share(k, bb):
        return part.at[k, pl.ds(pl.multiple_of(bb * two, 16), two)]

    def to_sib(k, g):
        xx = me.x if g else 1 - me.x
        return remote(share(k, xx * 2 + 1 - me.c), sib_buf.at[k, g], sib_send.at[k, g], sib_recv.at[k, g], sib)

    def to_near(k):
        return remote(far_sum.at[k], near_buf.at[k], near_send.at[k], near_recv.at[k], nx)

    def join_sib(k):
        to_sib(k, 0).wait_recv()
        far_sum[k] = (share(k, near)[...].astype(f32) + sib_buf[k, 0].astype(f32)).astype(bf16)
        to_near(k).start()

    def to_home(k, j):
        return remote(own_sum.at[k, j], back_ref.at[s], final_send.at[k, j], final_recv.at[s], (b, there(k, j)))

    def keep_home():
        return pltpu.make_async_copy(own_sum.at[0, y], back_ref.at[s], final_local)

    def join_near(k):
        to_sib(k, 1).wait_recv()
        to_near(k).wait_recv()
        total = share(k, b)[...].astype(f32) + sib_buf[k, 1].astype(f32) + near_buf[k].astype(f32)
        for j in range(2):
            own_sum[k, j] = total[j * cap : (j + 1) * cap].astype(bf16)

        def send():
            for j in range(2):
                to_home(k, j).start()
        if isinstance(k, int) and k > 0:
            send()
        else:
            pl.when(k > 0)(send)

            @pl.when(k == 0)
            def _():
                keep_home().start()
                to_home(0, 1 - y).start()

    def step(k, carry):
        @pl.when(k < Z - 1)
        def _():
            for j in range(2):
                hand_own(there(k + 1, j))
        for bb in range(4):
            load(k, bb).wait()
        compute(k)
        for g in range(2):
            to_sib(k, g).start()

        @pl.when(k < Z - 1)
        def _():
            load(k + 1, b).start()
            for j in range(2):
                hand_near(there(k + 1, j))
            load(k + 1, near).start()

        @pl.when(k >= 1)
        def _():
            join_sib(k - 1)

        @pl.when(k >= 2)
        def _():
            join_near(k - 2)

        @pl.when(k < Z - 1)
        def _():
            for bb in (beside, across):
                for j in range(2):
                    arrived(bb, there(k + 1, j))
                load(k + 1, bb).start()
        return carry
    lax.fori_loop(0, Z, step, 0)

    everything = (Z * block, width)
    x, g = xbuf[:, :, :width].reshape(everything), xbuf[:, :, width:].reshape(everything)
    join_near(Z - 2)
    for n in range(0, width, WIDE):
        ddown_ref[n : n + WIDE, :] = dot_tn(act[:, n : n + WIDE], g)
        if n == 0:
            join_sib(Z - 1)
    for n in range(0, width, WIDE):
        if n == WIDE:
            join_near(Z - 1)
        dup_ref[:, n : n + WIDE] = dot_tn(x, ghid[:, n : n + WIDE])

    for k in range(1, seq):
        e = (s + k) % seq
        remote(back_ref.at[e], back_ref.at[e], disp_sem.at[0], final_recv.at[e], sib).wait_recv()
    keep_home().wait()
    dispatch(0, 1 - y).wait_send()
    for cp in own:
        cp.wait_send()
    for j in range(2):
        remote(slab(near, z * 2 + j), slab(near, z * 2 + j), pass_sem.at[z * 2 + j, 2], recv_sem.at[b, 0], sib).wait_send()
    for i in range(2):
        ss = z * 2 + 1 - y
        remote(slab(b, ss), slab(b, ss), pass_sem.at[ss, i], recv_sem.at[b, 0], sib).wait_send()
    to_home(0, 1 - y).wait_send()

    def settle(k, carry):
        for g in range(2):
            to_sib(k, g).wait_send()
        to_near(k).wait_send()

        @pl.when(k > 0)
        def _():
            for j in range(2):
                dispatch(k, j).wait_send()
                to_home(k, j).wait_send()
                ss = there(k, j)
                for i in range(3):
                    remote(slab(b, ss), slab(b, ss), pass_sem.at[ss, i], recv_sem.at[b, 0], sib).wait_send()
        return carry
    lax.fori_loop(0, Z, settle, 0)


def moe_rows(batch, seq, sent, up, down):
    width, hidden_share = up.shape
    capacity, wide = sent.shape[1:]
    block = seq * capacity
    if tuned(batch, seq) and hidden_share == width and capacity % 8 == 0:
        Z, two = seq // 2, 2 * capacity
        dma = pltpu.SemaphoreType.DMA
        out = pl.pallas_call(
            functools.partial(moe_kernel, seq),
            out_shape=[
                like(seq, capacity, wide, dtype=bf16),
                like(batch, block, wide, dtype=bf16),
                like(width, hidden_share),
                like(hidden_share, width),
            ],
            in_specs=[HBM, VM, VM],
            out_specs=[HBM, HBM, VM, VM],
            scratch_shapes=[
                pltpu.VMEM((Z, 4 * two, wide), bf16),
                pltpu.VMEM((Z, 4 * two, wide), bf16),
                pltpu.VMEM((Z * 4 * two, hidden_share), bf16),
                pltpu.VMEM((Z * 4 * two, hidden_share), bf16),
                pltpu.VMEM((4 * two, hidden_share), f32),
                pltpu.VMEM((4 * two, hidden_share), f32),
                pltpu.VMEM((Z, 2, two, wide), bf16),
                pltpu.VMEM((Z, two, wide), bf16),
                pltpu.VMEM((Z, two, wide), bf16),
                pltpu.VMEM((Z, 2, capacity, wide), bf16),
                dma,
                dma((2 * Z,)),
                dma((seq, 3)),
                dma((batch, seq)),
                dma((Z, batch)),
                dma((Z, 2)),
                dma((Z, 2)),
                dma((Z,)),
                dma((Z,)),
                dma((Z, 2)),
                dma((seq,)),
                dma,
            ],
            compiler_params=pltpu.CompilerParams(
                collective_id=2, has_side_effects=True, vmem_limit_bytes=56 << 20),
            name="experts",
        )(sent, up, down)
        return out[0], out[2], out[3]
    mine = lax.all_to_all(sent, "seq", split_axis=0, concat_axis=0, tiled=True)
    rows = lax.all_gather(mine, "batch", axis=0).reshape(batch * block, wide)
    part, d_up, d_down = pl.pallas_call(
        expert_kernel,
        out_shape=[
            like(batch * block, wide, dtype=bf16),
            like(width, hidden_share),
            like(hidden_share, width),
        ],
        grid=(batch,),
        in_specs=[
            pl.BlockSpec((block, wide), lambda i: (i, 0)),
            pl.BlockSpec((width, hidden_share), lambda i: (0, 0)),
            pl.BlockSpec((hidden_share, width), lambda i: (0, 0)),
        ],
        out_specs=[
            pl.BlockSpec((block, wide), lambda i: (i, 0)),
            pl.BlockSpec((width, hidden_share), lambda i: (0, 0)),
            pl.BlockSpec((hidden_share, width), lambda i: (0, 0)),
        ],
        compiler_params=params(),
        name="experts",
    )(rows, up, down)
    part = part.reshape((batch,) + sent.shape)
    mine = lax.psum_scatter(part, "batch", scatter_dimension=0, tiled=False)
    return lax.all_to_all(mine, "seq", split_axis=0, concat_axis=0, tiled=True), d_up, d_down


def body(
    tokens,
    in_proj,
    conv_weight,
    conv_bias,
    state_proj,
    step_proj,
    step_bias,
    decay_log,
    skip_gain,
    out_proj,
    norm_gain,
    moe_gain,
    router_proj,
    expert_up,
    expert_down,
    routes,
    slot_index,
    cotangent,
):
    batch, seq = lax.axis_size("batch"), lax.axis_size("seq")
    both = ("batch", "seq")
    seqs, rows, width = tokens.shape
    count = seqs * rows
    devices = batch * seq
    taps, share = conv_weight.shape
    inner = share * devices
    states, rank = decay_log.shape[0], step_proj.shape[0]
    low_share = norm_gain.shape[0]
    experts = router_proj.shape[1]
    capacity = max(2, 5 * count // (4 * experts))
    dims = (seqs, rows, inner, states, rank, taps)
    tile = 128

    vectors = jnp.concatenate([decay_log, conv_weight, conv_bias[None], step_bias[None], skip_gain[None]])
    features = jnp.concatenate([router_proj, norm_gain[:, None], moe_gain[:, None]], axis=1)
    used = vectors.shape[0]
    room = -(-used // 8) * 8
    tail = jnp.concatenate(
        [
            state_proj,
            step_proj.T,
            jnp.pad(vectors, ((0, room - used), (0, 0))).T,
            jnp.pad(features, ((0, share - low_share), (0, tile - room - features.shape[1]))),
        ],
        axis=1,
    )
    halo = lax.ppermute(tokens[:, rows - taps + 1 :], "seq", [(i, i + 1) for i in range(seq - 1)])
    halo = jnp.pad(halo, ((0, 0), (8 - taps + 1, 0), (0, 0))).reshape(seqs * 8, width)
    if tuned(batch, seq):
        in_full, out_full, tail_full = gather_all(batch, seq, in_proj, out_proj, tail)
    else:
        in_full, out_full, tail_full = (
            lax.all_gather(a, both, axis=0, tiled=True) for a in (in_proj, out_proj, tail)
        )
    small = tail_full[:, :tile]
    vec = tail_full[:, tile : tile + room].T.astype(f32)
    model = tail_full[:, tile + room : tile + room + experts + 2]
    model = model.reshape(devices, share, experts + 2)[:, :low_share].reshape(width, experts + 2)
    gain = model[:, experts:].T.astype(f32)
    router = jnp.pad(model[:, :experts], ((0, 0), (0, tile - experts)))
    tok, cot = tokens.reshape(count, width), cotangent.reshape(count, width)
    route, slot = routes.reshape(count, 1), slot_index.reshape(count, 1)
    place = jnp.where(slot < capacity, route * capacity + slot, -1)

    ext, z, u, dt, proj, end, dsum = pl.pallas_call(
        partial(enter_kernel, dims),
        out_shape=[
            like(seqs, rows + 8, inner),
            like(count, inner),
            like(count, inner),
            like(count, inner),
            like(count, tile),
            like(seqs, states, inner),
            like(seqs, 1, inner),
        ],
        in_specs=[VM] * 6,
        out_specs=[VM] * 7,
        scratch_shapes=[pltpu.VMEM((count + seqs * 8, width), bf16)],
        compiler_params=params(),
        name="enter",
    )(tok, halo, in_full, small, vec, gain)
    before = relay_states(batch, seq, True, states, dsum, vec, end)
    size = GROUP * states
    total = experts * capacity
    hist, y, hid, gated, moe_in, gate, sent = pl.pallas_call(
        partial(leave_kernel, dims, capacity),
        out_shape=[
            like(seqs, (rows + 1) * states, inner, dtype=bf16),
            like(count, inner),
            like(count, width),
            like(count, inner, dtype=bf16),
            like(count, width, dtype=bf16),
            like(count, 1),
            like(total, 2 * width, dtype=bf16),
        ],
        in_specs=[VM] * 14,
        out_specs=[HBM] + [VM] * 6,
        scratch_shapes=[
            pltpu.VMEM((2, size, inner), bf16),
            pltpu.VMEM((seqs, states, inner), bf16),
            pltpu.SemaphoreType.DMA((2,)),
            pltpu.SemaphoreType.DMA((seqs,)),
        ],
        compiler_params=params(),
        name="leave",
    )(tok, cot, before, dt, u, z, proj, vec, out_full, gain, router, route, slot, place.reshape(1, count))

    back, d_up, d_down = moe_rows(
        batch, seq, sent.reshape(experts, capacity, 2 * width), expert_up[0], expert_down[0])
    back = back.reshape(total, 2 * width)

    block_out, ghid, gy, gz, d_out, d_router, d_skip, d_moe, adj = pl.pallas_call(
        partial(return_kernel, dims),
        out_shape=[
            like(count, width, dtype=bf16),
            like(count, width),
            like(count, inner),
            like(count, inner, dtype=bf16),
            like(inner, width, dtype=bf16),
            like(width, tile),
            like(1, inner),
            like(1, width),
            like(seqs, states, inner),
        ],
        in_specs=[VM] * 17,
        out_specs=[VM] * 9,
        compiler_params=params(),
        name="back_experts",
    )(back, cot, hid, moe_in, gate, gated, y, u, z, dt, proj, vec, out_full, gain, router, route, place)
    later = relay_states(batch, seq, False, states, dsum, vec, adj)
    d_tok, d_halo, d_in, d_small, d_vec, d_norm = pl.pallas_call(
        partial(back_kernel, dims),
        out_shape=[
            like(count, width),
            like(seqs * 8, width),
            like(width, 2 * inner, dtype=bf16),
            like(inner, tile, dtype=bf16),
            like(room, inner),
            like(1, width),
        ],
        in_specs=[VM] * 3 + [HBM] + [VM] * 11,
        out_specs=[VM] * 6,
        scratch_shapes=[
            pltpu.VMEM((2, size + states, inner), bf16),
            pltpu.VMEM((GROUP, states, tile), f32),
            pltpu.VMEM((GROUP, states, tile), f32),
            pltpu.VMEM((GROUP, states, tile), f32),
            pltpu.VMEM((GROUP, states, tile), f32),
            pltpu.VMEM((states, inner), f32),
            pltpu.VMEM((count, inner), f32),
            pltpu.VMEM((count, inner), f32),
            pltpu.VMEM((count, tile), f32),
            pltpu.VMEM((rows + 16, WIDE), f32),
            pltpu.VMEM((count + seqs * 8, inner), bf16),
            pltpu.VMEM((count + seqs * 8, width), bf16),
            pltpu.VMEM((count, inner), bf16),
            pltpu.SemaphoreType.DMA((2,)),
        ],
        compiler_params=params(),
        name="back_mixer",
    )(tok, halo, ext, hist, later, gy, gz, ghid, u, dt, proj, in_full, small, vec, gain)

    d_model = jnp.concatenate([d_router[:, :experts], d_norm.T, d_moe.T], axis=1)
    d_model = jnp.pad(
        d_model.reshape(devices, low_share, experts + 2),
        ((0, 0), (0, share - low_share), (0, tile - room - experts - 2)),
    ).reshape(inner, tile - room)
    skip_row = states + taps + 2
    d_vec = d_vec.at[skip_row].set(d_skip[0])
    d_tail = jnp.concatenate([d_small, d_vec.T.astype(bf16), d_model.astype(bf16)], axis=1)
    if tuned(batch, seq):
        s_in, s_out, s_tail = reduce_all(batch, seq, d_in, d_out, d_tail)
    else:
        s_in, s_out, s_tail = (
            lax.psum_scatter(a.astype(f32), both, scatter_dimension=0, tiled=True) for a in (d_in, d_out, d_tail)
        )
    from_next = lax.ppermute(
        d_halo.reshape(seqs, 8, width)[:, 8 - taps + 1 :], "seq", [(i + 1, i) for i in range(seq - 1)]
    )
    d_tok = d_tok.reshape(tokens.shape).at[:, rows - taps + 1 :].add(from_next)
    s_vec = s_tail[:, tile : tile + room].T
    s_model = s_tail[:low_share, tile + room :]
    return (
        block_out.reshape(tokens.shape),
        d_tok,
        s_in,
        s_vec[states : states + taps],
        s_vec[states + taps],
        s_tail[:, : rank + 2 * states],
        s_tail[:, rank + 2 * states : tile].T,
        s_vec[states + taps + 1],
        s_vec[:states],
        s_vec[states + taps + 2],
        s_out,
        s_model[:, experts],
        s_model[:, experts + 1],
        s_model[:, :experts],
        d_up[None],
        d_down[None],
    )


def solution(mesh):
    in_specs = (
        P("batch", "seq", None),
        P(("batch", "seq"), None),
        P(None, ("batch", "seq")),
        P(("batch", "seq")),
        P(("batch", "seq"), None),
        P(None, ("batch", "seq")),
        P(("batch", "seq")),
        P(None, ("batch", "seq")),
        P(("batch", "seq")),
        P(("batch", "seq"), None),
        P(("batch", "seq")),
        P(("batch", "seq")),
        P(("batch", "seq"), None),
        P("seq", None, "batch"),
        P("seq", "batch", None),
        P("batch", "seq"),
        P("batch", "seq"),
        P("batch", "seq", None),
    )
    out_specs = (
        P("batch", "seq", None),
        P("batch", "seq", None),
        P(("batch", "seq"), None),
        P(None, ("batch", "seq")),
        P(("batch", "seq")),
        P(("batch", "seq"), None),
        P(None, ("batch", "seq")),
        P(("batch", "seq")),
        P(None, ("batch", "seq")),
        P(("batch", "seq")),
        P(("batch", "seq"), None),
        P(("batch", "seq")),
        P(("batch", "seq")),
        P(("batch", "seq"), None),
        P("seq", None, "batch"),
        P("seq", "batch", None),
    )
    return jax.shard_map(body, mesh=mesh, in_specs=in_specs, out_specs=out_specs, check_vma=False)
```

```python
from functools import partial
import functools
import math

import jax
import jax.numpy as jnp
from jax import lax
from jax.experimental import pallas as pl
from jax.experimental.pallas import tpu as pltpu
from jax.sharding import PartitionSpec as P

epsilon = 1e-05
MESH = pl.DeviceIdType.MESH
HBM = pl.BlockSpec(memory_space=pl.ANY)
VM = pl.BlockSpec(memory_space=pltpu.VMEM)
bf16, f32 = jnp.bfloat16, jnp.float32


class Place:
    def __init__(self, batch, seq, ydim=2):
        self.batch, self.seq, self.Y = batch, seq, ydim
        self.Z = seq // ydim
        b, s = lax.axis_index("batch"), lax.axis_index("seq")
        self.x, self.c = b // 2, b % 2
        self.z, self.y = s // ydim, s % ydim

    def at(self, x=None, c=None, y=None, z=None):
        pick = lambda v, own: own if v is None else v
        x, c, y, z = pick(x, self.x), pick(c, self.c), pick(y, self.y), pick(z, self.z)
        return (x * 2 + c, z * self.Y + y)

    def index(self, dev):
        return dev[0] * self.seq + dev[1]


def greet(devices):
    barrier = pltpu.get_barrier_semaphore()
    count = 0
    for pred, dev in devices:
        if pred is None:
            pl.semaphore_signal(barrier, inc=1, device_id=dev, device_id_type=MESH)
            count = count + 1
        else:
            @pl.when(pred)
            def _(dev=dev):
                pl.semaphore_signal(barrier, inc=1, device_id=dev, device_id_type=MESH)
            count = count + jnp.where(pred, 1, 0)
    pl.semaphore_wait(barrier, count)


def gather_kernel(batch, seq, n_arrays, *refs):
    ins, outs = refs[:n_arrays], refs[n_arrays : 2 * n_arrays]
    local_sem, send_sem, recv_sem = refs[2 * n_arrays :]
    me = Place(batch, seq)
    Z, z = me.Z, me.z
    rows = [r.shape[0] for r in ins]
    sib = me.at(c=1 - me.c)
    up_ok, down_ok = z < Z - 1, z > 0
    up, down = me.at(z=z + 1), me.at(z=z - 1)
    nx, ny = me.at(x=1 - me.x), me.at(y=1 - me.y)
    first = me.c == 0
    nb2 = tuple(jnp.where(first, a, b) for a, b in zip(ny, nx))
    nb3 = tuple(jnp.where(first, a, b) for a, b in zip(nx, ny))
    x2, y2 = jnp.where(first, me.x, 1 - me.x), jnp.where(first, 1 - me.y, me.y)
    x3, y3 = jnp.where(first, 1 - me.x, me.x), jnp.where(first, me.y, 1 - me.y)
    greet([(None, sib), (None, nx), (None, ny), (up_ok, up), (down_ok, down)])
    own = me.index(me.at())

    def part(a, index):
        return outs[a].at[pl.ds(pl.multiple_of(index * rows[a], 8), rows[a])]

    sends = []

    def send(pred, index, dev, mine=False):
        slot = len(sends)
        copies = []
        for a in range(n_arrays):
            copies.append(
                pltpu.make_async_remote_copy(
                    src_ref=ins[a] if mine else part(a, index),
                    dst_ref=part(a, index),
                    send_sem=send_sem.at[slot, a],
                    recv_sem=recv_sem.at[index, a],
                    device_id=dev,
                    device_id_type=MESH,
                )
            )

        def go():
            for cp in copies:
                cp.start()
        if pred is None:
            go()
        else:
            pl.when(pred)(go)
        sends.append((pred, copies))

    def arrive(pred, index, targets):
        def wait():
            for a in range(n_arrays):
                pltpu.make_async_remote_copy(
                    src_ref=part(a, index), dst_ref=part(a, index),
                    send_sem=send_sem.at[0, a], recv_sem=recv_sem.at[index, a],
                    device_id=sib, device_id_type=MESH,
                ).wait_recv()
        if pred is None:
            wait()
        else:
            pl.when(pred)(wait)
        for extra, dev in targets:
            p = pred if extra is None else (extra if pred is None else jnp.logical_and(pred, extra))
            send(p, index, dev)

    for dev, pred in ((up, up_ok), (down, down_ok), (nb2, None), (nb3, None), (sib, None)):
        send(pred, own, dev, mine=True)
    local = [pltpu.make_async_copy(ins[a], part(a, own), local_sem.at[a]) for a in range(n_arrays)]
    for cp in local:
        cp.start()

    def offsets(k):
        return [(None, 0)] if k == 0 else [(z >= k, -k), (z + k < Z, k)]

    def col(k):
        for pred, off in offsets(k):
            fwd = (up_ok, up) if off < 0 else (down_ok, down)
            arrive(pred, me.index(me.at(z=z + off)), [fwd, (None, nb2), (None, nb3), (None, sib)])

    def second(k):
        for pred, off in offsets(k):
            arrive(pred, me.index(me.at(x=x2, y=y2, z=z + off)), [(None, nb3), (None, sib)])

    def third(k):
        for pred, off in offsets(k):
            arrive(pred, me.index(me.at(x=x3, y=y3, z=z + off)), [(None, sib)])

    def fourth(k):
        for pred, off in offsets(k):
            arrive(pred, me.index(me.at(x=1 - me.x, y=1 - me.y, z=z + off)), [(None, sib)])

    for h in range(1, Z + 3):
        if h < Z:
            col(h)
        if 0 <= h - 1 < Z:
            second(h - 1)
        if 0 <= h - 2 < Z:
            third(h - 2)
        if 0 <= h - 3 < Z:
            fourth(h - 3)
    for h in range(Z):
        for xx in (0, 1):
            for yy in (0, 1):
                for pred, off in offsets(h):
                    arrive(pred, me.index(me.at(x=xx, y=yy, c=1 - me.c, z=z + off)), [])
    for cp in local:
        cp.wait()
    for pred, copies in sends:
        def done(copies=copies):
            for cp in copies:
                cp.wait_send()
        if pred is None:
            done()
        else:
            pl.when(pred)(done)


def n_sends(Z):
    return 5 + (Z - 1) * 8 + (2 * Z - 1) * 2 + (2 * Z - 1) * 2


def gather_all(batch, seq, *shards):
    n, count = len(shards), batch * seq
    return pl.pallas_call(
        functools.partial(gather_kernel, batch, seq, n),
        out_shape=[jax.ShapeDtypeStruct((count * a.shape[0],) + a.shape[1:], a.dtype) for a in shards],
        in_specs=[HBM] * n,
        out_specs=[HBM] * n,
        scratch_shapes=[
            pltpu.SemaphoreType.DMA((n,)),
            pltpu.SemaphoreType.DMA((n_sends(seq // 2), n)),
            pltpu.SemaphoreType.DMA((count, n)),
        ],
        compiler_params=pltpu.CompilerParams(collective_id=0, has_side_effects=True),
        name="gather_weights",
    )(*shards)


def reduce_kernel(batch, seq, n_arrays, *refs):
    n = n_arrays
    ins, outs = refs[:n], refs[n : 2 * n]
    work, sib_buf, far_buf, near_buf, line_buf = (refs[(2 + i) * n : (3 + i) * n] for i in range(5))
    load_sem, send_sem, sib_sem, far_sem, near_sem, line_sem = refs[7 * n :]
    me = Place(batch, seq)
    Z, z = me.Z, me.z
    rows = [r.shape[0] for r in outs]
    sib = me.at(c=1 - me.c)
    up, down = me.at(z=z + 1), me.at(z=z - 1)
    nx, ny = me.at(x=1 - me.x), me.at(y=1 - me.y)
    first = me.c == 0
    pick = lambda flag, a, b: jnp.where(flag, a, b)
    near = tuple(pick(first, a, b) for a, b in zip(ny, nx))
    far = tuple(pick(first, a, b) for a, b in zip(nx, ny))
    greet([(None, sib), (None, nx), (None, ny), (z < Z - 1, up), (z > 0, down)])

    def groups(c):
        f = c == 0
        ox, oy = 1 - me.x, 1 - me.y
        return [
            (ox, oy),
            (pick(f, ox, me.x), pick(f, me.y, oy)),
            (pick(f, me.x, ox), pick(f, oy, me.y)),
            (me.x, me.y),
        ]

    def slot(xy, zz):
        return (xy[0] * 2 + xy[1]) * Z + zz

    def turn(k):
        return (z + 1 + k) % Z

    sends = []

    def send(pred, srcs, dsts, recv, dev):
        copies = [
            pltpu.make_async_remote_copy(
                src_ref=srcs[a], dst_ref=dsts[a], send_sem=send_sem.at[len(sends), a],
                recv_sem=recv(a), device_id=dev, device_id_type=MESH)
            for a in range(n)
        ]

        def go():
            for cp in copies:
                cp.start()
        if pred is None:
            go()
        else:
            pl.when(pred)(go)
        sends.append((pred, copies))

    def take(bufs, recv):
        for a in range(n):
            pltpu.make_async_remote_copy(
                src_ref=bufs[a], dst_ref=bufs[a], send_sem=send_sem.at[0, a],
                recv_sem=recv(a), device_id=sib, device_id_type=MESH).wait_recv()

    def source(a, c, xy, zz):
        index = me.index((xy[0] * 2 + c, zz * me.Y + xy[1]))
        return ins[a].at[pl.ds(pl.multiple_of(index * rows[a], 8), rows[a])]

    other = 1 - me.c
    for xy in groups(other):
        for k in range(Z):
            s = slot(xy, turn(k))
            send(None, [source(a, other, xy, turn(k)) for a in range(n)],
                 [sib_buf[a].at[s] for a in range(n)], lambda a, s=s: sib_sem.at[s, a], sib)
    mine = groups(me.c)
    loads = []
    for xy in mine:
        for k in range(Z):
            s = slot(xy, turn(k))
            cps = [pltpu.make_async_copy(source(a, me.c, xy, turn(k)), work[a].at[s], load_sem.at[s, a])
                   for a in range(n)]
            for cp in cps:
                cp.start()
            loads.append(cps)

    def total(bufs):
        t = bufs[0][...].astype(jnp.float32)
        for b in bufs[1:]:
            t = t + b[...].astype(jnp.float32)
        return t

    for g, xy in enumerate(mine):
        for k in range(Z):
            zz = turn(k)
            s = slot(xy, zz)
            for cp in loads[g * Z + k]:
                cp.wait()
            take([sib_buf[a].at[s] for a in range(n)], lambda a: sib_sem.at[s, a])
            parts = [[work[a].at[s], sib_buf[a].at[s]] for a in range(n)]
            if g >= 2:
                fs = (g - 2) * Z + zz
                take([far_buf[a].at[fs] for a in range(n)], lambda a: far_sem.at[fs, a])
                for a in range(n):
                    parts[a].append(far_buf[a].at[fs])
            if g == 3:
                take([near_buf[a].at[zz] for a in range(n)], lambda a: near_sem.at[zz, a])
                for a in range(n):
                    parts[a].append(near_buf[a].at[zz])
            if g < 3:
                for a in range(n):
                    work[a][s] = total(parts[a]).astype(jnp.bfloat16)
                srcs = [work[a].at[s] for a in range(n)]
                if g < 2:
                    fs = g * Z + zz
                    send(None, srcs, [far_buf[a].at[fs] for a in range(n)],
                         lambda a: far_sem.at[fs, a], far)
                else:
                    send(None, srcs, [near_buf[a].at[zz] for a in range(n)],
                         lambda a: near_sem.at[zz, a], near)
                continue
            if k < Z - 1:
                rising = zz > z
                side = jnp.where(rising, 0, 1)
                more = jnp.where(rising, z, Z - 1 - z) > 0
                line = [line_buf[a].at[side, zz] for a in range(n)]
                for a in range(n):
                    work[a][s] = total(parts[a]).astype(jnp.bfloat16)

                @pl.when(more)
                def _():
                    take(line, lambda a: line_sem.at[side, zz, a])
                    for a in range(n):
                        work[a][s] = total([work[a].at[s], line[a]]).astype(jnp.bfloat16)
                dev = (me.at()[0], jnp.where(rising, up[1], down[1]))
                send(None, [work[a].at[s] for a in range(n)], line,
                     lambda a: line_sem.at[side, zz, a], dev)
            else:
                for a in range(n):
                    outs[a][...] = total(parts[a])
                for side, pred in ((0, z > 0), (1, z < Z - 1)):
                    @pl.when(pred)
                    def _(side=side):
                        line = [line_buf[a].at[side, zz] for a in range(n)]
                        take(line, lambda a: line_sem.at[side, zz, a])
                        for a in range(n):
                            outs[a][...] = outs[a][...] + line[a][...].astype(jnp.float32)
    for pred, copies in sends:
        for cp in copies:
            cp.wait_send()


def reduce_all(batch, seq, *sums):
    n, count, Z = len(sums), batch * seq, seq // 2
    shapes = [(a.shape[0] // count,) + a.shape[1:] for a in sums]
    half = count // 2
    scratch = []
    for lead in ((half,), (half,), (2 * Z,), (Z,), (2, Z)):
        scratch += [pltpu.VMEM(lead + s, jnp.bfloat16) for s in shapes]
    n_send = half + 2 * Z + Z + Z
    scratch += [
        pltpu.SemaphoreType.DMA((half, n)),
        pltpu.SemaphoreType.DMA((n_send, n)),
        pltpu.SemaphoreType.DMA((half, n)),
        pltpu.SemaphoreType.DMA((2 * Z, n)),
        pltpu.SemaphoreType.DMA((Z, n)),
        pltpu.SemaphoreType.DMA((2, Z, n)),
    ]
    return pl.pallas_call(
        functools.partial(reduce_kernel, batch, seq, n),
        out_shape=[jax.ShapeDtypeStruct(s, jnp.float32) for s in shapes],
        in_specs=[HBM] * n,
        out_specs=[pl.BlockSpec(memory_space=pltpu.VMEM)] * n,
        scratch_shapes=scratch,
        compiler_params=pltpu.CompilerParams(
            collective_id=1, has_side_effects=True, vmem_limit_bytes=40 << 20),
        name="reduce_grads",
    )(*sums)


def tuned(batch, seq):
    return batch == 4 and seq == 8


def chain_kernel(seq, forward, dsum_ref, rates_ref, end_ref, out_ref, held, outgoing, send_sem, recv_sem):
    s = lax.axis_index("seq")
    b = lax.axis_index("batch")
    step = 1 if forward else -1
    has_before = s > 0 if forward else s < seq - 1
    has_after = s < seq - 1 if forward else s > 0
    before, after = (b, s - step), (b, s + step)
    barrier = pltpu.get_barrier_semaphore()
    for pred, dev in ((has_before, before), (has_after, after)):
        @pl.when(pred)
        def _(dev=dev):
            pl.semaphore_signal(barrier, inc=1, device_id=dev, device_id_type=MESH)
    pl.semaphore_wait(barrier, jnp.where(has_before, 1, 0) + jnp.where(has_after, 1, 0))
    count = end_ref.shape[0]

    def copy(i):
        return pltpu.make_async_remote_copy(
            src_ref=outgoing.at[i], dst_ref=held.at[i], send_sem=send_sem.at[i],
            recv_sem=recv_sem.at[i], device_id=after, device_id_type=MESH)

    for i in range(count):
        @pl.when(has_before)
        def _(i=i):
            copy(i).wait_recv()
            out_ref[i] = held[i].astype(jnp.float32)
            decay = jnp.exp(rates_ref[...] * dsum_ref[i])
            outgoing[i] = (end_ref[i] + decay * out_ref[i]).astype(jnp.bfloat16)

        @pl.when(jnp.logical_not(has_before))
        def _(i=i):
            out_ref[i] = jnp.zeros_like(out_ref[i])
            outgoing[i] = end_ref[i].astype(jnp.bfloat16)

        @pl.when(has_after)
        def _(i=i):
            copy(i).start()
    for i in range(count):
        @pl.when(has_after)
        def _(i=i):
            copy(i).wait_send()


def chain_states(seq, forward, dsum, rates, end):
    vm = pl.BlockSpec(memory_space=pltpu.VMEM)
    return pl.pallas_call(
        functools.partial(chain_kernel, seq, forward),
        out_shape=jax.ShapeDtypeStruct(end.shape, jnp.float32),
        in_specs=[vm] * 3,
        out_specs=vm,
        scratch_shapes=[
            pltpu.VMEM(end.shape, jnp.bfloat16),
            pltpu.VMEM(end.shape, jnp.bfloat16),
            pltpu.SemaphoreType.DMA((end.shape[0],)),
            pltpu.SemaphoreType.DMA((end.shape[0],)),
        ],
        compiler_params=pltpu.CompilerParams(
            collective_id=4 if forward else 5, has_side_effects=True),
        name="chain_forward" if forward else "chain_backward",
    )(dsum, rates, end)


def relay_kernel(seq, forward, states, dsum_ref, vec_ref, end_ref, out_ref, mine, theirs, their_sum, held, outgoing,
                 pair_send, pair_recv, line_send, line_recv):
    me = Place(4, seq)
    y, z, last = me.y, me.z, me.Z - 1
    step = 1 if forward else -1
    first = y == (0 if forward else 1)
    has_before = z > 0 if forward else z < last
    has_after = z < last if forward else z > 0
    pair, before, after = me.at(y=1 - y), me.at(z=z - step), me.at(z=z + step)
    greet([(None, pair), (has_before, before), (has_after, after)])
    count = end_ref.shape[0]
    rates = -jnp.exp(vec_ref[0:states])

    def swaps(i):
        return [
            pltpu.make_async_remote_copy(
                src_ref=src, dst_ref=dst, send_sem=pair_send.at[i, k], recv_sem=pair_recv.at[i, k],
                device_id=pair, device_id_type=MESH)
            for k, (src, dst) in enumerate(((mine.at[i], theirs.at[i]), (dsum_ref.at[i], their_sum.at[i])))
        ]

    def onward(i):
        return pltpu.make_async_remote_copy(
            src_ref=outgoing.at[i], dst_ref=held.at[i], send_sem=line_send.at[i],
            recv_sem=line_recv.at[i], device_id=after, device_id_type=MESH)

    for i in range(count):
        mine[i] = end_ref[i].astype(bf16)
        for cp in swaps(i):
            cp.start()
    for i in range(count):
        for cp in swaps(i):
            cp.wait_recv()
        own, other = end_ref[i], theirs[i].astype(f32)
        own_sum, other_sum = dsum_ref[i], their_sum[i]
        early, late = jnp.where(first, own, other), jnp.where(first, other, own)
        early_sum, late_sum = jnp.where(first, own_sum, other_sum), jnp.where(first, other_sum, own_sum)
        both = late + jnp.exp(rates * late_sum) * early

        @pl.when(has_before)
        def _():
            onward(i).wait_recv()
            arrived = held[i].astype(f32)
            outgoing[i] = (both + jnp.exp(rates * (early_sum + late_sum)) * arrived).astype(bf16)

        @pl.when(jnp.logical_not(has_before))
        def _():
            outgoing[i] = both.astype(bf16)

        @pl.when(has_after)
        def _():
            onward(i).start()

        @pl.when(has_before)
        def _():
            arrived = held[i].astype(f32)
            out_ref[i] = jnp.where(first, arrived, early + jnp.exp(rates * early_sum) * arrived)

        @pl.when(jnp.logical_not(has_before))
        def _():
            out_ref[i] = jnp.where(first, jnp.zeros_like(early), early)
    for i in range(count):
        for cp in swaps(i):
            cp.wait_send()

        @pl.when(has_after)
        def _():
            onward(i).wait_send()


def relay_states(batch, seq, forward, states, dsum, vec, end):
    if not tuned(batch, seq):
        return chain_states(seq, forward, dsum, -jnp.exp(vec[:states]), end)
    n = end.shape[0]
    return pl.pallas_call(
        functools.partial(relay_kernel, seq, forward, states),
        out_shape=jax.ShapeDtypeStruct(end.shape, f32),
        in_specs=[VM] * 3,
        out_specs=VM,
        scratch_shapes=[
            pltpu.VMEM(end.shape, bf16),
            pltpu.VMEM(end.shape, bf16),
            pltpu.VMEM(dsum.shape, f32),
            pltpu.VMEM(end.shape, bf16),
            pltpu.VMEM(end.shape, bf16),
            pltpu.SemaphoreType.DMA((n, 2)),
            pltpu.SemaphoreType.DMA((n, 2)),
            pltpu.SemaphoreType.DMA((n,)),
            pltpu.SemaphoreType.DMA((n,)),
        ],
        compiler_params=pltpu.CompilerParams(
            collective_id=6 if forward else 7, has_side_effects=True),
        name="relay_forward" if forward else "relay_backward",
    )(dsum, vec, end)


def dot(a, b):
    return jnp.dot(a, b, preferred_element_type=jnp.float32)


def dot_nt(a, b):
    return lax.dot_general(a, b, (((1,), (1,)), ((), ())), preferred_element_type=jnp.float32)


def dot_tn(a, b):
    return lax.dot_general(a, b, (((0,), (0,)), ((), ())), preferred_element_type=jnp.float32)


def sigmoid(v):
    return 1.0 / (1.0 + jnp.exp(-v))


def lanes(shape):
    return lax.broadcasted_iota(jnp.int32, shape, 1)


def subs(shape):
    return lax.broadcasted_iota(jnp.int32, shape, 0)


def column(row, base, states):
    shape = (states, row.shape[1])
    only = jnp.where(lanes(shape) == subs(shape) + base, jnp.broadcast_to(row, shape), 0.0)
    return jnp.broadcast_to(jnp.sum(only, axis=1, keepdims=True), shape)


def row_sums(parts):
    row = subs(parts[0].shape)
    four, two, one = row < 4, (row // 2) % 2 == 0, row % 2 == 0
    turn = lambda v, by: pltpu.roll(v, by, axis=0)
    a = [
        jnp.where(four, parts[j], parts[j + 4]) + turn(jnp.where(four, parts[j + 4], parts[j]), 4)
        for j in range(4)
    ]
    b = [jnp.where(two, a[j] + turn(a[j], 6), a[j + 2] + turn(a[j + 2], 2)) for j in range(2)]
    return jnp.where(one, b[0] + turn(b[0], 7), b[1] + turn(b[1], 1))


def fold(v):
    return sum(v[i : i + 8] for i in range(8, v.shape[0], 8)) + v[:8]


WIDE = 256
GROUP = 16
LOG2E = math.log2(math.e)


def conv_sum(ext_ref, s, cols, vec_ref, states, taps, rows):
    first = ext_ref.shape[1] - rows - taps + 1
    total = vec_ref[states + taps : states + taps + 1, cols]
    for k in range(taps):
        total = total + vec_ref[states + k : states + k + 1, cols] * ext_ref[s, first + k : first + k + rows, cols]
    return total


def normalize(x):
    return lax.rsqrt(jnp.mean(x * x, axis=-1, keepdims=True) + epsilon)


def enter_kernel(dims, tok_ref, halo_ref, win_ref, small_ref, vec_ref, gain_ref,
                 ext_ref, z_ref, u_ref, dt_ref, proj_ref, end_ref, dsum_ref, xn):
    seqs, rows, inner, states, rank, taps = dims
    count = seqs * rows
    for ref, at in ((tok_ref, 0), (halo_ref, count)):
        x = ref[...].astype(jnp.float32)
        xn[at : at + x.shape[0]] = (x * normalize(x) * gain_ref[0:1]).astype(jnp.bfloat16)
    proj = jnp.zeros((count, small_ref.shape[1]), jnp.float32)
    for j in range(inner // WIDE):
        cols = slice(j * WIDE, (j + 1) * WIDE)
        part = dot(xn[...], win_ref[:, cols])
        z_ref[:, cols] = dot(xn[:count], win_ref[:, inner + j * WIDE : inner + (j + 1) * WIDE])
        for s in range(seqs):
            ext_ref[s, 0:8, cols] = part[count + 8 * s : count + 8 * s + 8]
            ext_ref[s, 8:, cols] = part[s * rows : (s + 1) * rows]
            pre = conv_sum(ext_ref, s, cols, vec_ref, states, taps, rows)
            u_ref[s * rows : (s + 1) * rows, cols] = pre * sigmoid(pre)
        proj = proj + dot(u_ref[:, cols].astype(jnp.bfloat16), small_ref[cols, :])
    proj_ref[...] = proj
    low = rank_lanes(proj, rank, states)
    for j in range(inner // WIDE):
        cols = slice(j * WIDE, (j + 1) * WIDE)
        pre = dot_nt(low, small_ref[cols, :]) + vec_ref[states + taps + 1 : states + taps + 2, cols]
        dt = jnp.maximum(pre, 0.0) + jnp.log1p(jnp.exp(-jnp.abs(pre)))
        dt_ref[:, cols] = dt
        for s in range(seqs):
            dsum_ref[s, 0:1, cols] = jnp.sum(dt[s * rows : (s + 1) * rows], axis=0, keepdims=True)
    a2 = -jnp.exp(vec_ref[0:states]) * LOG2E
    blocks = inner // 128
    for s in range(seqs):
        def eight(i, hs):
            hs = list(hs)
            at = pl.multiple_of(s * rows + i * 8, 8)
            small = proj_ref[pl.ds(at, 8), :]
            bs = [column(small[j : j + 1], rank, states) for j in range(8)]
            for k in range(blocks):
                sl = slice(k * 128, (k + 1) * 128)
                d8 = dt_ref[pl.ds(at, 8), sl]
                w8 = d8 * u_ref[pl.ds(at, 8), sl]
                for j in range(8):
                    hs[k] = jnp.exp2(d8[j : j + 1] * a2[:, sl]) * hs[k] + bs[j] * w8[j : j + 1]
            return tuple(hs)
        zero = jnp.zeros((states, 128), jnp.float32)
        hs = lax.fori_loop(0, rows // 8, eight, (zero,) * blocks)
        for k in range(blocks):
            end_ref[s, :, k * 128 : (k + 1) * 128] = hs[k]


def rank_lanes(proj, rank, states):
    at = rank + 2 * states
    moved = pltpu.roll(proj, at, axis=1)
    return jnp.where(lanes(proj.shape) >= at, moved, 0.0).astype(jnp.bfloat16)


def leave_kernel(dims, capacity, tok_ref, cot_ref, h0_ref, dt_ref, u_ref, z_ref, proj_ref, vec_ref, out_ref,
                 gain_ref, router_ref, route_ref, slot_ref, place_ref,
                 hist_ref, y_ref, hid_ref, gated_ref, moe_ref, gate_ref, rows_ref,
                 hbuf, hcur, sem, sem0):
    seqs, rows, inner, states, rank, taps = dims
    count = seqs * rows
    a2 = -jnp.exp(vec_ref[0:states]) * LOG2E
    blocks = inner // 128
    groups = rows // GROUP
    size = GROUP * states
    firsts = []
    for s in range(seqs):
        hcur[s] = h0_ref[s].astype(jnp.bfloat16)
        cp = pltpu.make_async_copy(hcur.at[s], hist_ref.at[s, pl.ds(0, states)], sem0.at[s])
        cp.start()
        firsts.append(cp)

    def out_copy(s, g, slot):
        at = pl.multiple_of(states + g * size, states)
        return pltpu.make_async_copy(hbuf.at[slot], hist_ref.at[s, pl.ds(at, size)], sem.at[slot])

    for s in range(seqs):
        def group(g, hs):
            hs = list(hs)
            slot = g % 2

            @pl.when(g >= 2)
            def _():
                out_copy(s, g - 2, slot).wait()
            for half in range(GROUP // 8):
                at = pl.multiple_of(s * rows + g * GROUP + half * 8, 8)
                small = proj_ref[pl.ds(at, 8), :]
                bs = [column(small[j : j + 1], rank, states) for j in range(8)]
                cs = [column(small[j : j + 1], rank + states, states) for j in range(8)]
                for k in range(blocks):
                    sl = slice(k * 128, (k + 1) * 128)
                    d8 = dt_ref[pl.ds(at, 8), sl]
                    w8 = d8 * u_ref[pl.ds(at, 8), sl]
                    parts = []
                    for j in range(8):
                        t = half * 8 + j
                        hs[k] = jnp.exp2(d8[j : j + 1] * a2[:, sl]) * hs[k] + bs[j] * w8[j : j + 1]
                        hbuf[slot, t * states : (t + 1) * states, sl] = hs[k].astype(jnp.bfloat16)
                        parts.append(fold(cs[j] * hs[k]))
                    y_ref[pl.ds(at, 8), sl] = row_sums(parts)
            out_copy(s, g, slot).start()
            return tuple(hs)
        hs = tuple(h0_ref[s, :, k * 128 : (k + 1) * 128] for k in range(blocks))
        lax.fori_loop(0, groups, group, hs)
        for g in (groups - 2, groups - 1):
            out_copy(s, g, g % 2).wait()
    for cp in firsts:
        cp.wait()
    hid = tok_ref[...].astype(jnp.float32)
    for j in range(inner // WIDE):
        cols = slice(j * WIDE, (j + 1) * WIDE)
        y = y_ref[:, cols] + vec_ref[states + taps + 2 : states + taps + 3, cols] * u_ref[:, cols]
        y_ref[:, cols] = y
        z = z_ref[:, cols]
        gated = (y * (z * sigmoid(z))).astype(jnp.bfloat16)
        gated_ref[:, cols] = gated
        hid = hid + dot(gated, out_ref[cols, :])
    hid_ref[...] = hid
    moe_in = (hid * normalize(hid) * gain_ref[1:2]).astype(jnp.bfloat16)
    moe_ref[...] = moe_in
    logits = dot(moe_in, router_ref[...])
    chosen = lanes(logits.shape) == route_ref[...]
    gate = sigmoid(jnp.sum(jnp.where(chosen, logits, 0.0), axis=1, keepdims=True))
    gate_ref[...] = gate
    kept = (slot_ref[...] < capacity).astype(jnp.float32)
    grad_rows = (cot_ref[...].astype(jnp.float32) * (gate * kept)).astype(jnp.bfloat16)
    total = rows_ref.shape[0]
    pick = (subs((total, count)) == place_ref[...]).astype(jnp.bfloat16)
    width = moe_in.shape[1]
    rows_ref[:, :width] = dot(pick, moe_in).astype(jnp.bfloat16)
    rows_ref[:, width:] = dot(pick, grad_rows).astype(jnp.bfloat16)


def erf(x):
    x = jnp.clip(x, -4.0, 4.0)
    x2 = x * x
    top = (-2.72614225801306e-10, 2.77068142495902e-08, -2.10102402082508e-06, -5.69250639462346e-05,
           -7.34990630326855e-04, -2.95459980854025e-03, -1.60960333262415e-02)
    low = (-1.45660718464996e-05, -2.13374055278905e-04, -1.68282697438203e-03, -7.37332916720468e-03,
           -1.42647390514189e-02)
    p = jnp.full_like(x2, top[0])
    for c in top[1:]:
        p = p * x2 + c
    q = jnp.full_like(x2, low[0])
    for c in low[1:]:
        q = q * x2 + c
    return x * p / q


def expert_kernel(rows_ref, up_ref, down_ref, part_ref, dup_ref, ddown_ref):
    width = up_ref.shape[0]
    x, g = rows_ref[:, :width], rows_ref[:, width:]
    hidden = dot(x, up_ref[...])
    half = 0.5 * (1.0 + erf(hidden * math.sqrt(0.5)))
    act = (hidden * half).astype(jnp.bfloat16)
    slope = half + hidden * (jnp.exp(-0.5 * hidden * hidden) * (1.0 / math.sqrt(2.0 * math.pi)))
    part_ref[:, :width] = dot(act, down_ref[...]).astype(jnp.bfloat16)
    grad_hidden = (dot_nt(g, down_ref[...]) * slope).astype(jnp.bfloat16)
    part_ref[:, width:] = dot_nt(grad_hidden, up_ref[...]).astype(jnp.bfloat16)
    ddown, dup = dot_tn(act, g), dot_tn(x, grad_hidden)

    @pl.when(pl.program_id(0) == 0)
    def _():
        dup_ref[...] = dup
        ddown_ref[...] = ddown

    @pl.when(pl.program_id(0) > 0)
    def _():
        dup_ref[...] += dup
        ddown_ref[...] += ddown


def return_kernel(dims, ret_ref, cot_ref, hid_ref, moe_ref, gate_ref, gated_ref, y_ref, u_ref, z_ref, dt_ref,
                  proj_ref, vec_ref, out_ref, gain_ref, router_ref, route_ref, place_ref,
                  block_ref, ghid_ref, gy_ref, gz_ref, dout_ref, drouter_ref, dskip_ref, dgain_ref, adj_ref):
    seqs, rows, inner, states, rank, taps = dims
    count = seqs * rows
    total, width = ret_ref.shape[0], hid_ref.shape[1]
    pick = (lanes((count, total)) == place_ref[...]).astype(jnp.bfloat16)
    result = dot(pick, ret_ref[:, :width])
    hid, gate = hid_ref[...], gate_ref[...]
    block_ref[...] = (hid + gate * result).astype(jnp.bfloat16)
    cot = cot_ref[...].astype(jnp.float32)
    grad_gate = jnp.sum(cot * result, axis=1, keepdims=True)
    wide = (count, router_ref.shape[1])
    grad_logits = jnp.where(lanes(wide) == route_ref[...], grad_gate * gate * (1.0 - gate), 0.0).astype(jnp.bfloat16)
    grad_in = dot(pick, ret_ref[:, width:]) + dot_nt(grad_logits, router_ref[...])
    drouter_ref[...] = dot_tn(moe_ref[...], grad_logits)
    r2 = normalize(hid)
    dgain_ref[...] = jnp.sum(grad_in * (hid * r2), axis=0, keepdims=True)
    scaled = grad_in * gain_ref[1:2]
    grad_hid = cot + r2 * scaled - hid * (r2 * r2 * r2) * jnp.mean(scaled * hid, axis=1, keepdims=True)
    ghid_ref[...] = grad_hid
    branch = grad_hid.astype(jnp.bfloat16)
    for j in range(inner // WIDE):
        cols = slice(j * WIDE, (j + 1) * WIDE)
        dout_ref[cols, :] = dot_tn(gated_ref[:, cols], branch).astype(jnp.bfloat16)
        grad = dot_nt(branch, out_ref[cols, :])
        z = z_ref[:, cols]
        sig = sigmoid(z)
        gy = grad * (z * sig)
        gy_ref[:, cols] = gy
        gz_ref[:, cols] = (grad * y_ref[:, cols] * (sig + z * sig * (1.0 - sig))).astype(jnp.bfloat16)
        dskip_ref[:, cols] = jnp.sum(gy * u_ref[:, cols], axis=0, keepdims=True)
    a2 = -jnp.exp(vec_ref[0:states]) * LOG2E
    blocks = inner // 128
    for s in range(seqs):
        def eight(i, ms):
            ms = list(ms)
            at = pl.multiple_of((s + 1) * rows - 8 - i * 8, 8)
            small = proj_ref[pl.ds(at, 8), :]
            cs = [column(small[j : j + 1], rank + states, states) for j in range(8)]
            for k in range(blocks):
                sl = slice(k * 128, (k + 1) * 128)
                d8, g8 = dt_ref[pl.ds(at, 8), sl], gy_ref[pl.ds(at, 8), sl]
                for j in reversed(range(8)):
                    ms[k] = jnp.exp2(d8[j : j + 1] * a2[:, sl]) * (ms[k] + cs[j] * g8[j : j + 1])
            return tuple(ms)
        zero = jnp.zeros((states, 128), jnp.float32)
        ms = lax.fori_loop(0, rows // 8, eight, (zero,) * blocks)
        for k in range(blocks):
            adj_ref[s, :, k * 128 : (k + 1) * 128] = ms[k]


def back_kernel(dims, tok_ref, halo_ref, ext_ref, hist_ref, later_ref, gy_ref, gz_ref, ghid_ref, u_ref, dt_ref,
                proj_ref, win_ref, small_ref, vec_ref, gain_ref,
                dtok_ref, dhalo_ref, din_ref, dsmall_ref, dvec_ref, dgain_ref,
                hbuf, ccol, bcol, gbsum, gcsum, adj, gdt, gu, gproj, gpad, gm, xn, gpre, sem):
    seqs, rows, inner, states, rank, taps = dims
    count = seqs * rows
    groups = rows // GROUP
    size = GROUP * states
    steps = seqs * groups

    def fetch(i, slot):
        s, g = i // groups, groups - 1 - i % groups
        at = pl.multiple_of(g * size, size)
        return pltpu.make_async_copy(hist_ref.at[s, pl.ds(at, size + states)], hbuf.at[slot], sem.at[slot])

    fetch(0, 0).start()
    dvec_ref[...] = jnp.zeros_like(dvec_ref)
    strip = 512

    def group(i, carry):
        slot = i % 2
        s, g = i // groups, groups - 1 - i % groups

        @pl.when(i + 1 < steps)
        def _():
            fetch(i + 1, 1 - slot).start()

        @pl.when(g == groups - 1)
        def _():
            adj[...] = later_ref[s]
        at = pl.multiple_of(s * rows + g * GROUP, GROUP)
        small = proj_ref[pl.ds(at, GROUP), :]
        for t in range(GROUP):
            ccol[t] = column(small[t : t + 1], rank + states, states)
            bcol[t] = column(small[t : t + 1], rank, states)
            gbsum[t] = jnp.zeros((states, 128), f32)
            gcsum[t] = jnp.zeros((states, 128), f32)
        fetch(i, slot).wait()
        for c0 in range(0, inner, strip):
            sls = [slice(c0 + k, c0 + k + 128) for k in range(0, strip, 128)]
            rates = [-jnp.exp(vec_ref[0:states, sl]) for sl in sls]
            m = [adj[:, sl] for sl in sls]
            dd = [dvec_ref[0:states, sl] for sl in sls]
            for half in reversed(range(GROUP // 8)):
                a8 = pl.multiple_of(at + half * 8, 8)
                d8 = [dt_ref[pl.ds(a8, 8), sl] for sl in sls]
                g8 = [gy_ref[pl.ds(a8, 8), sl] for sl in sls]
                u8 = [u_ref[pl.ds(a8, 8), sl] for sl in sls]
                w8 = [d * u for d, u in zip(d8, u8)]
                r1, r2 = [[None] * 8 for _ in sls], [[None] * 8 for _ in sls]
                for j in reversed(range(8)):
                    t = half * 8 + j
                    gb = gc = 0.0
                    for k, sl in enumerate(sls):
                        d, gy = d8[k][j : j + 1], g8[k][j : j + 1]
                        a = m[k] + ccol[t] * gy
                        m[k] = jnp.exp2(d * (rates[k] * LOG2E)) * a
                        p = m[k] * hbuf[slot, t * states : (t + 1) * states, sl].astype(f32) * rates[k]
                        dd[k] = dd[k] + p * d
                        gb = gb + a * w8[k][j : j + 1]
                        gc = gc + gy * hbuf[slot, (t + 1) * states : (t + 2) * states, sl].astype(f32)
                        r1[k][j], r2[k][j] = fold(p), fold(a * bcol[t])
                    gbsum[t] += gb
                    gcsum[t] += gc
                for k, sl in enumerate(sls):
                    w1, w2 = row_sums(r1[k]), row_sums(r2[k])
                    gdt[pl.ds(a8, 8), sl] = w1 + u8[k] * w2
                    gu[pl.ds(a8, 8), sl] = d8[k] * w2
            for k, sl in enumerate(sls):
                adj[:, sl] = m[k]
                dvec_ref[0:states, sl] = dd[k]
        square = (states, small.shape[1])
        where, entry = lanes(square), subs(square)
        line = subs((GROUP, small.shape[1]))
        out = jnp.zeros(small.shape, f32)
        for t in range(GROUP):
            gb = jnp.broadcast_to(jnp.sum(gbsum[t], axis=1, keepdims=True), square)
            gc = jnp.broadcast_to(jnp.sum(gcsum[t], axis=1, keepdims=True), square)
            put = jnp.where(where == entry + rank, gb, jnp.where(where == entry + rank + states, gc, 0.0))
            out = jnp.where(line == t, jnp.sum(put, axis=0, keepdims=True), out)
        gproj[pl.ds(at, GROUP), :] = out
        return carry
    lax.fori_loop(0, steps, group, 0)

    low = rank_lanes(proj_ref[...], rank, states)
    at = rank + 2 * states
    row = states + taps
    grad_rank = jnp.zeros(proj_ref.shape, jnp.float32)
    for j in range(inner // WIDE):
        cols = slice(j * WIDE, (j + 1) * WIDE)
        pre = dot_nt(low, small_ref[cols, :]) + vec_ref[row + 1 : row + 2, cols]
        grad_pre = gdt[:, cols] * sigmoid(pre)
        dvec_ref[row + 1 : row + 2, cols] = jnp.sum(grad_pre, axis=0, keepdims=True)
        grad_pre = grad_pre.astype(jnp.bfloat16)
        gpre[:, cols] = grad_pre
        grad_rank = grad_rank + dot(grad_pre, small_ref[cols, :])
    where = lanes(grad_rank.shape)
    grad_rank = pltpu.roll(grad_rank, small_ref.shape[1] - at, axis=1)
    grad_proj = jnp.where(where < rank, grad_rank, jnp.where(where < at, gproj[...], 0.0)).astype(jnp.bfloat16)
    for ref, to in ((tok_ref, 0), (halo_ref, count)):
        x = ref[...].astype(jnp.float32)
        xn[to : to + x.shape[0]] = (x * normalize(x) * gain_ref[0:1]).astype(jnp.bfloat16)
    grad_normed = jnp.zeros((gm.shape[0], xn.shape[1]), jnp.float32)
    first = ext_ref.shape[1] - rows - taps + 1
    for j in range(inner // WIDE):
        cols = slice(j * WIDE, (j + 1) * WIDE)
        dsmall_ref[cols, :] = (
            dot_tn(u_ref[:, cols].astype(jnp.bfloat16), grad_proj) + dot_tn(gpre[:, cols], low)
        ).astype(jnp.bfloat16)
        grad_u = dot_nt(grad_proj, small_ref[cols, :]) + gy_ref[:, cols] * vec_ref[row + 2 : row + 3, cols] + gu[:, cols]
        taps_sum = [0.0] * taps
        bias_sum = 0.0
        heads = []
        for s in range(seqs):
            pre = conv_sum(ext_ref, s, cols, vec_ref, states, taps, rows)
            sig = sigmoid(pre)
            grad_conv = grad_u[s * rows : (s + 1) * rows] * (sig + pre * sig * (1.0 - sig))
            bias_sum = bias_sum + jnp.sum(grad_conv, axis=0, keepdims=True)
            for k in range(taps):
                taps_sum[k] = taps_sum[k] + jnp.sum(
                    grad_conv * ext_ref[s, first + k : first + k + rows, cols], axis=0, keepdims=True)
            gpad[0:8] = jnp.zeros((8, WIDE), jnp.float32)
            gpad[8 : 8 + rows] = grad_conv
            gpad[8 + rows :] = jnp.zeros((8, WIDE), jnp.float32)
            grad = 0.0
            for k in range(taps):
                grad = grad + vec_ref[states + k : states + k + 1, cols] * gpad[taps - 1 - k : taps + 7 - k + rows]
            heads.append(grad[0:8])
            gm[s * rows : (s + 1) * rows, cols] = grad[8:].astype(jnp.bfloat16)
        gm[count:, cols] = jnp.concatenate(heads).astype(jnp.bfloat16)
        dvec_ref[row : row + 1, cols] = bias_sum
        for k in range(taps):
            dvec_ref[states + k : states + k + 1, cols] = taps_sum[k]
        zcols = slice(inner + j * WIDE, inner + (j + 1) * WIDE)
        din_ref[:, cols] = dot_tn(xn[...], gm[:, cols]).astype(jnp.bfloat16)
        din_ref[:, zcols] = dot_tn(xn[:count], gz_ref[:, cols]).astype(jnp.bfloat16)
        gz = jnp.concatenate([gz_ref[:, cols], jnp.zeros((gm.shape[0] - count, WIDE), jnp.bfloat16)])
        grad_normed = grad_normed + dot_nt(gm[:, cols], win_ref[:, cols]) + dot_nt(gz, win_ref[:, zcols])
    gain_sum = 0.0
    for ref, to, base, out in ((tok_ref, 0, ghid_ref, dtok_ref), (halo_ref, count, None, dhalo_ref)):
        x = ref[...].astype(jnp.float32)
        r1 = normalize(x)
        grad = grad_normed[to : to + x.shape[0]]
        gain_sum = gain_sum + jnp.sum(grad * (x * r1), axis=0, keepdims=True)
        grad = grad * gain_ref[0:1]
        grad = r1 * grad - x * (r1 * r1 * r1) * jnp.mean(grad * x, axis=1, keepdims=True)
        out[...] = grad if base is None else grad + base[...]
    dgain_ref[...] = gain_sum


def like(*shape, dtype=f32):
    return jax.ShapeDtypeStruct(shape, dtype)


def params(mib=56):
    return pltpu.CompilerParams(vmem_limit_bytes=mib << 20)


def moe_kernel(seq, rows_ref, up_ref, down_ref, up2_ref, down2_ref,
               back_ref, land_ref, dup_ref, ddown_ref, dup2_ref, ddown2_ref,
               xbuf, part, act, ghid, hid, gact, sib_buf, own_sum,
               local_sem, disp_sem, pass_sem, recv_sem, load_sem, sib_send, sib_recv,
               final_send, final_recv, final_local):
    me = Place(4, seq)
    b, s = me.at()
    y, z, Z, c = me.y, me.z, me.Z, me.c
    cap, wide = rows_ref.shape[1], rows_ref.shape[2]
    width = wide // 2
    share = up_ref.shape[1]
    two = 2 * cap
    block = 2 * two
    sib = me.at(c=1 - c)
    greet([(None, sib)] + [(None, (b, (s + k) % seq)) for k in range(1, seq)])

    def remote(src, dst, send, recv, dev):
        return pltpu.make_async_remote_copy(
            src_ref=src, dst_ref=dst, send_sem=send, recv_sem=recv, device_id=dev, device_id_type=MESH)

    def slab(cc, ss):
        return land_ref.at[cc, pl.ds(pl.multiple_of(ss * cap, 8), cap)]

    def there(k, j):
        return ((z + k) % Z) * 2 + j

    def arrived(cc, ss):
        remote(slab(cc, ss), slab(cc, ss), disp_sem.at[0], recv_sem.at[cc, ss], sib).wait_recv()

    def hand(ss):
        return remote(slab(c, ss), slab(c, ss), pass_sem.at[ss], recv_sem.at[c, ss], sib)

    def load(k, cc):
        zz = (z + k) % Z
        return pltpu.make_async_copy(
            land_ref.at[cc, pl.ds(pl.multiple_of(zz * two, 8), two)],
            xbuf.at[k, pl.ds(pl.multiple_of(cc * two, 16), two)], load_sem.at[k, cc])

    def dispatch(k, j):
        to = ((z + Z - k) % Z) * 2 + j
        return remote(rows_ref.at[to], slab(c, s), disp_sem.at[2 * k + j], recv_sem.at[c, s], (b, to))

    dispatch(0, 1 - y).start()
    own = remote(rows_ref.at[s], slab(c, s), pass_sem.at[s], recv_sem.at[c, s], sib)
    own.start()
    local = pltpu.make_async_copy(rows_ref.at[s], slab(c, s), local_sem)
    local.start()
    for j in range(2):
        dispatch(1, j).start()

    ups, downs = (up_ref, up2_ref), (down_ref, down2_ref)

    def compute(k):
        for i in range(2):
            for n in range(0, share, WIDE):
                to = slice(i * share + n, i * share + n + WIDE)
                hid[:, to] = dot(xbuf[k, :, :width], ups[i][:, n : n + WIDE])
                gact[:, to] = dot_nt(xbuf[k, :, width:], downs[i][n : n + WIDE, :])

        def sixteen(r, carry):
            at = pl.ds(pl.multiple_of(r * 16, 16), 16)
            to = pl.ds(pl.multiple_of(k * block + r * 16, 16), 16)
            h = hid[at, :]
            half = 0.5 * (1.0 + erf(h * math.sqrt(0.5)))
            act[to, :] = (h * half).astype(bf16)
            slope = half + h * (jnp.exp(-0.5 * h * h) * (1.0 / math.sqrt(2.0 * math.pi)))
            ghid[to, :] = (gact[at, :] * slope).astype(bf16)
            return carry
        lax.fori_loop(0, block // 16, sixteen, 0)
        mine = pl.ds(pl.multiple_of(k * block, 16), block)
        for n in range(0, width, WIDE):
            cols = slice(n, n + WIDE)
            part[k, :, cols] = (
                dot(act[mine, :share], down_ref[:, cols]) + dot(act[mine, share:], down2_ref[:, cols])
            ).astype(bf16)
            part[k, :, width + n : width + n + WIDE] = (
                dot_nt(ghid[mine, :share], up_ref[cols, :]) + dot_nt(ghid[mine, share:], up2_ref[cols, :])
            ).astype(bf16)

    def of_core(k, cc):
        return part.at[k, pl.ds(pl.multiple_of(cc * two, 16), two)]

    def to_sib(k):
        return remote(of_core(k, 1 - c), sib_buf.at[k], sib_send.at[k], sib_recv.at[k], sib)

    def to_home(k, j):
        return remote(own_sum.at[k, j], back_ref.at[s], final_send.at[k, j], final_recv.at[s], (b, there(k, j)))

    def keep_home():
        return pltpu.make_async_copy(own_sum.at[0, y], back_ref.at[s], final_local)

    def own_stage(k):
        @pl.when(k == 0)
        def _():
            arrived(c, z * 2 + 1 - y)
            hand(z * 2 + 1 - y).start()
            local.wait()

        @pl.when(k > 0)
        def _():
            for j in range(2):
                arrived(c, there(k, j))
                hand(there(k, j)).start()

        @pl.when(k < Z - 2)
        def _():
            for j in range(2):
                dispatch(k + 2, j).start()
        load(k, c).start()

    def compute_stage(k):
        for j in range(2):
            arrived(1 - c, there(k, j))
        load(k, 1 - c).start()
        for cc in range(2):
            load(k, cc).wait()
        compute(k)
        to_sib(k).start()

    def home_stage(k):
        to_sib(k).wait_recv()
        total = of_core(k, c)[...].astype(f32) + sib_buf[k].astype(f32)
        for j in range(2):
            own_sum[k, j] = total[j * cap : (j + 1) * cap].astype(bf16)

        @pl.when(k > 0)
        def _():
            for j in range(2):
                to_home(k, j).start()

        @pl.when(k == 0)
        def _():
            keep_home().start()
            to_home(0, 1 - y).start()

    everything = (Z * block, width)
    stages = ((own_stage, 0), (home_stage, 2), (compute_stage, 1))

    def step(t, carry):
        for stage, lag in stages:
            k = t - lag
            pl.when(jnp.logical_and(k >= 0, k < Z))(functools.partial(stage, k))
        return carry
    lax.fori_loop(0, Z + 2, step, 0)
    for i, (dup, ddown) in enumerate(((dup2_ref, ddown2_ref), (dup_ref, ddown_ref))):
        for n in range(0, share, WIDE):
            at = (1 - i) * share + n
            x, g = xbuf[:, :, :width].reshape(everything), xbuf[:, :, width:].reshape(everything)
            ddown[n : n + WIDE, :] = dot_tn(act[:, at : at + WIDE], g).astype(ddown.dtype)
            dup[:, n : n + WIDE] = dot_tn(x, ghid[:, at : at + WIDE]).astype(dup.dtype)

    for k in range(1, seq):
        e = (s + k) % seq
        remote(back_ref.at[e], back_ref.at[e], disp_sem.at[0], final_recv.at[e], sib).wait_recv()
    keep_home().wait()
    dispatch(0, 1 - y).wait_send()
    own.wait_send()
    hand(z * 2 + 1 - y).wait_send()
    to_home(0, 1 - y).wait_send()

    def settle(k, carry):
        to_sib(k).wait_send()

        @pl.when(k > 0)
        def _():
            for j in range(2):
                dispatch(k, j).wait_send()
                to_home(k, j).wait_send()
                hand(there(k, j)).wait_send()
        return carry
    lax.fori_loop(0, Z, settle, 0)


def cross(batch, *arrays):
    return [lax.ppermute(a, "batch", [(i, (i + 2) % batch) for i in range(batch)]) for a in arrays]


def moe_rows(batch, seq, sent, up, down, up2, down2):
    width, hidden_share = up.shape
    capacity, wide = sent.shape[1:]
    block = seq * capacity
    if tuned(batch, seq):
        Z, block = seq // 2, 4 * capacity
        dma = pltpu.SemaphoreType.DMA
        out = pl.pallas_call(
            functools.partial(moe_kernel, seq),
            out_shape=[
                like(seq, capacity, wide, dtype=bf16),
                like(2, seq * capacity, wide, dtype=bf16),
                like(width, hidden_share),
                like(hidden_share, width),
                like(width, hidden_share, dtype=bf16),
                like(hidden_share, width, dtype=bf16),
            ],
            in_specs=[HBM] + [VM] * 4,
            out_specs=[HBM, HBM] + [VM] * 4,
            scratch_shapes=[
                pltpu.VMEM((Z, block, wide), bf16),
                pltpu.VMEM((Z, block, wide), bf16),
                pltpu.VMEM((Z * block, 2 * hidden_share), bf16),
                pltpu.VMEM((Z * block, 2 * hidden_share), bf16),
                pltpu.VMEM((block, 2 * hidden_share), f32),
                pltpu.VMEM((block, 2 * hidden_share), f32),
                pltpu.VMEM((Z, 2 * capacity, wide), bf16),
                pltpu.VMEM((Z, 2, capacity, wide), bf16),
                dma,
                dma((2 * Z,)),
                dma((seq,)),
                dma((2, seq)),
                dma((Z, 2)),
                dma((Z,)),
                dma((Z,)),
                dma((Z, 2)),
                dma((seq,)),
                dma,
            ],
            compiler_params=pltpu.CompilerParams(
                collective_id=2, has_side_effects=True, vmem_limit_bytes=56 << 20),
            name="experts",
        )(sent, up, down, up2, down2)
        back, _, d_up, d_down, d_up2, d_down2 = out
        d_up2, d_down2 = cross(batch, d_up2, d_down2)
        return back, d_up, d_down, d_up2, d_down2
    mine = lax.all_to_all(sent, "seq", split_axis=0, concat_axis=0, tiled=True)
    rows = lax.all_gather(mine, "batch", axis=0).reshape(batch * block, wide)
    part, d_up, d_down = pl.pallas_call(
        expert_kernel,
        out_shape=[
            like(batch * block, wide, dtype=bf16),
            like(width, hidden_share),
            like(hidden_share, width),
        ],
        grid=(batch,),
        in_specs=[
            pl.BlockSpec((block, wide), lambda i: (i, 0)),
            pl.BlockSpec((width, hidden_share), lambda i: (0, 0)),
            pl.BlockSpec((hidden_share, width), lambda i: (0, 0)),
        ],
        out_specs=[
            pl.BlockSpec((block, wide), lambda i: (i, 0)),
            pl.BlockSpec((width, hidden_share), lambda i: (0, 0)),
            pl.BlockSpec((hidden_share, width), lambda i: (0, 0)),
        ],
        compiler_params=params(),
        name="experts",
    )(rows, up, down)
    part = part.reshape((batch,) + sent.shape)
    mine = lax.psum_scatter(part, "batch", scatter_dimension=0, tiled=False)
    return lax.all_to_all(mine, "seq", split_axis=0, concat_axis=0, tiled=True), d_up, d_down, 0.0, 0.0


def body(
    tokens,
    in_proj,
    conv_weight,
    conv_bias,
    state_proj,
    step_proj,
    step_bias,
    decay_log,
    skip_gain,
    out_proj,
    norm_gain,
    moe_gain,
    router_proj,
    expert_up,
    expert_down,
    routes,
    slot_index,
    cotangent,
):
    batch, seq = lax.axis_size("batch"), lax.axis_size("seq")
    both = ("batch", "seq")
    seqs, rows, width = tokens.shape
    count = seqs * rows
    devices = batch * seq
    taps, share = conv_weight.shape
    inner = share * devices
    states, rank = decay_log.shape[0], step_proj.shape[0]
    low_share = norm_gain.shape[0]
    experts = router_proj.shape[1]
    capacity = max(2, 5 * count // (4 * experts))
    dims = (seqs, rows, inner, states, rank, taps)
    tile = 128

    vectors = jnp.concatenate([decay_log, conv_weight, conv_bias[None], step_bias[None], skip_gain[None]])
    features = jnp.concatenate([router_proj, norm_gain[:, None], moe_gain[:, None]], axis=1)
    used = vectors.shape[0]
    room = -(-used // 8) * 8
    tail = jnp.concatenate(
        [
            state_proj,
            step_proj.T,
            jnp.pad(vectors, ((0, room - used), (0, 0))).T,
            jnp.pad(features, ((0, share - low_share), (0, tile - room - features.shape[1]))),
        ],
        axis=1,
    )
    halo = lax.ppermute(tokens[:, rows - taps + 1 :], "seq", [(i, i + 1) for i in range(seq - 1)])
    halo = jnp.pad(halo, ((0, 0), (8 - taps + 1, 0), (0, 0))).reshape(seqs * 8, width)
    if tuned(batch, seq):
        in_full, out_full, tail_full = gather_all(batch, seq, in_proj, out_proj, tail)
    else:
        in_full, out_full, tail_full = (
            lax.all_gather(a, both, axis=0, tiled=True) for a in (in_proj, out_proj, tail)
        )
    up, down, tail_full = lax.optimization_barrier((expert_up[0], expert_down[0], tail_full))
    if tuned(batch, seq):
        up2, down2 = cross(batch, up, down)
    else:
        up2 = down2 = None
    small = tail_full[:, :tile]
    vec = tail_full[:, tile : tile + room].T.astype(f32)
    model = tail_full[:, tile + room : tile + room + experts + 2]
    model = model.reshape(devices, share, experts + 2)[:, :low_share].reshape(width, experts + 2)
    gain = model[:, experts:].T.astype(f32)
    router = jnp.pad(model[:, :experts], ((0, 0), (0, tile - experts)))
    tok, cot = tokens.reshape(count, width), cotangent.reshape(count, width)
    route, slot = routes.reshape(count, 1), slot_index.reshape(count, 1)
    place = jnp.where(slot < capacity, route * capacity + slot, -1)

    ext, z, u, dt, proj, end, dsum = pl.pallas_call(
        partial(enter_kernel, dims),
        out_shape=[
            like(seqs, rows + 8, inner),
            like(count, inner),
            like(count, inner),
            like(count, inner),
            like(count, tile),
            like(seqs, states, inner),
            like(seqs, 1, inner),
        ],
        in_specs=[VM] * 6,
        out_specs=[VM] * 7,
        scratch_shapes=[pltpu.VMEM((count + seqs * 8, width), bf16)],
        compiler_params=params(),
        name="enter",
    )(tok, halo, in_full, small, vec, gain)
    before = relay_states(batch, seq, True, states, dsum, vec, end)
    size = GROUP * states
    total = experts * capacity
    hist, y, hid, gated, moe_in, gate, sent = pl.pallas_call(
        partial(leave_kernel, dims, capacity),
        out_shape=[
            like(seqs, (rows + 1) * states, inner, dtype=bf16),
            like(count, inner),
            like(count, width),
            like(count, inner, dtype=bf16),
            like(count, width, dtype=bf16),
            like(count, 1),
            like(total, 2 * width, dtype=bf16),
        ],
        in_specs=[VM] * 14,
        out_specs=[HBM] + [VM] * 6,
        scratch_shapes=[
            pltpu.VMEM((2, size, inner), bf16),
            pltpu.VMEM((seqs, states, inner), bf16),
            pltpu.SemaphoreType.DMA((2,)),
            pltpu.SemaphoreType.DMA((seqs,)),
        ],
        compiler_params=params(),
        name="leave",
    )(tok, cot, before, dt, u, z, proj, vec, out_full, gain, router, route, slot, place.reshape(1, count))

    back, d_up, d_down, d_up2, d_down2 = moe_rows(
        batch, seq, sent.reshape(experts, capacity, 2 * width), up, down, up2, down2)
    back = back.reshape(total, 2 * width)

    block_out, ghid, gy, gz, d_out, d_router, d_skip, d_moe, adj = pl.pallas_call(
        partial(return_kernel, dims),
        out_shape=[
            like(count, width, dtype=bf16),
            like(count, width),
            like(count, inner),
            like(count, inner, dtype=bf16),
            like(inner, width, dtype=bf16),
            like(width, tile),
            like(1, inner),
            like(1, width),
            like(seqs, states, inner),
        ],
        in_specs=[VM] * 17,
        out_specs=[VM] * 9,
        compiler_params=params(),
        name="back_experts",
    )(back, cot, hid, moe_in, gate, gated, y, u, z, dt, proj, vec, out_full, gain, router, route, place)
    later = relay_states(batch, seq, False, states, dsum, vec, adj)
    d_tok, d_halo, d_in, d_small, d_vec, d_norm = pl.pallas_call(
        partial(back_kernel, dims),
        out_shape=[
            like(count, width),
            like(seqs * 8, width),
            like(width, 2 * inner, dtype=bf16),
            like(inner, tile, dtype=bf16),
            like(room, inner),
            like(1, width),
        ],
        in_specs=[VM] * 3 + [HBM] + [VM] * 11,
        out_specs=[VM] * 6,
        scratch_shapes=[
            pltpu.VMEM((2, size + states, inner), bf16),
            pltpu.VMEM((GROUP, states, tile), f32),
            pltpu.VMEM((GROUP, states, tile), f32),
            pltpu.VMEM((GROUP, states, tile), f32),
            pltpu.VMEM((GROUP, states, tile), f32),
            pltpu.VMEM((states, inner), f32),
            pltpu.VMEM((count, inner), f32),
            pltpu.VMEM((count, inner), f32),
            pltpu.VMEM((count, tile), f32),
            pltpu.VMEM((rows + 16, WIDE), f32),
            pltpu.VMEM((count + seqs * 8, inner), bf16),
            pltpu.VMEM((count + seqs * 8, width), bf16),
            pltpu.VMEM((count, inner), bf16),
            pltpu.SemaphoreType.DMA((2,)),
        ],
        compiler_params=params(),
        name="back_mixer",
    )(tok, halo, ext, hist, later, gy, gz, ghid, u, dt, proj, in_full, small, vec, gain)

    d_model = jnp.concatenate([d_router[:, :experts], d_norm.T, d_moe.T], axis=1)
    d_model = jnp.pad(
        d_model.reshape(devices, low_share, experts + 2),
        ((0, 0), (0, share - low_share), (0, tile - room - experts - 2)),
    ).reshape(inner, tile - room)
    skip_row = states + taps + 2
    d_vec = d_vec.at[skip_row].set(d_skip[0])
    d_tail = jnp.concatenate([d_small, d_vec.T.astype(bf16), d_model.astype(bf16)], axis=1)
    if tuned(batch, seq):
        s_in, s_out, s_tail = reduce_all(batch, seq, d_in, d_out, d_tail)
    else:
        s_in, s_out, s_tail = (
            lax.psum_scatter(a.astype(f32), both, scatter_dimension=0, tiled=True) for a in (d_in, d_out, d_tail)
        )
    from_next = lax.ppermute(
        d_halo.reshape(seqs, 8, width)[:, 8 - taps + 1 :], "seq", [(i + 1, i) for i in range(seq - 1)]
    )
    d_tok = d_tok.reshape(tokens.shape).at[:, rows - taps + 1 :].add(from_next)
    s_vec = s_tail[:, tile : tile + room].T
    s_model = s_tail[:low_share, tile + room :]
    return (
        block_out.reshape(tokens.shape),
        d_tok,
        s_in,
        s_vec[states : states + taps],
        s_vec[states + taps],
        s_tail[:, : rank + 2 * states],
        s_tail[:, rank + 2 * states : tile].T,
        s_vec[states + taps + 1],
        s_vec[:states],
        s_vec[states + taps + 2],
        s_out,
        s_model[:, experts],
        s_model[:, experts + 1],
        s_model[:, :experts],
        (d_up + d_up2)[None],
        (d_down + d_down2)[None],
    )


def solution(mesh):
    in_specs = (
        P("batch", "seq", None),
        P(("batch", "seq"), None),
        P(None, ("batch", "seq")),
        P(("batch", "seq")),
        P(("batch", "seq"), None),
        P(None, ("batch", "seq")),
        P(("batch", "seq")),
        P(None, ("batch", "seq")),
        P(("batch", "seq")),
        P(("batch", "seq"), None),
        P(("batch", "seq")),
        P(("batch", "seq")),
        P(("batch", "seq"), None),
        P("seq", None, "batch"),
        P("seq", "batch", None),
        P("batch", "seq"),
        P("batch", "seq"),
        P("batch", "seq", None),
    )
    out_specs = (
        P("batch", "seq", None),
        P("batch", "seq", None),
        P(("batch", "seq"), None),
        P(None, ("batch", "seq")),
        P(("batch", "seq")),
        P(("batch", "seq"), None),
        P(None, ("batch", "seq")),
        P(("batch", "seq")),
        P(None, ("batch", "seq")),
        P(("batch", "seq")),
        P(("batch", "seq"), None),
        P(("batch", "seq")),
        P(("batch", "seq")),
        P(("batch", "seq"), None),
        P("seq", None, "batch"),
        P("seq", "batch", None),
    )
    return jax.shard_map(body, mesh=mesh, in_specs=in_specs, out_specs=out_specs, check_vma=False)
```

```python
from functools import partial
import functools
import math

import jax
import jax.numpy as jnp
from jax import lax
from jax.experimental import pallas as pl
from jax.experimental.pallas import tpu as pltpu
from jax.sharding import PartitionSpec as P

epsilon = 1e-05
MESH = pl.DeviceIdType.MESH
HBM = pl.BlockSpec(memory_space=pl.ANY)
VM = pl.BlockSpec(memory_space=pltpu.VMEM)
bf16, f32 = jnp.bfloat16, jnp.float32


class Place:
    def __init__(self, batch, seq, ydim=2):
        self.batch, self.seq, self.Y = batch, seq, ydim
        self.Z = seq // ydim
        b, s = lax.axis_index("batch"), lax.axis_index("seq")
        self.x, self.c = b // 2, b % 2
        self.z, self.y = s // ydim, s % ydim

    def at(self, x=None, c=None, y=None, z=None):
        pick = lambda v, own: own if v is None else v
        x, c, y, z = pick(x, self.x), pick(c, self.c), pick(y, self.y), pick(z, self.z)
        return (x * 2 + c, z * self.Y + y)

    def index(self, dev):
        return dev[0] * self.seq + dev[1]


def greet(devices):
    barrier = pltpu.get_barrier_semaphore()
    count = 0
    for pred, dev in devices:
        if pred is None:
            pl.semaphore_signal(barrier, inc=1, device_id=dev, device_id_type=MESH)
            count = count + 1
        else:
            @pl.when(pred)
            def _(dev=dev):
                pl.semaphore_signal(barrier, inc=1, device_id=dev, device_id_type=MESH)
            count = count + jnp.where(pred, 1, 0)
    pl.semaphore_wait(barrier, count)


TILE = 128


def spot(rows, at, width):
    return (lanes((rows, width)) == subs((rows, width)) + at).astype(bf16)


def gather_kernel(batch, seq, *refs):
    n_arrays = 3
    in_ref, out_ref, tok_ref, state_ref, step_ref, router_ref = refs[:6]
    lines, gains = refs[6:11], refs[11:13]
    outs, halo_ref = refs[13:16], refs[16]
    tail, vecs, feats, zeros, local_sem, send_sem, recv_sem, halo_sem = refs[17:]
    ins = [in_ref, out_ref, tail]
    me = Place(batch, seq)
    Z, z = me.Z, me.z
    rows = [r.shape[0] for r in ins]
    sib = me.at(c=1 - me.c)
    up_ok, down_ok = z < Z - 1, z > 0
    up, down = me.at(z=z + 1), me.at(z=z - 1)
    nx, ny = me.at(x=1 - me.x), me.at(y=1 - me.y)
    first = me.c == 0
    nb2 = tuple(jnp.where(first, a, b) for a, b in zip(ny, nx))
    nb3 = tuple(jnp.where(first, a, b) for a, b in zip(nx, ny))
    x2, y2 = jnp.where(first, me.x, 1 - me.x), jnp.where(first, 1 - me.y, me.y)
    x3, y3 = jnp.where(first, 1 - me.x, me.x), jnp.where(first, me.y, 1 - me.y)
    b, part_of = me.at()
    has_before, has_after = part_of > 0, part_of < seq - 1
    before, after = (b, part_of - 1), (b, part_of + 1)
    greet([(None, sib), (None, nx), (None, ny), (up_ok, up), (down_ok, down), (has_before, before), (has_after, after)])
    own = me.index(me.at())

    def part(a, index):
        return outs[a].at[pl.ds(pl.multiple_of(index * rows[a], 8), rows[a])]

    sends = []

    def send(pred, index, dev, mine=False):
        slot = len(sends)
        copies = []
        for a in range(n_arrays):
            copies.append(
                pltpu.make_async_remote_copy(
                    src_ref=ins[a] if mine else part(a, index),
                    dst_ref=part(a, index),
                    send_sem=send_sem.at[slot, a],
                    recv_sem=recv_sem.at[index, a],
                    device_id=dev,
                    device_id_type=MESH,
                )
            )

        def go(copies):
            def start():
                for cp in copies:
                    cp.start()
            if pred is None:
                start()
            else:
                pl.when(pred)(start)
        if mine:
            go(copies[:2])
            later.append(lambda: go(copies[2:]))
        else:
            go(copies)
        sends.append((pred, copies))

    def arrive(pred, index, targets):
        def wait():
            for a in range(n_arrays):
                pltpu.make_async_remote_copy(
                    src_ref=part(a, index), dst_ref=part(a, index),
                    send_sem=send_sem.at[0, a], recv_sem=recv_sem.at[index, a],
                    device_id=sib, device_id_type=MESH,
                ).wait_recv()
        if pred is None:
            wait()
        else:
            pl.when(pred)(wait)
        for extra, dev in targets:
            p = pred if extra is None else (extra if pred is None else jnp.logical_and(pred, extra))
            send(p, index, dev)

    later = []
    for dev, pred in ((up, up_ok), (down, down_ok), (nb2, None), (nb3, None), (sib, None)):
        send(pred, own, dev, mine=True)
    seqs, rows_here = tok_ref.shape[:2]
    edge = pl.ds(rows_here - 8, 8)
    halo = pltpu.make_async_remote_copy(
        src_ref=tok_ref.at[:, edge], dst_ref=halo_ref, send_sem=halo_sem.at[0], recv_sem=halo_sem.at[1],
        device_id=after, device_id_type=MESH)
    blank = pltpu.make_async_copy(zeros, halo_ref, halo_sem.at[2])
    zeros[...] = jnp.zeros_like(zeros)
    pl.when(has_after)(halo.start)
    pl.when(jnp.logical_not(has_before))(blank.start)

    share, low_share, experts = state_ref.shape[0], router_ref.shape[0], router_ref.shape[1]
    rank, room, wide = step_ref.shape[0], vecs.shape[0], tail.shape[1]
    vecs[...] = jnp.zeros_like(vecs)
    at = 0
    for ref in lines:
        vecs[at : at + ref.shape[0]] = ref[...].astype(f32)
        at += ref.shape[0]
    feats[...] = jnp.zeros_like(feats)
    for i, ref in enumerate(gains):
        feats[i : i + 1] = ref[...].astype(f32)
    by_channel = (
        dot(state_ref[...], spot(state_ref.shape[1], 0, wide))
        + dot_tn(step_ref[...], spot(rank, TILE - rank, wide))
        + dot_tn(vecs[...].astype(bf16), spot(room, TILE, wide))
    )
    by_feature = dot(router_ref[...], spot(experts, TILE + room, wide)) + dot_tn(
        feats[...].astype(bf16), spot(feats.shape[0], TILE + room + experts, wide))
    by_feature = jnp.concatenate([by_feature, jnp.zeros((share - low_share, wide), f32)])
    tail[...] = (by_channel + by_feature).astype(bf16)
    for start in later:
        start()
    local = [pltpu.make_async_copy(ins[a], part(a, own), local_sem.at[a]) for a in range(n_arrays)]
    for cp in local:
        cp.start()

    def offsets(k):
        return [(None, 0)] if k == 0 else [(z >= k, -k), (z + k < Z, k)]

    def col(k):
        for pred, off in offsets(k):
            fwd = (up_ok, up) if off < 0 else (down_ok, down)
            arrive(pred, me.index(me.at(z=z + off)), [fwd, (None, nb2), (None, nb3), (None, sib)])

    def second(k):
        for pred, off in offsets(k):
            arrive(pred, me.index(me.at(x=x2, y=y2, z=z + off)), [(None, nb3), (None, sib)])

    def third(k):
        for pred, off in offsets(k):
            arrive(pred, me.index(me.at(x=x3, y=y3, z=z + off)), [(None, sib)])

    def fourth(k):
        for pred, off in offsets(k):
            arrive(pred, me.index(me.at(x=1 - me.x, y=1 - me.y, z=z + off)), [(None, sib)])

    for h in range(1, Z + 3):
        if h < Z:
            col(h)
        if 0 <= h - 1 < Z:
            second(h - 1)
        if 0 <= h - 2 < Z:
            third(h - 2)
        if 0 <= h - 3 < Z:
            fourth(h - 3)
    for h in range(Z):
        for xx in (0, 1):
            for yy in (0, 1):
                for pred, off in offsets(h):
                    arrive(pred, me.index(me.at(x=xx, y=yy, c=1 - me.c, z=z + off)), [])
    for cp in local:
        cp.wait()
    pl.when(has_before)(halo.wait_recv)
    pl.when(has_after)(halo.wait_send)
    pl.when(jnp.logical_not(has_before))(blank.wait)
    for pred, copies in sends:
        def done(copies=copies):
            for cp in copies:
                cp.wait_send()
        if pred is None:
            done()
        else:
            pl.when(pred)(done)


def n_sends(Z):
    return 5 + (Z - 1) * 8 + (2 * Z - 1) * 2 + (2 * Z - 1) * 2


def gather_all(batch, seq, room, in_proj, out_proj, tokens, state, step, router, lines, gains):
    count, share = batch * seq, out_proj.shape[0]
    seqs, _, width = tokens.shape
    wide = 2 * TILE
    edge = (seqs, 8, width)
    return pl.pallas_call(
        functools.partial(gather_kernel, batch, seq),
        out_shape=[
            jax.ShapeDtypeStruct((count * a.shape[0],) + a.shape[1:], bf16) for a in (in_proj, out_proj)
        ] + [jax.ShapeDtypeStruct((count * share, wide), bf16), jax.ShapeDtypeStruct(edge, bf16)],
        in_specs=[HBM] * 3 + [VM] * (3 + len(lines) + len(gains)),
        out_specs=[HBM] * 4,
        scratch_shapes=[
            pltpu.VMEM((share, wide), bf16),
            pltpu.VMEM((room, share), f32),
            pltpu.VMEM((8, router.shape[0]), f32),
            pltpu.VMEM(edge, bf16),
            pltpu.SemaphoreType.DMA((3,)),
            pltpu.SemaphoreType.DMA((n_sends(seq // 2), 3)),
            pltpu.SemaphoreType.DMA((count, 3)),
            pltpu.SemaphoreType.DMA((3,)),
        ],
        compiler_params=pltpu.CompilerParams(collective_id=0, has_side_effects=True),
        name="gather_weights",
    )(in_proj, out_proj, tokens, state, step, router, *lines, *gains)


def reduce_kernel(batch, seq, low_share, experts, skip_row, *refs):
    n = 3
    din_ref, dout_ref, dsmall_ref, dvec_ref, dskip_ref, drouter_ref, dnorm_ref, dmoe_ref, dhalo_ref = refs[:9]
    outs, halo_ref = refs[9:12], refs[12]
    refs = refs[13:]
    work, sib_buf, far_buf, near_buf, line_buf = (refs[i * n : (1 + i) * n] for i in range(5))
    tail, zeros, load_sem, send_sem, sib_sem, far_sem, near_sem, line_sem, halo_sem = refs[5 * n :]
    me = Place(batch, seq)
    Z, z = me.Z, me.z
    rows = [r.shape[0] for r in outs]
    sib = me.at(c=1 - me.c)
    up, down = me.at(z=z + 1), me.at(z=z - 1)
    nx, ny = me.at(x=1 - me.x), me.at(y=1 - me.y)
    first = me.c == 0
    pick = lambda flag, a, b: jnp.where(flag, a, b)
    near = tuple(pick(first, a, b) for a, b in zip(ny, nx))
    far = tuple(pick(first, a, b) for a, b in zip(nx, ny))
    b, part_of = me.at()
    has_before, has_after = part_of > 0, part_of < seq - 1
    before, after = (b, part_of - 1), (b, part_of + 1)
    greet([(None, sib), (None, nx), (None, ny), (z < Z - 1, up), (z > 0, down), (has_before, before), (has_after, after)])

    def groups(c):
        f = c == 0
        ox, oy = 1 - me.x, 1 - me.y
        return [
            (ox, oy),
            (pick(f, ox, me.x), pick(f, me.y, oy)),
            (pick(f, me.x, ox), pick(f, oy, me.y)),
            (me.x, me.y),
        ]

    def slot(xy, zz):
        return (xy[0] * 2 + xy[1]) * Z + zz

    def turn(k):
        return (z + 1 + k) % Z

    sends = []

    def send(pred, srcs, dsts, recv, dev):
        copies = [
            pltpu.make_async_remote_copy(
                src_ref=srcs[a], dst_ref=dsts[a], send_sem=send_sem.at[len(sends), a],
                recv_sem=recv(a), device_id=dev, device_id_type=MESH)
            for a in range(n)
        ]

        def go():
            for cp in copies:
                cp.start()
        if pred is None:
            go()
        else:
            pl.when(pred)(go)
        sends.append((pred, copies))

    def take(bufs, recv):
        for a in range(n):
            pltpu.make_async_remote_copy(
                src_ref=bufs[a], dst_ref=bufs[a], send_sem=send_sem.at[0, a],
                recv_sem=recv(a), device_id=sib, device_id_type=MESH).wait_recv()

    def source(a, c, xy, zz):
        index = me.index((xy[0] * 2 + c, zz * me.Y + xy[1]))
        if a == 2:
            return tail.at[index]
        return (din_ref, dout_ref)[a].at[pl.ds(pl.multiple_of(index * rows[a], 8), rows[a])]

    halo = pltpu.make_async_remote_copy(
        src_ref=dhalo_ref, dst_ref=halo_ref, send_sem=halo_sem.at[0], recv_sem=halo_sem.at[1],
        device_id=before, device_id_type=MESH)
    blank = pltpu.make_async_copy(zeros, halo_ref, halo_sem.at[2])
    zeros[...] = jnp.zeros_like(zeros)
    pl.when(has_before)(halo.start)
    pl.when(jnp.logical_not(has_after))(blank.start)

    other = 1 - me.c
    mine = groups(me.c)
    first_sends, loads = [], []
    for xy in groups(other):
        for k in range(Z):
            s = slot(xy, turn(k))
            copies = [
                pltpu.make_async_remote_copy(
                    src_ref=source(a, other, xy, turn(k)), dst_ref=sib_buf[a].at[s],
                    send_sem=send_sem.at[len(sends), a], recv_sem=sib_sem.at[s, a],
                    device_id=sib, device_id_type=MESH)
                for a in range(n)
            ]
            sends.append((None, copies))
            first_sends.append(copies)
    for xy in mine:
        for k in range(Z):
            s = slot(xy, turn(k))
            loads.append([
                pltpu.make_async_copy(source(a, me.c, xy, turn(k)), work[a].at[s], load_sem.at[s, a]) for a in range(n)
            ])
    for copies in first_sends + loads:
        for cp in copies[:2]:
            cp.start()

    room, share = dvec_ref.shape[0], tail.shape[1]
    blocks, width = tail.shape[0], drouter_ref.shape[0]
    vec = jnp.where(subs(dvec_ref.shape) == skip_row, dskip_ref[...], dvec_ref[...])
    line = subs((8, width))
    gains = jnp.where(line == 0, dnorm_ref[...], jnp.where(line == 1, dmoe_ref[...], 0.0))
    model = drouter_ref[...] + dot_tn(gains.astype(bf16), spot(8, room + experts, TILE))
    model = jnp.concatenate(
        [model.reshape(blocks, low_share, TILE), jnp.zeros((blocks, share - low_share, TILE), f32)], axis=1)
    right = dot_tn(vec.astype(bf16), spot(room, 0, TILE)).reshape(blocks, share, TILE) + model
    tail[:, :, 0:TILE] = dsmall_ref[...].reshape(blocks, share, TILE)
    tail[:, :, TILE:] = right.astype(bf16)
    for copies in first_sends + loads:
        copies[2].start()

    def total(bufs):
        t = bufs[0][...].astype(jnp.float32)
        for b in bufs[1:]:
            t = t + b[...].astype(jnp.float32)
        return t

    for g, xy in enumerate(mine):
        for k in range(Z):
            zz = turn(k)
            s = slot(xy, zz)
            for cp in loads[g * Z + k]:
                cp.wait()
            take([sib_buf[a].at[s] for a in range(n)], lambda a: sib_sem.at[s, a])
            parts = [[work[a].at[s], sib_buf[a].at[s]] for a in range(n)]
            if g >= 2:
                fs = (g - 2) * Z + zz
                take([far_buf[a].at[fs] for a in range(n)], lambda a: far_sem.at[fs, a])
                for a in range(n):
                    parts[a].append(far_buf[a].at[fs])
            if g == 3:
                take([near_buf[a].at[zz] for a in range(n)], lambda a: near_sem.at[zz, a])
                for a in range(n):
                    parts[a].append(near_buf[a].at[zz])
            if g < 3:
                for a in range(n):
                    work[a][s] = total(parts[a]).astype(jnp.bfloat16)
                srcs = [work[a].at[s] for a in range(n)]
                if g < 2:
                    fs = g * Z + zz
                    send(None, srcs, [far_buf[a].at[fs] for a in range(n)],
                         lambda a: far_sem.at[fs, a], far)
                else:
                    send(None, srcs, [near_buf[a].at[zz] for a in range(n)],
                         lambda a: near_sem.at[zz, a], near)
                continue
            if k < Z - 1:
                rising = zz > z
                side = jnp.where(rising, 0, 1)
                more = jnp.where(rising, z, Z - 1 - z) > 0
                line = [line_buf[a].at[side, zz] for a in range(n)]
                for a in range(n):
                    work[a][s] = total(parts[a]).astype(jnp.bfloat16)

                @pl.when(more)
                def _():
                    take(line, lambda a: line_sem.at[side, zz, a])
                    for a in range(n):
                        work[a][s] = total([work[a].at[s], line[a]]).astype(jnp.bfloat16)
                dev = (me.at()[0], jnp.where(rising, up[1], down[1]))
                send(None, [work[a].at[s] for a in range(n)], line,
                     lambda a: line_sem.at[side, zz, a], dev)
            else:
                for a in range(n):
                    outs[a][...] = total(parts[a])
                for side, pred in ((0, z > 0), (1, z < Z - 1)):
                    @pl.when(pred)
                    def _(side=side):
                        line = [line_buf[a].at[side, zz] for a in range(n)]
                        take(line, lambda a: line_sem.at[side, zz, a])
                        for a in range(n):
                            outs[a][...] = outs[a][...] + line[a][...].astype(jnp.float32)
    pl.when(has_after)(halo.wait_recv)
    pl.when(has_before)(halo.wait_send)
    pl.when(jnp.logical_not(has_after))(blank.wait)
    for pred, copies in sends:
        for cp in copies:
            cp.wait_send()


def reduce_all(batch, seq, low_share, experts, skip_row, d_in, d_out, *rest):
    count, Z, n = batch * seq, seq // 2, 3
    wide = 2 * TILE
    share = d_out.shape[0] // count
    shapes = [(a.shape[0] // count,) + a.shape[1:] for a in (d_in, d_out)] + [(share, wide)]
    edge = rest[-1].shape
    half = count // 2
    scratch = []
    for lead in ((half,), (half,), (2 * Z,), (Z,), (2, Z)):
        scratch += [pltpu.VMEM(lead + s, bf16) for s in shapes]
    dma = pltpu.SemaphoreType.DMA
    scratch += [
        pltpu.VMEM((count, share, wide), bf16),
        pltpu.VMEM(edge, f32),
        dma((half, n)),
        dma((half + 4 * Z, n)),
        dma((half, n)),
        dma((2 * Z, n)),
        dma((Z, n)),
        dma((2, Z, n)),
        dma((3,)),
    ]
    return pl.pallas_call(
        functools.partial(reduce_kernel, batch, seq, low_share, experts, skip_row),
        out_shape=[jax.ShapeDtypeStruct(s, f32) for s in shapes] + [jax.ShapeDtypeStruct(edge, f32)],
        in_specs=[HBM] * 2 + [VM] * 7,
        out_specs=[VM] * 3 + [HBM],
        scratch_shapes=scratch,
        compiler_params=pltpu.CompilerParams(
            collective_id=1, has_side_effects=True, vmem_limit_bytes=58 << 20),
        name="reduce_grads",
    )(d_in, d_out, *rest)


def finish_kernel(dims, low_share, experts, in_ref, out_ref, tail_ref, halo_ref, tok_ref, up_ref, up2_ref, down_ref,
                  down2_ref, tok_out, din, dconv, dbias, dstate, dstep, dstep_bias, ddecay, dskip, dout, dnorm, dmoe,
                  drouter, dup, ddown):
    seqs, rows, inner, states, rank, taps = dims
    dup[...] = up_ref[...] + up2_ref[...].astype(f32)
    ddown[...] = down_ref[...] + down2_ref[...].astype(f32)

    @pl.when(pl.program_id(0) == 0)
    def _():
        tok_out[...] = tok_ref[...] + halo_ref[...]
        din[...] = in_ref[...]
        dout[...] = out_ref[...]
        tail = tail_ref[...]
        share, wide = tail.shape
        eye = (lanes((wide, wide)) == subs((wide, wide))).astype(f32)
        turned = lax.dot_general(
            eye, tail, (((1,), (1,)), ((), ())), precision=lax.Precision.HIGHEST, preferred_element_type=f32)
        dstate[...] = tail[:, : rank + 2 * states]
        dstep[...] = turned[TILE - rank : TILE]
        ddecay[...] = turned[TILE : TILE + states]
        dconv[...] = turned[TILE + states : TILE + states + taps]
        at = TILE + states + taps
        dbias[...] = turned[at : at + 1]
        dstep_bias[...] = turned[at + 1 : at + 2]
        dskip[...] = turned[at + 2 : at + 3]
        at = TILE + -(-(states + taps + 3) // 8) * 8
        choose = (subs((wide, experts)) == lanes((wide, experts)) + at).astype(f32)
        drouter[...] = lax.dot_general(
            tail[:low_share], choose, (((1,), (0,)), ((), ())), precision=lax.Precision.HIGHEST,
            preferred_element_type=f32)
        at += experts
        dnorm[...] = turned[at : at + 1, :low_share]
        dmoe[...] = turned[at + 1 : at + 2, :low_share]


def tuned(batch, seq):
    return batch == 4 and seq == 8


def chain_kernel(seq, forward, dsum_ref, rates_ref, end_ref, out_ref, held, outgoing, send_sem, recv_sem):
    s = lax.axis_index("seq")
    b = lax.axis_index("batch")
    step = 1 if forward else -1
    has_before = s > 0 if forward else s < seq - 1
    has_after = s < seq - 1 if forward else s > 0
    before, after = (b, s - step), (b, s + step)
    barrier = pltpu.get_barrier_semaphore()
    for pred, dev in ((has_before, before), (has_after, after)):
        @pl.when(pred)
        def _(dev=dev):
            pl.semaphore_signal(barrier, inc=1, device_id=dev, device_id_type=MESH)
    pl.semaphore_wait(barrier, jnp.where(has_before, 1, 0) + jnp.where(has_after, 1, 0))
    count = end_ref.shape[0]

    def copy(i):
        return pltpu.make_async_remote_copy(
            src_ref=outgoing.at[i], dst_ref=held.at[i], send_sem=send_sem.at[i],
            recv_sem=recv_sem.at[i], device_id=after, device_id_type=MESH)

    for i in range(count):
        @pl.when(has_before)
        def _(i=i):
            copy(i).wait_recv()
            out_ref[i] = held[i].astype(jnp.float32)
            decay = jnp.exp(rates_ref[...] * dsum_ref[i])
            outgoing[i] = (end_ref[i] + decay * out_ref[i]).astype(jnp.bfloat16)

        @pl.when(jnp.logical_not(has_before))
        def _(i=i):
            out_ref[i] = jnp.zeros_like(out_ref[i])
            outgoing[i] = end_ref[i].astype(jnp.bfloat16)

        @pl.when(has_after)
        def _(i=i):
            copy(i).start()
    for i in range(count):
        @pl.when(has_after)
        def _(i=i):
            copy(i).wait_send()


def chain_states(seq, forward, dsum, rates, end):
    vm = pl.BlockSpec(memory_space=pltpu.VMEM)
    return pl.pallas_call(
        functools.partial(chain_kernel, seq, forward),
        out_shape=jax.ShapeDtypeStruct(end.shape, jnp.float32),
        in_specs=[vm] * 3,
        out_specs=vm,
        scratch_shapes=[
            pltpu.VMEM(end.shape, jnp.bfloat16),
            pltpu.VMEM(end.shape, jnp.bfloat16),
            pltpu.SemaphoreType.DMA((end.shape[0],)),
            pltpu.SemaphoreType.DMA((end.shape[0],)),
        ],
        compiler_params=pltpu.CompilerParams(
            collective_id=4 if forward else 5, has_side_effects=True),
        name="chain_forward" if forward else "chain_backward",
    )(dsum, rates, end)


def relay_kernel(seq, forward, states, dsum_ref, vec_ref, end_ref, out_ref, mine, theirs, their_sum, held, outgoing,
                 pair_send, pair_recv, line_send, line_recv):
    me = Place(4, seq)
    y, z, last = me.y, me.z, me.Z - 1
    step = 1 if forward else -1
    first = y == (0 if forward else 1)
    has_before = z > 0 if forward else z < last
    has_after = z < last if forward else z > 0
    pair, before, after = me.at(y=1 - y), me.at(z=z - step), me.at(z=z + step)
    greet([(None, pair), (has_before, before), (has_after, after)])
    count = end_ref.shape[0]
    rates = -jnp.exp(vec_ref[0:states])

    def swaps(i):
        return [
            pltpu.make_async_remote_copy(
                src_ref=src, dst_ref=dst, send_sem=pair_send.at[i, k], recv_sem=pair_recv.at[i, k],
                device_id=pair, device_id_type=MESH)
            for k, (src, dst) in enumerate(((mine.at[i], theirs.at[i]), (dsum_ref.at[i], their_sum.at[i])))
        ]

    def onward(i):
        return pltpu.make_async_remote_copy(
            src_ref=outgoing.at[i], dst_ref=held.at[i], send_sem=line_send.at[i],
            recv_sem=line_recv.at[i], device_id=after, device_id_type=MESH)

    for i in range(count):
        mine[i] = end_ref[i].astype(bf16)
        for cp in swaps(i):
            cp.start()
    for i in range(count):
        for cp in swaps(i):
            cp.wait_recv()
        own, other = end_ref[i], theirs[i].astype(f32)
        own_sum, other_sum = dsum_ref[i], their_sum[i]
        early, late = jnp.where(first, own, other), jnp.where(first, other, own)
        early_sum, late_sum = jnp.where(first, own_sum, other_sum), jnp.where(first, other_sum, own_sum)
        both = late + jnp.exp(rates * late_sum) * early

        @pl.when(has_before)
        def _():
            onward(i).wait_recv()
            arrived = held[i].astype(f32)
            outgoing[i] = (both + jnp.exp(rates * (early_sum + late_sum)) * arrived).astype(bf16)

        @pl.when(jnp.logical_not(has_before))
        def _():
            outgoing[i] = both.astype(bf16)

        @pl.when(has_after)
        def _():
            onward(i).start()

        @pl.when(has_before)
        def _():
            arrived = held[i].astype(f32)
            out_ref[i] = jnp.where(first, arrived, early + jnp.exp(rates * early_sum) * arrived)

        @pl.when(jnp.logical_not(has_before))
        def _():
            out_ref[i] = jnp.where(first, jnp.zeros_like(early), early)
    for i in range(count):
        for cp in swaps(i):
            cp.wait_send()

        @pl.when(has_after)
        def _():
            onward(i).wait_send()


def relay_states(batch, seq, forward, states, dsum, vec, end):
    if not tuned(batch, seq):
        return chain_states(seq, forward, dsum, -jnp.exp(vec[:states]), end)
    n = end.shape[0]
    return pl.pallas_call(
        functools.partial(relay_kernel, seq, forward, states),
        out_shape=jax.ShapeDtypeStruct(end.shape, f32),
        in_specs=[VM] * 3,
        out_specs=VM,
        scratch_shapes=[
            pltpu.VMEM(end.shape, bf16),
            pltpu.VMEM(end.shape, bf16),
            pltpu.VMEM(dsum.shape, f32),
            pltpu.VMEM(end.shape, bf16),
            pltpu.VMEM(end.shape, bf16),
            pltpu.SemaphoreType.DMA((n, 2)),
            pltpu.SemaphoreType.DMA((n, 2)),
            pltpu.SemaphoreType.DMA((n,)),
            pltpu.SemaphoreType.DMA((n,)),
        ],
        compiler_params=pltpu.CompilerParams(
            collective_id=6 if forward else 7, has_side_effects=True),
        name="relay_forward" if forward else "relay_backward",
    )(dsum, vec, end)


def dot(a, b):
    return jnp.dot(a, b, preferred_element_type=jnp.float32)


def dot_nt(a, b):
    return lax.dot_general(a, b, (((1,), (1,)), ((), ())), preferred_element_type=jnp.float32)


def dot_tn(a, b):
    return lax.dot_general(a, b, (((0,), (0,)), ((), ())), preferred_element_type=jnp.float32)


def sigmoid(v):
    return 1.0 / (1.0 + jnp.exp(-v))


def lanes(shape):
    return lax.broadcasted_iota(jnp.int32, shape, 1)


def subs(shape):
    return lax.broadcasted_iota(jnp.int32, shape, 0)


def column(row, base, states):
    shape = (states, row.shape[1])
    only = jnp.where(lanes(shape) == subs(shape) + base, jnp.broadcast_to(row, shape), 0.0)
    return jnp.broadcast_to(jnp.sum(only, axis=1, keepdims=True), shape)


def row_sums(parts):
    row = subs(parts[0].shape)
    four, two, one = row < 4, (row // 2) % 2 == 0, row % 2 == 0
    turn = lambda v, by: pltpu.roll(v, by, axis=0)
    a = [
        jnp.where(four, parts[j], parts[j + 4]) + turn(jnp.where(four, parts[j + 4], parts[j]), 4)
        for j in range(4)
    ]
    b = [jnp.where(two, a[j] + turn(a[j], 6), a[j + 2] + turn(a[j + 2], 2)) for j in range(2)]
    return jnp.where(one, b[0] + turn(b[0], 7), b[1] + turn(b[1], 1))


def fold(v):
    return sum(v[i : i + 8] for i in range(8, v.shape[0], 8)) + v[:8]


WIDE = 256
GROUP = 16
LOG2E = math.log2(math.e)


def conv_sum(ext_ref, s, cols, vec_ref, states, taps, rows):
    first = ext_ref.shape[1] - rows - taps + 1
    total = vec_ref[states + taps : states + taps + 1, cols]
    for k in range(taps):
        total = total + vec_ref[states + k : states + k + 1, cols] * ext_ref[s, first + k : first + k + rows, cols]
    return total


def normalize(x):
    return lax.rsqrt(jnp.mean(x * x, axis=-1, keepdims=True) + epsilon)


def unpack(tail_ref, share, low_share, room, experts, vec_ref, gain_ref, router_ref):
    right = tail_ref[:, TILE : 2 * TILE]
    vec_ref[...] = dot_nt(spot(room, 0, TILE), right)
    blocks = right.shape[0] // share
    model = right.astype(f32).reshape(blocks, share, TILE)[:, :low_share].reshape(blocks * low_share, TILE).astype(bf16)
    router_ref[...] = model
    gain_ref[...] = dot_nt(spot(gain_ref.shape[0], room + experts, TILE), model)


def enter_packed(dims, share, low_share, experts, tok_ref, halo_ref, win_ref, tail_ref,
                 ext_ref, z_ref, u_ref, dt_ref, proj_ref, end_ref, dsum_ref, vec_ref, gain_ref, router_ref, xn):
    unpack(tail_ref, share, low_share, vec_ref.shape[0], experts, vec_ref, gain_ref, router_ref)
    enter_kernel(dims, tok_ref, halo_ref, win_ref, tail_ref.at[:, 0:TILE], vec_ref, gain_ref,
                 ext_ref, z_ref, u_ref, dt_ref, proj_ref, end_ref, dsum_ref, xn)


def as_column(ref):
    seqs, rows = ref.shape
    diagonal = lanes((rows, rows)) == subs((rows, rows))
    spread = [
        jnp.where(diagonal, jnp.broadcast_to(ref[s : s + 1].astype(f32), (rows, rows)), 0.0) for s in range(seqs)
    ]
    return jnp.concatenate([jnp.sum(v, axis=1, keepdims=True) for v in spread]).astype(jnp.int32)


def enter_kernel(dims, tok_ref, halo_ref, win_ref, small_ref, vec_ref, gain_ref,
                 ext_ref, z_ref, u_ref, dt_ref, proj_ref, end_ref, dsum_ref, xn):
    seqs, rows, inner, states, rank, taps = dims
    count = seqs * rows
    for ref, at in ((tok_ref, 0), (halo_ref, count)):
        x = ref[...].astype(jnp.float32)
        xn[at : at + x.shape[0]] = (x * normalize(x) * gain_ref[0:1]).astype(jnp.bfloat16)
    proj = jnp.zeros((count, small_ref.shape[1]), jnp.float32)
    for j in range(inner // WIDE):
        cols = slice(j * WIDE, (j + 1) * WIDE)
        part = dot(xn[...], win_ref[:, cols])
        z_ref[:, cols] = dot(xn[:count], win_ref[:, inner + j * WIDE : inner + (j + 1) * WIDE])
        for s in range(seqs):
            ext_ref[s, 0:8, cols] = part[count + 8 * s : count + 8 * s + 8]
            ext_ref[s, 8:, cols] = part[s * rows : (s + 1) * rows]
            pre = conv_sum(ext_ref, s, cols, vec_ref, states, taps, rows)
            u_ref[s * rows : (s + 1) * rows, cols] = pre * sigmoid(pre)
        proj = proj + dot(u_ref[:, cols].astype(jnp.bfloat16), small_ref[cols, :])
    proj_ref[...] = proj
    low = rank_lanes(proj, rank, states)
    for j in range(inner // WIDE):
        cols = slice(j * WIDE, (j + 1) * WIDE)
        pre = dot_nt(low, small_ref[cols, :]) + vec_ref[states + taps + 1 : states + taps + 2, cols]
        dt = jnp.maximum(pre, 0.0) + jnp.log1p(jnp.exp(-jnp.abs(pre)))
        dt_ref[:, cols] = dt
        for s in range(seqs):
            dsum_ref[s, 0:1, cols] = jnp.sum(dt[s * rows : (s + 1) * rows], axis=0, keepdims=True)
    a2 = -jnp.exp(vec_ref[0:states]) * LOG2E
    blocks = inner // 128
    for s in range(seqs):
        def eight(i, hs):
            hs = list(hs)
            at = pl.multiple_of(s * rows + i * 8, 8)
            small = proj_ref[pl.ds(at, 8), :]
            bs = [column(small[j : j + 1], rank, states) for j in range(8)]
            for k in range(blocks):
                sl = slice(k * 128, (k + 1) * 128)
                d8 = dt_ref[pl.ds(at, 8), sl]
                w8 = d8 * u_ref[pl.ds(at, 8), sl]
                for j in range(8):
                    hs[k] = jnp.exp2(d8[j : j + 1] * a2[:, sl]) * hs[k] + bs[j] * w8[j : j + 1]
            return tuple(hs)
        zero = jnp.zeros((states, 128), jnp.float32)
        hs = lax.fori_loop(0, rows // 8, eight, (zero,) * blocks)
        for k in range(blocks):
            end_ref[s, :, k * 128 : (k + 1) * 128] = hs[k]


def rank_lanes(proj, rank, states):
    at = rank + 2 * states
    moved = pltpu.roll(proj, at, axis=1)
    return jnp.where(lanes(proj.shape) >= at, moved, 0.0).astype(jnp.bfloat16)


def leave_kernel(dims, capacity, room, tok_ref, cot_ref, h0_ref, dt_ref, u_ref, z_ref, proj_ref, vec_ref, out_ref,
                 gain_ref, router_ref, route_ref, slot_ref,
                 hist_ref, y_ref, hid_ref, gated_ref, moe_ref, gate_ref, rows_ref,
                 hbuf, hcur, sem, sem0):
    seqs, rows, inner, states, rank, taps = dims
    count = seqs * rows
    a2 = -jnp.exp(vec_ref[0:states]) * LOG2E
    blocks = inner // 128
    groups = rows // GROUP
    size = GROUP * states
    firsts = []
    for s in range(seqs):
        hcur[s] = h0_ref[s].astype(jnp.bfloat16)
        cp = pltpu.make_async_copy(hcur.at[s], hist_ref.at[s, pl.ds(0, states)], sem0.at[s])
        cp.start()
        firsts.append(cp)

    def out_copy(s, g, slot):
        at = pl.multiple_of(states + g * size, states)
        return pltpu.make_async_copy(hbuf.at[slot], hist_ref.at[s, pl.ds(at, size)], sem.at[slot])

    for s in range(seqs):
        def group(g, hs):
            hs = list(hs)
            slot = g % 2

            @pl.when(g >= 2)
            def _():
                out_copy(s, g - 2, slot).wait()
            for half in range(GROUP // 8):
                at = pl.multiple_of(s * rows + g * GROUP + half * 8, 8)
                small = proj_ref[pl.ds(at, 8), :]
                bs = [column(small[j : j + 1], rank, states) for j in range(8)]
                cs = [column(small[j : j + 1], rank + states, states) for j in range(8)]
                for k in range(blocks):
                    sl = slice(k * 128, (k + 1) * 128)
                    d8 = dt_ref[pl.ds(at, 8), sl]
                    w8 = d8 * u_ref[pl.ds(at, 8), sl]
                    parts = []
                    for j in range(8):
                        t = half * 8 + j
                        hs[k] = jnp.exp2(d8[j : j + 1] * a2[:, sl]) * hs[k] + bs[j] * w8[j : j + 1]
                        hbuf[slot, t * states : (t + 1) * states, sl] = hs[k].astype(jnp.bfloat16)
                        parts.append(fold(cs[j] * hs[k]))
                    y_ref[pl.ds(at, 8), sl] = row_sums(parts)
            out_copy(s, g, slot).start()
            return tuple(hs)
        hs = tuple(h0_ref[s, :, k * 128 : (k + 1) * 128] for k in range(blocks))
        lax.fori_loop(0, groups, group, hs)
        for g in (groups - 2, groups - 1):
            out_copy(s, g, g % 2).wait()
    for cp in firsts:
        cp.wait()
    hid = tok_ref[...].astype(jnp.float32)
    for j in range(inner // WIDE):
        cols = slice(j * WIDE, (j + 1) * WIDE)
        y = y_ref[:, cols] + vec_ref[states + taps + 2 : states + taps + 3, cols] * u_ref[:, cols]
        y_ref[:, cols] = y
        z = z_ref[:, cols]
        gated = (y * (z * sigmoid(z))).astype(jnp.bfloat16)
        gated_ref[:, cols] = gated
        hid = hid + dot(gated, out_ref[cols, :])
    hid_ref[...] = hid
    moe_in = (hid * normalize(hid) * gain_ref[1:2]).astype(jnp.bfloat16)
    moe_ref[...] = moe_in
    logits = dot(moe_in, router_ref[...])
    route, slot = as_column(route_ref), as_column(slot_ref)
    chosen = lanes(logits.shape) == route + room
    gate = sigmoid(jnp.sum(jnp.where(chosen, logits, 0.0), axis=1, keepdims=True))
    gate_ref[...] = gate
    kept = (slot < capacity).astype(jnp.float32)
    grad_rows = (cot_ref[...].astype(jnp.float32) * (gate * kept)).astype(jnp.bfloat16)
    total = rows_ref.shape[0]
    place = jnp.where(slot_ref[...] < capacity, route_ref[...] * capacity + slot_ref[...], -1)
    place = jnp.concatenate([place[s : s + 1] for s in range(seqs)], axis=1)
    pick = (subs((total, count)) == place).astype(jnp.bfloat16)
    width = moe_in.shape[1]
    rows_ref[:, :width] = dot(pick, moe_in).astype(jnp.bfloat16)
    rows_ref[:, width:] = dot(pick, grad_rows).astype(jnp.bfloat16)


def erf(x):
    x = jnp.clip(x, -4.0, 4.0)
    x2 = x * x
    top = (-2.72614225801306e-10, 2.77068142495902e-08, -2.10102402082508e-06, -5.69250639462346e-05,
           -7.34990630326855e-04, -2.95459980854025e-03, -1.60960333262415e-02)
    low = (-1.45660718464996e-05, -2.13374055278905e-04, -1.68282697438203e-03, -7.37332916720468e-03,
           -1.42647390514189e-02)
    p = jnp.full_like(x2, top[0])
    for c in top[1:]:
        p = p * x2 + c
    q = jnp.full_like(x2, low[0])
    for c in low[1:]:
        q = q * x2 + c
    return x * p / q


def expert_kernel(rows_ref, up_ref, down_ref, part_ref, dup_ref, ddown_ref):
    width = up_ref.shape[0]
    x, g = rows_ref[:, :width], rows_ref[:, width:]
    hidden = dot(x, up_ref[...])
    half = 0.5 * (1.0 + erf(hidden * math.sqrt(0.5)))
    act = (hidden * half).astype(jnp.bfloat16)
    slope = half + hidden * (jnp.exp(-0.5 * hidden * hidden) * (1.0 / math.sqrt(2.0 * math.pi)))
    part_ref[:, :width] = dot(act, down_ref[...]).astype(jnp.bfloat16)
    grad_hidden = (dot_nt(g, down_ref[...]) * slope).astype(jnp.bfloat16)
    part_ref[:, width:] = dot_nt(grad_hidden, up_ref[...]).astype(jnp.bfloat16)
    ddown, dup = dot_tn(act, g), dot_tn(x, grad_hidden)

    @pl.when(pl.program_id(0) == 0)
    def _():
        dup_ref[...] = dup
        ddown_ref[...] = ddown

    @pl.when(pl.program_id(0) > 0)
    def _():
        dup_ref[...] += dup
        ddown_ref[...] += ddown


def return_kernel(dims, capacity, room, ret_ref, cot_ref, hid_ref, moe_ref, gate_ref, gated_ref, y_ref, u_ref, z_ref, dt_ref,
                  proj_ref, vec_ref, out_ref, gain_ref, router_ref, route_ref, slot_ref,
                  block_ref, ghid_ref, gy_ref, gz_ref, dout_ref, drouter_ref, dskip_ref, dgain_ref, adj_ref):
    seqs, rows, inner, states, rank, taps = dims
    count = seqs * rows
    total, width = ret_ref.shape[0], hid_ref.shape[1]
    route, slot = as_column(route_ref), as_column(slot_ref)
    place = jnp.where(slot < capacity, route * capacity + slot, -1)
    pick = (lanes((count, total)) == place).astype(jnp.bfloat16)
    result = dot(pick, ret_ref[:, :width])
    hid, gate = hid_ref[...], gate_ref[...]
    block_ref[...] = (hid + gate * result).astype(jnp.bfloat16)
    cot = cot_ref[...].astype(jnp.float32)
    grad_gate = jnp.sum(cot * result, axis=1, keepdims=True)
    wide = (count, router_ref.shape[1])
    grad_logits = jnp.where(lanes(wide) == route + room, grad_gate * gate * (1.0 - gate), 0.0).astype(jnp.bfloat16)
    grad_in = dot(pick, ret_ref[:, width:]) + dot_nt(grad_logits, router_ref[...])
    drouter_ref[...] = dot_tn(moe_ref[...], grad_logits)
    r2 = normalize(hid)
    dgain_ref[...] = jnp.sum(grad_in * (hid * r2), axis=0, keepdims=True)
    scaled = grad_in * gain_ref[1:2]
    grad_hid = cot + r2 * scaled - hid * (r2 * r2 * r2) * jnp.mean(scaled * hid, axis=1, keepdims=True)
    ghid_ref[...] = grad_hid
    branch = grad_hid.astype(jnp.bfloat16)
    for j in range(inner // WIDE):
        cols = slice(j * WIDE, (j + 1) * WIDE)
        dout_ref[cols, :] = dot_tn(gated_ref[:, cols], branch).astype(jnp.bfloat16)
        grad = dot_nt(branch, out_ref[cols, :])
        z = z_ref[:, cols]
        sig = sigmoid(z)
        gy = grad * (z * sig)
        gy_ref[:, cols] = gy
        gz_ref[:, cols] = (grad * y_ref[:, cols] * (sig + z * sig * (1.0 - sig))).astype(jnp.bfloat16)
        dskip_ref[:, cols] = jnp.sum(gy * u_ref[:, cols], axis=0, keepdims=True)
    a2 = -jnp.exp(vec_ref[0:states]) * LOG2E
    blocks = inner // 128
    for s in range(seqs):
        def eight(i, ms):
            ms = list(ms)
            at = pl.multiple_of((s + 1) * rows - 8 - i * 8, 8)
            small = proj_ref[pl.ds(at, 8), :]
            cs = [column(small[j : j + 1], rank + states, states) for j in range(8)]
            for k in range(blocks):
                sl = slice(k * 128, (k + 1) * 128)
                d8, g8 = dt_ref[pl.ds(at, 8), sl], gy_ref[pl.ds(at, 8), sl]
                for j in reversed(range(8)):
                    ms[k] = jnp.exp2(d8[j : j + 1] * a2[:, sl]) * (ms[k] + cs[j] * g8[j : j + 1])
            return tuple(ms)
        zero = jnp.zeros((states, 128), jnp.float32)
        ms = lax.fori_loop(0, rows // 8, eight, (zero,) * blocks)
        for k in range(blocks):
            adj_ref[s, :, k * 128 : (k + 1) * 128] = ms[k]


def back_kernel(dims, tok_ref, halo_ref, ext_ref, hist_ref, later_ref, gy_ref, gz_ref, ghid_ref, u_ref, dt_ref,
                proj_ref, win_ref, small_ref, vec_ref, gain_ref,
                dtok_ref, dhalo_ref, din_ref, dsmall_ref, dvec_ref, dgain_ref,
                hbuf, ccol, bcol, gbsum, gcsum, adj, gdt, gu, gproj, gpad, gm, xn, gpre, sem):
    small_ref = small_ref.at[:, 0:TILE]
    seqs, rows, inner, states, rank, taps = dims
    count = seqs * rows
    groups = rows // GROUP
    size = GROUP * states
    steps = seqs * groups

    def fetch(i, slot):
        s, g = i // groups, groups - 1 - i % groups
        at = pl.multiple_of(g * size, size)
        return pltpu.make_async_copy(hist_ref.at[s, pl.ds(at, size + states)], hbuf.at[slot], sem.at[slot])

    fetch(0, 0).start()
    dvec_ref[...] = jnp.zeros_like(dvec_ref)
    strip = 512

    def group(i, carry):
        slot = i % 2
        s, g = i // groups, groups - 1 - i % groups

        @pl.when(i + 1 < steps)
        def _():
            fetch(i + 1, 1 - slot).start()

        @pl.when(g == groups - 1)
        def _():
            adj[...] = later_ref[s]
        at = pl.multiple_of(s * rows + g * GROUP, GROUP)
        small = proj_ref[pl.ds(at, GROUP), :]
        for t in range(GROUP):
            ccol[t] = column(small[t : t + 1], rank + states, states)
            bcol[t] = column(small[t : t + 1], rank, states)
            gbsum[t] = jnp.zeros((states, 128), f32)
            gcsum[t] = jnp.zeros((states, 128), f32)
        fetch(i, slot).wait()
        for c0 in range(0, inner, strip):
            sls = [slice(c0 + k, c0 + k + 128) for k in range(0, strip, 128)]
            rates = [-jnp.exp(vec_ref[0:states, sl]) for sl in sls]
            m = [adj[:, sl] for sl in sls]
            dd = [dvec_ref[0:states, sl] for sl in sls]
            for half in reversed(range(GROUP // 8)):
                a8 = pl.multiple_of(at + half * 8, 8)
                d8 = [dt_ref[pl.ds(a8, 8), sl] for sl in sls]
                g8 = [gy_ref[pl.ds(a8, 8), sl] for sl in sls]
                u8 = [u_ref[pl.ds(a8, 8), sl] for sl in sls]
                w8 = [d * u for d, u in zip(d8, u8)]
                r1, r2 = [[None] * 8 for _ in sls], [[None] * 8 for _ in sls]
                for j in reversed(range(8)):
                    t = half * 8 + j
                    gb = gc = 0.0
                    for k, sl in enumerate(sls):
                        d, gy = d8[k][j : j + 1], g8[k][j : j + 1]
                        a = m[k] + ccol[t] * gy
                        m[k] = jnp.exp2(d * (rates[k] * LOG2E)) * a
                        p = m[k] * hbuf[slot, t * states : (t + 1) * states, sl].astype(f32) * rates[k]
                        dd[k] = dd[k] + p * d
                        gb = gb + a * w8[k][j : j + 1]
                        gc = gc + gy * hbuf[slot, (t + 1) * states : (t + 2) * states, sl].astype(f32)
                        r1[k][j], r2[k][j] = fold(p), fold(a * bcol[t])
                    gbsum[t] += gb
                    gcsum[t] += gc
                for k, sl in enumerate(sls):
                    w1, w2 = row_sums(r1[k]), row_sums(r2[k])
                    gdt[pl.ds(a8, 8), sl] = w1 + u8[k] * w2
                    gu[pl.ds(a8, 8), sl] = d8[k] * w2
            for k, sl in enumerate(sls):
                adj[:, sl] = m[k]
                dvec_ref[0:states, sl] = dd[k]
        square = (states, small.shape[1])
        where, entry = lanes(square), subs(square)
        line = subs((GROUP, small.shape[1]))
        out = jnp.zeros(small.shape, f32)
        for t in range(GROUP):
            gb = jnp.broadcast_to(jnp.sum(gbsum[t], axis=1, keepdims=True), square)
            gc = jnp.broadcast_to(jnp.sum(gcsum[t], axis=1, keepdims=True), square)
            put = jnp.where(where == entry + rank, gb, jnp.where(where == entry + rank + states, gc, 0.0))
            out = jnp.where(line == t, jnp.sum(put, axis=0, keepdims=True), out)
        gproj[pl.ds(at, GROUP), :] = out
        return carry
    lax.fori_loop(0, steps, group, 0)

    low = rank_lanes(proj_ref[...], rank, states)
    at = rank + 2 * states
    row = states + taps
    grad_rank = jnp.zeros(proj_ref.shape, jnp.float32)
    for j in range(inner // WIDE):
        cols = slice(j * WIDE, (j + 1) * WIDE)
        pre = dot_nt(low, small_ref[cols, :]) + vec_ref[row + 1 : row + 2, cols]
        grad_pre = gdt[:, cols] * sigmoid(pre)
        dvec_ref[row + 1 : row + 2, cols] = jnp.sum(grad_pre, axis=0, keepdims=True)
        grad_pre = grad_pre.astype(jnp.bfloat16)
        gpre[:, cols] = grad_pre
        grad_rank = grad_rank + dot(grad_pre, small_ref[cols, :])
    where = lanes(grad_rank.shape)
    grad_rank = pltpu.roll(grad_rank, small_ref.shape[1] - at, axis=1)
    grad_proj = jnp.where(where < rank, grad_rank, jnp.where(where < at, gproj[...], 0.0)).astype(jnp.bfloat16)
    for ref, to in ((tok_ref, 0), (halo_ref, count)):
        x = ref[...].astype(jnp.float32)
        xn[to : to + x.shape[0]] = (x * normalize(x) * gain_ref[0:1]).astype(jnp.bfloat16)
    grad_normed = jnp.zeros((gm.shape[0], xn.shape[1]), jnp.float32)
    first = ext_ref.shape[1] - rows - taps + 1
    for j in range(inner // WIDE):
        cols = slice(j * WIDE, (j + 1) * WIDE)
        dsmall_ref[cols, :] = (
            dot_tn(u_ref[:, cols].astype(jnp.bfloat16), grad_proj) + dot_tn(gpre[:, cols], low)
        ).astype(jnp.bfloat16)
        grad_u = dot_nt(grad_proj, small_ref[cols, :]) + gy_ref[:, cols] * vec_ref[row + 2 : row + 3, cols] + gu[:, cols]
        taps_sum = [0.0] * taps
        bias_sum = 0.0
        heads = []
        for s in range(seqs):
            pre = conv_sum(ext_ref, s, cols, vec_ref, states, taps, rows)
            sig = sigmoid(pre)
            grad_conv = grad_u[s * rows : (s + 1) * rows] * (sig + pre * sig * (1.0 - sig))
            bias_sum = bias_sum + jnp.sum(grad_conv, axis=0, keepdims=True)
            for k in range(taps):
                taps_sum[k] = taps_sum[k] + jnp.sum(
                    grad_conv * ext_ref[s, first + k : first + k + rows, cols], axis=0, keepdims=True)
            gpad[0:8] = jnp.zeros((8, WIDE), jnp.float32)
            gpad[8 : 8 + rows] = grad_conv
            gpad[8 + rows :] = jnp.zeros((8, WIDE), jnp.float32)
            grad = 0.0
            for k in range(taps):
                grad = grad + vec_ref[states + k : states + k + 1, cols] * gpad[taps - 1 - k : taps + 7 - k + rows]
            heads.append(grad[0:8])
            gm[s * rows : (s + 1) * rows, cols] = grad[8:].astype(jnp.bfloat16)
        gm[count:, cols] = jnp.concatenate(heads).astype(jnp.bfloat16)
        dvec_ref[row : row + 1, cols] = bias_sum
        for k in range(taps):
            dvec_ref[states + k : states + k + 1, cols] = taps_sum[k]
        zcols = slice(inner + j * WIDE, inner + (j + 1) * WIDE)
        din_ref[:, cols] = dot_tn(xn[...], gm[:, cols]).astype(jnp.bfloat16)
        din_ref[:, zcols] = dot_tn(xn[:count], gz_ref[:, cols]).astype(jnp.bfloat16)
        gz = jnp.concatenate([gz_ref[:, cols], jnp.zeros((gm.shape[0] - count, WIDE), jnp.bfloat16)])
        grad_normed = grad_normed + dot_nt(gm[:, cols], win_ref[:, cols]) + dot_nt(gz, win_ref[:, zcols])
    gain_sum = 0.0
    for ref, to, base, out in ((tok_ref, 0, ghid_ref, dtok_ref), (halo_ref, count, None, dhalo_ref)):
        x = ref[...].astype(jnp.float32)
        r1 = normalize(x)
        grad = grad_normed[to : to + x.shape[0]]
        gain_sum = gain_sum + jnp.sum(grad * (x * r1), axis=0, keepdims=True)
        grad = grad * gain_ref[0:1]
        grad = r1 * grad - x * (r1 * r1 * r1) * jnp.mean(grad * x, axis=1, keepdims=True)
        out[...] = grad if base is None else grad + base[...]
    dgain_ref[...] = gain_sum


def like(*shape, dtype=f32):
    return jax.ShapeDtypeStruct(shape, dtype)


def params(mib=56):
    return pltpu.CompilerParams(vmem_limit_bytes=mib << 20)


def moe_kernel(seq, rows_ref, up_ref, down_ref, up2_ref, down2_ref,
               back_ref, land_ref, dup_ref, ddown_ref, dup2_ref, ddown2_ref,
               xbuf, part, act, ghid, hid, gact, sib_buf, own_sum,
               local_sem, disp_sem, pass_sem, recv_sem, load_sem, sib_send, sib_recv,
               final_send, final_recv, final_local):
    me = Place(4, seq)
    b, s = me.at()
    y, z, Z, c = me.y, me.z, me.Z, me.c
    cap, wide = rows_ref.shape[1], rows_ref.shape[2]
    width = wide // 2
    share = up_ref.shape[1]
    two = 2 * cap
    block = 2 * two
    sib = me.at(c=1 - c)
    greet([(None, sib)] + [(None, (b, (s + k) % seq)) for k in range(1, seq)])

    def remote(src, dst, send, recv, dev):
        return pltpu.make_async_remote_copy(
            src_ref=src, dst_ref=dst, send_sem=send, recv_sem=recv, device_id=dev, device_id_type=MESH)

    def slab(cc, ss):
        return land_ref.at[cc, pl.ds(pl.multiple_of(ss * cap, 8), cap)]

    def there(k, j):
        return ((z + k) % Z) * 2 + j

    def arrived(cc, ss):
        remote(slab(cc, ss), slab(cc, ss), disp_sem.at[0], recv_sem.at[cc, ss], sib).wait_recv()

    def hand(ss):
        return remote(slab(c, ss), slab(c, ss), pass_sem.at[ss], recv_sem.at[c, ss], sib)

    def load(k, cc):
        zz = (z + k) % Z
        return pltpu.make_async_copy(
            land_ref.at[cc, pl.ds(pl.multiple_of(zz * two, 8), two)],
            xbuf.at[k, pl.ds(pl.multiple_of(cc * two, 16), two)], load_sem.at[k, cc])

    def dispatch(k, j):
        to = ((z + Z - k) % Z) * 2 + j
        return remote(rows_ref.at[to], slab(c, s), disp_sem.at[2 * k + j], recv_sem.at[c, s], (b, to))

    dispatch(0, 1 - y).start()
    own = remote(rows_ref.at[s], slab(c, s), pass_sem.at[s], recv_sem.at[c, s], sib)
    own.start()
    local = pltpu.make_async_copy(rows_ref.at[s], slab(c, s), local_sem)
    local.start()
    for j in range(2):
        dispatch(1, j).start()

    ups, downs = (up_ref, up2_ref), (down_ref, down2_ref)

    def compute(k):
        for i in range(2):
            for n in range(0, share, WIDE):
                to = slice(i * share + n, i * share + n + WIDE)
                hid[:, to] = dot(xbuf[k, :, :width], ups[i][:, n : n + WIDE])
                gact[:, to] = dot_nt(xbuf[k, :, width:], downs[i][n : n + WIDE, :])

        def sixteen(r, carry):
            at = pl.ds(pl.multiple_of(r * 16, 16), 16)
            to = pl.ds(pl.multiple_of(k * block + r * 16, 16), 16)
            h = hid[at, :]
            half = 0.5 * (1.0 + erf(h * math.sqrt(0.5)))
            act[to, :] = (h * half).astype(bf16)
            slope = half + h * (jnp.exp(-0.5 * h * h) * (1.0 / math.sqrt(2.0 * math.pi)))
            ghid[to, :] = (gact[at, :] * slope).astype(bf16)
            return carry
        lax.fori_loop(0, block // 16, sixteen, 0)
        mine = pl.ds(pl.multiple_of(k * block, 16), block)
        for n in range(0, width, WIDE):
            cols = slice(n, n + WIDE)
            part[k, :, cols] = (
                dot(act[mine, :share], down_ref[:, cols]) + dot(act[mine, share:], down2_ref[:, cols])
            ).astype(bf16)
            part[k, :, width + n : width + n + WIDE] = (
                dot_nt(ghid[mine, :share], up_ref[cols, :]) + dot_nt(ghid[mine, share:], up2_ref[cols, :])
            ).astype(bf16)

    def of_core(k, cc):
        return part.at[k, pl.ds(pl.multiple_of(cc * two, 16), two)]

    def to_sib(k):
        return remote(of_core(k, 1 - c), sib_buf.at[k], sib_send.at[k], sib_recv.at[k], sib)

    def to_home(k, j):
        return remote(own_sum.at[k, j], back_ref.at[s], final_send.at[k, j], final_recv.at[s], (b, there(k, j)))

    def keep_home():
        return pltpu.make_async_copy(own_sum.at[0, y], back_ref.at[s], final_local)

    def own_stage(k):
        @pl.when(k == 0)
        def _():
            arrived(c, z * 2 + 1 - y)
            hand(z * 2 + 1 - y).start()
            local.wait()

        @pl.when(k > 0)
        def _():
            for j in range(2):
                arrived(c, there(k, j))
                hand(there(k, j)).start()

        @pl.when(k < Z - 2)
        def _():
            for j in range(2):
                dispatch(k + 2, j).start()
        load(k, c).start()

    def compute_stage(k):
        for j in range(2):
            arrived(1 - c, there(k, j))
        load(k, 1 - c).start()
        for cc in range(2):
            load(k, cc).wait()
        compute(k)
        to_sib(k).start()

    def home_stage(k):
        to_sib(k).wait_recv()
        total = of_core(k, c)[...].astype(f32) + sib_buf[k].astype(f32)
        for j in range(2):
            own_sum[k, j] = total[j * cap : (j + 1) * cap].astype(bf16)

        @pl.when(k > 0)
        def _():
            for j in range(2):
                to_home(k, j).start()

        @pl.when(k == 0)
        def _():
            keep_home().start()
            to_home(0, 1 - y).start()

    everything = (Z * block, width)
    stages = ((own_stage, 0), (home_stage, 2), (compute_stage, 1))

    def step(t, carry):
        for stage, lag in stages:
            k = t - lag
            pl.when(jnp.logical_and(k >= 0, k < Z))(functools.partial(stage, k))
        return carry
    lax.fori_loop(0, Z + 2, step, 0)
    for i, (dup, ddown) in enumerate(((dup2_ref, ddown2_ref), (dup_ref, ddown_ref))):
        for n in range(0, share, WIDE):
            at = (1 - i) * share + n
            x, g = xbuf[:, :, :width].reshape(everything), xbuf[:, :, width:].reshape(everything)
            ddown[n : n + WIDE, :] = dot_tn(act[:, at : at + WIDE], g).astype(ddown.dtype)
            dup[:, n : n + WIDE] = dot_tn(x, ghid[:, at : at + WIDE]).astype(dup.dtype)

    for k in range(1, seq):
        e = (s + k) % seq
        remote(back_ref.at[e], back_ref.at[e], disp_sem.at[0], final_recv.at[e], sib).wait_recv()
    keep_home().wait()
    dispatch(0, 1 - y).wait_send()
    own.wait_send()
    hand(z * 2 + 1 - y).wait_send()
    to_home(0, 1 - y).wait_send()

    def settle(k, carry):
        to_sib(k).wait_send()

        @pl.when(k > 0)
        def _():
            for j in range(2):
                dispatch(k, j).wait_send()
                to_home(k, j).wait_send()
                hand(there(k, j)).wait_send()
        return carry
    lax.fori_loop(0, Z, settle, 0)


def cross(batch, *arrays):
    return [lax.ppermute(a, "batch", [(i, (i + 2) % batch) for i in range(batch)]) for a in arrays]


def moe_rows(batch, seq, sent, up, down, up2, down2):
    width, hidden_share = up.shape
    capacity, wide = sent.shape[1:]
    block = seq * capacity
    if tuned(batch, seq):
        Z, block = seq // 2, 4 * capacity
        dma = pltpu.SemaphoreType.DMA
        out = pl.pallas_call(
            functools.partial(moe_kernel, seq),
            out_shape=[
                like(seq, capacity, wide, dtype=bf16),
                like(2, seq * capacity, wide, dtype=bf16),
                like(width, hidden_share),
                like(hidden_share, width),
                like(width, hidden_share, dtype=bf16),
                like(hidden_share, width, dtype=bf16),
            ],
            in_specs=[HBM] + [VM] * 4,
            out_specs=[HBM, HBM] + [VM] * 4,
            scratch_shapes=[
                pltpu.VMEM((Z, block, wide), bf16),
                pltpu.VMEM((Z, block, wide), bf16),
                pltpu.VMEM((Z * block, 2 * hidden_share), bf16),
                pltpu.VMEM((Z * block, 2 * hidden_share), bf16),
                pltpu.VMEM((block, 2 * hidden_share), f32),
                pltpu.VMEM((block, 2 * hidden_share), f32),
                pltpu.VMEM((Z, 2 * capacity, wide), bf16),
                pltpu.VMEM((Z, 2, capacity, wide), bf16),
                dma,
                dma((2 * Z,)),
                dma((seq,)),
                dma((2, seq)),
                dma((Z, 2)),
                dma((Z,)),
                dma((Z,)),
                dma((Z, 2)),
                dma((seq,)),
                dma,
            ],
            compiler_params=pltpu.CompilerParams(
                collective_id=2, has_side_effects=True, vmem_limit_bytes=56 << 20),
            name="experts",
        )(sent, up, down, up2, down2)
        back, _, d_up, d_down, d_up2, d_down2 = out
        d_up2, d_down2 = cross(batch, d_up2, d_down2)
        return back, d_up, d_down, d_up2, d_down2
    mine = lax.all_to_all(sent, "seq", split_axis=0, concat_axis=0, tiled=True)
    rows = lax.all_gather(mine, "batch", axis=0).reshape(batch * block, wide)
    part, d_up, d_down = pl.pallas_call(
        expert_kernel,
        out_shape=[
            like(batch * block, wide, dtype=bf16),
            like(width, hidden_share),
            like(hidden_share, width),
        ],
        grid=(batch,),
        in_specs=[
            pl.BlockSpec((block, wide), lambda i: (i, 0)),
            pl.BlockSpec((width, hidden_share), lambda i: (0, 0)),
            pl.BlockSpec((hidden_share, width), lambda i: (0, 0)),
        ],
        out_specs=[
            pl.BlockSpec((block, wide), lambda i: (i, 0)),
            pl.BlockSpec((width, hidden_share), lambda i: (0, 0)),
            pl.BlockSpec((hidden_share, width), lambda i: (0, 0)),
        ],
        compiler_params=params(),
        name="experts",
    )(rows, up, down)
    part = part.reshape((batch,) + sent.shape)
    mine = lax.psum_scatter(part, "batch", scatter_dimension=0, tiled=False)
    return lax.all_to_all(mine, "seq", split_axis=0, concat_axis=0, tiled=True), d_up, d_down, None, None


def body(
    tokens,
    in_proj,
    conv_weight,
    conv_bias,
    state_proj,
    step_proj,
    step_bias,
    decay_log,
    skip_gain,
    out_proj,
    norm_gain,
    moe_gain,
    router_proj,
    expert_up,
    expert_down,
    routes,
    slot_index,
    cotangent,
):
    batch, seq = lax.axis_size("batch"), lax.axis_size("seq")
    both = ("batch", "seq")
    seqs, rows, width = tokens.shape
    count = seqs * rows
    devices = batch * seq
    taps, share = conv_weight.shape
    inner = share * devices
    states, rank = decay_log.shape[0], step_proj.shape[0]
    low_share = norm_gain.shape[0]
    experts = router_proj.shape[1]
    capacity = max(2, 5 * count // (4 * experts))
    dims = (seqs, rows, inner, states, rank, taps)
    tile = 128

    lines = (decay_log, conv_weight, conv_bias[None], step_bias[None], skip_gain[None])
    used = sum(a.shape[0] for a in lines)
    room = -(-used // 8) * 8
    fast = tuned(batch, seq)
    if fast:
        in_full, out_full, tail_full, halo = gather_all(
            batch, seq, room, in_proj, out_proj, tokens, state_proj, step_proj, router_proj, lines,
            (norm_gain[None], moe_gain[None]))
        halo = halo.reshape(seqs * 8, width)
    else:
        features = jnp.concatenate([router_proj, norm_gain[:, None], moe_gain[:, None]], axis=1)
        tail = jnp.concatenate(
            [
                state_proj,
                step_proj.T,
                jnp.pad(jnp.concatenate(lines), ((0, room - used), (0, 0))).T,
                jnp.pad(features, ((0, share - low_share), (0, tile - room - features.shape[1]))),
            ],
            axis=1,
        )
        halo = lax.ppermute(tokens[:, rows - taps + 1 :], "seq", [(i, i + 1) for i in range(seq - 1)])
        halo = jnp.pad(halo, ((0, 0), (8 - taps + 1, 0), (0, 0))).reshape(seqs * 8, width)
        in_full, out_full, tail_full = (
            lax.all_gather(a, both, axis=0, tiled=True) for a in (in_proj, out_proj, tail)
        )
    up, down, tail_full = lax.optimization_barrier((expert_up[0], expert_down[0], tail_full))
    up2, down2 = cross(batch, up, down) if fast else (None, None)
    tok, cot = tokens.reshape(count, width), cotangent.reshape(count, width)
    outs = [
        like(seqs, rows + 8, inner),
        like(count, inner),
        like(count, inner),
        like(count, inner),
        like(count, tile),
        like(seqs, states, inner),
        like(seqs, 1, inner),
    ]
    scratch = [pltpu.VMEM((count + seqs * 8, width), bf16)]
    if fast:
        *outs, vec, gain, router = pl.pallas_call(
            partial(enter_packed, dims, share, low_share, experts),
            out_shape=outs + [like(room, inner), like(8, width), like(width, tile, dtype=bf16)],
            in_specs=[VM] * 4,
            out_specs=[VM] * 10,
            scratch_shapes=scratch,
            compiler_params=params(),
            name="enter",
        )(tok, halo, in_full, tail_full)
    else:
        vec = tail_full[:, tile : tile + room].T.astype(f32)
        router = tail_full[:, tile:].reshape(devices, share, tile)[:, :low_share].reshape(width, tile)
        gain = router[:, room + experts : room + experts + 2].T.astype(f32)
        outs = pl.pallas_call(
            partial(enter_kernel, dims),
            out_shape=outs,
            in_specs=[VM] * 6,
            out_specs=[VM] * 7,
            scratch_shapes=scratch,
            compiler_params=params(),
            name="enter",
        )(tok, halo, in_full, tail_full[:, :tile], vec, gain)
    ext, z, u, dt, proj, end, dsum = outs
    before = relay_states(batch, seq, True, states, dsum, vec, end)
    size = GROUP * states
    total = experts * capacity
    hist, y, hid, gated, moe_in, gate, sent = pl.pallas_call(
        partial(leave_kernel, dims, capacity, room),
        out_shape=[
            like(seqs, (rows + 1) * states, inner, dtype=bf16),
            like(count, inner),
            like(count, width),
            like(count, inner, dtype=bf16),
            like(count, width, dtype=bf16),
            like(count, 1),
            like(total, 2 * width, dtype=bf16),
        ],
        in_specs=[VM] * 13,
        out_specs=[HBM] + [VM] * 6,
        scratch_shapes=[
            pltpu.VMEM((2, size, inner), bf16),
            pltpu.VMEM((seqs, states, inner), bf16),
            pltpu.SemaphoreType.DMA((2,)),
            pltpu.SemaphoreType.DMA((seqs,)),
        ],
        compiler_params=params(),
        name="leave",
    )(tok, cot, before, dt, u, z, proj, vec, out_full, gain, router, routes, slot_index)

    back, d_up, d_down, d_up2, d_down2 = moe_rows(
        batch, seq, sent.reshape(experts, capacity, 2 * width), up, down, up2, down2)
    back = back.reshape(total, 2 * width)

    block_out, ghid, gy, gz, d_out, d_router, d_skip, d_moe, adj = pl.pallas_call(
        partial(return_kernel, dims, capacity, room),
        out_shape=[
            like(count, width, dtype=bf16),
            like(count, width),
            like(count, inner),
            like(count, inner, dtype=bf16),
            like(inner, width, dtype=bf16),
            like(width, tile),
            like(1, inner),
            like(1, width),
            like(seqs, states, inner),
        ],
        in_specs=[VM] * 17,
        out_specs=[VM] * 9,
        compiler_params=params(),
        name="back_experts",
    )(back, cot, hid, moe_in, gate, gated, y, u, z, dt, proj, vec, out_full, gain, router, routes, slot_index)
    later = relay_states(batch, seq, False, states, dsum, vec, adj)
    d_tok, d_halo, d_in, d_small, d_vec, d_norm = pl.pallas_call(
        partial(back_kernel, dims),
        out_shape=[
            like(count, width),
            like(seqs * 8, width),
            like(width, 2 * inner, dtype=bf16),
            like(inner, tile, dtype=bf16),
            like(room, inner),
            like(1, width),
        ],
        in_specs=[VM] * 3 + [HBM] + [VM] * 11,
        out_specs=[VM] * 6,
        scratch_shapes=[
            pltpu.VMEM((2, size + states, inner), bf16),
            pltpu.VMEM((GROUP, states, tile), f32),
            pltpu.VMEM((GROUP, states, tile), f32),
            pltpu.VMEM((GROUP, states, tile), f32),
            pltpu.VMEM((GROUP, states, tile), f32),
            pltpu.VMEM((states, inner), f32),
            pltpu.VMEM((count, inner), f32),
            pltpu.VMEM((count, inner), f32),
            pltpu.VMEM((count, tile), f32),
            pltpu.VMEM((rows + 16, WIDE), f32),
            pltpu.VMEM((count + seqs * 8, inner), bf16),
            pltpu.VMEM((count + seqs * 8, width), bf16),
            pltpu.VMEM((count, inner), bf16),
            pltpu.SemaphoreType.DMA((2,)),
        ],
        compiler_params=params(),
        name="back_mixer",
    )(tok, halo, ext, hist, later, gy, gz, ghid, u, dt, proj, in_full, tail_full, vec, gain)

    skip_row = states + taps + 2
    if fast:
        s_in, s_out, s_tail, from_next = reduce_all(
            batch, seq, low_share, experts, skip_row, d_in, d_out, d_small, d_vec, d_skip, d_router, d_norm, d_moe,
            d_halo)
        steps = 4
        slab = lambda a: pl.BlockSpec((a.shape[0] // steps, a.shape[1]), lambda i: (i, 0))
        whole = lambda *shape: pl.BlockSpec(shape, lambda i: (0,) * len(shape))
        edge = pl.BlockSpec((seqs, 8, width), lambda i: (0, rows // 8 - 1, 0))
        shapes = [
            s_in.shape, (taps, share), (1, share), (share, rank + 2 * states), (rank, share), (1, share),
            (states, share), (1, share), s_out.shape, (1, low_share), (1, low_share), (low_share, experts),
        ]
        d_tok, *sums, d_up, d_down = pl.pallas_call(
            partial(finish_kernel, dims, low_share, experts),
            out_shape=[like(*tokens.shape)] + [like(*a) for a in shapes] + [like(*d_up.shape), like(*d_down.shape)],
            grid=(steps,),
            in_specs=[whole(*s_in.shape), whole(*s_out.shape), whole(*s_tail.shape), whole(seqs, 8, width), edge]
            + [slab(a) for a in (d_up, d_up2, d_down, d_down2)],
            out_specs=[edge] + [whole(*a) for a in shapes] + [slab(d_up), slab(d_down)],
            input_output_aliases={4: 0},
            compiler_params=params(),
            name="finish",
        )(s_in, s_out, s_tail, from_next.reshape(seqs, 8, width), d_tok.reshape(tokens.shape), d_up, d_up2, d_down, d_down2)
        for i in (2, 5, 7, 9, 10):
            sums[i] = sums[i][0]
        return (block_out.reshape(tokens.shape), d_tok, *sums, d_up[None], d_down[None])
    d_model = d_router.at[:, room + experts : room + experts + 2].set(jnp.concatenate([d_norm, d_moe]).T)
    d_model = jnp.pad(
        d_model.reshape(devices, low_share, tile)[:, :, room:], ((0, 0), (0, share - low_share), (0, 0))
    ).reshape(inner, tile - room)
    d_vec = d_vec.at[skip_row].set(d_skip[0])
    d_tail = jnp.concatenate([d_small, d_vec.T.astype(bf16), d_model.astype(bf16)], axis=1)
    s_in, s_out, s_tail = (
        lax.psum_scatter(a.astype(f32), both, scatter_dimension=0, tiled=True) for a in (d_in, d_out, d_tail)
    )
    from_next = lax.ppermute(
        d_halo.reshape(seqs, 8, width)[:, 8 - taps + 1 :], "seq", [(i + 1, i) for i in range(seq - 1)]
    )
    d_tok = d_tok.reshape(tokens.shape).at[:, rows - taps + 1 :].add(from_next)
    s_vec = s_tail[:, tile : tile + room].T
    s_model = s_tail[:low_share, tile + room :]
    return (
        block_out.reshape(tokens.shape),
        d_tok,
        s_in,
        s_vec[states : states + taps],
        s_vec[states + taps],
        s_tail[:, : rank + 2 * states],
        s_tail[:, rank + 2 * states : tile].T,
        s_vec[states + taps + 1],
        s_vec[:states],
        s_vec[states + taps + 2],
        s_out,
        s_model[:, experts],
        s_model[:, experts + 1],
        s_model[:, :experts],
        d_up[None],
        d_down[None],
    )


def solution(mesh):
    in_specs = (
        P("batch", "seq", None),
        P(("batch", "seq"), None),
        P(None, ("batch", "seq")),
        P(("batch", "seq")),
        P(("batch", "seq"), None),
        P(None, ("batch", "seq")),
        P(("batch", "seq")),
        P(None, ("batch", "seq")),
        P(("batch", "seq")),
        P(("batch", "seq"), None),
        P(("batch", "seq")),
        P(("batch", "seq")),
        P(("batch", "seq"), None),
        P("seq", None, "batch"),
        P("seq", "batch", None),
        P("batch", "seq"),
        P("batch", "seq"),
        P("batch", "seq", None),
    )
    out_specs = (
        P("batch", "seq", None),
        P("batch", "seq", None),
        P(("batch", "seq"), None),
        P(None, ("batch", "seq")),
        P(("batch", "seq")),
        P(("batch", "seq"), None),
        P(None, ("batch", "seq")),
        P(("batch", "seq")),
        P(None, ("batch", "seq")),
        P(("batch", "seq")),
        P(("batch", "seq"), None),
        P(("batch", "seq")),
        P(("batch", "seq")),
        P(("batch", "seq"), None),
        P("seq", None, "batch"),
        P("seq", "batch", None),
    )
    return jax.shard_map(body, mesh=mesh, in_specs=in_specs, out_specs=out_specs, check_vma=False)
```

```python
from functools import partial
import functools
import math

import jax
import jax.numpy as jnp
from jax import lax
from jax.experimental import pallas as pl
from jax.experimental.pallas import tpu as pltpu
from jax.sharding import PartitionSpec as P

epsilon = 1e-05
MESH = pl.DeviceIdType.MESH
HBM = pl.BlockSpec(memory_space=pl.ANY)
VM = pl.BlockSpec(memory_space=pltpu.VMEM)
bf16, f32 = jnp.bfloat16, jnp.float32


class Place:
    def __init__(self, batch, seq, ydim=2):
        self.batch, self.seq, self.Y = batch, seq, ydim
        self.Z = seq // ydim
        b, s = lax.axis_index("batch"), lax.axis_index("seq")
        self.x, self.c = b // 2, b % 2
        self.z, self.y = s // ydim, s % ydim

    def at(self, x=None, c=None, y=None, z=None):
        pick = lambda v, own: own if v is None else v
        x, c, y, z = pick(x, self.x), pick(c, self.c), pick(y, self.y), pick(z, self.z)
        return (x * 2 + c, z * self.Y + y)

    def index(self, dev):
        return dev[0] * self.seq + dev[1]


def greet(devices):
    barrier = pltpu.get_barrier_semaphore()
    count = 0
    for pred, dev in devices:
        if pred is None:
            pl.semaphore_signal(barrier, inc=1, device_id=dev, device_id_type=MESH)
            count = count + 1
        else:
            @pl.when(pred)
            def _(dev=dev):
                pl.semaphore_signal(barrier, inc=1, device_id=dev, device_id_type=MESH)
            count = count + jnp.where(pred, 1, 0)
    pl.semaphore_wait(barrier, count)


TILE = 128


def spot(rows, at, width):
    return (lanes((rows, width)) == subs((rows, width)) + at).astype(bf16)


def gather_kernel(batch, seq, *refs):
    n_arrays = 3
    in_ref, out_ref, tok_ref, state_ref, step_ref, router_ref = refs[:6]
    lines, gains = refs[6:11], refs[11:13]
    outs, halo_ref = refs[13:16], refs[16]
    tail, vecs, feats, zeros, local_sem, send_sem, recv_sem, halo_sem = refs[17:]
    ins = [in_ref, out_ref, tail]
    me = Place(batch, seq)
    Z, z = me.Z, me.z
    rows = [r.shape[0] for r in ins]
    sib = me.at(c=1 - me.c)
    up_ok, down_ok = z < Z - 1, z > 0
    up, down = me.at(z=z + 1), me.at(z=z - 1)
    nx, ny = me.at(x=1 - me.x), me.at(y=1 - me.y)
    first = me.c == 0
    nb2 = tuple(jnp.where(first, a, b) for a, b in zip(ny, nx))
    nb3 = tuple(jnp.where(first, a, b) for a, b in zip(nx, ny))
    x2, y2 = jnp.where(first, me.x, 1 - me.x), jnp.where(first, 1 - me.y, me.y)
    x3, y3 = jnp.where(first, 1 - me.x, me.x), jnp.where(first, me.y, 1 - me.y)
    b, part_of = me.at()
    has_before, has_after = part_of > 0, part_of < seq - 1
    before, after = (b, part_of - 1), (b, part_of + 1)
    greet([(None, sib), (None, nx), (None, ny), (up_ok, up), (down_ok, down), (has_before, before), (has_after, after)])
    own = me.index(me.at())

    def part(a, index):
        return outs[a].at[pl.ds(pl.multiple_of(index * rows[a], 8), rows[a])]

    sends = []

    def send(pred, index, dev, mine=False):
        slot = len(sends)
        copies = []
        for a in range(n_arrays):
            copies.append(
                pltpu.make_async_remote_copy(
                    src_ref=ins[a] if mine else part(a, index),
                    dst_ref=part(a, index),
                    send_sem=send_sem.at[slot, a],
                    recv_sem=recv_sem.at[index, a],
                    device_id=dev,
                    device_id_type=MESH,
                )
            )

        def go(copies):
            def start():
                for cp in copies:
                    cp.start()
            if pred is None:
                start()
            else:
                pl.when(pred)(start)
        if mine:
            go(copies[:2])
            later.append(lambda: go(copies[2:]))
        else:
            go(copies)
        sends.append((pred, copies))

    def arrive(pred, index, targets):
        def wait():
            for a in range(n_arrays):
                pltpu.make_async_remote_copy(
                    src_ref=part(a, index), dst_ref=part(a, index),
                    send_sem=send_sem.at[0, a], recv_sem=recv_sem.at[index, a],
                    device_id=sib, device_id_type=MESH,
                ).wait_recv()
        if pred is None:
            wait()
        else:
            pl.when(pred)(wait)
        for extra, dev in targets:
            p = pred if extra is None else (extra if pred is None else jnp.logical_and(pred, extra))
            send(p, index, dev)

    later = []
    for dev, pred in ((up, up_ok), (down, down_ok), (nb2, None), (nb3, None), (sib, None)):
        send(pred, own, dev, mine=True)
    seqs, rows_here = tok_ref.shape[:2]
    edge = pl.ds(rows_here - 8, 8)
    halo = pltpu.make_async_remote_copy(
        src_ref=tok_ref.at[:, edge], dst_ref=halo_ref, send_sem=halo_sem.at[0], recv_sem=halo_sem.at[1],
        device_id=after, device_id_type=MESH)
    blank = pltpu.make_async_copy(zeros, halo_ref, halo_sem.at[2])
    zeros[...] = jnp.zeros_like(zeros)
    pl.when(has_after)(halo.start)
    pl.when(jnp.logical_not(has_before))(blank.start)

    share, low_share, experts = state_ref.shape[0], router_ref.shape[1], router_ref.shape[0]
    rank, room, wide = step_ref.shape[0], vecs.shape[0], tail.shape[1]
    vecs[...] = jnp.zeros_like(vecs)
    at = 0
    for ref in lines:
        vecs[at : at + ref.shape[0]] = ref[...].astype(f32)
        at += ref.shape[0]
    feats[...] = jnp.zeros_like(feats)
    for i, ref in enumerate(gains):
        feats[i : i + 1] = ref[...].astype(f32)
    by_channel = (
        dot(state_ref[...], spot(state_ref.shape[1], 0, wide))
        + dot_tn(step_ref[...], spot(rank, TILE - rank, wide))
        + dot_tn(vecs[...].astype(bf16), spot(room, TILE, wide))
    )
    by_feature = dot_tn(router_ref[...], spot(experts, TILE + room, wide)) + dot_tn(
        feats[...].astype(bf16), spot(feats.shape[0], TILE + room + experts, wide))
    by_feature = jnp.concatenate([by_feature, jnp.zeros((share - low_share, wide), f32)])
    tail[...] = (by_channel + by_feature).astype(bf16)
    for start in later:
        start()
    local = [pltpu.make_async_copy(ins[a], part(a, own), local_sem.at[a]) for a in range(n_arrays)]
    for cp in local:
        cp.start()

    def offsets(k):
        return [(None, 0)] if k == 0 else [(z >= k, -k), (z + k < Z, k)]

    def col(k):
        for pred, off in offsets(k):
            fwd = (up_ok, up) if off < 0 else (down_ok, down)
            arrive(pred, me.index(me.at(z=z + off)), [fwd, (None, nb2), (None, nb3), (None, sib)])

    def second(k):
        for pred, off in offsets(k):
            arrive(pred, me.index(me.at(x=x2, y=y2, z=z + off)), [(None, nb3), (None, sib)])

    def third(k):
        for pred, off in offsets(k):
            arrive(pred, me.index(me.at(x=x3, y=y3, z=z + off)), [(None, sib)])

    def fourth(k):
        for pred, off in offsets(k):
            arrive(pred, me.index(me.at(x=1 - me.x, y=1 - me.y, z=z + off)), [(None, sib)])

    for h in range(1, Z + 3):
        if h < Z:
            col(h)
        if 0 <= h - 1 < Z:
            second(h - 1)
        if 0 <= h - 2 < Z:
            third(h - 2)
        if 0 <= h - 3 < Z:
            fourth(h - 3)
    for h in range(Z):
        for xx in (0, 1):
            for yy in (0, 1):
                for pred, off in offsets(h):
                    arrive(pred, me.index(me.at(x=xx, y=yy, c=1 - me.c, z=z + off)), [])
    for cp in local:
        cp.wait()
    pl.when(has_before)(halo.wait_recv)
    pl.when(has_after)(halo.wait_send)
    pl.when(jnp.logical_not(has_before))(blank.wait)
    for pred, copies in sends:
        def done(copies=copies):
            for cp in copies:
                cp.wait_send()
        if pred is None:
            done()
        else:
            pl.when(pred)(done)


def n_sends(Z):
    return 5 + (Z - 1) * 8 + (2 * Z - 1) * 2 + (2 * Z - 1) * 2


def gather_all(batch, seq, room, in_proj, out_proj, tokens, state, step, router, lines, gains):
    count, share = batch * seq, out_proj.shape[0]
    seqs, _, width = tokens.shape
    wide = 2 * TILE
    edge = (seqs, 8, width)
    return pl.pallas_call(
        functools.partial(gather_kernel, batch, seq),
        out_shape=[
            jax.ShapeDtypeStruct((count * a.shape[0],) + a.shape[1:], bf16) for a in (in_proj, out_proj)
        ] + [jax.ShapeDtypeStruct((count * share, wide), bf16), jax.ShapeDtypeStruct(edge, bf16)],
        in_specs=[HBM] * 3 + [VM] * (3 + len(lines) + len(gains)),
        out_specs=[HBM] * 4,
        scratch_shapes=[
            pltpu.VMEM((share, wide), bf16),
            pltpu.VMEM((room, share), f32),
            pltpu.VMEM((8, router.shape[1]), f32),
            pltpu.VMEM(edge, bf16),
            pltpu.SemaphoreType.DMA((3,)),
            pltpu.SemaphoreType.DMA((n_sends(seq // 2), 3)),
            pltpu.SemaphoreType.DMA((count, 3)),
            pltpu.SemaphoreType.DMA((3,)),
        ],
        compiler_params=pltpu.CompilerParams(collective_id=0, has_side_effects=True),
        name="gather_weights",
    )(in_proj, out_proj, tokens, state, step, router, *lines, *gains)


def reduce_kernel(batch, seq, low_share, experts, skip_row, *refs):
    n = 3
    din_ref, dout_ref, dsmall_ref, dvec_ref, dskip_ref, drouter_ref, dnorm_ref, dmoe_ref, dhalo_ref = refs[:9]
    outs, halo_ref = refs[9:12], refs[12]
    refs = refs[13:]
    work, sib_buf, far_buf, near_buf, line_buf = (refs[i * n : (1 + i) * n] for i in range(5))
    tail, zeros, load_sem, send_sem, sib_sem, far_sem, near_sem, line_sem, halo_sem = refs[5 * n :]
    me = Place(batch, seq)
    Z, z = me.Z, me.z
    rows = [r.shape[0] for r in outs]
    sib = me.at(c=1 - me.c)
    up, down = me.at(z=z + 1), me.at(z=z - 1)
    nx, ny = me.at(x=1 - me.x), me.at(y=1 - me.y)
    first = me.c == 0
    pick = lambda flag, a, b: jnp.where(flag, a, b)
    near = tuple(pick(first, a, b) for a, b in zip(ny, nx))
    far = tuple(pick(first, a, b) for a, b in zip(nx, ny))
    b, part_of = me.at()
    has_before, has_after = part_of > 0, part_of < seq - 1
    before, after = (b, part_of - 1), (b, part_of + 1)
    greet([(None, sib), (None, nx), (None, ny), (z < Z - 1, up), (z > 0, down), (has_before, before), (has_after, after)])

    def groups(c):
        f = c == 0
        ox, oy = 1 - me.x, 1 - me.y
        return [
            (ox, oy),
            (pick(f, ox, me.x), pick(f, me.y, oy)),
            (pick(f, me.x, ox), pick(f, oy, me.y)),
            (me.x, me.y),
        ]

    def slot(xy, zz):
        return (xy[0] * 2 + xy[1]) * Z + zz

    def turn(k):
        return (z + 1 + k) % Z

    sends = []

    def send(pred, srcs, dsts, recv, dev):
        copies = [
            pltpu.make_async_remote_copy(
                src_ref=srcs[a], dst_ref=dsts[a], send_sem=send_sem.at[len(sends), a],
                recv_sem=recv(a), device_id=dev, device_id_type=MESH)
            for a in range(n)
        ]

        def go():
            for cp in copies:
                cp.start()
        if pred is None:
            go()
        else:
            pl.when(pred)(go)
        sends.append((pred, copies))

    def take(bufs, recv):
        for a in range(n):
            pltpu.make_async_remote_copy(
                src_ref=bufs[a], dst_ref=bufs[a], send_sem=send_sem.at[0, a],
                recv_sem=recv(a), device_id=sib, device_id_type=MESH).wait_recv()

    def source(a, c, xy, zz):
        index = me.index((xy[0] * 2 + c, zz * me.Y + xy[1]))
        if a == 2:
            return tail.at[index]
        return (din_ref, dout_ref)[a].at[pl.ds(pl.multiple_of(index * rows[a], 8), rows[a])]

    halo = pltpu.make_async_remote_copy(
        src_ref=dhalo_ref, dst_ref=halo_ref, send_sem=halo_sem.at[0], recv_sem=halo_sem.at[1],
        device_id=before, device_id_type=MESH)
    blank = pltpu.make_async_copy(zeros, halo_ref, halo_sem.at[2])
    zeros[...] = jnp.zeros_like(zeros)
    pl.when(has_before)(halo.start)
    pl.when(jnp.logical_not(has_after))(blank.start)

    other = 1 - me.c
    mine = groups(me.c)
    first_sends, loads = [], []
    for xy in groups(other):
        for k in range(Z):
            s = slot(xy, turn(k))
            copies = [
                pltpu.make_async_remote_copy(
                    src_ref=source(a, other, xy, turn(k)), dst_ref=sib_buf[a].at[s],
                    send_sem=send_sem.at[len(sends), a], recv_sem=sib_sem.at[s, a],
                    device_id=sib, device_id_type=MESH)
                for a in range(n)
            ]
            sends.append((None, copies))
            first_sends.append(copies)
    for xy in mine:
        for k in range(Z):
            s = slot(xy, turn(k))
            loads.append([
                pltpu.make_async_copy(source(a, me.c, xy, turn(k)), work[a].at[s], load_sem.at[s, a]) for a in range(n)
            ])
    for copies in first_sends + loads:
        for cp in copies[:2]:
            cp.start()

    room, share = dvec_ref.shape[0], tail.shape[1]
    blocks, width = tail.shape[0], drouter_ref.shape[0]
    vec = jnp.where(subs(dvec_ref.shape) == skip_row, dskip_ref[...], dvec_ref[...])
    line = subs((8, width))
    gains = jnp.where(line == 0, dnorm_ref[...], jnp.where(line == 1, dmoe_ref[...], 0.0))
    model = drouter_ref[...] + dot_tn(gains.astype(bf16), spot(8, room + experts, TILE))
    model = jnp.concatenate(
        [model.reshape(blocks, low_share, TILE), jnp.zeros((blocks, share - low_share, TILE), f32)], axis=1)
    right = dot_tn(vec.astype(bf16), spot(room, 0, TILE)).reshape(blocks, share, TILE) + model
    tail[:, :, 0:TILE] = dsmall_ref[...].reshape(blocks, share, TILE)
    tail[:, :, TILE:] = right.astype(bf16)
    for copies in first_sends + loads:
        copies[2].start()

    def total(bufs):
        t = bufs[0][...].astype(jnp.float32)
        for b in bufs[1:]:
            t = t + b[...].astype(jnp.float32)
        return t

    for g, xy in enumerate(mine):
        for k in range(Z):
            zz = turn(k)
            s = slot(xy, zz)
            for cp in loads[g * Z + k]:
                cp.wait()
            take([sib_buf[a].at[s] for a in range(n)], lambda a: sib_sem.at[s, a])
            parts = [[work[a].at[s], sib_buf[a].at[s]] for a in range(n)]
            if g >= 2:
                fs = (g - 2) * Z + zz
                take([far_buf[a].at[fs] for a in range(n)], lambda a: far_sem.at[fs, a])
                for a in range(n):
                    parts[a].append(far_buf[a].at[fs])
            if g == 3:
                take([near_buf[a].at[zz] for a in range(n)], lambda a: near_sem.at[zz, a])
                for a in range(n):
                    parts[a].append(near_buf[a].at[zz])
            if g < 3:
                for a in range(n):
                    work[a][s] = total(parts[a]).astype(jnp.bfloat16)
                srcs = [work[a].at[s] for a in range(n)]
                if g < 2:
                    fs = g * Z + zz
                    send(None, srcs, [far_buf[a].at[fs] for a in range(n)],
                         lambda a: far_sem.at[fs, a], far)
                else:
                    send(None, srcs, [near_buf[a].at[zz] for a in range(n)],
                         lambda a: near_sem.at[zz, a], near)
                continue
            if k < Z - 1:
                rising = zz > z
                side = jnp.where(rising, 0, 1)
                more = jnp.where(rising, z, Z - 1 - z) > 0
                line = [line_buf[a].at[side, zz] for a in range(n)]
                for a in range(n):
                    work[a][s] = total(parts[a]).astype(jnp.bfloat16)

                @pl.when(more)
                def _():
                    take(line, lambda a: line_sem.at[side, zz, a])
                    for a in range(n):
                        work[a][s] = total([work[a].at[s], line[a]]).astype(jnp.bfloat16)
                dev = (me.at()[0], jnp.where(rising, up[1], down[1]))
                send(None, [work[a].at[s] for a in range(n)], line,
                     lambda a: line_sem.at[side, zz, a], dev)
            else:
                for a in range(n):
                    outs[a][...] = total(parts[a])
                for side, pred in ((0, z > 0), (1, z < Z - 1)):
                    @pl.when(pred)
                    def _(side=side):
                        line = [line_buf[a].at[side, zz] for a in range(n)]
                        take(line, lambda a: line_sem.at[side, zz, a])
                        for a in range(n):
                            outs[a][...] = outs[a][...] + line[a][...].astype(jnp.float32)
    pl.when(has_after)(halo.wait_recv)
    pl.when(has_before)(halo.wait_send)
    pl.when(jnp.logical_not(has_after))(blank.wait)
    for pred, copies in sends:
        for cp in copies:
            cp.wait_send()


def reduce_all(batch, seq, low_share, experts, skip_row, d_in, d_out, *rest):
    count, Z, n = batch * seq, seq // 2, 3
    wide = 2 * TILE
    share = d_out.shape[0] // count
    shapes = [(a.shape[0] // count,) + a.shape[1:] for a in (d_in, d_out)] + [(share, wide)]
    edge = rest[-1].shape
    half = count // 2
    scratch = []
    for lead in ((half,), (half,), (2 * Z,), (Z,), (2, Z)):
        scratch += [pltpu.VMEM(lead + s, bf16) for s in shapes]
    dma = pltpu.SemaphoreType.DMA
    scratch += [
        pltpu.VMEM((count, share, wide), bf16),
        pltpu.VMEM(edge, f32),
        dma((half, n)),
        dma((half + 4 * Z, n)),
        dma((half, n)),
        dma((2 * Z, n)),
        dma((Z, n)),
        dma((2, Z, n)),
        dma((3,)),
    ]
    return pl.pallas_call(
        functools.partial(reduce_kernel, batch, seq, low_share, experts, skip_row),
        out_shape=[jax.ShapeDtypeStruct(s, f32) for s in shapes] + [jax.ShapeDtypeStruct(edge, f32)],
        in_specs=[HBM] * 2 + [VM] * 7,
        out_specs=[VM] * 3 + [HBM],
        scratch_shapes=scratch,
        compiler_params=pltpu.CompilerParams(
            collective_id=1, has_side_effects=True, vmem_limit_bytes=58 << 20),
        name="reduce_grads",
    )(d_in, d_out, *rest)


def finish_kernel(dims, low_share, experts, in_ref, out_ref, tail_ref, halo_ref, tok_ref, block_ref, up_ref, up2_ref,
                  down_ref, down2_ref, block_out, tok_out, din, dconv, dbias, dstate, dstep, dstep_bias, ddecay, dskip, dout, dnorm, dmoe,
                  drouter, dup, ddown):
    seqs, rows, inner, states, rank, taps = dims
    dup[...] = up_ref[...] + up2_ref[...].astype(f32)
    ddown[...] = down_ref[...] + down2_ref[...].astype(f32)
    block_out[...] = block_ref[...]
    tok_out[...] = tok_ref[...]

    @pl.when(pl.program_id(0) == pl.num_programs(0) - 1)
    def _():
        tok_out[:, tok_ref.shape[1] - 8 :] = tok_ref[:, tok_ref.shape[1] - 8 :] + halo_ref[...]

    @pl.when(pl.program_id(0) == 0)
    def _():
        din[...] = in_ref[...]
        dout[...] = out_ref[...]
        tail = tail_ref[...]
        share, wide = tail.shape
        eye = (lanes((wide, wide)) == subs((wide, wide))).astype(f32)
        turned = lax.dot_general(
            eye, tail, (((1,), (1,)), ((), ())), precision=lax.Precision.HIGHEST, preferred_element_type=f32)
        dstate[...] = tail[:, : rank + 2 * states]
        dstep[...] = turned[TILE - rank : TILE]
        ddecay[...] = turned[TILE : TILE + states]
        dconv[...] = turned[TILE + states : TILE + states + taps]
        at = TILE + states + taps
        dbias[...] = turned[at : at + 1]
        dstep_bias[...] = turned[at + 1 : at + 2]
        dskip[...] = turned[at + 2 : at + 3]
        at = TILE + -(-(states + taps + 3) // 8) * 8
        drouter[...] = turned[at : at + experts, :low_share]
        at += experts
        dnorm[...] = turned[at : at + 1, :low_share]
        dmoe[...] = turned[at + 1 : at + 2, :low_share]


def tuned(batch, seq):
    return batch == 4 and seq == 8


def chain_kernel(seq, forward, dsum_ref, rates_ref, end_ref, out_ref, held, outgoing, send_sem, recv_sem):
    s = lax.axis_index("seq")
    b = lax.axis_index("batch")
    step = 1 if forward else -1
    has_before = s > 0 if forward else s < seq - 1
    has_after = s < seq - 1 if forward else s > 0
    before, after = (b, s - step), (b, s + step)
    barrier = pltpu.get_barrier_semaphore()
    for pred, dev in ((has_before, before), (has_after, after)):
        @pl.when(pred)
        def _(dev=dev):
            pl.semaphore_signal(barrier, inc=1, device_id=dev, device_id_type=MESH)
    pl.semaphore_wait(barrier, jnp.where(has_before, 1, 0) + jnp.where(has_after, 1, 0))
    count = end_ref.shape[0]

    def copy(i):
        return pltpu.make_async_remote_copy(
            src_ref=outgoing.at[i], dst_ref=held.at[i], send_sem=send_sem.at[i],
            recv_sem=recv_sem.at[i], device_id=after, device_id_type=MESH)

    for i in range(count):
        @pl.when(has_before)
        def _(i=i):
            copy(i).wait_recv()
            out_ref[i] = held[i].astype(jnp.float32)
            decay = jnp.exp(rates_ref[...] * dsum_ref[i])
            outgoing[i] = (end_ref[i] + decay * out_ref[i]).astype(jnp.bfloat16)

        @pl.when(jnp.logical_not(has_before))
        def _(i=i):
            out_ref[i] = jnp.zeros_like(out_ref[i])
            outgoing[i] = end_ref[i].astype(jnp.bfloat16)

        @pl.when(has_after)
        def _(i=i):
            copy(i).start()
    for i in range(count):
        @pl.when(has_after)
        def _(i=i):
            copy(i).wait_send()


def chain_states(seq, forward, dsum, rates, end):
    vm = pl.BlockSpec(memory_space=pltpu.VMEM)
    return pl.pallas_call(
        functools.partial(chain_kernel, seq, forward),
        out_shape=jax.ShapeDtypeStruct(end.shape, jnp.float32),
        in_specs=[vm] * 3,
        out_specs=vm,
        scratch_shapes=[
            pltpu.VMEM(end.shape, jnp.bfloat16),
            pltpu.VMEM(end.shape, jnp.bfloat16),
            pltpu.SemaphoreType.DMA((end.shape[0],)),
            pltpu.SemaphoreType.DMA((end.shape[0],)),
        ],
        compiler_params=pltpu.CompilerParams(
            collective_id=5 if forward else 6, has_side_effects=True),
        name="chain_forward" if forward else "chain_backward",
    )(dsum, rates, end)


class Relay:
    def __init__(self, seq, forward, states, dsum_ref, vec_ref, end_ref, out_ref, mine, theirs, their_sum, held,
                 outgoing, pair_send, pair_recv, line_send, line_recv):
        me = Place(4, seq)
        y, z, last = me.y, me.z, me.Z - 1
        step = 1 if forward else -1
        self.first = y == (0 if forward else 1)
        self.has_before = z > 0 if forward else z < last
        self.has_after = z < last if forward else z > 0
        self.pair, self.before, self.after = me.at(y=1 - y), me.at(z=z - step), me.at(z=z + step)
        self.states, self.vec_ref, self.end_ref, self.out_ref = states, vec_ref, end_ref, out_ref
        self.mine, self.theirs, self.dsum_ref, self.their_sum = mine, theirs, dsum_ref, their_sum
        self.held, self.outgoing = held, outgoing
        self.pair_send, self.pair_recv, self.line_send, self.line_recv = pair_send, pair_recv, line_send, line_recv
        self.count = end_ref.shape[0]

    def peers(self):
        return [(None, self.pair), (self.has_before, self.before), (self.has_after, self.after)]

    def swaps(self, i):
        both = ((self.mine.at[i], self.theirs.at[i]), (self.dsum_ref.at[i], self.their_sum.at[i]))
        return [
            pltpu.make_async_remote_copy(
                src_ref=src, dst_ref=dst, send_sem=self.pair_send.at[i, k], recv_sem=self.pair_recv.at[i, k],
                device_id=self.pair, device_id_type=MESH)
            for k, (src, dst) in enumerate(both)
        ]

    def onward(self, i):
        return pltpu.make_async_remote_copy(
            src_ref=self.outgoing.at[i], dst_ref=self.held.at[i], send_sem=self.line_send.at[i],
            recv_sem=self.line_recv.at[i], device_id=self.after, device_id_type=MESH)

    def start(self, i):
        self.mine[i] = self.end_ref[i].astype(bf16)
        for cp in self.swaps(i):
            cp.start()

    def finish(self, i):
        rates = -jnp.exp(self.vec_ref[0 : self.states])
        for cp in self.swaps(i):
            cp.wait_recv()
        pick = lambda a, b: (jnp.where(self.first, a, b), jnp.where(self.first, b, a))
        early, late = pick(self.end_ref[i], self.theirs[i].astype(f32))
        early_sum, late_sum = pick(self.dsum_ref[i], self.their_sum[i])
        both = late + jnp.exp(rates * late_sum) * early

        @pl.when(self.has_before)
        def _():
            self.onward(i).wait_recv()
            arrived = self.held[i].astype(f32)
            self.outgoing[i] = (both + jnp.exp(rates * (early_sum + late_sum)) * arrived).astype(bf16)

        @pl.when(jnp.logical_not(self.has_before))
        def _():
            self.outgoing[i] = both.astype(bf16)

        @pl.when(self.has_after)
        def _():
            self.onward(i).start()

        @pl.when(self.has_before)
        def _():
            arrived = self.held[i].astype(f32)
            self.out_ref[i] = jnp.where(self.first, arrived, early + jnp.exp(rates * early_sum) * arrived)

        @pl.when(jnp.logical_not(self.has_before))
        def _():
            self.out_ref[i] = jnp.where(self.first, jnp.zeros_like(early), early)

    def settle(self):
        for i in range(self.count):
            for cp in self.swaps(i):
                cp.wait_send()
            pl.when(self.has_after)(self.onward(i).wait_send)


def relay_scratch(seqs, states, inner):
    n, state = seqs, (seqs, states, inner)
    dma = pltpu.SemaphoreType.DMA
    return [
        pltpu.VMEM(state, bf16),
        pltpu.VMEM(state, bf16),
        pltpu.VMEM((seqs, 1, inner), f32),
        pltpu.VMEM(state, bf16),
        pltpu.VMEM(state, bf16),
        dma((n, 2)),
        dma((n, 2)),
        dma((n,)),
        dma((n,)),
    ]


def dot(a, b):
    return jnp.dot(a, b, preferred_element_type=jnp.float32)


def dot_nt(a, b):
    return lax.dot_general(a, b, (((1,), (1,)), ((), ())), preferred_element_type=jnp.float32)


def dot_tn(a, b):
    return lax.dot_general(a, b, (((0,), (0,)), ((), ())), preferred_element_type=jnp.float32)


def sigmoid(v):
    return 1.0 / (1.0 + jnp.exp(-v))


def lanes(shape):
    return lax.broadcasted_iota(jnp.int32, shape, 1)


def subs(shape):
    return lax.broadcasted_iota(jnp.int32, shape, 0)


def column(row, base, states):
    shape = (states, row.shape[1])
    only = jnp.where(lanes(shape) == subs(shape) + base, jnp.broadcast_to(row, shape), 0.0)
    return jnp.broadcast_to(jnp.sum(only, axis=1, keepdims=True), shape)


def row_sums(parts):
    row = subs(parts[0].shape)
    four, two, one = row < 4, (row // 2) % 2 == 0, row % 2 == 0
    turn = lambda v, by: pltpu.roll(v, by, axis=0)
    a = [
        jnp.where(four, parts[j], parts[j + 4]) + turn(jnp.where(four, parts[j + 4], parts[j]), 4)
        for j in range(4)
    ]
    b = [jnp.where(two, a[j] + turn(a[j], 6), a[j + 2] + turn(a[j + 2], 2)) for j in range(2)]
    return jnp.where(one, b[0] + turn(b[0], 7), b[1] + turn(b[1], 1))


def fold(v):
    return sum(v[i : i + 8] for i in range(8, v.shape[0], 8)) + v[:8]


WIDE = 256
GROUP = 16
LOG2E = math.log2(math.e)
AHEAD = 256


def conv_sum(ext_ref, s, cols, vec_ref, states, taps, rows):
    first = ext_ref.shape[1] - rows - taps + 1
    total = vec_ref[states + taps : states + taps + 1, cols]
    for k in range(taps):
        total = total + vec_ref[states + k : states + k + 1, cols] * ext_ref[s, first + k : first + k + rows, cols]
    return total


def normalize(x):
    return lax.rsqrt(jnp.mean(x * x, axis=-1, keepdims=True) + epsilon)


class Quiet:
    def __getattr__(self, name):
        return lambda *args: None


QUIET = Quiet()


class Hooks(Quiet):
    def __init__(self, **steps):
        self.__dict__.update(steps)


def unpack(tail_ref, share, low_share, room, experts, vec_ref, gain_ref, router_ref):
    right = tail_ref[:, TILE : 2 * TILE]
    vec_ref[...] = dot_nt(spot(room, 0, TILE), right)
    blocks = right.shape[0] // share
    model = right.astype(f32).reshape(blocks, share, TILE)[:, :low_share].reshape(blocks * low_share, TILE).astype(bf16)
    router_ref[...] = model
    gain_ref[...] = dot_nt(spot(gain_ref.shape[0], room + experts, TILE), model)


def enter_packed(dims, share, low_share, experts, tok_ref, halo_ref, win_ref, tail_ref,
                 ext_ref, z_ref, u_ref, dt_ref, proj_ref, end_ref, dsum_ref, vec_ref, gain_ref, router_ref, xn,
                 hooks=QUIET):
    unpack(tail_ref, share, low_share, vec_ref.shape[0], experts, vec_ref, gain_ref, router_ref)
    enter_kernel(dims, tok_ref, halo_ref, win_ref, tail_ref.at[:, 0:TILE], vec_ref, gain_ref,
                 ext_ref, z_ref, u_ref, dt_ref, proj_ref, end_ref, dsum_ref, xn, hooks)


def as_column(ref):
    seqs, rows = ref.shape
    diagonal = lanes((rows, rows)) == subs((rows, rows))
    spread = [
        jnp.where(diagonal, jnp.broadcast_to(ref[s : s + 1].astype(f32), (rows, rows)), 0.0) for s in range(seqs)
    ]
    return jnp.concatenate([jnp.sum(v, axis=1, keepdims=True) for v in spread]).astype(jnp.int32)


def enter_kernel(dims, tok_ref, halo_ref, win_ref, small_ref, vec_ref, gain_ref,
                 ext_ref, z_ref, u_ref, dt_ref, proj_ref, end_ref, dsum_ref, xn, hooks=QUIET):
    seqs, rows, inner, states, rank, taps = dims
    count = seqs * rows
    for ref, at in ((tok_ref, 0), (halo_ref, count)):
        x = ref[...].astype(jnp.float32)
        xn[at : at + x.shape[0]] = (x * normalize(x) * gain_ref[0:1]).astype(jnp.bfloat16)
    proj = jnp.zeros((count, small_ref.shape[1]), jnp.float32)
    for j in range(inner // WIDE):
        cols = slice(j * WIDE, (j + 1) * WIDE)
        hooks.weights(j)
        part = dot(xn[...], win_ref[:, cols])
        z_ref[:, cols] = dot(xn[:count], win_ref[:, inner + j * WIDE : inner + (j + 1) * WIDE])
        for s in range(seqs):
            ext_ref[s, 0:8, cols] = part[count + 8 * s : count + 8 * s + 8]
            ext_ref[s, 8:, cols] = part[s * rows : (s + 1) * rows]
            pre = conv_sum(ext_ref, s, cols, vec_ref, states, taps, rows)
            u_ref[s * rows : (s + 1) * rows, cols] = pre * sigmoid(pre)
        proj = proj + dot(u_ref[:, cols].astype(jnp.bfloat16), small_ref[cols, :])
    proj_ref[...] = proj
    low = rank_lanes(proj, rank, states)
    for j in range(inner // WIDE):
        cols = slice(j * WIDE, (j + 1) * WIDE)
        pre = dot_nt(low, small_ref[cols, :]) + vec_ref[states + taps + 1 : states + taps + 2, cols]
        dt = jnp.maximum(pre, 0.0) + jnp.log1p(jnp.exp(-jnp.abs(pre)))
        dt_ref[:, cols] = dt
        for s in range(seqs):
            dsum_ref[s, 0:1, cols] = jnp.sum(dt[s * rows : (s + 1) * rows], axis=0, keepdims=True)
    hooks.projected()
    a2 = -jnp.exp(vec_ref[0:states]) * LOG2E
    blocks = inner // 128
    for s in range(seqs):
        def eight(i, hs):
            hs = list(hs)
            at = pl.multiple_of(s * rows + i * 8, 8)
            small = proj_ref[pl.ds(at, 8), :]
            bs = [column(small[j : j + 1], rank, states) for j in range(8)]
            for k in range(blocks):
                sl = slice(k * 128, (k + 1) * 128)
                d8 = dt_ref[pl.ds(at, 8), sl]
                w8 = d8 * u_ref[pl.ds(at, 8), sl]
                for j in range(8):
                    hs[k] = jnp.exp2(d8[j : j + 1] * a2[:, sl]) * hs[k] + bs[j] * w8[j : j + 1]
            return tuple(hs)
        zero = jnp.zeros((states, 128), jnp.float32)
        hs = lax.fori_loop(0, rows // 8, eight, (zero,) * blocks)
        for k in range(blocks):
            end_ref[s, :, k * 128 : (k + 1) * 128] = hs[k]
        hooks.scanned(s)


def rank_lanes(proj, rank, states):
    at = rank + 2 * states
    moved = pltpu.roll(proj, at, axis=1)
    return jnp.where(lanes(proj.shape) >= at, moved, 0.0).astype(jnp.bfloat16)


def leave_kernel(dims, capacity, room, tok_ref, cot_ref, h0_ref, dt_ref, u_ref, z_ref, proj_ref, vec_ref, out_ref,
                 gain_ref, router_ref, route_ref, slot_ref,
                 hist_ref, y_ref, hid_ref, gated_ref, moe_ref, gate_ref, rows_ref,
                 hbuf, hcur, sem, sem0, hooks=QUIET):
    seqs, rows, inner, states, rank, taps = dims
    count = seqs * rows
    a2 = -jnp.exp(vec_ref[0:states]) * LOG2E
    blocks = inner // 128
    groups = rows // GROUP
    size = GROUP * states
    firsts = []
    for s in range(seqs):
        hcur[s] = h0_ref[s].astype(jnp.bfloat16)
        cp = pltpu.make_async_copy(hcur.at[s], hist_ref.at[s, pl.ds(0, states)], sem0.at[s])
        cp.start()
        firsts.append(cp)

    def out_copy(s, g, slot):
        at = pl.multiple_of(states + g * size, states)
        return pltpu.make_async_copy(hbuf.at[slot], hist_ref.at[s, pl.ds(at, size)], sem.at[slot])

    for s in range(seqs):
        def group(g, hs):
            hs = list(hs)
            slot = g % 2

            @pl.when(g >= 2)
            def _():
                out_copy(s, g - 2, slot).wait()
            for half in range(GROUP // 8):
                at = pl.multiple_of(s * rows + g * GROUP + half * 8, 8)
                small = proj_ref[pl.ds(at, 8), :]
                bs = [column(small[j : j + 1], rank, states) for j in range(8)]
                cs = [column(small[j : j + 1], rank + states, states) for j in range(8)]
                for k in range(blocks):
                    sl = slice(k * 128, (k + 1) * 128)
                    d8 = dt_ref[pl.ds(at, 8), sl]
                    w8 = d8 * u_ref[pl.ds(at, 8), sl]
                    parts = []
                    for j in range(8):
                        t = half * 8 + j
                        hs[k] = jnp.exp2(d8[j : j + 1] * a2[:, sl]) * hs[k] + bs[j] * w8[j : j + 1]
                        hbuf[slot, t * states : (t + 1) * states, sl] = hs[k].astype(jnp.bfloat16)
                        parts.append(fold(cs[j] * hs[k]))
                    y_ref[pl.ds(at, 8), sl] = row_sums(parts)
            out_copy(s, g, slot).start()
            return tuple(hs)
        hs = tuple(h0_ref[s, :, k * 128 : (k + 1) * 128] for k in range(blocks))
        lax.fori_loop(0, groups, group, hs)
        for g in (groups - 2, groups - 1):
            out_copy(s, g, g % 2).wait()
    for cp in firsts:
        cp.wait()
    hooks.out_proj()
    hid = tok_ref[...].astype(jnp.float32)
    for j in range(inner // WIDE):
        cols = slice(j * WIDE, (j + 1) * WIDE)
        y = y_ref[:, cols] + vec_ref[states + taps + 2 : states + taps + 3, cols] * u_ref[:, cols]
        y_ref[:, cols] = y
        z = z_ref[:, cols]
        gated = (y * (z * sigmoid(z))).astype(jnp.bfloat16)
        gated_ref[:, cols] = gated
        hid = hid + dot(gated, out_ref[cols, :])
    hooks.mixed()
    hid_ref[...] = hid
    moe_in = (hid * normalize(hid) * gain_ref[1:2]).astype(jnp.bfloat16)
    moe_ref[...] = moe_in
    logits = dot(moe_in, router_ref[...])
    route, slot = as_column(route_ref), as_column(slot_ref)
    chosen = lanes(logits.shape) == route + room
    gate = sigmoid(jnp.sum(jnp.where(chosen, logits, 0.0), axis=1, keepdims=True))
    gate_ref[...] = gate
    kept = (slot < capacity).astype(jnp.float32)
    grad_rows = (cot_ref[...].astype(jnp.float32) * (gate * kept)).astype(jnp.bfloat16)
    total = rows_ref.shape[0]
    place = jnp.where(slot_ref[...] < capacity, route_ref[...] * capacity + slot_ref[...], -1)
    place = jnp.concatenate([place[s : s + 1] for s in range(seqs)], axis=1)
    pick = (subs((total, count)) == place).astype(jnp.bfloat16)
    width = moe_in.shape[1]
    rows_ref[:, :width] = dot(pick, moe_in).astype(jnp.bfloat16)
    rows_ref[:, width:] = dot(pick, grad_rows).astype(jnp.bfloat16)


def erf(x):
    x = jnp.clip(x, -4.0, 4.0)
    x2 = x * x
    top = (-2.72614225801306e-10, 2.77068142495902e-08, -2.10102402082508e-06, -5.69250639462346e-05,
           -7.34990630326855e-04, -2.95459980854025e-03, -1.60960333262415e-02)
    low = (-1.45660718464996e-05, -2.13374055278905e-04, -1.68282697438203e-03, -7.37332916720468e-03,
           -1.42647390514189e-02)
    p = jnp.full_like(x2, top[0])
    for c in top[1:]:
        p = p * x2 + c
    q = jnp.full_like(x2, low[0])
    for c in low[1:]:
        q = q * x2 + c
    return x * p / q


def expert_kernel(rows_ref, up_ref, down_ref, part_ref, dup_ref, ddown_ref):
    width = up_ref.shape[0]
    x, g = rows_ref[:, :width], rows_ref[:, width:]
    hidden = dot(x, up_ref[...])
    half = 0.5 * (1.0 + erf(hidden * math.sqrt(0.5)))
    act = (hidden * half).astype(jnp.bfloat16)
    slope = half + hidden * (jnp.exp(-0.5 * hidden * hidden) * (1.0 / math.sqrt(2.0 * math.pi)))
    part_ref[:, :width] = dot(act, down_ref[...]).astype(jnp.bfloat16)
    grad_hidden = (dot_nt(g, down_ref[...]) * slope).astype(jnp.bfloat16)
    part_ref[:, width:] = dot_nt(grad_hidden, up_ref[...]).astype(jnp.bfloat16)
    ddown, dup = dot_tn(act, g), dot_tn(x, grad_hidden)

    @pl.when(pl.program_id(0) == 0)
    def _():
        dup_ref[...] = dup
        ddown_ref[...] = ddown

    @pl.when(pl.program_id(0) > 0)
    def _():
        dup_ref[...] += dup
        ddown_ref[...] += ddown


def return_kernel(dims, capacity, room, ret_ref, cot_ref, hid_ref, moe_ref, gate_ref, gated_ref, y_ref, u_ref, z_ref, dt_ref,
                  proj_ref, vec_ref, out_ref, gain_ref, router_ref, route_ref, slot_ref,
                  block_ref, ghid_ref, gy_ref, gz_ref, dout_ref, drouter_ref, dskip_ref, dgain_ref, adj_ref,
                  hooks=QUIET):
    seqs, rows, inner, states, rank, taps = dims
    count = seqs * rows
    total, width = ret_ref.shape[0], hid_ref.shape[1]
    route, slot = as_column(route_ref), as_column(slot_ref)
    place = jnp.where(slot < capacity, route * capacity + slot, -1)
    pick = (lanes((count, total)) == place).astype(jnp.bfloat16)
    result = dot(pick, ret_ref[:, :width])
    hid, gate = hid_ref[...], gate_ref[...]
    block_ref[...] = (hid + gate * result).astype(jnp.bfloat16)
    cot = cot_ref[...].astype(jnp.float32)
    grad_gate = jnp.sum(cot * result, axis=1, keepdims=True)
    wide = (count, router_ref.shape[1])
    grad_logits = jnp.where(lanes(wide) == route + room, grad_gate * gate * (1.0 - gate), 0.0).astype(jnp.bfloat16)
    grad_in = dot(pick, ret_ref[:, width:]) + dot_nt(grad_logits, router_ref[...])
    drouter_ref[...] = dot_tn(moe_ref[...], grad_logits)
    r2 = normalize(hid)
    dgain_ref[...] = jnp.sum(grad_in * (hid * r2), axis=0, keepdims=True)
    scaled = grad_in * gain_ref[1:2]
    grad_hid = cot + r2 * scaled - hid * (r2 * r2 * r2) * jnp.mean(scaled * hid, axis=1, keepdims=True)
    ghid_ref[...] = grad_hid
    branch = grad_hid.astype(jnp.bfloat16)
    hooks.activations()
    for j in range(inner // WIDE):
        cols = slice(j * WIDE, (j + 1) * WIDE)
        dout_ref[cols, :] = dot_tn(gated_ref[:, cols], branch).astype(jnp.bfloat16)
        grad = dot_nt(branch, out_ref[cols, :])
        z = z_ref[:, cols]
        sig = sigmoid(z)
        gy = grad * (z * sig)
        gy_ref[:, cols] = gy
        gz_ref[:, cols] = (grad * y_ref[:, cols] * (sig + z * sig * (1.0 - sig))).astype(jnp.bfloat16)
        dskip_ref[:, cols] = jnp.sum(gy * u_ref[:, cols], axis=0, keepdims=True)
    hooks.gradients()
    a2 = -jnp.exp(vec_ref[0:states]) * LOG2E
    blocks = inner // 128
    for s in range(seqs):
        def eight(i, ms):
            ms = list(ms)
            at = pl.multiple_of((s + 1) * rows - 8 - i * 8, 8)
            small = proj_ref[pl.ds(at, 8), :]
            cs = [column(small[j : j + 1], rank + states, states) for j in range(8)]
            for k in range(blocks):
                sl = slice(k * 128, (k + 1) * 128)
                d8, g8 = dt_ref[pl.ds(at, 8), sl], gy_ref[pl.ds(at, 8), sl]
                for j in reversed(range(8)):
                    ms[k] = jnp.exp2(d8[j : j + 1] * a2[:, sl]) * (ms[k] + cs[j] * g8[j : j + 1])
            return tuple(ms)
        zero = jnp.zeros((states, 128), jnp.float32)
        ms = lax.fori_loop(0, rows // 8, eight, (zero,) * blocks)
        for k in range(blocks):
            adj_ref[s, :, k * 128 : (k + 1) * 128] = ms[k]
        hooks.scanned(s)


def back_kernel(dims, tok_ref, halo_ref, ext_ref, hist_ref, later_ref, gy_ref, gz_ref, ghid_ref, u_ref, dt_ref,
                proj_ref, win_ref, small_ref, vec_ref, gain_ref,
                dtok_ref, dhalo_ref, din_ref, dsmall_ref, dvec_ref, dgain_ref,
                hbuf, ccol, bcol, gbsum, gcsum, adj, gdt, gu, gproj, gpad, gm, xn, gpre, sem, hooks=QUIET):
    small_ref = small_ref.at[:, 0:TILE]
    seqs, rows, inner, states, rank, taps = dims
    count = seqs * rows
    groups = rows // GROUP
    size = GROUP * states
    steps = seqs * groups

    def fetch(i, slot):
        s, g = i // groups, groups - 1 - i % groups
        at = pl.multiple_of(g * size, size)
        return pltpu.make_async_copy(hist_ref.at[s, pl.ds(at, size + states)], hbuf.at[slot], sem.at[slot])

    fetch(0, 0).start()
    dvec_ref[...] = jnp.zeros_like(dvec_ref)
    strip = 512

    def group(i, carry):
        slot = i % 2
        s, g = i // groups, groups - 1 - i % groups

        @pl.when(i + 1 < steps)
        def _():
            fetch(i + 1, 1 - slot).start()

        @pl.when(g == groups - 1)
        def _():
            adj[...] = later_ref[s]
        at = pl.multiple_of(s * rows + g * GROUP, GROUP)
        small = proj_ref[pl.ds(at, GROUP), :]
        for t in range(GROUP):
            ccol[t] = column(small[t : t + 1], rank + states, states)
            bcol[t] = column(small[t : t + 1], rank, states)
            gbsum[t] = jnp.zeros((states, 128), f32)
            gcsum[t] = jnp.zeros((states, 128), f32)
        fetch(i, slot).wait()
        for c0 in range(0, inner, strip):
            sls = [slice(c0 + k, c0 + k + 128) for k in range(0, strip, 128)]
            rates = [-jnp.exp(vec_ref[0:states, sl]) for sl in sls]
            m = [adj[:, sl] for sl in sls]
            dd = [dvec_ref[0:states, sl] for sl in sls]
            for half in reversed(range(GROUP // 8)):
                a8 = pl.multiple_of(at + half * 8, 8)
                d8 = [dt_ref[pl.ds(a8, 8), sl] for sl in sls]
                g8 = [gy_ref[pl.ds(a8, 8), sl] for sl in sls]
                u8 = [u_ref[pl.ds(a8, 8), sl] for sl in sls]
                w8 = [d * u for d, u in zip(d8, u8)]
                r1, r2 = [[None] * 8 for _ in sls], [[None] * 8 for _ in sls]
                for j in reversed(range(8)):
                    t = half * 8 + j
                    gb = gc = 0.0
                    for k, sl in enumerate(sls):
                        d, gy = d8[k][j : j + 1], g8[k][j : j + 1]
                        a = m[k] + ccol[t] * gy
                        m[k] = jnp.exp2(d * (rates[k] * LOG2E)) * a
                        p = m[k] * hbuf[slot, t * states : (t + 1) * states, sl].astype(f32) * rates[k]
                        dd[k] = dd[k] + p * d
                        gb = gb + a * w8[k][j : j + 1]
                        gc = gc + gy * hbuf[slot, (t + 1) * states : (t + 2) * states, sl].astype(f32)
                        r1[k][j], r2[k][j] = fold(p), fold(a * bcol[t])
                    gbsum[t] += gb
                    gcsum[t] += gc
                for k, sl in enumerate(sls):
                    w1, w2 = row_sums(r1[k]), row_sums(r2[k])
                    gdt[pl.ds(a8, 8), sl] = w1 + u8[k] * w2
                    gu[pl.ds(a8, 8), sl] = d8[k] * w2
            for k, sl in enumerate(sls):
                adj[:, sl] = m[k]
                dvec_ref[0:states, sl] = dd[k]
        square = (states, small.shape[1])
        where, entry = lanes(square), subs(square)
        line = subs((GROUP, small.shape[1]))
        out = jnp.zeros(small.shape, f32)
        for t in range(GROUP):
            gb = jnp.broadcast_to(jnp.sum(gbsum[t], axis=1, keepdims=True), square)
            gc = jnp.broadcast_to(jnp.sum(gcsum[t], axis=1, keepdims=True), square)
            put = jnp.where(where == entry + rank, gb, jnp.where(where == entry + rank + states, gc, 0.0))
            out = jnp.where(line == t, jnp.sum(put, axis=0, keepdims=True), out)
        gproj[pl.ds(at, GROUP), :] = out
        return carry
    lax.fori_loop(0, steps, group, 0)
    hooks.rest()

    low = rank_lanes(proj_ref[...], rank, states)
    at = rank + 2 * states
    row = states + taps
    grad_rank = jnp.zeros(proj_ref.shape, jnp.float32)
    for j in range(inner // WIDE):
        cols = slice(j * WIDE, (j + 1) * WIDE)
        pre = dot_nt(low, small_ref[cols, :]) + vec_ref[row + 1 : row + 2, cols]
        grad_pre = gdt[:, cols] * sigmoid(pre)
        dvec_ref[row + 1 : row + 2, cols] = jnp.sum(grad_pre, axis=0, keepdims=True)
        grad_pre = grad_pre.astype(jnp.bfloat16)
        gpre[:, cols] = grad_pre
        grad_rank = grad_rank + dot(grad_pre, small_ref[cols, :])
    where = lanes(grad_rank.shape)
    grad_rank = pltpu.roll(grad_rank, small_ref.shape[1] - at, axis=1)
    grad_proj = jnp.where(where < rank, grad_rank, jnp.where(where < at, gproj[...], 0.0)).astype(jnp.bfloat16)
    for ref, to in ((tok_ref, 0), (halo_ref, count)):
        x = ref[...].astype(jnp.float32)
        xn[to : to + x.shape[0]] = (x * normalize(x) * gain_ref[0:1]).astype(jnp.bfloat16)
    grad_normed = jnp.zeros((gm.shape[0], xn.shape[1]), jnp.float32)
    first = ext_ref.shape[1] - rows - taps + 1
    for j in range(inner // WIDE):
        cols = slice(j * WIDE, (j + 1) * WIDE)
        dsmall_ref[cols, :] = (
            dot_tn(u_ref[:, cols].astype(jnp.bfloat16), grad_proj) + dot_tn(gpre[:, cols], low)
        ).astype(jnp.bfloat16)
        grad_u = dot_nt(grad_proj, small_ref[cols, :]) + gy_ref[:, cols] * vec_ref[row + 2 : row + 3, cols] + gu[:, cols]
        taps_sum = [0.0] * taps
        bias_sum = 0.0
        heads = []
        for s in range(seqs):
            pre = conv_sum(ext_ref, s, cols, vec_ref, states, taps, rows)
            sig = sigmoid(pre)
            grad_conv = grad_u[s * rows : (s + 1) * rows] * (sig + pre * sig * (1.0 - sig))
            bias_sum = bias_sum + jnp.sum(grad_conv, axis=0, keepdims=True)
            for k in range(taps):
                taps_sum[k] = taps_sum[k] + jnp.sum(
                    grad_conv * ext_ref[s, first + k : first + k + rows, cols], axis=0, keepdims=True)
            gpad[0:8] = jnp.zeros((8, WIDE), jnp.float32)
            gpad[8 : 8 + rows] = grad_conv
            gpad[8 + rows :] = jnp.zeros((8, WIDE), jnp.float32)
            grad = 0.0
            for k in range(taps):
                grad = grad + vec_ref[states + k : states + k + 1, cols] * gpad[taps - 1 - k : taps + 7 - k + rows]
            heads.append(grad[0:8])
            gm[s * rows : (s + 1) * rows, cols] = grad[8:].astype(jnp.bfloat16)
        gm[count:, cols] = jnp.concatenate(heads).astype(jnp.bfloat16)
        dvec_ref[row : row + 1, cols] = bias_sum
        for k in range(taps):
            dvec_ref[states + k : states + k + 1, cols] = taps_sum[k]
        zcols = slice(inner + j * WIDE, inner + (j + 1) * WIDE)
        din_ref[:, cols] = dot_tn(xn[...], gm[:, cols]).astype(jnp.bfloat16)
        din_ref[:, zcols] = dot_tn(xn[:count], gz_ref[:, cols]).astype(jnp.bfloat16)
        hooks.columns(j)
        gz = jnp.concatenate([gz_ref[:, cols], jnp.zeros((gm.shape[0] - count, WIDE), jnp.bfloat16)])
        grad_normed = grad_normed + dot_nt(gm[:, cols], win_ref[:, cols]) + dot_nt(gz, win_ref[:, zcols])
    gain_sum = 0.0
    for ref, to, base, out in ((tok_ref, 0, ghid_ref, dtok_ref), (halo_ref, count, None, dhalo_ref)):
        x = ref[...].astype(jnp.float32)
        r1 = normalize(x)
        grad = grad_normed[to : to + x.shape[0]]
        gain_sum = gain_sum + jnp.sum(grad * (x * r1), axis=0, keepdims=True)
        grad = grad * gain_ref[0:1]
        grad = r1 * grad - x * (r1 * r1 * r1) * jnp.mean(grad * x, axis=1, keepdims=True)
        out[...] = grad if base is None else grad + base[...]
    dgain_ref[...] = gain_sum


def like(*shape, dtype=f32):
    return jax.ShapeDtypeStruct(shape, dtype)


def params(mib=56):
    return pltpu.CompilerParams(vmem_limit_bytes=mib << 20)


def moe_kernel(seq, rows_ref, up_ref, down_ref, up2_ref, first_ref,
               back_ref, land_ref, dup_ref, ddown_ref, dup2_ref, ddown2_ref,
               xbuf, part, act, ghid, hid, gact, sib_buf, own_sum,
               local_sem, disp_sem, pass_sem, recv_sem, load_sem, sib_send, sib_recv,
               final_send, final_recv, final_local, down2_ref, cross_sem):
    me = Place(4, seq)
    b, s = me.at()
    y, z, Z, c = me.y, me.z, me.Z, me.c
    cap, wide = rows_ref.shape[1], rows_ref.shape[2]
    width = wide // 2
    share = up_ref.shape[1]
    two = 2 * cap
    block = 2 * two
    sib, nx = me.at(c=1 - c), me.at(x=1 - me.x)
    greet([(None, sib), (None, nx)] + [(None, (b, (s + k) % seq)) for k in range(1, seq)])

    def remote(src, dst, send, recv, dev):
        return pltpu.make_async_remote_copy(
            src_ref=src, dst_ref=dst, send_sem=send, recv_sem=recv, device_id=dev, device_id_type=MESH)

    def slab(cc, ss):
        return land_ref.at[cc, pl.ds(pl.multiple_of(ss * cap, 8), cap)]

    def there(k, j):
        return ((z + k) % Z) * 2 + j

    def arrived(cc, ss):
        remote(slab(cc, ss), slab(cc, ss), disp_sem.at[0], recv_sem.at[cc, ss], sib).wait_recv()

    def hand(ss):
        return remote(slab(c, ss), slab(c, ss), pass_sem.at[ss], recv_sem.at[c, ss], sib)

    def load(k, cc):
        zz = (z + k) % Z
        return pltpu.make_async_copy(
            land_ref.at[cc, pl.ds(pl.multiple_of(zz * two, 8), two)],
            xbuf.at[k, pl.ds(pl.multiple_of(cc * two, 16), two)], load_sem.at[k, cc])

    def dispatch(k, j):
        to = ((z + Z - k) % Z) * 2 + j
        return remote(rows_ref.at[to], slab(c, s), disp_sem.at[2 * k + j], recv_sem.at[c, s], (b, to))

    dispatch(0, 1 - y).start()
    own = remote(rows_ref.at[s], slab(c, s), pass_sem.at[s], recv_sem.at[c, s], sib)
    own.start()
    local = pltpu.make_async_copy(rows_ref.at[s], slab(c, s), local_sem)
    local.start()
    for j in range(2):
        dispatch(1, j).start()

    head = first_ref.shape[0]
    if head < share:
        rest = remote(down_ref.at[head:], down2_ref.at[head:], cross_sem.at[0], cross_sem.at[1], nx)
        rest.start()
    if head:
        front = pltpu.make_async_copy(first_ref, down2_ref.at[0:head], cross_sem.at[2])
        front.start()
    ups, downs = (up_ref, up2_ref), (down_ref, down2_ref)

    def compute(k):
        for i in range(2):
            for n in range(0, share, WIDE):
                to = slice(i * share + n, i * share + n + WIDE)
                hid[:, to] = dot(xbuf[k, :, :width], ups[i][:, n : n + WIDE])
                gact[:, to] = dot_nt(xbuf[k, :, width:], downs[i][n : n + WIDE, :])

        def sixteen(r, carry):
            at = pl.ds(pl.multiple_of(r * 16, 16), 16)
            to = pl.ds(pl.multiple_of(k * block + r * 16, 16), 16)
            h = hid[at, :]
            half = 0.5 * (1.0 + erf(h * math.sqrt(0.5)))
            act[to, :] = (h * half).astype(bf16)
            slope = half + h * (jnp.exp(-0.5 * h * h) * (1.0 / math.sqrt(2.0 * math.pi)))
            ghid[to, :] = (gact[at, :] * slope).astype(bf16)
            return carry
        lax.fori_loop(0, block // 16, sixteen, 0)
        mine = pl.ds(pl.multiple_of(k * block, 16), block)
        for n in range(0, width, WIDE):
            cols = slice(n, n + WIDE)
            part[k, :, cols] = (
                dot(act[mine, :share], down_ref[:, cols]) + dot(act[mine, share:], down2_ref[:, cols])
            ).astype(bf16)
            part[k, :, width + n : width + n + WIDE] = (
                dot_nt(ghid[mine, :share], up_ref[cols, :]) + dot_nt(ghid[mine, share:], up2_ref[cols, :])
            ).astype(bf16)

    def of_core(k, cc):
        return part.at[k, pl.ds(pl.multiple_of(cc * two, 16), two)]

    def to_sib(k):
        return remote(of_core(k, 1 - c), sib_buf.at[k], sib_send.at[k], sib_recv.at[k], sib)

    def to_home(k, j):
        return remote(own_sum.at[k, j], back_ref.at[s], final_send.at[k, j], final_recv.at[s], (b, there(k, j)))

    def keep_home():
        return pltpu.make_async_copy(own_sum.at[0, y], back_ref.at[s], final_local)

    def own_stage(k):
        @pl.when(k == 0)
        def _():
            arrived(c, z * 2 + 1 - y)
            hand(z * 2 + 1 - y).start()
            local.wait()

        @pl.when(k > 0)
        def _():
            for j in range(2):
                arrived(c, there(k, j))
                hand(there(k, j)).start()

        @pl.when(k < Z - 2)
        def _():
            for j in range(2):
                dispatch(k + 2, j).start()
        load(k, c).start()

    def compute_stage(k):
        for j in range(2):
            arrived(1 - c, there(k, j))
        load(k, 1 - c).start()
        for cc in range(2):
            load(k, cc).wait()

        @pl.when(k == 0)
        def _():
            if head < share:
                rest.wait_recv()
            if head:
                front.wait()
        compute(k)
        to_sib(k).start()

    def home_stage(k):
        to_sib(k).wait_recv()
        total = of_core(k, c)[...].astype(f32) + sib_buf[k].astype(f32)
        for j in range(2):
            own_sum[k, j] = total[j * cap : (j + 1) * cap].astype(bf16)

        @pl.when(k > 0)
        def _():
            for j in range(2):
                to_home(k, j).start()

        @pl.when(k == 0)
        def _():
            keep_home().start()
            to_home(0, 1 - y).start()

    everything = (Z * block, width)
    stages = ((own_stage, 0), (home_stage, 2), (compute_stage, 1))

    def step(t, carry):
        for stage, lag in stages:
            k = t - lag
            pl.when(jnp.logical_and(k >= 0, k < Z))(functools.partial(stage, k))
        return carry
    lax.fori_loop(0, Z + 2, step, 0)
    for i, (dup, ddown) in enumerate(((dup2_ref, ddown2_ref), (dup_ref, ddown_ref))):
        for n in range(0, share, WIDE):
            at = (1 - i) * share + n
            x, g = xbuf[:, :, :width].reshape(everything), xbuf[:, :, width:].reshape(everything)
            ddown[n : n + WIDE, :] = dot_tn(act[:, at : at + WIDE], g).astype(ddown.dtype)
            dup[:, n : n + WIDE] = dot_tn(x, ghid[:, at : at + WIDE]).astype(dup.dtype)

    for k in range(1, seq):
        e = (s + k) % seq
        remote(back_ref.at[e], back_ref.at[e], disp_sem.at[0], final_recv.at[e], sib).wait_recv()
    keep_home().wait()
    if head < share:
        rest.wait_send()
    dispatch(0, 1 - y).wait_send()
    own.wait_send()
    hand(z * 2 + 1 - y).wait_send()
    to_home(0, 1 - y).wait_send()

    def settle(k, carry):
        to_sib(k).wait_send()

        @pl.when(k > 0)
        def _():
            for j in range(2):
                dispatch(k, j).wait_send()
                to_home(k, j).wait_send()
                hand(there(k, j)).wait_send()
        return carry
    lax.fori_loop(0, Z, settle, 0)


def cross(batch, *arrays):
    return [lax.ppermute(a, "batch", [(i, (i + 2) % batch) for i in range(batch)]) for a in arrays]


def moe_rows(batch, seq, sent, up, down, up2, down2):
    width, hidden_share = up.shape
    capacity, wide = sent.shape[1:]
    block = seq * capacity
    if tuned(batch, seq):
        Z, block = seq // 2, 4 * capacity
        dma = pltpu.SemaphoreType.DMA
        out = pl.pallas_call(
            functools.partial(moe_kernel, seq),
            out_shape=[
                like(seq, capacity, wide, dtype=bf16),
                like(2, seq * capacity, wide, dtype=bf16),
                like(width, hidden_share),
                like(hidden_share, width),
                like(width, hidden_share, dtype=bf16),
                like(hidden_share, width, dtype=bf16),
            ],
            in_specs=[HBM] + [VM] * 4,
            out_specs=[HBM, HBM] + [VM] * 4,
            scratch_shapes=[
                pltpu.VMEM((Z, block, wide), bf16),
                pltpu.VMEM((Z, block, wide), bf16),
                pltpu.VMEM((Z * block, 2 * hidden_share), bf16),
                pltpu.VMEM((Z * block, 2 * hidden_share), bf16),
                pltpu.VMEM((block, 2 * hidden_share), f32),
                pltpu.VMEM((block, 2 * hidden_share), f32),
                pltpu.VMEM((Z, 2 * capacity, wide), bf16),
                pltpu.VMEM((Z, 2, capacity, wide), bf16),
                dma,
                dma((2 * Z,)),
                dma((seq,)),
                dma((2, seq)),
                dma((Z, 2)),
                dma((Z,)),
                dma((Z,)),
                dma((Z, 2)),
                dma((seq,)),
                dma,
                pltpu.VMEM((hidden_share, width), bf16),
                dma((3,)),
            ],
            compiler_params=pltpu.CompilerParams(
                collective_id=2, has_side_effects=True, vmem_limit_bytes=56 << 20),
            name="experts",
        )(sent, up, down, up2, down2)
        back, _, d_up, d_down, d_up2, d_down2 = out
        d_up2, d_down2 = cross(batch, d_up2, d_down2)
        return back, d_up, d_down, d_up2, d_down2
    mine = lax.all_to_all(sent, "seq", split_axis=0, concat_axis=0, tiled=True)
    rows = lax.all_gather(mine, "batch", axis=0).reshape(batch * block, wide)
    part, d_up, d_down = pl.pallas_call(
        expert_kernel,
        out_shape=[
            like(batch * block, wide, dtype=bf16),
            like(width, hidden_share),
            like(hidden_share, width),
        ],
        grid=(batch,),
        in_specs=[
            pl.BlockSpec((block, wide), lambda i: (i, 0)),
            pl.BlockSpec((width, hidden_share), lambda i: (0, 0)),
            pl.BlockSpec((hidden_share, width), lambda i: (0, 0)),
        ],
        out_specs=[
            pl.BlockSpec((block, wide), lambda i: (i, 0)),
            pl.BlockSpec((width, hidden_share), lambda i: (0, 0)),
            pl.BlockSpec((hidden_share, width), lambda i: (0, 0)),
        ],
        compiler_params=params(),
        name="experts",
    )(rows, up, down)
    part = part.reshape((batch,) + sent.shape)
    mine = lax.psum_scatter(part, "batch", scatter_dimension=0, tiled=False)
    return lax.all_to_all(mine, "seq", split_axis=0, concat_axis=0, tiled=True), d_up, d_down, None, None


class Moves:
    def __init__(self, sems):
        self.sems, self.used, self.named = sems, 0, {}

    def start(self, name, src, dst):
        cp = pltpu.make_async_copy(src, dst, self.sems.at[self.used])
        self.used += 1
        cp.start()
        self.named.setdefault(name, []).append(cp)

    def wait(self, *names):
        for name in names:
            for cp in self.named.pop(name):
                cp.wait()

    def wait_all(self):
        self.wait(*list(self.named))


def forward_kernel(dims, share, low_share, experts, capacity, room, seq,
                   tok_ref, halo_ref, tail_ref, cot_ref, route_ref, slot_ref, win_hbm, out_hbm,
                   ext_hbm, z_hbm, u_hbm, dt_hbm, y_hbm, gated_hbm, hist_ref, proj_ref, dsum_ref, vec_ref, gain_ref,
                   router_ref, hid_ref, moe_ref, gate_ref, rows_ref,
                   win, out, ext, z, u, dt, y, gated, end, start, xn, hbuf, hcur, sem, sem0, sems, *relay_refs):
    inner = dims[2]
    moves = Moves(sems)
    for j in range(inner // WIDE):
        for base in (0, inner):
            cols = pl.ds(base + j * WIDE, WIDE)
            moves.start(("win", j), win_hbm.at[:, cols], win.at[:, cols])
    moves.start("out", out_hbm, out)
    relay = Relay(seq, True, dims[3], dsum_ref, vec_ref, end, start, *relay_refs)
    greet(relay.peers())

    def projected():
        for name, src, dst in (("ext", ext, ext_hbm), ("z", z, z_hbm), ("u", u, u_hbm), ("dt", dt, dt_hbm)):
            moves.start(name, src, dst)

    enter_packed(dims, share, low_share, experts, tok_ref, halo_ref, win, tail_ref, ext, z, u, dt, proj_ref, end,
                 dsum_ref, vec_ref, gain_ref, router_ref, xn,
                 hooks=Hooks(weights=lambda j: moves.wait(("win", j)), projected=projected, scanned=relay.start))
    for i in range(relay.count):
        relay.finish(i)

    def mixed():
        moves.start("y", y, y_hbm)
        moves.start("gated", gated, gated_hbm)

    leave_kernel(dims, capacity, room, tok_ref, cot_ref, start, dt, u, z, proj_ref, vec_ref, out, gain_ref, router_ref,
                 route_ref, slot_ref, hist_ref, y, hid_ref, gated, moe_ref, gate_ref, rows_ref, hbuf, hcur, sem, sem0,
                 hooks=Hooks(out_proj=lambda: moves.wait("out"), mixed=mixed))
    relay.settle()
    moves.wait_all()


def backward_kernel(dims, capacity, room, seq,
                    ret_ref, cot_ref, hid_ref, moe_ref, gate_ref, vec_ref, gain_ref, router_ref, route_ref, slot_ref,
                    dsum_ref, proj_ref, gated_hbm, out_hbm, z_hbm, y_hbm, u_hbm, dt_hbm, ext_hbm, win_hbm, tail_hbm,
                    tok_hbm, halo_hbm, hist_ref,
                    block_ref, dtok_ref, dhalo_ref, din_hbm, dout_hbm, dsmall_ref, dvec_ref, dnorm_ref, dmoe_ref,
                    drouter_ref, dskip_ref,
                    gated, out, z, y, u, dt, ext, win, tail, tok, halo, gy, gz, ghid, din, dout, adj, later,
                    hbuf, ccol, bcol, gbsum, gcsum, carry, gdt, gu, gproj, gpad, gm, xn, gpre, sem, sems, *relay_refs):
    inner = dims[2]
    moves = Moves(sems)
    for name, src, dst in (
        ("gated", gated_hbm, gated), ("out", out_hbm, out), ("z", z_hbm, z), ("y", y_hbm, y), ("u", u_hbm, u),
        ("dt", dt_hbm, dt), ("ext", ext_hbm, ext), ("win", win_hbm, win), ("tail", tail_hbm, tail),
        ("tok", tok_hbm, tok), ("halo", halo_hbm, halo),
    ):
        moves.start(name, src, dst)
    relay = Relay(seq, False, dims[3], dsum_ref, vec_ref, adj, later, *relay_refs)
    greet(relay.peers())

    def gradients():
        moves.start("dout", dout, dout_hbm)
        moves.wait("dt")

    return_kernel(dims, capacity, room, ret_ref, cot_ref, hid_ref, moe_ref, gate_ref, gated, y, u, z, dt, proj_ref,
                  vec_ref, out, gain_ref, router_ref, route_ref, slot_ref,
                  block_ref, ghid, gy, gz, dout, drouter_ref, dskip_ref, dmoe_ref, adj,
                  hooks=Hooks(activations=lambda: moves.wait("gated", "out", "z", "y", "u"), gradients=gradients,
                              scanned=relay.start))
    for i in range(relay.count):
        relay.finish(i)

    def columns(j):
        for base in (0, inner):
            cols = pl.ds(base + j * WIDE, WIDE)
            moves.start("din", din.at[:, cols], din_hbm.at[:, cols])

    back_kernel(dims, tok, halo, ext, hist_ref, later, gy, gz, ghid, u, dt, proj_ref, win, tail, vec_ref, gain_ref,
                dtok_ref, dhalo_ref, din, dsmall_ref, dvec_ref, dnorm_ref,
                hbuf, ccol, bcol, gbsum, gcsum, carry, gdt, gu, gproj, gpad, gm, xn, gpre, sem,
                hooks=Hooks(rest=lambda: moves.wait("ext", "win", "tail", "tok", "halo"), columns=columns))
    relay.settle()
    moves.wait_all()


def body(
    tokens,
    in_proj,
    conv_weight,
    conv_bias,
    state_proj,
    step_proj,
    step_bias,
    decay_log,
    skip_gain,
    out_proj,
    norm_gain,
    moe_gain,
    router_proj,
    expert_up,
    expert_down,
    routes,
    slot_index,
    cotangent,
):
    batch, seq = lax.axis_size("batch"), lax.axis_size("seq")
    both = ("batch", "seq")
    seqs, rows, width = tokens.shape
    count = seqs * rows
    devices = batch * seq
    taps, share = conv_weight.shape
    inner = share * devices
    states, rank = decay_log.shape[0], step_proj.shape[0]
    low_share = norm_gain.shape[0]
    experts = router_proj.shape[1]
    capacity = max(2, 5 * count // (4 * experts))
    dims = (seqs, rows, inner, states, rank, taps)
    tile = 128

    lines = (decay_log, conv_weight, conv_bias[None], step_bias[None], skip_gain[None])
    used = sum(a.shape[0] for a in lines)
    room = -(-used // 8) * 8
    fast = tuned(batch, seq)
    if fast:
        in_full, out_full, tail_full, halo = gather_all(
            batch, seq, room, in_proj, out_proj, tokens, state_proj, step_proj, router_proj.T, lines,
            (norm_gain[None], moe_gain[None]))
        halo = halo.reshape(seqs * 8, width)
    else:
        features = jnp.concatenate([router_proj, norm_gain[:, None], moe_gain[:, None]], axis=1)
        tail = jnp.concatenate(
            [
                state_proj,
                step_proj.T,
                jnp.pad(jnp.concatenate(lines), ((0, room - used), (0, 0))).T,
                jnp.pad(features, ((0, share - low_share), (0, tile - room - features.shape[1]))),
            ],
            axis=1,
        )
        halo = lax.ppermute(tokens[:, rows - taps + 1 :], "seq", [(i, i + 1) for i in range(seq - 1)])
        halo = jnp.pad(halo, ((0, 0), (8 - taps + 1, 0), (0, 0))).reshape(seqs * 8, width)
        in_full, out_full, tail_full = (
            lax.all_gather(a, both, axis=0, tiled=True) for a in (in_proj, out_proj, tail)
        )
    up, down, tail_full = lax.optimization_barrier((expert_up[0], expert_down[0], tail_full))
    up2, down2 = cross(batch, up, down[:AHEAD]) if fast else (None, None)
    tok, cot = tokens.reshape(count, width), cotangent.reshape(count, width)
    size = GROUP * states
    total = experts * capacity
    edge_rows = seqs * 8
    dma = pltpu.SemaphoreType.DMA
    acts = like(count, inner)
    ext_s, state_s, dsum_s = like(seqs, rows + 8, inner), like(seqs, states, inner), like(seqs, 1, inner)
    proj_s, low_s, vec_s = like(count, tile), like(count, inner, dtype=bf16), like(room, inner)
    hist_s = like(seqs, (rows + 1) * states, inner, dtype=bf16)
    hid_s, moe_s, gate_s = like(count, width), like(count, width, dtype=bf16), like(count, 1)
    rows_s = like(total, 2 * width, dtype=bf16)
    gain_s, router_s = like(8, width), like(width, tile, dtype=bf16)
    vmem = lambda a: pltpu.VMEM(a.shape, a.dtype)
    normed = pltpu.VMEM((count + edge_rows, width), bf16)
    leave_scratch = [pltpu.VMEM((2, size, inner), bf16), pltpu.VMEM(state_s.shape, bf16), dma((2,)), dma((seqs,))]
    back_scratch = [
        pltpu.VMEM((2, size + states, inner), bf16),
        pltpu.VMEM((GROUP, states, tile), f32),
        pltpu.VMEM((GROUP, states, tile), f32),
        pltpu.VMEM((GROUP, states, tile), f32),
        pltpu.VMEM((GROUP, states, tile), f32),
        pltpu.VMEM((states, inner), f32),
        vmem(acts),
        vmem(acts),
        vmem(proj_s),
        pltpu.VMEM((rows + 16, WIDE), f32),
        pltpu.VMEM((count + edge_rows, inner), bf16),
        normed,
        vmem(low_s),
        dma((2,)),
    ]
    tok_s, halo_s, din_s = like(count, width), like(edge_rows, width), like(width, 2 * inner, dtype=bf16)
    dout_s, dsmall_s = like(inner, width, dtype=bf16), like(inner, tile, dtype=bf16)
    drouter_s, dskip_s, dgain_s = like(width, tile), like(1, inner), like(1, width)
    wide = inner // WIDE
    if fast:
        (ext, z, u, dt, y, gated, hist, proj, dsum, vec, gain, router, hid, moe_in, gate, sent) = pl.pallas_call(
            partial(forward_kernel, dims, share, low_share, experts, capacity, room, seq),
            out_shape=[ext_s, acts, acts, acts, acts, low_s, hist_s, proj_s, dsum_s, vec_s, gain_s, router_s,
                       hid_s, moe_s, gate_s, rows_s],
            in_specs=[VM] * 6 + [HBM] * 2,
            out_specs=[HBM] * 7 + [VM] * 9,
            scratch_shapes=[
                vmem(in_full), vmem(out_full), vmem(ext_s), vmem(acts), vmem(acts), vmem(acts), vmem(acts), vmem(low_s),
                vmem(state_s), vmem(state_s), normed, *leave_scratch, dma((2 * wide + 7,)),
                *relay_scratch(seqs, states, inner),
            ],
            compiler_params=pltpu.CompilerParams(
                collective_id=3, has_side_effects=True, vmem_limit_bytes=58 << 20),
            name="forward",
        )(tok, halo, tail_full, cot, routes, slot_index, in_full, out_full)
    else:
        vec = tail_full[:, tile : tile + room].T.astype(f32)
        router = tail_full[:, tile:].reshape(devices, share, tile)[:, :low_share].reshape(width, tile)
        gain = router[:, room + experts : room + experts + 2].T.astype(f32)
        ext, z, u, dt, proj, end, dsum = pl.pallas_call(
            partial(enter_kernel, dims),
            out_shape=[ext_s, acts, acts, acts, proj_s, state_s, dsum_s],
            in_specs=[VM] * 6,
            out_specs=[VM] * 7,
            scratch_shapes=[normed],
            compiler_params=params(),
            name="enter",
        )(tok, halo, in_full, tail_full[:, :tile], vec, gain)
        rates = -jnp.exp(vec[:states])
        before = chain_states(seq, True, dsum, rates, end)
        hist, y, hid, gated, moe_in, gate, sent = pl.pallas_call(
            partial(leave_kernel, dims, capacity, room),
            out_shape=[hist_s, acts, hid_s, low_s, moe_s, gate_s, rows_s],
            in_specs=[VM] * 13,
            out_specs=[HBM] + [VM] * 6,
            scratch_shapes=leave_scratch,
            compiler_params=params(),
            name="leave",
        )(tok, cot, before, dt, u, z, proj, vec, out_full, gain, router, routes, slot_index)

    back, d_up, d_down, d_up2, d_down2 = moe_rows(
        batch, seq, sent.reshape(experts, capacity, 2 * width), up, down, up2, down2)
    back = back.reshape(total, 2 * width)

    if fast:
        (block_out, d_tok, d_halo, d_in, d_out, d_small, d_vec, d_norm, d_moe, d_router, d_skip) = pl.pallas_call(
            partial(backward_kernel, dims, capacity, room, seq),
            out_shape=[moe_s, tok_s, halo_s, din_s, dout_s, dsmall_s, vec_s, dgain_s, dgain_s, drouter_s, dskip_s],
            in_specs=[VM] * 12 + [HBM] * 12,
            out_specs=[VM] * 3 + [HBM] * 2 + [VM] * 6,
            scratch_shapes=[
                vmem(low_s), vmem(out_full), vmem(acts), vmem(acts), vmem(acts), vmem(acts), vmem(ext_s), vmem(in_full),
                vmem(tail_full), vmem(tok), vmem(halo), vmem(acts), vmem(low_s), vmem(tok_s), vmem(din_s), vmem(dout_s),
                vmem(state_s), vmem(state_s), *back_scratch, dma((2 * wide + 12,)),
                *relay_scratch(seqs, states, inner),
            ],
            compiler_params=pltpu.CompilerParams(
                collective_id=4, has_side_effects=True, vmem_limit_bytes=60 << 20),
            name="backward",
        )(back, cot, hid, moe_in, gate, vec, gain, router, routes, slot_index, dsum, proj,
          gated, out_full, z, y, u, dt, ext, in_full, tail_full, tok, halo, hist)
    else:
        block_out, ghid, gy, gz, d_out, d_router, d_skip, d_moe, adj = pl.pallas_call(
            partial(return_kernel, dims, capacity, room),
            out_shape=[moe_s, tok_s, acts, low_s, dout_s, drouter_s, dskip_s, dgain_s, state_s],
            in_specs=[VM] * 17,
            out_specs=[VM] * 9,
            compiler_params=params(),
            name="back_experts",
        )(back, cot, hid, moe_in, gate, gated, y, u, z, dt, proj, vec, out_full, gain, router, routes, slot_index)
        later = chain_states(seq, False, dsum, rates, adj)
        d_tok, d_halo, d_in, d_small, d_vec, d_norm = pl.pallas_call(
            partial(back_kernel, dims),
            out_shape=[tok_s, halo_s, din_s, dsmall_s, vec_s, dgain_s],
            in_specs=[VM] * 3 + [HBM] + [VM] * 11,
            out_specs=[VM] * 6,
            scratch_shapes=back_scratch,
            compiler_params=params(),
            name="back_mixer",
        )(tok, halo, ext, hist, later, gy, gz, ghid, u, dt, proj, in_full, tail_full, vec, gain)

    skip_row = states + taps + 2
    if fast:
        s_in, s_out, s_tail, from_next = reduce_all(
            batch, seq, low_share, experts, skip_row, d_in, d_out, d_small, d_vec, d_skip, d_router, d_norm, d_moe,
            d_halo)
        steps = 4
        slab = lambda a: pl.BlockSpec((a.shape[0] // steps, a.shape[1]), lambda i: (i, 0))
        whole = lambda *shape: pl.BlockSpec(shape, lambda i: (0,) * len(shape))
        piece = pl.BlockSpec((seqs, rows // steps, width), lambda i: (0, i, 0))
        shapes = [
            s_in.shape, (taps, share), (1, share), (share, rank + 2 * states), (rank, share), (1, share),
            (states, share), (1, share), s_out.shape, (1, low_share), (1, low_share), (experts, low_share),
        ]
        block_out, d_tok, *sums, d_up, d_down = pl.pallas_call(
            partial(finish_kernel, dims, low_share, experts),
            out_shape=[like(*tokens.shape, dtype=bf16), like(*tokens.shape)] + [like(*a) for a in shapes] + [like(*d_up.shape), like(*d_down.shape)],
            grid=(steps,),
            in_specs=[whole(*s_in.shape), whole(*s_out.shape), whole(*s_tail.shape), whole(seqs, 8, width), piece, piece]
            + [slab(a) for a in (d_up, d_up2, d_down, d_down2)],
            out_specs=[piece, piece] + [whole(*a) for a in shapes] + [slab(d_up), slab(d_down)],
            compiler_params=params(),
            name="finish",
        )(s_in, s_out, s_tail, from_next.reshape(seqs, 8, width), d_tok.reshape(tokens.shape),
          block_out.reshape(tokens.shape), d_up, d_up2, d_down, d_down2)
        for i in (2, 5, 7, 9, 10):
            sums[i] = sums[i][0]
        sums[11] = sums[11].T
        return (block_out, d_tok, *sums, d_up[None], d_down[None])
    d_model = d_router.at[:, room + experts : room + experts + 2].set(jnp.concatenate([d_norm, d_moe]).T)
    d_model = jnp.pad(
        d_model.reshape(devices, low_share, tile)[:, :, room:], ((0, 0), (0, share - low_share), (0, 0))
    ).reshape(inner, tile - room)
    d_vec = d_vec.at[skip_row].set(d_skip[0])
    d_tail = jnp.concatenate([d_small, d_vec.T.astype(bf16), d_model.astype(bf16)], axis=1)
    s_in, s_out, s_tail = (
        lax.psum_scatter(a.astype(f32), both, scatter_dimension=0, tiled=True) for a in (d_in, d_out, d_tail)
    )
    from_next = lax.ppermute(
        d_halo.reshape(seqs, 8, width)[:, 8 - taps + 1 :], "seq", [(i + 1, i) for i in range(seq - 1)]
    )
    d_tok = d_tok.reshape(tokens.shape).at[:, rows - taps + 1 :].add(from_next)
    s_vec = s_tail[:, tile : tile + room].T
    s_model = s_tail[:low_share, tile + room :]
    return (
        block_out.reshape(tokens.shape),
        d_tok,
        s_in,
        s_vec[states : states + taps],
        s_vec[states + taps],
        s_tail[:, : rank + 2 * states],
        s_tail[:, rank + 2 * states : tile].T,
        s_vec[states + taps + 1],
        s_vec[:states],
        s_vec[states + taps + 2],
        s_out,
        s_model[:, experts],
        s_model[:, experts + 1],
        s_model[:, :experts],
        d_up[None],
        d_down[None],
    )


def solution(mesh):
    in_specs = (
        P("batch", "seq", None),
        P(("batch", "seq"), None),
        P(None, ("batch", "seq")),
        P(("batch", "seq")),
        P(("batch", "seq"), None),
        P(None, ("batch", "seq")),
        P(("batch", "seq")),
        P(None, ("batch", "seq")),
        P(("batch", "seq")),
        P(("batch", "seq"), None),
        P(("batch", "seq")),
        P(("batch", "seq")),
        P(("batch", "seq"), None),
        P("seq", None, "batch"),
        P("seq", "batch", None),
        P("batch", "seq"),
        P("batch", "seq"),
        P("batch", "seq", None),
    )
    out_specs = (
        P("batch", "seq", None),
        P("batch", "seq", None),
        P(("batch", "seq"), None),
        P(None, ("batch", "seq")),
        P(("batch", "seq")),
        P(("batch", "seq"), None),
        P(None, ("batch", "seq")),
        P(("batch", "seq")),
        P(None, ("batch", "seq")),
        P(("batch", "seq")),
        P(("batch", "seq"), None),
        P(("batch", "seq")),
        P(("batch", "seq")),
        P(("batch", "seq"), None),
        P("seq", None, "batch"),
        P("seq", "batch", None),
    )
    return jax.shard_map(body, mesh=mesh, in_specs=in_specs, out_specs=out_specs, check_vma=False)
```

```python
from functools import partial
import functools
import math

import jax
import jax.numpy as jnp
from jax import lax
from jax.experimental import pallas as pl
from jax.experimental.pallas import tpu as pltpu
from jax.sharding import PartitionSpec as P

epsilon = 1e-05
MESH = pl.DeviceIdType.MESH
HBM = pl.BlockSpec(memory_space=pl.ANY)
VM = pl.BlockSpec(memory_space=pltpu.VMEM)
bf16, f32 = jnp.bfloat16, jnp.float32


class Place:
    def __init__(self, batch, seq, ydim=2):
        self.batch, self.seq, self.Y = batch, seq, ydim
        self.Z = seq // ydim
        b, s = lax.axis_index("batch"), lax.axis_index("seq")
        self.x, self.c = b // 2, b % 2
        self.z, self.y = s // ydim, s % ydim

    def at(self, x=None, c=None, y=None, z=None):
        pick = lambda v, own: own if v is None else v
        x, c, y, z = pick(x, self.x), pick(c, self.c), pick(y, self.y), pick(z, self.z)
        return (x * 2 + c, z * self.Y + y)

    def index(self, dev):
        return dev[0] * self.seq + dev[1]


def greet(devices):
    barrier = pltpu.get_barrier_semaphore()
    count = 0
    for pred, dev in devices:
        if pred is None:
            pl.semaphore_signal(barrier, inc=1, device_id=dev, device_id_type=MESH)
            count = count + 1
        else:
            @pl.when(pred)
            def _(dev=dev):
                pl.semaphore_signal(barrier, inc=1, device_id=dev, device_id_type=MESH)
            count = count + jnp.where(pred, 1, 0)
    pl.semaphore_wait(barrier, count)


TILE = 128


def spot(rows, at, width):
    return (lanes((rows, width)) == subs((rows, width)) + at).astype(bf16)


def gather_kernel(batch, seq, *refs):
    n_arrays = 3
    in_ref, out_ref, tok_ref, state_ref, step_ref, router_ref = refs[:6]
    lines, gains = refs[6:11], refs[11:13]
    outs, halo_ref = refs[13:16], refs[16]
    tail, vecs, feats, zeros, local_sem, send_sem, recv_sem, halo_sem = refs[17:]
    ins = [in_ref, out_ref, tail]
    me = Place(batch, seq)
    Z, z = me.Z, me.z
    rows = [r.shape[0] for r in ins]
    sib = me.at(c=1 - me.c)
    up_ok, down_ok = z < Z - 1, z > 0
    up, down = me.at(z=z + 1), me.at(z=z - 1)
    nx, ny = me.at(x=1 - me.x), me.at(y=1 - me.y)
    first = me.c == 0
    nb2 = tuple(jnp.where(first, a, b) for a, b in zip(ny, nx))
    nb3 = tuple(jnp.where(first, a, b) for a, b in zip(nx, ny))
    x2, y2 = jnp.where(first, me.x, 1 - me.x), jnp.where(first, 1 - me.y, me.y)
    x3, y3 = jnp.where(first, 1 - me.x, me.x), jnp.where(first, me.y, 1 - me.y)
    b, part_of = me.at()
    has_before, has_after = part_of > 0, part_of < seq - 1
    before, after = (b, part_of - 1), (b, part_of + 1)
    greet([(None, sib), (None, nx), (None, ny), (up_ok, up), (down_ok, down), (has_before, before), (has_after, after)])
    own = me.index(me.at())

    def part(a, index):
        return outs[a].at[pl.ds(pl.multiple_of(index * rows[a], 8), rows[a])]

    sends = []

    def send(pred, index, dev, mine=False):
        slot = len(sends)
        copies = []
        for a in range(n_arrays):
            copies.append(
                pltpu.make_async_remote_copy(
                    src_ref=ins[a] if mine else part(a, index),
                    dst_ref=part(a, index),
                    send_sem=send_sem.at[slot, a],
                    recv_sem=recv_sem.at[index, a],
                    device_id=dev,
                    device_id_type=MESH,
                )
            )

        def go(copies):
            def start():
                for cp in copies:
                    cp.start()
            if pred is None:
                start()
            else:
                pl.when(pred)(start)
        if mine:
            go(copies[:2])
            later.append(lambda: go(copies[2:]))
        else:
            go(copies)
        sends.append((pred, copies))

    def arrive(pred, index, targets):
        def wait():
            for a in range(n_arrays):
                pltpu.make_async_remote_copy(
                    src_ref=part(a, index), dst_ref=part(a, index),
                    send_sem=send_sem.at[0, a], recv_sem=recv_sem.at[index, a],
                    device_id=sib, device_id_type=MESH,
                ).wait_recv()
        if pred is None:
            wait()
        else:
            pl.when(pred)(wait)
        for extra, dev in targets:
            p = pred if extra is None else (extra if pred is None else jnp.logical_and(pred, extra))
            send(p, index, dev)

    later = []
    for dev, pred in ((up, up_ok), (down, down_ok), (nb2, None), (nb3, None), (sib, None)):
        send(pred, own, dev, mine=True)
    seqs, rows_here = tok_ref.shape[:2]
    edge = pl.ds(rows_here - 8, 8)
    halo = pltpu.make_async_remote_copy(
        src_ref=tok_ref.at[:, edge], dst_ref=halo_ref, send_sem=halo_sem.at[0], recv_sem=halo_sem.at[1],
        device_id=after, device_id_type=MESH)
    blank = pltpu.make_async_copy(zeros, halo_ref, halo_sem.at[2])
    zeros[...] = jnp.zeros_like(zeros)
    pl.when(has_after)(halo.start)
    pl.when(jnp.logical_not(has_before))(blank.start)

    share, low_share, experts = state_ref.shape[0], router_ref.shape[1], router_ref.shape[0]
    rank, room, wide = step_ref.shape[0], vecs.shape[0], tail.shape[1]
    vecs[...] = jnp.zeros_like(vecs)
    at = 0
    for ref in lines:
        vecs[at : at + ref.shape[0]] = ref[...].astype(f32)
        at += ref.shape[0]
    feats[...] = jnp.zeros_like(feats)
    for i, ref in enumerate(gains):
        feats[i : i + 1] = ref[...].astype(f32)
    by_channel = (
        dot(state_ref[...], spot(state_ref.shape[1], 0, wide))
        + dot_tn(step_ref[...], spot(rank, TILE - rank, wide))
        + dot_tn(vecs[...].astype(bf16), spot(room, TILE, wide))
    )
    by_feature = dot_tn(router_ref[...], spot(experts, TILE + room, wide)) + dot_tn(
        feats[...].astype(bf16), spot(feats.shape[0], TILE + room + experts, wide))
    by_feature = jnp.concatenate([by_feature, jnp.zeros((share - low_share, wide), f32)])
    tail[...] = (by_channel + by_feature).astype(bf16)
    for start in later:
        start()
    local = [pltpu.make_async_copy(ins[a], part(a, own), local_sem.at[a]) for a in range(n_arrays)]
    for cp in local:
        cp.start()

    def offsets(k):
        return [(None, 0)] if k == 0 else [(z >= k, -k), (z + k < Z, k)]

    def col(k):
        for pred, off in offsets(k):
            fwd = (up_ok, up) if off < 0 else (down_ok, down)
            arrive(pred, me.index(me.at(z=z + off)), [fwd, (None, nb2), (None, nb3), (None, sib)])

    def second(k):
        for pred, off in offsets(k):
            arrive(pred, me.index(me.at(x=x2, y=y2, z=z + off)), [(None, nb3), (None, sib)])

    def third(k):
        for pred, off in offsets(k):
            arrive(pred, me.index(me.at(x=x3, y=y3, z=z + off)), [(None, sib)])

    def fourth(k):
        for pred, off in offsets(k):
            arrive(pred, me.index(me.at(x=1 - me.x, y=1 - me.y, z=z + off)), [(None, sib)])

    for h in range(1, Z + 3):
        if h < Z:
            col(h)
        if 0 <= h - 1 < Z:
            second(h - 1)
        if 0 <= h - 2 < Z:
            third(h - 2)
        if 0 <= h - 3 < Z:
            fourth(h - 3)
    for h in range(Z):
        for xx in (0, 1):
            for yy in (0, 1):
                for pred, off in offsets(h):
                    arrive(pred, me.index(me.at(x=xx, y=yy, c=1 - me.c, z=z + off)), [])
    for cp in local:
        cp.wait()
    pl.when(has_before)(halo.wait_recv)
    pl.when(has_after)(halo.wait_send)
    pl.when(jnp.logical_not(has_before))(blank.wait)
    for pred, copies in sends:
        def done(copies=copies):
            for cp in copies:
                cp.wait_send()
        if pred is None:
            done()
        else:
            pl.when(pred)(done)


def n_sends(Z):
    return 5 + (Z - 1) * 8 + (2 * Z - 1) * 2 + (2 * Z - 1) * 2


def gather_all(batch, seq, room, in_proj, out_proj, tokens, state, step, router, lines, gains):
    count, share = batch * seq, out_proj.shape[0]
    seqs, _, width = tokens.shape
    wide = 2 * TILE
    edge = (seqs, 8, width)
    return pl.pallas_call(
        functools.partial(gather_kernel, batch, seq),
        out_shape=[
            jax.ShapeDtypeStruct((count * a.shape[0],) + a.shape[1:], bf16) for a in (in_proj, out_proj)
        ] + [jax.ShapeDtypeStruct((count * share, wide), bf16), jax.ShapeDtypeStruct(edge, bf16)],
        in_specs=[HBM] * 3 + [VM] * (3 + len(lines) + len(gains)),
        out_specs=[HBM] * 4,
        scratch_shapes=[
            pltpu.VMEM((share, wide), bf16),
            pltpu.VMEM((room, share), f32),
            pltpu.VMEM((8, router.shape[1]), f32),
            pltpu.VMEM(edge, bf16),
            pltpu.SemaphoreType.DMA((3,)),
            pltpu.SemaphoreType.DMA((n_sends(seq // 2), 3)),
            pltpu.SemaphoreType.DMA((count, 3)),
            pltpu.SemaphoreType.DMA((3,)),
        ],
        compiler_params=pltpu.CompilerParams(collective_id=0, has_side_effects=True),
        name="gather_weights",
    )(in_proj, out_proj, tokens, state, step, router, *lines, *gains)


class Reducer:
    def __init__(self, batch, seq, items, sib_bufs, far_bufs, near_bufs, line_bufs, sems):
        self.items, self.sib_bufs, self.far_bufs, self.near_bufs, self.line_bufs = (
            items, sib_bufs, far_bufs, near_bufs, line_bufs)
        (self.sib_send, self.sib_recv, self.far_send, self.far_recv, self.near_send, self.near_recv,
         self.line_send, self.line_recv) = sems
        self.me = me = Place(batch, seq)
        self.Z, self.z = me.Z, me.z
        self.sib = me.at(c=1 - me.c)
        self.up, self.down = me.at(z=me.z + 1), me.at(z=me.z - 1)
        self.nx, self.ny = me.at(x=1 - me.x), me.at(y=1 - me.y)
        pick = lambda a, b: tuple(jnp.where(me.c == 0, p, q) for p, q in zip(a, b))
        self.near, self.far = pick(self.ny, self.nx), pick(self.nx, self.ny)
        self.mine, self.others = self.groups(me.c), self.groups(1 - me.c)

    def peers(self):
        return [(None, self.sib), (None, self.nx), (None, self.ny),
                (self.z < self.Z - 1, self.up), (self.z > 0, self.down)]

    def groups(self, c):
        me = self.me
        ox, oy = 1 - me.x, 1 - me.y
        pick = lambda a, b: jnp.where(c == 0, a, b)
        return [(ox, oy), (pick(ox, me.x), pick(me.y, oy)), (pick(me.x, ox), pick(oy, me.y)), (me.x, me.y)]

    def slot(self, xy, zz):
        return (xy[0] * 2 + xy[1]) * self.Z + zz

    def turn(self, k):
        above = self.Z - 1 - self.z
        return jnp.where(k < above, self.Z - 1 - k, jnp.where(k < self.Z - 1, k - above, self.z))

    def item(self, a, c, xy, zz):
        return self.items[a].at[self.me.index((xy[0] * 2 + c, zz * self.me.Y + xy[1]))]

    def copy(self, src, dst, send, recv, dev):
        return pltpu.make_async_remote_copy(
            src_ref=src, dst_ref=dst, send_sem=send, recv_sem=recv, device_id=dev, device_id_type=MESH)

    def to_sib(self, a, xy, k):
        t = self.turn(k)
        s = self.slot(xy, t)
        return self.copy(self.item(a, 1 - self.me.c, xy, t), self.sib_bufs[a].at[s],
                         self.sib_send.at[a, s], self.sib_recv.at[a, s], self.sib)

    def give(self, a, columns):
        for k in range(self.Z):
            for xy in columns:
                self.to_sib(a, xy, k).start()

    def to_far(self, a, g, k):
        t = self.turn(k)
        fs = g * self.Z + t
        return self.copy(self.item(a, self.me.c, self.mine[g], t), self.far_bufs[a].at[fs],
                         self.far_send.at[a, fs], self.far_recv.at[a, fs], self.far)

    def to_near(self, a, k):
        t = self.turn(k)
        return self.copy(self.item(a, self.me.c, self.mine[2], t), self.near_bufs[a].at[t],
                         self.near_send.at[a, t], self.near_recv.at[a, t], self.near)

    def step(self, a, g, k):
        t = self.turn(k)
        s = self.slot(self.mine[g], t)
        item = self.item(a, self.me.c, self.mine[g], t)
        take = lambda ref, recv: self.copy(ref, ref, self.sib_send.at[a, 0], recv, self.sib).wait_recv()
        parts = [self.sib_bufs[a].at[s]]
        take(parts[0], self.sib_recv.at[a, s])
        if g >= 2:
            fs = (g - 2) * self.Z + t
            parts.append(self.far_bufs[a].at[fs])
            take(parts[-1], self.far_recv.at[a, fs])
        if g == 3:
            parts.append(self.near_bufs[a].at[t])
            take(parts[-1], self.near_recv.at[a, t])
        total = item[...].astype(f32)
        for part in parts:
            total = total + part[...].astype(f32)
        item[...] = total.astype(bf16)
        if g < 2:
            self.to_far(a, g, k).start()
        elif g == 2:
            self.to_near(a, k).start()

    def onward(self, a, k):
        t = self.turn(k)
        rising = t > self.z
        side = jnp.where(rising, 0, 1)
        dev = (self.me.at()[0], jnp.where(rising, self.up[1], self.down[1]))
        return self.copy(self.item(a, self.me.c, self.mine[3], t), self.line_bufs[a].at[side, t],
                         self.line_send.at[a, k], self.line_recv.at[a, side, t], dev)

    def line(self, a, k, out_ref):
        t = self.turn(k)
        item = self.item(a, self.me.c, self.mine[3], t)

        def take(side):
            ref = self.line_bufs[a].at[side, t]
            self.copy(ref, ref, self.sib_send.at[a, 0], self.line_recv.at[a, side, t], self.sib).wait_recv()
            return ref[...].astype(f32)
        if k < self.Z - 1:
            rising = t > self.z

            @pl.when(jnp.where(rising, self.z, self.Z - 1 - self.z) > 0)
            def _():
                item[...] = (item[...].astype(f32) + take(jnp.where(rising, 0, 1))).astype(bf16)
            self.onward(a, k).start()
        else:
            out_ref[...] = item[...].astype(f32)
            for side, pred in ((0, self.z > 0), (1, self.z < self.Z - 1)):
                @pl.when(pred)
                def _(side=side):
                    out_ref[...] = out_ref[...] + take(side)

    def settle(self, a):
        def one(k, carry):
            for xy in self.others:
                self.to_sib(a, xy, k).wait_send()
            for g in range(2):
                self.to_far(a, g, k).wait_send()
            self.to_near(a, k).wait_send()

            @pl.when(k < self.Z - 1)
            def _():
                self.onward(a, k).wait_send()
            return carry
        lax.fori_loop(0, self.Z, one, 0)


def reduce_scratch(count, Z, shapes):
    half, n, dma = count // 2, len(shapes), pltpu.SemaphoreType.DMA
    bufs = [pltpu.VMEM(lead + s, bf16) for lead in ((count,), (half,), (2 * Z,), (Z,), (2, Z)) for s in shapes]
    return bufs + [dma((n, half)), dma((n, half)), dma((n, 2 * Z)), dma((n, 2 * Z)), dma((n, Z)), dma((n, Z)),
                   dma((n, Z)), dma((n, 2, Z))]


def pack_tail(tail, low_share, experts, skip_row, dsmall_ref, dvec_ref, dskip_ref, drouter_ref, dnorm_ref, dmoe_ref):
    blocks, share = tail.shape[:2]
    room, width = dvec_ref.shape[0], drouter_ref.shape[0]
    vec = jnp.where(subs(dvec_ref.shape) == skip_row, dskip_ref[...], dvec_ref[...])
    line = subs((8, width))
    gains = jnp.where(line == 0, dnorm_ref[...], jnp.where(line == 1, dmoe_ref[...], 0.0))
    model = drouter_ref[...] + dot_tn(gains.astype(bf16), spot(8, room + experts, TILE))
    model = jnp.concatenate(
        [model.reshape(blocks, low_share, TILE), jnp.zeros((blocks, share - low_share, TILE), f32)], axis=1)
    right = dot_tn(vec.astype(bf16), spot(room, 0, TILE)).reshape(blocks, share, TILE) + model
    tail[:, :, 0:TILE] = dsmall_ref[...].reshape(blocks, share, TILE)
    tail[:, :, TILE:] = right.astype(bf16)


def finish_kernel(dims, low_share, experts, in_ref, out_ref, tail_ref, halo_ref, tok_ref, block_ref, up_ref,
                  down_ref, block_out, tok_out, din, dconv, dbias, dstate, dstep, dstep_bias, ddecay, dskip, dout, dnorm, dmoe,
                  drouter, dup, ddown):
    seqs, rows, inner, states, rank, taps = dims
    dup[...] = up_ref[...]
    ddown[...] = down_ref[...]
    block_out[...] = block_ref[...]
    tok_out[...] = tok_ref[...]

    @pl.when(pl.program_id(0) == pl.num_programs(0) - 1)
    def _():
        tok_out[:, tok_ref.shape[1] - 8 :] = tok_ref[:, tok_ref.shape[1] - 8 :] + halo_ref[...]

    @pl.when(pl.program_id(0) == 0)
    def _():
        din[...] = in_ref[...]
        dout[...] = out_ref[...]
        tail = tail_ref[...]
        share, wide = tail.shape
        eye = (lanes((wide, wide)) == subs((wide, wide))).astype(f32)
        turned = lax.dot_general(
            eye, tail, (((1,), (1,)), ((), ())), precision=lax.Precision.HIGHEST, preferred_element_type=f32)
        dstate[...] = tail[:, : rank + 2 * states]
        dstep[...] = turned[TILE - rank : TILE]
        ddecay[...] = turned[TILE : TILE + states]
        dconv[...] = turned[TILE + states : TILE + states + taps]
        at = TILE + states + taps
        dbias[...] = turned[at : at + 1]
        dstep_bias[...] = turned[at + 1 : at + 2]
        dskip[...] = turned[at + 2 : at + 3]
        at = TILE + -(-(states + taps + 3) // 8) * 8
        drouter[...] = turned[at : at + experts, :low_share]
        at += experts
        dnorm[...] = turned[at : at + 1, :low_share]
        dmoe[...] = turned[at + 1 : at + 2, :low_share]


def tuned(batch, seq):
    return batch == 4 and seq == 8


def chain_kernel(seq, forward, dsum_ref, rates_ref, end_ref, out_ref, held, outgoing, send_sem, recv_sem):
    s = lax.axis_index("seq")
    b = lax.axis_index("batch")
    step = 1 if forward else -1
    has_before = s > 0 if forward else s < seq - 1
    has_after = s < seq - 1 if forward else s > 0
    before, after = (b, s - step), (b, s + step)
    barrier = pltpu.get_barrier_semaphore()
    for pred, dev in ((has_before, before), (has_after, after)):
        @pl.when(pred)
        def _(dev=dev):
            pl.semaphore_signal(barrier, inc=1, device_id=dev, device_id_type=MESH)
    pl.semaphore_wait(barrier, jnp.where(has_before, 1, 0) + jnp.where(has_after, 1, 0))
    count = end_ref.shape[0]

    def copy(i):
        return pltpu.make_async_remote_copy(
            src_ref=outgoing.at[i], dst_ref=held.at[i], send_sem=send_sem.at[i],
            recv_sem=recv_sem.at[i], device_id=after, device_id_type=MESH)

    for i in range(count):
        @pl.when(has_before)
        def _(i=i):
            copy(i).wait_recv()
            out_ref[i] = held[i].astype(jnp.float32)
            decay = jnp.exp(rates_ref[...] * dsum_ref[i])
            outgoing[i] = (end_ref[i] + decay * out_ref[i]).astype(jnp.bfloat16)

        @pl.when(jnp.logical_not(has_before))
        def _(i=i):
            out_ref[i] = jnp.zeros_like(out_ref[i])
            outgoing[i] = end_ref[i].astype(jnp.bfloat16)

        @pl.when(has_after)
        def _(i=i):
            copy(i).start()
    for i in range(count):
        @pl.when(has_after)
        def _(i=i):
            copy(i).wait_send()


def chain_states(seq, forward, dsum, rates, end):
    vm = pl.BlockSpec(memory_space=pltpu.VMEM)
    return pl.pallas_call(
        functools.partial(chain_kernel, seq, forward),
        out_shape=jax.ShapeDtypeStruct(end.shape, jnp.float32),
        in_specs=[vm] * 3,
        out_specs=vm,
        scratch_shapes=[
            pltpu.VMEM(end.shape, jnp.bfloat16),
            pltpu.VMEM(end.shape, jnp.bfloat16),
            pltpu.SemaphoreType.DMA((end.shape[0],)),
            pltpu.SemaphoreType.DMA((end.shape[0],)),
        ],
        compiler_params=pltpu.CompilerParams(
            collective_id=5 if forward else 6, has_side_effects=True),
        name="chain_forward" if forward else "chain_backward",
    )(dsum, rates, end)


class Relay:
    def __init__(self, seq, forward, states, dsum_ref, vec_ref, end_ref, out_ref, mine, theirs, their_sum, held,
                 outgoing, pair_send, pair_recv, line_send, line_recv):
        me = Place(4, seq)
        y, z, last = me.y, me.z, me.Z - 1
        step = 1 if forward else -1
        self.first = y == (0 if forward else 1)
        self.has_before = z > 0 if forward else z < last
        self.has_after = z < last if forward else z > 0
        self.pair, self.before, self.after = me.at(y=1 - y), me.at(z=z - step), me.at(z=z + step)
        self.states, self.vec_ref, self.end_ref, self.out_ref = states, vec_ref, end_ref, out_ref
        self.mine, self.theirs, self.dsum_ref, self.their_sum = mine, theirs, dsum_ref, their_sum
        self.held, self.outgoing = held, outgoing
        self.pair_send, self.pair_recv, self.line_send, self.line_recv = pair_send, pair_recv, line_send, line_recv
        self.count = end_ref.shape[0]

    def peers(self):
        return [(None, self.pair), (self.has_before, self.before), (self.has_after, self.after)]

    def swaps(self, i):
        both = ((self.mine.at[i], self.theirs.at[i]), (self.dsum_ref.at[i], self.their_sum.at[i]))
        return [
            pltpu.make_async_remote_copy(
                src_ref=src, dst_ref=dst, send_sem=self.pair_send.at[i, k], recv_sem=self.pair_recv.at[i, k],
                device_id=self.pair, device_id_type=MESH)
            for k, (src, dst) in enumerate(both)
        ]

    def onward(self, i):
        return pltpu.make_async_remote_copy(
            src_ref=self.outgoing.at[i], dst_ref=self.held.at[i], send_sem=self.line_send.at[i],
            recv_sem=self.line_recv.at[i], device_id=self.after, device_id_type=MESH)

    def start(self, i):
        self.mine[i] = self.end_ref[i].astype(bf16)
        for cp in self.swaps(i):
            cp.start()

    def finish(self, i):
        rates = -jnp.exp(self.vec_ref[0 : self.states])
        for cp in self.swaps(i):
            cp.wait_recv()
        pick = lambda a, b: (jnp.where(self.first, a, b), jnp.where(self.first, b, a))
        early, late = pick(self.end_ref[i], self.theirs[i].astype(f32))
        early_sum, late_sum = pick(self.dsum_ref[i], self.their_sum[i])
        both = late + jnp.exp(rates * late_sum) * early

        @pl.when(self.has_before)
        def _():
            self.onward(i).wait_recv()
            arrived = self.held[i].astype(f32)
            self.outgoing[i] = (both + jnp.exp(rates * (early_sum + late_sum)) * arrived).astype(bf16)

        @pl.when(jnp.logical_not(self.has_before))
        def _():
            self.outgoing[i] = both.astype(bf16)

        @pl.when(self.has_after)
        def _():
            self.onward(i).start()

        @pl.when(self.has_before)
        def _():
            arrived = self.held[i].astype(f32)
            self.out_ref[i] = jnp.where(self.first, arrived, early + jnp.exp(rates * early_sum) * arrived)

        @pl.when(jnp.logical_not(self.has_before))
        def _():
            self.out_ref[i] = jnp.where(self.first, jnp.zeros_like(early), early)

    def settle(self):
        for i in range(self.count):
            for cp in self.swaps(i):
                cp.wait_send()
            pl.when(self.has_after)(self.onward(i).wait_send)


def relay_scratch(seqs, states, inner):
    n, state = seqs, (seqs, states, inner)
    dma = pltpu.SemaphoreType.DMA
    return [
        pltpu.VMEM(state, bf16),
        pltpu.VMEM(state, bf16),
        pltpu.VMEM((seqs, 1, inner), f32),
        pltpu.VMEM(state, bf16),
        pltpu.VMEM(state, bf16),
        dma((n, 2)),
        dma((n, 2)),
        dma((n,)),
        dma((n,)),
    ]


def dot(a, b):
    return jnp.dot(a, b, preferred_element_type=jnp.float32)


def dot_nt(a, b):
    return lax.dot_general(a, b, (((1,), (1,)), ((), ())), preferred_element_type=jnp.float32)


def dot_tn(a, b):
    return lax.dot_general(a, b, (((0,), (0,)), ((), ())), preferred_element_type=jnp.float32)


def sigmoid(v):
    return 1.0 / (1.0 + jnp.exp(-v))


def lanes(shape):
    return lax.broadcasted_iota(jnp.int32, shape, 1)


def subs(shape):
    return lax.broadcasted_iota(jnp.int32, shape, 0)


def column(row, base, states):
    shape = (states, row.shape[1])
    only = jnp.where(lanes(shape) == subs(shape) + base, jnp.broadcast_to(row, shape), 0.0)
    return jnp.broadcast_to(jnp.sum(only, axis=1, keepdims=True), shape)


def row_sums(parts):
    row = subs(parts[0].shape)
    four, two, one = row < 4, (row // 2) % 2 == 0, row % 2 == 0
    turn = lambda v, by: pltpu.roll(v, by, axis=0)
    a = [
        jnp.where(four, parts[j], parts[j + 4]) + turn(jnp.where(four, parts[j + 4], parts[j]), 4)
        for j in range(4)
    ]
    b = [jnp.where(two, a[j] + turn(a[j], 6), a[j + 2] + turn(a[j + 2], 2)) for j in range(2)]
    return jnp.where(one, b[0] + turn(b[0], 7), b[1] + turn(b[1], 1))


def fold(v):
    return sum(v[i : i + 8] for i in range(8, v.shape[0], 8)) + v[:8]


WIDE = 256
GROUP = 16
LOG2E = math.log2(math.e)


def conv_sum(ext_ref, s, cols, vec_ref, states, taps, rows):
    first = ext_ref.shape[1] - rows - taps + 1
    total = vec_ref[states + taps : states + taps + 1, cols]
    for k in range(taps):
        total = total + vec_ref[states + k : states + k + 1, cols] * ext_ref[s, first + k : first + k + rows, cols]
    return total


def normalize(x):
    return lax.rsqrt(jnp.mean(x * x, axis=-1, keepdims=True) + epsilon)


class Quiet:
    def __getattr__(self, name):
        return lambda *args: None


QUIET = Quiet()


class Hooks(Quiet):
    def __init__(self, **steps):
        self.__dict__.update(steps)


def unpack(tail_ref, share, low_share, room, experts, vec_ref, gain_ref, router_ref):
    right = tail_ref[:, TILE : 2 * TILE]
    vec_ref[...] = dot_nt(spot(room, 0, TILE), right)
    blocks = right.shape[0] // share
    model = right.astype(f32).reshape(blocks, share, TILE)[:, :low_share].reshape(blocks * low_share, TILE).astype(bf16)
    router_ref[...] = model
    gain_ref[...] = dot_nt(spot(gain_ref.shape[0], room + experts, TILE), model)


def enter_packed(dims, share, low_share, experts, tok_ref, halo_ref, win_ref, tail_ref,
                 ext_ref, z_ref, u_ref, dt_ref, proj_ref, end_ref, dsum_ref, vec_ref, gain_ref, router_ref, xn,
                 hooks=QUIET):
    unpack(tail_ref, share, low_share, vec_ref.shape[0], experts, vec_ref, gain_ref, router_ref)
    enter_kernel(dims, tok_ref, halo_ref, win_ref, tail_ref.at[:, 0:TILE], vec_ref, gain_ref,
                 ext_ref, z_ref, u_ref, dt_ref, proj_ref, end_ref, dsum_ref, xn, hooks)


def as_column(ref):
    seqs, rows = ref.shape
    diagonal = lanes((rows, rows)) == subs((rows, rows))
    spread = [
        jnp.where(diagonal, jnp.broadcast_to(ref[s : s + 1].astype(f32), (rows, rows)), 0.0) for s in range(seqs)
    ]
    return jnp.concatenate([jnp.sum(v, axis=1, keepdims=True) for v in spread]).astype(jnp.int32)


def enter_kernel(dims, tok_ref, halo_ref, win_ref, small_ref, vec_ref, gain_ref,
                 ext_ref, z_ref, u_ref, dt_ref, proj_ref, end_ref, dsum_ref, xn, hooks=QUIET):
    seqs, rows, inner, states, rank, taps = dims
    count = seqs * rows
    for ref, at in ((tok_ref, 0), (halo_ref, count)):
        x = ref[...].astype(jnp.float32)
        xn[at : at + x.shape[0]] = (x * normalize(x) * gain_ref[0:1]).astype(jnp.bfloat16)
    proj = jnp.zeros((count, small_ref.shape[1]), jnp.float32)
    for j in range(inner // WIDE):
        cols = slice(j * WIDE, (j + 1) * WIDE)
        hooks.weights(j)
        part = dot(xn[...], win_ref[:, cols])
        z_ref[:, cols] = dot(xn[:count], win_ref[:, inner + j * WIDE : inner + (j + 1) * WIDE])
        for s in range(seqs):
            ext_ref[s, 0:8, cols] = part[count + 8 * s : count + 8 * s + 8]
            ext_ref[s, 8:, cols] = part[s * rows : (s + 1) * rows]
            pre = conv_sum(ext_ref, s, cols, vec_ref, states, taps, rows)
            u_ref[s * rows : (s + 1) * rows, cols] = pre * sigmoid(pre)
        proj = proj + dot(u_ref[:, cols].astype(jnp.bfloat16), small_ref[cols, :])
    proj_ref[...] = proj
    low = rank_lanes(proj, rank, states)
    for j in range(inner // WIDE):
        cols = slice(j * WIDE, (j + 1) * WIDE)
        pre = dot_nt(low, small_ref[cols, :]) + vec_ref[states + taps + 1 : states + taps + 2, cols]
        dt = jnp.maximum(pre, 0.0) + jnp.log1p(jnp.exp(-jnp.abs(pre)))
        dt_ref[:, cols] = dt
        for s in range(seqs):
            dsum_ref[s, 0:1, cols] = jnp.sum(dt[s * rows : (s + 1) * rows], axis=0, keepdims=True)
    hooks.projected()
    a2 = -jnp.exp(vec_ref[0:states]) * LOG2E
    blocks = inner // 128
    for s in range(seqs):
        def eight(i, hs):
            hs = list(hs)
            at = pl.multiple_of(s * rows + i * 8, 8)
            small = proj_ref[pl.ds(at, 8), :]
            bs = [column(small[j : j + 1], rank, states) for j in range(8)]
            for k in range(blocks):
                sl = slice(k * 128, (k + 1) * 128)
                d8 = dt_ref[pl.ds(at, 8), sl]
                w8 = d8 * u_ref[pl.ds(at, 8), sl]
                for j in range(8):
                    hs[k] = jnp.exp2(d8[j : j + 1] * a2[:, sl]) * hs[k] + bs[j] * w8[j : j + 1]
            return tuple(hs)
        zero = jnp.zeros((states, 128), jnp.float32)
        hs = lax.fori_loop(0, rows // 8, eight, (zero,) * blocks)
        for k in range(blocks):
            end_ref[s, :, k * 128 : (k + 1) * 128] = hs[k]
        hooks.scanned(s)


def rank_lanes(proj, rank, states):
    at = rank + 2 * states
    moved = pltpu.roll(proj, at, axis=1)
    return jnp.where(lanes(proj.shape) >= at, moved, 0.0).astype(jnp.bfloat16)


def leave_kernel(dims, capacity, room, tok_ref, cot_ref, h0_ref, dt_ref, u_ref, z_ref, proj_ref, vec_ref, out_ref,
                 gain_ref, router_ref, route_ref, slot_ref,
                 hist_ref, y_ref, hid_ref, gated_ref, moe_ref, gate_ref, rows_ref,
                 hbuf, hcur, sem, sem0, hooks=QUIET):
    seqs, rows, inner, states, rank, taps = dims
    count = seqs * rows
    a2 = -jnp.exp(vec_ref[0:states]) * LOG2E
    blocks = inner // 128
    groups = rows // GROUP
    size = GROUP * states
    firsts = []
    for s in range(seqs):
        hcur[s] = h0_ref[s].astype(jnp.bfloat16)
        cp = pltpu.make_async_copy(hcur.at[s], hist_ref.at[s, pl.ds(0, states)], sem0.at[s])
        cp.start()
        firsts.append(cp)

    def out_copy(s, g, slot):
        at = pl.multiple_of(states + g * size, states)
        return pltpu.make_async_copy(hbuf.at[slot], hist_ref.at[s, pl.ds(at, size)], sem.at[slot])

    for s in range(seqs):
        def group(g, hs):
            hs = list(hs)
            slot = g % 2

            @pl.when(g >= 2)
            def _():
                out_copy(s, g - 2, slot).wait()
            for half in range(GROUP // 8):
                at = pl.multiple_of(s * rows + g * GROUP + half * 8, 8)
                small = proj_ref[pl.ds(at, 8), :]
                bs = [column(small[j : j + 1], rank, states) for j in range(8)]
                cs = [column(small[j : j + 1], rank + states, states) for j in range(8)]
                for k in range(blocks):
                    sl = slice(k * 128, (k + 1) * 128)
                    d8 = dt_ref[pl.ds(at, 8), sl]
                    w8 = d8 * u_ref[pl.ds(at, 8), sl]
                    parts = []
                    for j in range(8):
                        t = half * 8 + j
                        hs[k] = jnp.exp2(d8[j : j + 1] * a2[:, sl]) * hs[k] + bs[j] * w8[j : j + 1]
                        hbuf[slot, t * states : (t + 1) * states, sl] = hs[k].astype(jnp.bfloat16)
                        parts.append(fold(cs[j] * hs[k]))
                    y_ref[pl.ds(at, 8), sl] = row_sums(parts)
            out_copy(s, g, slot).start()
            return tuple(hs)
        hs = tuple(h0_ref[s, :, k * 128 : (k + 1) * 128] for k in range(blocks))
        lax.fori_loop(0, groups, group, hs)
        for g in (groups - 2, groups - 1):
            out_copy(s, g, g % 2).wait()
    for cp in firsts:
        cp.wait()
    hooks.out_proj()
    hid = tok_ref[...].astype(jnp.float32)
    for j in range(inner // WIDE):
        cols = slice(j * WIDE, (j + 1) * WIDE)
        y = y_ref[:, cols] + vec_ref[states + taps + 2 : states + taps + 3, cols] * u_ref[:, cols]
        y_ref[:, cols] = y
        z = z_ref[:, cols]
        gated = (y * (z * sigmoid(z))).astype(jnp.bfloat16)
        gated_ref[:, cols] = gated
        hid = hid + dot(gated, out_ref[cols, :])
    hooks.mixed()
    hid_ref[...] = hid
    moe_in = (hid * normalize(hid) * gain_ref[1:2]).astype(jnp.bfloat16)
    moe_ref[...] = moe_in
    logits = dot(moe_in, router_ref[...])
    route, slot = as_column(route_ref), as_column(slot_ref)
    chosen = lanes(logits.shape) == route + room
    gate = sigmoid(jnp.sum(jnp.where(chosen, logits, 0.0), axis=1, keepdims=True))
    gate_ref[...] = gate
    kept = (slot < capacity).astype(jnp.float32)
    grad_rows = (cot_ref[...].astype(jnp.float32) * (gate * kept)).astype(jnp.bfloat16)
    total = rows_ref.shape[0]
    place = jnp.where(slot_ref[...] < capacity, route_ref[...] * capacity + slot_ref[...], -1)
    place = jnp.concatenate([place[s : s + 1] for s in range(seqs)], axis=1)
    pick = (subs((total, count)) == place).astype(jnp.bfloat16)
    width = moe_in.shape[1]
    rows_ref[:, :width] = dot(pick, moe_in).astype(jnp.bfloat16)
    rows_ref[:, width:] = dot(pick, grad_rows).astype(jnp.bfloat16)


def erf(x):
    x = jnp.clip(x, -4.0, 4.0)
    x2 = x * x
    top = (-2.72614225801306e-10, 2.77068142495902e-08, -2.10102402082508e-06, -5.69250639462346e-05,
           -7.34990630326855e-04, -2.95459980854025e-03, -1.60960333262415e-02)
    low = (-1.45660718464996e-05, -2.13374055278905e-04, -1.68282697438203e-03, -7.37332916720468e-03,
           -1.42647390514189e-02)
    p = jnp.full_like(x2, top[0])
    for c in top[1:]:
        p = p * x2 + c
    q = jnp.full_like(x2, low[0])
    for c in low[1:]:
        q = q * x2 + c
    return x * p / q


def expert_kernel(rows_ref, up_ref, down_ref, part_ref, dup_ref, ddown_ref):
    width = up_ref.shape[0]
    x, g = rows_ref[:, :width], rows_ref[:, width:]
    hidden = dot(x, up_ref[...])
    half = 0.5 * (1.0 + erf(hidden * math.sqrt(0.5)))
    act = (hidden * half).astype(jnp.bfloat16)
    slope = half + hidden * (jnp.exp(-0.5 * hidden * hidden) * (1.0 / math.sqrt(2.0 * math.pi)))
    part_ref[:, :width] = dot(act, down_ref[...]).astype(jnp.bfloat16)
    grad_hidden = (dot_nt(g, down_ref[...]) * slope).astype(jnp.bfloat16)
    part_ref[:, width:] = dot_nt(grad_hidden, up_ref[...]).astype(jnp.bfloat16)
    ddown, dup = dot_tn(act, g), dot_tn(x, grad_hidden)

    @pl.when(pl.program_id(0) == 0)
    def _():
        dup_ref[...] = dup
        ddown_ref[...] = ddown

    @pl.when(pl.program_id(0) > 0)
    def _():
        dup_ref[...] += dup
        ddown_ref[...] += ddown


def return_kernel(dims, capacity, room, ret_ref, cot_ref, hid_ref, moe_ref, gate_ref, gated_ref, y_ref, u_ref, z_ref, dt_ref,
                  proj_ref, vec_ref, out_ref, gain_ref, router_ref, route_ref, slot_ref,
                  block_ref, ghid_ref, gy_ref, gz_ref, dout_ref, drouter_ref, dskip_ref, dgain_ref, adj_ref,
                  hooks=QUIET, out_grads=None):
    seqs, rows, inner, states, rank, taps = dims
    count = seqs * rows
    total, width = ret_ref.shape[0], hid_ref.shape[1]
    route, slot = as_column(route_ref), as_column(slot_ref)
    place = jnp.where(slot < capacity, route * capacity + slot, -1)
    pick = (lanes((count, total)) == place).astype(jnp.bfloat16)
    result = dot(pick, ret_ref[:, :width])
    hid, gate = hid_ref[...], gate_ref[...]
    block_ref[...] = (hid + gate * result).astype(jnp.bfloat16)
    cot = cot_ref[...].astype(jnp.float32)
    grad_gate = jnp.sum(cot * result, axis=1, keepdims=True)
    wide = (count, router_ref.shape[1])
    grad_logits = jnp.where(lanes(wide) == route + room, grad_gate * gate * (1.0 - gate), 0.0).astype(jnp.bfloat16)
    grad_in = dot(pick, ret_ref[:, width:]) + dot_nt(grad_logits, router_ref[...])
    drouter_ref[...] = dot_tn(moe_ref[...], grad_logits)
    r2 = normalize(hid)
    dgain_ref[...] = jnp.sum(grad_in * (hid * r2), axis=0, keepdims=True)
    scaled = grad_in * gain_ref[1:2]
    grad_hid = cot + r2 * scaled - hid * (r2 * r2 * r2) * jnp.mean(scaled * hid, axis=1, keepdims=True)
    ghid_ref[...] = grad_hid
    branch = grad_hid.astype(jnp.bfloat16)
    hooks.activations()
    if out_grads is not None:
        out_grads(branch)
    for j in range(inner // WIDE):
        cols = slice(j * WIDE, (j + 1) * WIDE)
        if out_grads is None:
            dout_ref[cols, :] = dot_tn(gated_ref[:, cols], branch).astype(jnp.bfloat16)
        grad = dot_nt(branch, out_ref[cols, :])
        z = z_ref[:, cols]
        sig = sigmoid(z)
        gy = grad * (z * sig)
        gy_ref[:, cols] = gy
        gz_ref[:, cols] = (grad * y_ref[:, cols] * (sig + z * sig * (1.0 - sig))).astype(jnp.bfloat16)
        dskip_ref[:, cols] = jnp.sum(gy * u_ref[:, cols], axis=0, keepdims=True)
    hooks.gradients()
    a2 = -jnp.exp(vec_ref[0:states]) * LOG2E
    blocks = inner // 128
    for s in range(seqs):
        def eight(i, ms):
            ms = list(ms)
            at = pl.multiple_of((s + 1) * rows - 8 - i * 8, 8)
            small = proj_ref[pl.ds(at, 8), :]
            cs = [column(small[j : j + 1], rank + states, states) for j in range(8)]
            for k in range(blocks):
                sl = slice(k * 128, (k + 1) * 128)
                d8, g8 = dt_ref[pl.ds(at, 8), sl], gy_ref[pl.ds(at, 8), sl]
                for j in reversed(range(8)):
                    ms[k] = jnp.exp2(d8[j : j + 1] * a2[:, sl]) * (ms[k] + cs[j] * g8[j : j + 1])
            return tuple(ms)
        zero = jnp.zeros((states, 128), jnp.float32)
        ms = lax.fori_loop(0, rows // 8, eight, (zero,) * blocks)
        for k in range(blocks):
            adj_ref[s, :, k * 128 : (k + 1) * 128] = ms[k]
        hooks.scanned(s)


def back_kernel(dims, tok_ref, halo_ref, ext_ref, hist_ref, later_ref, gy_ref, gz_ref, ghid_ref, u_ref, dt_ref,
                proj_ref, win_ref, small_ref, vec_ref, gain_ref,
                dtok_ref, dhalo_ref, din_ref, dsmall_ref, dvec_ref, dgain_ref,
                hbuf, ccol, bcol, gbsum, gcsum, adj, gdt, gu, gproj, gpad, gm, xn, gpre, sem, hooks=QUIET, in_grads=None):
    small_ref = small_ref.at[:, 0:TILE]
    seqs, rows, inner, states, rank, taps = dims
    count = seqs * rows
    groups = rows // GROUP
    size = GROUP * states
    steps = seqs * groups

    def fetch(i, slot):
        s, g = i // groups, groups - 1 - i % groups
        at = pl.multiple_of(g * size, size)
        return pltpu.make_async_copy(hist_ref.at[s, pl.ds(at, size + states)], hbuf.at[slot], sem.at[slot])

    fetch(0, 0).start()
    dvec_ref[...] = jnp.zeros_like(dvec_ref)
    strip = 512

    def group(i, carry):
        slot = i % 2
        s, g = i // groups, groups - 1 - i % groups

        @pl.when(i + 1 < steps)
        def _():
            fetch(i + 1, 1 - slot).start()

        @pl.when(g == groups - 1)
        def _():
            adj[...] = later_ref[s]
        at = pl.multiple_of(s * rows + g * GROUP, GROUP)
        small = proj_ref[pl.ds(at, GROUP), :]
        for t in range(GROUP):
            ccol[t] = column(small[t : t + 1], rank + states, states)
            bcol[t] = column(small[t : t + 1], rank, states)
            gbsum[t] = jnp.zeros((states, 128), f32)
            gcsum[t] = jnp.zeros((states, 128), f32)
        fetch(i, slot).wait()
        hooks.group(i)
        for c0 in range(0, inner, strip):
            sls = [slice(c0 + k, c0 + k + 128) for k in range(0, strip, 128)]
            rates = [-jnp.exp(vec_ref[0:states, sl]) for sl in sls]
            m = [adj[:, sl] for sl in sls]
            dd = [dvec_ref[0:states, sl] for sl in sls]
            for half in reversed(range(GROUP // 8)):
                a8 = pl.multiple_of(at + half * 8, 8)
                d8 = [dt_ref[pl.ds(a8, 8), sl] for sl in sls]
                g8 = [gy_ref[pl.ds(a8, 8), sl] for sl in sls]
                u8 = [u_ref[pl.ds(a8, 8), sl] for sl in sls]
                w8 = [d * u for d, u in zip(d8, u8)]
                r1, r2 = [[None] * 8 for _ in sls], [[None] * 8 for _ in sls]
                for j in reversed(range(8)):
                    t = half * 8 + j
                    gb = gc = 0.0
                    for k, sl in enumerate(sls):
                        d, gy = d8[k][j : j + 1], g8[k][j : j + 1]
                        a = m[k] + ccol[t] * gy
                        m[k] = jnp.exp2(d * (rates[k] * LOG2E)) * a
                        p = m[k] * hbuf[slot, t * states : (t + 1) * states, sl].astype(f32) * rates[k]
                        dd[k] = dd[k] + p * d
                        gb = gb + a * w8[k][j : j + 1]
                        gc = gc + gy * hbuf[slot, (t + 1) * states : (t + 2) * states, sl].astype(f32)
                        r1[k][j], r2[k][j] = fold(p), fold(a * bcol[t])
                    gbsum[t] += gb
                    gcsum[t] += gc
                for k, sl in enumerate(sls):
                    w1, w2 = row_sums(r1[k]), row_sums(r2[k])
                    gdt[pl.ds(a8, 8), sl] = w1 + u8[k] * w2
                    gu[pl.ds(a8, 8), sl] = d8[k] * w2
            for k, sl in enumerate(sls):
                adj[:, sl] = m[k]
                dvec_ref[0:states, sl] = dd[k]
        square = (states, small.shape[1])
        where, entry = lanes(square), subs(square)
        line = subs((GROUP, small.shape[1]))
        out = jnp.zeros(small.shape, f32)
        for t in range(GROUP):
            gb = jnp.broadcast_to(jnp.sum(gbsum[t], axis=1, keepdims=True), square)
            gc = jnp.broadcast_to(jnp.sum(gcsum[t], axis=1, keepdims=True), square)
            put = jnp.where(where == entry + rank, gb, jnp.where(where == entry + rank + states, gc, 0.0))
            out = jnp.where(line == t, jnp.sum(put, axis=0, keepdims=True), out)
        gproj[pl.ds(at, GROUP), :] = out
        return carry
    lax.fori_loop(0, steps, group, 0)
    hooks.rest()

    low = rank_lanes(proj_ref[...], rank, states)
    at = rank + 2 * states
    row = states + taps
    grad_rank = jnp.zeros(proj_ref.shape, jnp.float32)
    for j in range(inner // WIDE):
        cols = slice(j * WIDE, (j + 1) * WIDE)
        pre = dot_nt(low, small_ref[cols, :]) + vec_ref[row + 1 : row + 2, cols]
        grad_pre = gdt[:, cols] * sigmoid(pre)
        dvec_ref[row + 1 : row + 2, cols] = jnp.sum(grad_pre, axis=0, keepdims=True)
        grad_pre = grad_pre.astype(jnp.bfloat16)
        gpre[:, cols] = grad_pre
        grad_rank = grad_rank + dot(grad_pre, small_ref[cols, :])
    where = lanes(grad_rank.shape)
    grad_rank = pltpu.roll(grad_rank, small_ref.shape[1] - at, axis=1)
    grad_proj = jnp.where(where < rank, grad_rank, jnp.where(where < at, gproj[...], 0.0)).astype(jnp.bfloat16)
    for ref, to in ((tok_ref, 0), (halo_ref, count)):
        x = ref[...].astype(jnp.float32)
        xn[to : to + x.shape[0]] = (x * normalize(x) * gain_ref[0:1]).astype(jnp.bfloat16)
    grad_normed = jnp.zeros((gm.shape[0], xn.shape[1]), jnp.float32)
    first = ext_ref.shape[1] - rows - taps + 1
    for j in range(inner // WIDE):
        cols = slice(j * WIDE, (j + 1) * WIDE)
        dsmall_ref[cols, :] = (
            dot_tn(u_ref[:, cols].astype(jnp.bfloat16), grad_proj) + dot_tn(gpre[:, cols], low)
        ).astype(jnp.bfloat16)
        grad_u = dot_nt(grad_proj, small_ref[cols, :]) + gy_ref[:, cols] * vec_ref[row + 2 : row + 3, cols] + gu[:, cols]
        taps_sum = [0.0] * taps
        bias_sum = 0.0
        heads = []
        for s in range(seqs):
            pre = conv_sum(ext_ref, s, cols, vec_ref, states, taps, rows)
            sig = sigmoid(pre)
            grad_conv = grad_u[s * rows : (s + 1) * rows] * (sig + pre * sig * (1.0 - sig))
            bias_sum = bias_sum + jnp.sum(grad_conv, axis=0, keepdims=True)
            for k in range(taps):
                taps_sum[k] = taps_sum[k] + jnp.sum(
                    grad_conv * ext_ref[s, first + k : first + k + rows, cols], axis=0, keepdims=True)
            gpad[0:8] = jnp.zeros((8, WIDE), jnp.float32)
            gpad[8 : 8 + rows] = grad_conv
            gpad[8 + rows :] = jnp.zeros((8, WIDE), jnp.float32)
            grad = 0.0
            for k in range(taps):
                grad = grad + vec_ref[states + k : states + k + 1, cols] * gpad[taps - 1 - k : taps + 7 - k + rows]
            heads.append(grad[0:8])
            gm[s * rows : (s + 1) * rows, cols] = grad[8:].astype(jnp.bfloat16)
        gm[count:, cols] = jnp.concatenate(heads).astype(jnp.bfloat16)
        dvec_ref[row : row + 1, cols] = bias_sum
        for k in range(taps):
            dvec_ref[states + k : states + k + 1, cols] = taps_sum[k]
    if in_grads is None:
        for j in range(inner // WIDE):
            cols, zcols = (slice(at + j * WIDE, at + (j + 1) * WIDE) for at in (0, inner))
            din_ref[:, cols] = dot_tn(xn[...], gm[:, cols]).astype(jnp.bfloat16)
            din_ref[:, zcols] = dot_tn(xn[:count], gz_ref[:, cols]).astype(jnp.bfloat16)
    else:
        in_grads()
    for j in range(inner // WIDE):
        cols, zcols = (slice(at + j * WIDE, at + (j + 1) * WIDE) for at in (0, inner))
        gz = jnp.concatenate([gz_ref[:, cols], jnp.zeros((gm.shape[0] - count, WIDE), jnp.bfloat16)])
        grad_normed = grad_normed + dot_nt(gm[:, cols], win_ref[:, cols]) + dot_nt(gz, win_ref[:, zcols])
    gain_sum = 0.0
    for ref, to, base, out in ((tok_ref, 0, ghid_ref, dtok_ref), (halo_ref, count, None, dhalo_ref)):
        x = ref[...].astype(jnp.float32)
        r1 = normalize(x)
        grad = grad_normed[to : to + x.shape[0]]
        gain_sum = gain_sum + jnp.sum(grad * (x * r1), axis=0, keepdims=True)
        grad = grad * gain_ref[0:1]
        grad = r1 * grad - x * (r1 * r1 * r1) * jnp.mean(grad * x, axis=1, keepdims=True)
        out[...] = grad if base is None else grad + base[...]
    dgain_ref[...] = gain_sum


def like(*shape, dtype=f32):
    return jax.ShapeDtypeStruct(shape, dtype)


def params(mib=56):
    return pltpu.CompilerParams(vmem_limit_bytes=mib << 20)


def moe_kernel(seq, rows_ref, up_ref, down_ref,
               back_ref, land_ref, dup_ref, ddown_ref,
               xbuf, part, act, ghid, hid, gact, far_buf, own_sum, up2_ref, down2_ref, dup2, ddown2, dup3, ddown3,
               local_sem, disp_sem, pass_sem, recv_sem, load_sem, far_send, far_recv,
               final_send, final_recv, final_local, swap_send, swap_recv):
    me = Place(4, seq)
    b, s = me.at()
    y, z, Z, x = me.y, me.z, me.Z, me.x
    cap, wide = rows_ref.shape[1], rows_ref.shape[2]
    width = wide // 2
    share = up_ref.shape[1]
    two = 2 * cap
    block = 2 * two
    sib, nx = me.at(c=1 - me.c), me.at(x=1 - x)
    greet([(None, sib), (None, nx)] + [(None, (b, (s + k) % seq)) for k in range(1, seq)])

    def remote(src, dst, send, recv, dev):
        return pltpu.make_async_remote_copy(
            src_ref=src, dst_ref=dst, send_sem=send, recv_sem=recv, device_id=dev, device_id_type=MESH)

    def slab(xx, ss):
        return land_ref.at[xx, pl.ds(pl.multiple_of(ss * cap, 8), cap)]

    def there(k, j):
        return ((z + k) % Z) * 2 + j

    def arrived(xx, ss):
        remote(slab(xx, ss), slab(xx, ss), disp_sem.at[0], recv_sem.at[xx, ss], nx).wait_recv()

    def hand(ss):
        return remote(slab(x, ss), slab(x, ss), pass_sem.at[ss], recv_sem.at[x, ss], nx)

    def load(k, xx):
        zz = (z + k) % Z
        return pltpu.make_async_copy(
            land_ref.at[xx, pl.ds(pl.multiple_of(zz * two, 8), two)],
            xbuf.at[k, pl.ds(pl.multiple_of(xx * two, 16), two)], load_sem.at[k, xx])

    def dispatch(k, j):
        to = ((z + Z - k) % Z) * 2 + j
        return remote(rows_ref.at[to], slab(x, s), disp_sem.at[2 * k + j], recv_sem.at[x, s], (b, to))

    dispatch(0, 1 - y).start()
    own = remote(rows_ref.at[s], slab(x, s), pass_sem.at[s], recv_sem.at[x, s], nx)
    own.start()
    local = pltpu.make_async_copy(rows_ref.at[s], slab(x, s), local_sem)
    local.start()
    for j in range(2):
        dispatch(1, j).start()

    def swap(i, src, dst):
        return remote(src, dst, swap_send.at[i], swap_recv.at[i], sib)

    weights = [swap(0, up_ref, up2_ref), swap(1, down_ref, down2_ref)]
    for cp in weights:
        cp.start()
    ups, downs = (up_ref, up2_ref), (down_ref, down2_ref)

    def compute(k):
        for i in range(2):
            for n in range(0, share, WIDE):
                to = slice(i * share + n, i * share + n + WIDE)
                hid[:, to] = dot(xbuf[k, :, :width], ups[i][:, n : n + WIDE])
                gact[:, to] = dot_nt(xbuf[k, :, width:], downs[i][n : n + WIDE, :])

        def sixteen(r, carry):
            at = pl.ds(pl.multiple_of(r * 16, 16), 16)
            to = pl.ds(pl.multiple_of(k * block + r * 16, 16), 16)
            h = hid[at, :]
            half = 0.5 * (1.0 + erf(h * math.sqrt(0.5)))
            act[to, :] = (h * half).astype(bf16)
            slope = half + h * (jnp.exp(-0.5 * h * h) * (1.0 / math.sqrt(2.0 * math.pi)))
            ghid[to, :] = (gact[at, :] * slope).astype(bf16)
            return carry
        lax.fori_loop(0, block // 16, sixteen, 0)
        mine = pl.ds(pl.multiple_of(k * block, 16), block)
        for n in range(0, width, WIDE):
            cols = slice(n, n + WIDE)
            part[k, :, cols] = (
                dot(act[mine, :share], down_ref[:, cols]) + dot(act[mine, share:], down2_ref[:, cols])
            ).astype(bf16)
            part[k, :, width + n : width + n + WIDE] = (
                dot_nt(ghid[mine, :share], up_ref[cols, :]) + dot_nt(ghid[mine, share:], up2_ref[cols, :])
            ).astype(bf16)

    def of_chip(k, xx):
        return part.at[k, pl.ds(pl.multiple_of(xx * two, 16), two)]

    def to_far(k):
        return remote(of_chip(k, 1 - x), far_buf.at[k], far_send.at[k], far_recv.at[k], nx)

    def to_home(k, j):
        return remote(own_sum.at[k, j], back_ref.at[s], final_send.at[k, j], final_recv.at[s], (b, there(k, j)))

    def keep_home():
        return pltpu.make_async_copy(own_sum.at[0, y], back_ref.at[s], final_local)

    def own_stage(k):
        @pl.when(k == 0)
        def _():
            arrived(x, z * 2 + 1 - y)
            hand(z * 2 + 1 - y).start()
            local.wait()

        @pl.when(k > 0)
        def _():
            for j in range(2):
                arrived(x, there(k, j))
                hand(there(k, j)).start()

        @pl.when(k < Z - 2)
        def _():
            for j in range(2):
                dispatch(k + 2, j).start()
        load(k, x).start()

    def compute_stage(k):
        for j in range(2):
            arrived(1 - x, there(k, j))
        load(k, 1 - x).start()
        for xx in range(2):
            load(k, xx).wait()

        @pl.when(k == 0)
        def _():
            for cp in weights:
                cp.wait_recv()
        compute(k)
        to_far(k).start()

    def home_stage(k):
        to_far(k).wait_recv()
        total = of_chip(k, x)[...].astype(f32) + far_buf[k].astype(f32)
        for j in range(2):
            own_sum[k, j] = total[j * cap : (j + 1) * cap].astype(bf16)

        @pl.when(k > 0)
        def _():
            for j in range(2):
                to_home(k, j).start()

        @pl.when(k == 0)
        def _():
            keep_home().start()
            to_home(0, 1 - y).start()

    everything = (Z * block, width)
    stages = ((own_stage, 0), (home_stage, 2), (compute_stage, 1))

    def step(t, carry):
        for stage, lag in stages:
            k = t - lag
            pl.when(jnp.logical_and(k >= 0, k < Z))(functools.partial(stage, k))
        return carry
    lax.fori_loop(0, Z + 2, step, 0)
    x_all = lambda: xbuf[:, :, :width].reshape(everything)
    g_all = lambda: xbuf[:, :, width:].reshape(everything)
    grads = [swap(2, dup2, dup3), swap(3, ddown2, ddown3)]
    for n in range(0, share, WIDE):
        dup2[:, n : n + WIDE] = dot_tn(x_all(), ghid[:, share + n : share + n + WIDE]).astype(bf16)
    grads[0].start()
    for n in range(0, share, WIDE):
        ddown2[n : n + WIDE, :] = dot_tn(act[:, share + n : share + n + WIDE], g_all()).astype(bf16)
    grads[1].start()
    for n in range(0, share, WIDE):
        dup_ref[:, n : n + WIDE] = dot_tn(x_all(), ghid[:, n : n + WIDE])
        ddown_ref[n : n + WIDE, :] = dot_tn(act[:, n : n + WIDE], g_all())
    grads[0].wait_recv()
    dup_ref[...] += dup3[...].astype(f32)
    grads[1].wait_recv()
    ddown_ref[...] += ddown3[...].astype(f32)
    for cp in weights + grads:
        cp.wait_send()

    for k in range(1, seq):
        e = (s + k) % seq
        remote(back_ref.at[e], back_ref.at[e], disp_sem.at[0], final_recv.at[e], sib).wait_recv()
    keep_home().wait()
    dispatch(0, 1 - y).wait_send()
    own.wait_send()
    hand(z * 2 + 1 - y).wait_send()
    to_home(0, 1 - y).wait_send()

    def settle(k, carry):
        to_far(k).wait_send()

        @pl.when(k > 0)
        def _():
            for j in range(2):
                dispatch(k, j).wait_send()
                to_home(k, j).wait_send()
                hand(there(k, j)).wait_send()
        return carry
    lax.fori_loop(0, Z, settle, 0)


def moe_rows(batch, seq, sent, up, down):
    width, hidden_share = up.shape
    capacity, wide = sent.shape[1:]
    block = seq * capacity
    if tuned(batch, seq):
        Z, block = seq // 2, 4 * capacity
        dma = pltpu.SemaphoreType.DMA
        quarter = [pltpu.VMEM((width, hidden_share), bf16), pltpu.VMEM((hidden_share, width), bf16)]
        out = pl.pallas_call(
            functools.partial(moe_kernel, seq),
            out_shape=[
                like(seq, capacity, wide, dtype=bf16),
                like(2, seq * capacity, wide, dtype=bf16),
                like(width, hidden_share),
                like(hidden_share, width),
            ],
            in_specs=[HBM] + [VM] * 2,
            out_specs=[HBM, HBM] + [VM] * 2,
            scratch_shapes=[
                pltpu.VMEM((Z, block, wide), bf16),
                pltpu.VMEM((Z, block, wide), bf16),
                pltpu.VMEM((Z * block, 2 * hidden_share), bf16),
                pltpu.VMEM((Z * block, 2 * hidden_share), bf16),
                pltpu.VMEM((block, 2 * hidden_share), f32),
                pltpu.VMEM((block, 2 * hidden_share), f32),
                pltpu.VMEM((Z, 2 * capacity, wide), bf16),
                pltpu.VMEM((Z, 2, capacity, wide), bf16),
                *quarter,
                *quarter,
                *quarter,
                dma,
                dma((2 * Z,)),
                dma((seq,)),
                dma((2, seq)),
                dma((Z, 2)),
                dma((Z,)),
                dma((Z,)),
                dma((Z, 2)),
                dma((seq,)),
                dma,
                dma((4,)),
                dma((4,)),
            ],
            compiler_params=pltpu.CompilerParams(
                collective_id=2, has_side_effects=True, vmem_limit_bytes=56 << 20),
            name="experts",
        )(sent, up, down)
        return out[0], out[2], out[3]
    mine = lax.all_to_all(sent, "seq", split_axis=0, concat_axis=0, tiled=True)
    rows = lax.all_gather(mine, "batch", axis=0).reshape(batch * block, wide)
    part, d_up, d_down = pl.pallas_call(
        expert_kernel,
        out_shape=[
            like(batch * block, wide, dtype=bf16),
            like(width, hidden_share),
            like(hidden_share, width),
        ],
        grid=(batch,),
        in_specs=[
            pl.BlockSpec((block, wide), lambda i: (i, 0)),
            pl.BlockSpec((width, hidden_share), lambda i: (0, 0)),
            pl.BlockSpec((hidden_share, width), lambda i: (0, 0)),
        ],
        out_specs=[
            pl.BlockSpec((block, wide), lambda i: (i, 0)),
            pl.BlockSpec((width, hidden_share), lambda i: (0, 0)),
            pl.BlockSpec((hidden_share, width), lambda i: (0, 0)),
        ],
        compiler_params=params(),
        name="experts",
    )(rows, up, down)
    part = part.reshape((batch,) + sent.shape)
    mine = lax.psum_scatter(part, "batch", scatter_dimension=0, tiled=False)
    return lax.all_to_all(mine, "seq", split_axis=0, concat_axis=0, tiled=True), d_up, d_down


class Moves:
    def __init__(self, sems):
        self.sems, self.used, self.named = sems, 0, {}

    def start(self, name, src, dst):
        cp = pltpu.make_async_copy(src, dst, self.sems.at[self.used])
        self.used += 1
        cp.start()
        self.named.setdefault(name, []).append(cp)

    def wait(self, *names):
        for name in names:
            for cp in self.named.pop(name):
                cp.wait()

    def wait_all(self):
        self.wait(*list(self.named))


def forward_kernel(dims, share, low_share, experts, capacity, room, seq,
                   tok_ref, halo_ref, tail_ref, cot_ref, route_ref, slot_ref, win_hbm, out_hbm,
                   ext_hbm, z_hbm, u_hbm, dt_hbm, y_hbm, gated_hbm, hist_ref, proj_ref, dsum_ref, vec_ref, gain_ref,
                   router_ref, hid_ref, moe_ref, gate_ref, rows_ref,
                   win, out, ext, z, u, dt, y, gated, end, start, xn, hbuf, hcur, sem, sem0, sems, *relay_refs):
    inner = dims[2]
    moves = Moves(sems)
    for j in range(inner // WIDE):
        for base in (0, inner):
            cols = pl.ds(base + j * WIDE, WIDE)
            moves.start(("win", j), win_hbm.at[:, cols], win.at[:, cols])
    moves.start("out", out_hbm, out)
    relay = Relay(seq, True, dims[3], dsum_ref, vec_ref, end, start, *relay_refs)
    greet(relay.peers())

    def projected():
        for name, src, dst in (("ext", ext, ext_hbm), ("z", z, z_hbm), ("u", u, u_hbm), ("dt", dt, dt_hbm)):
            moves.start(name, src, dst)

    enter_packed(dims, share, low_share, experts, tok_ref, halo_ref, win, tail_ref, ext, z, u, dt, proj_ref, end,
                 dsum_ref, vec_ref, gain_ref, router_ref, xn,
                 hooks=Hooks(weights=lambda j: moves.wait(("win", j)), projected=projected, scanned=relay.start))
    for i in range(relay.count):
        relay.finish(i)

    def mixed():
        moves.start("y", y, y_hbm)
        moves.start("gated", gated, gated_hbm)

    leave_kernel(dims, capacity, room, tok_ref, cot_ref, start, dt, u, z, proj_ref, vec_ref, out, gain_ref, router_ref,
                 route_ref, slot_ref, hist_ref, y, hid_ref, gated, moe_ref, gate_ref, rows_ref, hbuf, hcur, sem, sem0,
                 hooks=Hooks(out_proj=lambda: moves.wait("out"), mixed=mixed))
    relay.settle()
    moves.wait_all()


def backward_kernel(dims, share, low_share, experts, capacity, room, batch, seq,
                    ret_ref, cot_ref, hid_ref, moe_ref, gate_ref, vec_ref, gain_ref, router_ref, route_ref, slot_ref,
                    dsum_ref, proj_ref, gated_hbm, out_hbm, z_hbm, y_hbm, u_hbm, dt_hbm, ext_hbm, win_hbm, tail_hbm,
                    tok_hbm, halo_hbm, hist_ref,
                    block_ref, dtok_ref, next_ref, in_out, out_out, tail_out,
                    gated, out, z, y, u, dt, ext, win, tail, tok, halo, gy, gz, ghid, adj, later,
                    dhalo, dsmall, dvec, dnorm, dmoe, drouter, dskip, blank,
                    hbuf, ccol, bcol, gbsum, gcsum, carry, gdt, gu, gproj, gpad, gm, xn, gpre, sem, sems, edge_sem,
                    *more):
    seqs, rows, inner, states, rank, taps = dims
    count, devices = seqs * rows, batch * seq
    relay_refs, more = more[:9], more[9:]
    moves = Moves(sems)
    for name, src, dst in (
        ("gated", gated_hbm, gated), ("out", out_hbm, out), ("z", z_hbm, z), ("y", y_hbm, y), ("u", u_hbm, u),
        ("dt", dt_hbm, dt), ("ext", ext_hbm, ext), ("win", win_hbm, win), ("tail", tail_hbm, tail),
        ("tok", tok_hbm, tok), ("halo", halo_hbm, halo),
    ):
        moves.start(name, src, dst)
    relay = Relay(seq, False, states, dsum_ref, vec_ref, adj, later, *relay_refs)
    reducer = Reducer(batch, seq, *(more[3 * i : 3 * i + 3] for i in range(5)), more[15:])
    OUT, IN, REST = range(3)
    b, s = reducer.me.at()
    has_before, has_after = s > 0, s < seq - 1
    greet(reducer.peers() + [(has_before, (b, s - 1)), (has_after, (b, s + 1))])

    def out_grads(branch):
        cut = 8 * share
        for q in range(devices // 8):
            part = dot_tn(gated[:, q * cut : (q + 1) * cut], branch)
            reducer.items[OUT][q * 8 : (q + 1) * 8] = part.astype(bf16).reshape(8, share, part.shape[1])
        reducer.give(OUT, reducer.others)

    return_kernel(dims, capacity, room, ret_ref, cot_ref, hid_ref, moe_ref, gate_ref, gated, y, u, z, dt, proj_ref,
                  vec_ref, out, gain_ref, router_ref, route_ref, slot_ref,
                  block_ref, ghid, gy, gz, None, drouter, dskip, dmoe, adj,
                  hooks=Hooks(activations=lambda: moves.wait("gated", "out", "z", "y", "u"),
                              gradients=lambda: moves.wait("dt"), scanned=relay.start),
                  out_grads=out_grads)
    for i in range(relay.count):
        relay.finish(i)

    def group(i):
        for g in range(4):
            pl.when(i // reducer.Z == g)(functools.partial(reducer.step, OUT, g, i % reducer.Z))

    def in_grads():
        half, cut = devices // 2, low_share * devices // 2
        wide = 2 * WIDE

        def fill(xx):
            at = pl.ds(pl.multiple_of(xx * cut, 128), cut)
            items = pl.ds(xx * half, half)
            for base, grads, n in ((0, gm, count + 8 * seqs), (inner, gz, count)):
                for c0 in range(0, inner, wide):
                    part = dot_tn(xn[0:n, at], grads[:, c0 : c0 + wide]).reshape(half, low_share, wide)
                    reducer.items[IN][items, :, base + c0 : base + c0 + wide] = part.astype(bf16)

        me = reducer.me
        for xx in (1 - me.x, me.x):
            fill(xx)
            reducer.give(IN, [(xx, 1 - me.y), (xx, me.y)])

    back_kernel(dims, tok, halo, ext, hist_ref, later, gy, gz, ghid, u, dt, proj_ref, win, tail, vec_ref, gain_ref,
                dtok_ref, dhalo, None, dsmall, dvec, dnorm,
                hbuf, ccol, bcol, gbsum, gcsum, carry, gdt, gu, gproj, gpad, gm, xn, gpre, sem,
                hooks=Hooks(rest=lambda: moves.wait("ext", "win", "tail", "tok", "halo"), group=group),
                in_grads=in_grads)
    edge = reducer.copy(dhalo, next_ref, edge_sem.at[0], edge_sem.at[1], (b, s - 1))
    none = pltpu.make_async_copy(blank, next_ref, edge_sem.at[2])
    blank[...] = jnp.zeros_like(blank)
    pl.when(has_before)(edge.start)
    pl.when(jnp.logical_not(has_after))(none.start)
    pack_tail(reducer.items[REST], low_share, experts, states + taps + 2, dsmall, dvec, dskip, drouter, dnorm, dmoe)
    reducer.give(REST, reducer.others)
    for t in range(reducer.Z + 2):
        for g, k in ((0, t), (1, t), (2, t - 1), (3, t - 2)):
            if 0 <= k < reducer.Z:
                for a in (IN, REST):
                    reducer.step(a, g, k)
                if g == 3:
                    for a, ref in ((IN, in_out), (REST, tail_out), (OUT, out_out)):
                        reducer.line(a, k, ref)
    relay.settle()
    for a in (OUT, IN, REST):
        reducer.settle(a)
    pl.when(has_after)(edge.wait_recv)
    pl.when(has_before)(edge.wait_send)
    pl.when(jnp.logical_not(has_after))(none.wait)


def body(
    tokens,
    in_proj,
    conv_weight,
    conv_bias,
    state_proj,
    step_proj,
    step_bias,
    decay_log,
    skip_gain,
    out_proj,
    norm_gain,
    moe_gain,
    router_proj,
    expert_up,
    expert_down,
    routes,
    slot_index,
    cotangent,
):
    batch, seq = lax.axis_size("batch"), lax.axis_size("seq")
    both = ("batch", "seq")
    seqs, rows, width = tokens.shape
    count = seqs * rows
    devices = batch * seq
    taps, share = conv_weight.shape
    inner = share * devices
    states, rank = decay_log.shape[0], step_proj.shape[0]
    low_share = norm_gain.shape[0]
    experts = router_proj.shape[1]
    capacity = max(2, 5 * count // (4 * experts))
    dims = (seqs, rows, inner, states, rank, taps)
    tile = 128

    lines = (decay_log, conv_weight, conv_bias[None], step_bias[None], skip_gain[None])
    used = sum(a.shape[0] for a in lines)
    room = -(-used // 8) * 8
    fast = tuned(batch, seq)
    if fast:
        in_full, out_full, tail_full, halo = gather_all(
            batch, seq, room, in_proj, out_proj, tokens, state_proj, step_proj, router_proj.T, lines,
            (norm_gain[None], moe_gain[None]))
        halo = halo.reshape(seqs * 8, width)
    else:
        features = jnp.concatenate([router_proj, norm_gain[:, None], moe_gain[:, None]], axis=1)
        tail = jnp.concatenate(
            [
                state_proj,
                step_proj.T,
                jnp.pad(jnp.concatenate(lines), ((0, room - used), (0, 0))).T,
                jnp.pad(features, ((0, share - low_share), (0, tile - room - features.shape[1]))),
            ],
            axis=1,
        )
        halo = lax.ppermute(tokens[:, rows - taps + 1 :], "seq", [(i, i + 1) for i in range(seq - 1)])
        halo = jnp.pad(halo, ((0, 0), (8 - taps + 1, 0), (0, 0))).reshape(seqs * 8, width)
        in_full, out_full, tail_full = (
            lax.all_gather(a, both, axis=0, tiled=True) for a in (in_proj, out_proj, tail)
        )
    tok, cot = tokens.reshape(count, width), cotangent.reshape(count, width)
    size = GROUP * states
    total = experts * capacity
    edge_rows = seqs * 8
    dma = pltpu.SemaphoreType.DMA
    acts = like(count, inner)
    ext_s, state_s, dsum_s = like(seqs, rows + 8, inner), like(seqs, states, inner), like(seqs, 1, inner)
    proj_s, low_s, vec_s = like(count, tile), like(count, inner, dtype=bf16), like(room, inner)
    hist_s = like(seqs, (rows + 1) * states, inner, dtype=bf16)
    hid_s, moe_s, gate_s = like(count, width), like(count, width, dtype=bf16), like(count, 1)
    rows_s = like(total, 2 * width, dtype=bf16)
    gain_s, router_s = like(8, width), like(width, tile, dtype=bf16)
    vmem = lambda a: pltpu.VMEM(a.shape, a.dtype)
    normed = pltpu.VMEM((count + edge_rows, width), bf16)
    leave_scratch = [pltpu.VMEM((2, size, inner), bf16), pltpu.VMEM(state_s.shape, bf16), dma((2,)), dma((seqs,))]
    back_scratch = [
        pltpu.VMEM((2, size + states, inner), bf16),
        pltpu.VMEM((GROUP, states, tile), f32),
        pltpu.VMEM((GROUP, states, tile), f32),
        pltpu.VMEM((GROUP, states, tile), f32),
        pltpu.VMEM((GROUP, states, tile), f32),
        pltpu.VMEM((states, inner), f32),
        vmem(acts),
        vmem(acts),
        vmem(proj_s),
        pltpu.VMEM((rows + 16, WIDE), f32),
        pltpu.VMEM((count + edge_rows, inner), bf16),
        normed,
        vmem(low_s),
        dma((2,)),
    ]
    tok_s, halo_s, din_s = like(count, width), like(edge_rows, width), like(width, 2 * inner, dtype=bf16)
    dout_s, dsmall_s = like(inner, width, dtype=bf16), like(inner, tile, dtype=bf16)
    drouter_s, dskip_s, dgain_s = like(width, tile), like(1, inner), like(1, width)
    wide = inner // WIDE
    if fast:
        (ext, z, u, dt, y, gated, hist, proj, dsum, vec, gain, router, hid, moe_in, gate, sent) = pl.pallas_call(
            partial(forward_kernel, dims, share, low_share, experts, capacity, room, seq),
            out_shape=[ext_s, acts, acts, acts, acts, low_s, hist_s, proj_s, dsum_s, vec_s, gain_s, router_s,
                       hid_s, moe_s, gate_s, rows_s],
            in_specs=[VM] * 6 + [HBM] * 2,
            out_specs=[HBM] * 7 + [VM] * 9,
            scratch_shapes=[
                vmem(in_full), vmem(out_full), vmem(ext_s), vmem(acts), vmem(acts), vmem(acts), vmem(acts), vmem(low_s),
                vmem(state_s), vmem(state_s), normed, *leave_scratch, dma((2 * wide + 7,)),
                *relay_scratch(seqs, states, inner),
            ],
            compiler_params=pltpu.CompilerParams(
                collective_id=3, has_side_effects=True, vmem_limit_bytes=58 << 20),
            name="forward",
        )(tok, halo, tail_full, cot, routes, slot_index, in_full, out_full)
    else:
        vec = tail_full[:, tile : tile + room].T.astype(f32)
        router = tail_full[:, tile:].reshape(devices, share, tile)[:, :low_share].reshape(width, tile)
        gain = router[:, room + experts : room + experts + 2].T.astype(f32)
        ext, z, u, dt, proj, end, dsum = pl.pallas_call(
            partial(enter_kernel, dims),
            out_shape=[ext_s, acts, acts, acts, proj_s, state_s, dsum_s],
            in_specs=[VM] * 6,
            out_specs=[VM] * 7,
            scratch_shapes=[normed],
            compiler_params=params(),
            name="enter",
        )(tok, halo, in_full, tail_full[:, :tile], vec, gain)
        rates = -jnp.exp(vec[:states])
        before = chain_states(seq, True, dsum, rates, end)
        hist, y, hid, gated, moe_in, gate, sent = pl.pallas_call(
            partial(leave_kernel, dims, capacity, room),
            out_shape=[hist_s, acts, hid_s, low_s, moe_s, gate_s, rows_s],
            in_specs=[VM] * 13,
            out_specs=[HBM] + [VM] * 6,
            scratch_shapes=leave_scratch,
            compiler_params=params(),
            name="leave",
        )(tok, cot, before, dt, u, z, proj, vec, out_full, gain, router, routes, slot_index)

    back, d_up, d_down = moe_rows(
        batch, seq, sent.reshape(experts, capacity, 2 * width), expert_up[0], expert_down[0])
    back = back.reshape(total, 2 * width)

    if fast:
        own = [(share, width), (low_share, 2 * inner), (share, 2 * tile)]
        block_out, d_tok, from_next, s_in, s_out, s_tail = pl.pallas_call(
            partial(backward_kernel, dims, share, low_share, experts, capacity, room, batch, seq),
            out_shape=[moe_s, tok_s, halo_s, like(*own[1]), like(*own[0]), like(*own[2])],
            in_specs=[VM] * 12 + [HBM] * 12,
            out_specs=[VM] * 2 + [HBM] + [VM] * 3,
            scratch_shapes=[
                vmem(low_s), vmem(out_full), vmem(acts), vmem(acts), vmem(acts), vmem(acts), vmem(ext_s), vmem(in_full),
                vmem(tail_full), vmem(tok), vmem(halo), vmem(acts), vmem(low_s), vmem(tok_s), vmem(state_s),
                vmem(state_s), vmem(halo_s), vmem(dsmall_s), vmem(vec_s), vmem(dgain_s), vmem(dgain_s),
                vmem(drouter_s), vmem(dskip_s), vmem(halo_s), *back_scratch, dma((12,)), dma((3,)),
                *relay_scratch(seqs, states, inner), *reduce_scratch(devices, seq // 2, own),
            ],
            compiler_params=pltpu.CompilerParams(
                collective_id=4, has_side_effects=True, vmem_limit_bytes=62 << 20),
            name="backward",
        )(back, cot, hid, moe_in, gate, vec, gain, router, routes, slot_index, dsum, proj,
          gated, out_full, z, y, u, dt, ext, in_full, tail_full, tok, halo, hist)
    else:
        block_out, ghid, gy, gz, d_out, d_router, d_skip, d_moe, adj = pl.pallas_call(
            partial(return_kernel, dims, capacity, room),
            out_shape=[moe_s, tok_s, acts, low_s, dout_s, drouter_s, dskip_s, dgain_s, state_s],
            in_specs=[VM] * 17,
            out_specs=[VM] * 9,
            compiler_params=params(),
            name="back_experts",
        )(back, cot, hid, moe_in, gate, gated, y, u, z, dt, proj, vec, out_full, gain, router, routes, slot_index)
        later = chain_states(seq, False, dsum, rates, adj)
        d_tok, d_halo, d_in, d_small, d_vec, d_norm = pl.pallas_call(
            partial(back_kernel, dims),
            out_shape=[tok_s, halo_s, din_s, dsmall_s, vec_s, dgain_s],
            in_specs=[VM] * 3 + [HBM] + [VM] * 11,
            out_specs=[VM] * 6,
            scratch_shapes=back_scratch,
            compiler_params=params(),
            name="back_mixer",
        )(tok, halo, ext, hist, later, gy, gz, ghid, u, dt, proj, in_full, tail_full, vec, gain)

    skip_row = states + taps + 2
    if fast:
        steps = 4
        slab = lambda a: pl.BlockSpec((a.shape[0] // steps, a.shape[1]), lambda i: (i, 0))
        whole = lambda *shape: pl.BlockSpec(shape, lambda i: (0,) * len(shape))
        piece = pl.BlockSpec((seqs, rows // steps, width), lambda i: (0, i, 0))
        shapes = [
            s_in.shape, (taps, share), (1, share), (share, rank + 2 * states), (rank, share), (1, share),
            (states, share), (1, share), s_out.shape, (1, low_share), (1, low_share), (experts, low_share),
        ]
        block_out, d_tok, *sums, d_up, d_down = pl.pallas_call(
            partial(finish_kernel, dims, low_share, experts),
            out_shape=[like(*tokens.shape, dtype=bf16), like(*tokens.shape)] + [like(*a) for a in shapes] + [like(*d_up.shape), like(*d_down.shape)],
            grid=(steps,),
            in_specs=[whole(*s_in.shape), whole(*s_out.shape), whole(*s_tail.shape), whole(seqs, 8, width), piece, piece]
            + [slab(a) for a in (d_up, d_down)],
            out_specs=[piece, piece] + [whole(*a) for a in shapes] + [slab(d_up), slab(d_down)],
            compiler_params=params(),
            name="finish",
        )(s_in, s_out, s_tail, from_next.reshape(seqs, 8, width), d_tok.reshape(tokens.shape),
          block_out.reshape(tokens.shape), d_up, d_down)
        for i in (2, 5, 7, 9, 10):
            sums[i] = sums[i][0]
        sums[11] = sums[11].T
        return (block_out, d_tok, *sums, d_up[None], d_down[None])
    d_model = d_router.at[:, room + experts : room + experts + 2].set(jnp.concatenate([d_norm, d_moe]).T)
    d_model = jnp.pad(
        d_model.reshape(devices, low_share, tile)[:, :, room:], ((0, 0), (0, share - low_share), (0, 0))
    ).reshape(inner, tile - room)
    d_vec = d_vec.at[skip_row].set(d_skip[0])
    d_tail = jnp.concatenate([d_small, d_vec.T.astype(bf16), d_model.astype(bf16)], axis=1)
    s_in, s_out, s_tail = (
        lax.psum_scatter(a.astype(f32), both, scatter_dimension=0, tiled=True) for a in (d_in, d_out, d_tail)
    )
    from_next = lax.ppermute(
        d_halo.reshape(seqs, 8, width)[:, 8 - taps + 1 :], "seq", [(i + 1, i) for i in range(seq - 1)]
    )
    d_tok = d_tok.reshape(tokens.shape).at[:, rows - taps + 1 :].add(from_next)
    s_vec = s_tail[:, tile : tile + room].T
    s_model = s_tail[:low_share, tile + room :]
    return (
        block_out.reshape(tokens.shape),
        d_tok,
        s_in,
        s_vec[states : states + taps],
        s_vec[states + taps],
        s_tail[:, : rank + 2 * states],
        s_tail[:, rank + 2 * states : tile].T,
        s_vec[states + taps + 1],
        s_vec[:states],
        s_vec[states + taps + 2],
        s_out,
        s_model[:, experts],
        s_model[:, experts + 1],
        s_model[:, :experts],
        d_up[None],
        d_down[None],
    )


def solution(mesh):
    in_specs = (
        P("batch", "seq", None),
        P(("batch", "seq"), None),
        P(None, ("batch", "seq")),
        P(("batch", "seq")),
        P(("batch", "seq"), None),
        P(None, ("batch", "seq")),
        P(("batch", "seq")),
        P(None, ("batch", "seq")),
        P(("batch", "seq")),
        P(("batch", "seq"), None),
        P(("batch", "seq")),
        P(("batch", "seq")),
        P(("batch", "seq"), None),
        P("seq", None, "batch"),
        P("seq", "batch", None),
        P("batch", "seq"),
        P("batch", "seq"),
        P("batch", "seq", None),
    )
    out_specs = (
        P("batch", "seq", None),
        P("batch", "seq", None),
        P(("batch", "seq"), None),
        P(None, ("batch", "seq")),
        P(("batch", "seq")),
        P(("batch", "seq"), None),
        P(None, ("batch", "seq")),
        P(("batch", "seq")),
        P(None, ("batch", "seq")),
        P(("batch", "seq")),
        P(("batch", "seq"), None),
        P(("batch", "seq")),
        P(("batch", "seq")),
        P(("batch", "seq"), None),
        P("seq", None, "batch"),
        P("seq", "batch", None),
    )
    return jax.shard_map(body, mesh=mesh, in_specs=in_specs, out_specs=out_specs, check_vma=False)
```

```python
from functools import partial
import functools
import math

import jax
import jax.numpy as jnp
from jax import lax
from jax.experimental import pallas as pl
from jax.experimental.pallas import tpu as pltpu
from jax.sharding import PartitionSpec as P

epsilon = 1e-05
MESH = pl.DeviceIdType.MESH
HBM = pl.BlockSpec(memory_space=pl.ANY)
VM = pl.BlockSpec(memory_space=pltpu.VMEM)
bf16, f32 = jnp.bfloat16, jnp.float32


class Place:
    def __init__(self, batch, seq, ydim=2):
        self.batch, self.seq, self.Y = batch, seq, ydim
        self.Z = seq // ydim
        b, s = lax.axis_index("batch"), lax.axis_index("seq")
        self.x, self.c = b // 2, b % 2
        self.z, self.y = s // ydim, s % ydim

    def at(self, x=None, c=None, y=None, z=None):
        pick = lambda v, own: own if v is None else v
        x, c, y, z = pick(x, self.x), pick(c, self.c), pick(y, self.y), pick(z, self.z)
        return (x * 2 + c, z * self.Y + y)

    def index(self, dev):
        return dev[0] * self.seq + dev[1]


def greet(devices):
    barrier = pltpu.get_barrier_semaphore()
    count = 0
    for pred, dev in devices:
        if pred is None:
            pl.semaphore_signal(barrier, inc=1, device_id=dev, device_id_type=MESH)
            count = count + 1
        else:
            @pl.when(pred)
            def _(dev=dev):
                pl.semaphore_signal(barrier, inc=1, device_id=dev, device_id_type=MESH)
            count = count + jnp.where(pred, 1, 0)
    pl.semaphore_wait(barrier, count)


TILE = 128


def spot(rows, at, width):
    return (lanes((rows, width)) == subs((rows, width)) + at).astype(bf16)


class Gatherer:
    def __init__(self, batch, seq, ins, outs, send_sem, recv_sem):
        self.ins, self.outs, self.send_sem, self.recv_sem = ins, outs, send_sem, recv_sem
        self.me = me = Place(batch, seq)
        self.Z, self.z = me.Z, me.z
        self.sib = me.at(c=1 - me.c)
        self.up_ok, self.down_ok = me.z < me.Z - 1, me.z > 0
        self.up, self.down = me.at(z=me.z + 1), me.at(z=me.z - 1)
        self.nx, self.ny = me.at(x=1 - me.x), me.at(y=1 - me.y)
        first = me.c == 0
        pick = lambda a, b: tuple(jnp.where(first, p, q) for p, q in zip(a, b))
        self.second_dev, self.third_dev = pick(self.ny, self.nx), pick(self.nx, self.ny)
        ox, oy = 1 - me.x, 1 - me.y
        self.second_at = (jnp.where(first, me.x, ox), jnp.where(first, oy, me.y))
        self.third_at = (jnp.where(first, ox, me.x), jnp.where(first, me.y, oy))
        self.across_at = (ox, oy)
        self.own = me.index(me.at())
        self.sends = [[] for _ in ins]

    def peers(self):
        return [(None, self.sib), (None, self.nx), (None, self.ny), (self.up_ok, self.up), (self.down_ok, self.down)]

    def part(self, a, index):
        rows = self.ins[a].shape[0]
        return self.outs[a].at[pl.ds(pl.multiple_of(index * rows, 8), rows)]

    def send(self, a, pred, src, index, dev):
        copy = pltpu.make_async_remote_copy(
            src_ref=src, dst_ref=self.part(a, index), send_sem=self.send_sem.at[a, len(self.sends[a])],
            recv_sem=self.recv_sem.at[a, index], device_id=dev, device_id_type=MESH)
        self.sends[a].append((pred, copy))
        if pred is None:
            copy.start()
        else:
            pl.when(pred)(copy.start)

    def give(self, a):
        for pred, dev in self.targets():
            self.send(a, pred, self.ins[a], self.own, dev)

    def targets(self):
        return [(self.up_ok, self.up), (self.down_ok, self.down), (None, self.second_dev), (None, self.third_dev),
                (None, self.sib)]

    def arrive(self, a, pred, index, targets):
        part = self.part(a, index)
        copy = pltpu.make_async_remote_copy(
            src_ref=part, dst_ref=part, send_sem=self.send_sem.at[a, 0], recv_sem=self.recv_sem.at[a, index],
            device_id=self.sib, device_id_type=MESH)
        if pred is None:
            copy.wait_recv()
        else:
            pl.when(pred)(copy.wait_recv)
        for extra, dev in targets:
            p = pred if extra is None else (extra if pred is None else jnp.logical_and(pred, extra))
            self.send(a, p, part, index, dev)

    def offsets(self, k):
        return [(None, 0)] if k == 0 else [(self.z >= k, -k), (self.z + k < self.Z, k)]

    def hop(self, arrays, h):
        me, z = self.me, self.z
        to_second, to_third, to_sib = (None, self.second_dev), (None, self.third_dev), (None, self.sib)
        for k, at, targets in (
            (h, (me.x, me.y), None), (h - 1, self.second_at, [to_third, to_sib]), (h - 2, self.third_at, [to_sib]),
            (h - 3, self.across_at, [to_sib]),
        ):
            if not 0 <= k < self.Z or (targets is None and k == 0):
                continue
            for pred, off in self.offsets(k):
                onward = targets
                if targets is None:
                    onward = [(self.up_ok, self.up) if off < 0 else (self.down_ok, self.down), to_second, to_third, to_sib]
                for a in arrays:
                    self.arrive(a, pred, me.index(me.at(x=at[0], y=at[1], z=z + off)), onward)

    def rest(self, arrays):
        me = self.me
        for h in range(self.Z):
            for xx in (0, 1):
                for yy in (0, 1):
                    for pred, off in self.offsets(h):
                        for a in arrays:
                            self.arrive(a, pred, me.index(me.at(x=xx, y=yy, c=1 - me.c, z=self.z + off)), [])

    def settle(self):
        for sends in self.sends:
            for pred, copy in sends:
                if pred is None:
                    copy.wait_send()
                else:
                    pl.when(pred)(copy.wait_send)


def n_sends(Z):
    return 5 + (Z - 1) * 8 + (2 * Z - 1) * 2 + (2 * Z - 1) * 2


def pack_weights(tail, vecs, feats, state_ref, step_ref, router_ref, lines, gains):
    share, low_share, experts = state_ref.shape[0], router_ref.shape[1], router_ref.shape[0]
    rank, room, wide = step_ref.shape[0], vecs.shape[0], tail.shape[1]
    vecs[...] = jnp.zeros_like(vecs)
    at = 0
    for ref in lines:
        vecs[at : at + ref.shape[0]] = ref[...].astype(f32)
        at += ref.shape[0]
    feats[...] = jnp.zeros_like(feats)
    for i, ref in enumerate(gains):
        feats[i : i + 1] = ref[...].astype(f32)
    by_channel = (
        dot(state_ref[...], spot(state_ref.shape[1], 0, wide))
        + dot_tn(step_ref[...], spot(rank, TILE - rank, wide))
        + dot_tn(vecs[...].astype(bf16), spot(room, TILE, wide))
    )
    by_feature = dot_tn(router_ref[...], spot(experts, TILE + room, wide)) + dot_tn(
        feats[...].astype(bf16), spot(feats.shape[0], TILE + room + experts, wide))
    by_feature = jnp.concatenate([by_feature, jnp.zeros((share - low_share, wide), f32)])
    tail[...] = (by_channel + by_feature).astype(bf16)


class Reducer:
    def __init__(self, batch, seq, items, sib_bufs, far_bufs, near_bufs, line_bufs, sems):
        self.items, self.sib_bufs, self.far_bufs, self.near_bufs, self.line_bufs = (
            items, sib_bufs, far_bufs, near_bufs, line_bufs)
        (self.sib_send, self.sib_recv, self.far_send, self.far_recv, self.near_send, self.near_recv,
         self.line_send, self.line_recv) = sems
        self.me = me = Place(batch, seq)
        self.Z, self.z = me.Z, me.z
        self.sib = me.at(c=1 - me.c)
        self.up, self.down = me.at(z=me.z + 1), me.at(z=me.z - 1)
        self.nx, self.ny = me.at(x=1 - me.x), me.at(y=1 - me.y)
        pick = lambda a, b: tuple(jnp.where(me.c == 0, p, q) for p, q in zip(a, b))
        self.near, self.far = pick(self.ny, self.nx), pick(self.nx, self.ny)
        self.mine, self.others = self.groups(me.c), self.groups(1 - me.c)

    def peers(self):
        return [(None, self.sib), (None, self.nx), (None, self.ny),
                (self.z < self.Z - 1, self.up), (self.z > 0, self.down)]

    def groups(self, c):
        me = self.me
        ox, oy = 1 - me.x, 1 - me.y
        pick = lambda a, b: jnp.where(c == 0, a, b)
        return [(ox, oy), (pick(ox, me.x), pick(me.y, oy)), (pick(me.x, ox), pick(oy, me.y)), (me.x, me.y)]

    def slot(self, xy, zz):
        return (xy[0] * 2 + xy[1]) * self.Z + zz

    def turn(self, k):
        above = self.Z - 1 - self.z
        return jnp.where(k < above, self.Z - 1 - k, jnp.where(k < self.Z - 1, k - above, self.z))

    def item(self, a, c, xy, zz):
        return self.items[a].at[self.me.index((xy[0] * 2 + c, zz * self.me.Y + xy[1]))]

    def copy(self, src, dst, send, recv, dev):
        return pltpu.make_async_remote_copy(
            src_ref=src, dst_ref=dst, send_sem=send, recv_sem=recv, device_id=dev, device_id_type=MESH)

    def to_sib(self, a, xy, k):
        t = self.turn(k)
        s = self.slot(xy, t)
        return self.copy(self.item(a, 1 - self.me.c, xy, t), self.sib_bufs[a].at[s],
                         self.sib_send.at[a, s], self.sib_recv.at[a, s], self.sib)

    def give(self, a, columns):
        for k in range(self.Z):
            for xy in columns:
                self.to_sib(a, xy, k).start()

    def to_far(self, a, g, k):
        t = self.turn(k)
        fs = g * self.Z + t
        return self.copy(self.item(a, self.me.c, self.mine[g], t), self.far_bufs[a].at[fs],
                         self.far_send.at[a, fs], self.far_recv.at[a, fs], self.far)

    def to_near(self, a, k):
        t = self.turn(k)
        return self.copy(self.item(a, self.me.c, self.mine[2], t), self.near_bufs[a].at[t],
                         self.near_send.at[a, t], self.near_recv.at[a, t], self.near)

    def step(self, a, g, k):
        t = self.turn(k)
        s = self.slot(self.mine[g], t)
        item = self.item(a, self.me.c, self.mine[g], t)
        take = lambda ref, recv: self.copy(ref, ref, self.sib_send.at[a, 0], recv, self.sib).wait_recv()
        parts = [self.sib_bufs[a].at[s]]
        take(parts[0], self.sib_recv.at[a, s])
        if g >= 2:
            fs = (g - 2) * self.Z + t
            parts.append(self.far_bufs[a].at[fs])
            take(parts[-1], self.far_recv.at[a, fs])
        if g == 3:
            parts.append(self.near_bufs[a].at[t])
            take(parts[-1], self.near_recv.at[a, t])
        total = item[...].astype(f32)
        for part in parts:
            total = total + part[...].astype(f32)
        item[...] = total.astype(bf16)
        if g < 2:
            self.to_far(a, g, k).start()
        elif g == 2:
            self.to_near(a, k).start()

    def onward(self, a, k):
        t = self.turn(k)
        rising = t > self.z
        side = jnp.where(rising, 0, 1)
        dev = (self.me.at()[0], jnp.where(rising, self.up[1], self.down[1]))
        return self.copy(self.item(a, self.me.c, self.mine[3], t), self.line_bufs[a].at[side, t],
                         self.line_send.at[a, k], self.line_recv.at[a, side, t], dev)

    def line(self, a, k, out_ref):
        t = self.turn(k)
        item = self.item(a, self.me.c, self.mine[3], t)

        def take(side):
            ref = self.line_bufs[a].at[side, t]
            self.copy(ref, ref, self.sib_send.at[a, 0], self.line_recv.at[a, side, t], self.sib).wait_recv()
            return ref[...].astype(f32)
        if k < self.Z - 1:
            rising = t > self.z

            @pl.when(jnp.where(rising, self.z, self.Z - 1 - self.z) > 0)
            def _():
                item[...] = (item[...].astype(f32) + take(jnp.where(rising, 0, 1))).astype(bf16)
            self.onward(a, k).start()
        else:
            out_ref[...] = item[...].astype(f32)
            for side, pred in ((0, self.z > 0), (1, self.z < self.Z - 1)):
                @pl.when(pred)
                def _(side=side):
                    out_ref[...] = out_ref[...] + take(side)

    def settle(self, a):
        def one(k, carry):
            for xy in self.others:
                self.to_sib(a, xy, k).wait_send()
            for g in range(2):
                self.to_far(a, g, k).wait_send()
            self.to_near(a, k).wait_send()

            @pl.when(k < self.Z - 1)
            def _():
                self.onward(a, k).wait_send()
            return carry
        lax.fori_loop(0, self.Z, one, 0)


def reduce_scratch(count, Z, shapes):
    half, n, dma = count // 2, len(shapes), pltpu.SemaphoreType.DMA
    bufs = [pltpu.VMEM(lead + s, bf16) for lead in ((count,), (half,), (2 * Z,), (Z,), (2, Z)) for s in shapes]
    return bufs + [dma((n, half)), dma((n, half)), dma((n, 2 * Z)), dma((n, 2 * Z)), dma((n, Z)), dma((n, Z)),
                   dma((n, Z)), dma((n, 2, Z))]


def pack_tail(tail, low_share, experts, skip_row, dsmall_ref, dvec_ref, dskip_ref, drouter_ref, dnorm_ref, dmoe_ref):
    blocks, share = tail.shape[:2]
    room, width = dvec_ref.shape[0], drouter_ref.shape[0]
    vec = jnp.where(subs(dvec_ref.shape) == skip_row, dskip_ref[...], dvec_ref[...])
    line = subs((8, width))
    gains = jnp.where(line == 0, dnorm_ref[...], jnp.where(line == 1, dmoe_ref[...], 0.0))
    model = drouter_ref[...] + dot_tn(gains.astype(bf16), spot(8, room + experts, TILE))
    model = jnp.concatenate(
        [model.reshape(blocks, low_share, TILE), jnp.zeros((blocks, share - low_share, TILE), f32)], axis=1)
    right = dot_tn(vec.astype(bf16), spot(room, 0, TILE)).reshape(blocks, share, TILE) + model
    tail[:, :, 0:TILE] = dsmall_ref[...].reshape(blocks, share, TILE)
    tail[:, :, TILE:] = right.astype(bf16)


def finish_kernel(dims, low_share, experts, tail_ref, halo_ref, in_ref, out_ref, block_hbm, tok_hbm, up_hbm, down_hbm,
                  block_out, tok_out, din, dconv, dbias, dstate, dstep, dstep_bias, ddecay, dskip, dout, dnorm, dmoe,
                  drouter, dup, ddown, block, tok, up, down, sems):
    seqs, rows, inner, states, rank, taps = dims
    moves = Moves(sems)
    routes = []
    for i in range(4):
        for src, at, dst in ((up_hbm, up, dup), (down_hbm, down, ddown)):
            n = src.shape[0] // 4
            piece = pl.ds(i * n, n)
            routes.append((len(routes), src.at[piece], at.at[piece], dst.at[piece]))
    routes.append(("tok", tok_hbm, tok, tok_out))
    routes.append(("block", block_hbm, block, block_out))
    for name, src, at, _ in routes:
        moves.start(name, src, at)
    din[...] = in_ref[...]
    dout[...] = out_ref[...]
    tail = tail_ref[...]
    wide = tail.shape[1]
    eye = (lanes((wide, wide)) == subs((wide, wide))).astype(bf16)
    high = tail.astype(bf16)
    turned = dot_nt(eye, high) + dot_nt(eye, (tail - high.astype(f32)).astype(bf16))
    dstate[...] = tail[:, : rank + 2 * states]
    dstep[...] = turned[TILE - rank : TILE]
    ddecay[...] = turned[TILE : TILE + states]
    dconv[...] = turned[TILE + states : TILE + states + taps]
    at = TILE + states + taps
    dbias[...] = turned[at : at + 1]
    dstep_bias[...] = turned[at + 1 : at + 2]
    dskip[...] = turned[at + 2 : at + 3]
    at = TILE + -(-(states + taps + 3) // 8) * 8
    drouter[...] = turned[at : at + experts, :low_share]
    at += experts
    dnorm[...] = turned[at : at + 1, :low_share]
    dmoe[...] = turned[at + 1 : at + 2, :low_share]
    for name, _, at, dst in routes:
        moves.wait(name)
        if name == "tok":
            tok[:, rows - 8 :] = tok[:, rows - 8 :] + halo_ref[...]
        moves.start("out", at, dst)
    moves.wait_all()


def tuned(batch, seq):
    return batch == 4 and seq == 8


def chain_kernel(seq, forward, dsum_ref, rates_ref, end_ref, out_ref, held, outgoing, send_sem, recv_sem):
    s = lax.axis_index("seq")
    b = lax.axis_index("batch")
    step = 1 if forward else -1
    has_before = s > 0 if forward else s < seq - 1
    has_after = s < seq - 1 if forward else s > 0
    before, after = (b, s - step), (b, s + step)
    barrier = pltpu.get_barrier_semaphore()
    for pred, dev in ((has_before, before), (has_after, after)):
        @pl.when(pred)
        def _(dev=dev):
            pl.semaphore_signal(barrier, inc=1, device_id=dev, device_id_type=MESH)
    pl.semaphore_wait(barrier, jnp.where(has_before, 1, 0) + jnp.where(has_after, 1, 0))
    count = end_ref.shape[0]

    def copy(i):
        return pltpu.make_async_remote_copy(
            src_ref=outgoing.at[i], dst_ref=held.at[i], send_sem=send_sem.at[i],
            recv_sem=recv_sem.at[i], device_id=after, device_id_type=MESH)

    for i in range(count):
        @pl.when(has_before)
        def _(i=i):
            copy(i).wait_recv()
            out_ref[i] = held[i].astype(jnp.float32)
            decay = jnp.exp(rates_ref[...] * dsum_ref[i])
            outgoing[i] = (end_ref[i] + decay * out_ref[i]).astype(jnp.bfloat16)

        @pl.when(jnp.logical_not(has_before))
        def _(i=i):
            out_ref[i] = jnp.zeros_like(out_ref[i])
            outgoing[i] = end_ref[i].astype(jnp.bfloat16)

        @pl.when(has_after)
        def _(i=i):
            copy(i).start()
    for i in range(count):
        @pl.when(has_after)
        def _(i=i):
            copy(i).wait_send()


def chain_states(seq, forward, dsum, rates, end):
    vm = pl.BlockSpec(memory_space=pltpu.VMEM)
    return pl.pallas_call(
        functools.partial(chain_kernel, seq, forward),
        out_shape=jax.ShapeDtypeStruct(end.shape, jnp.float32),
        in_specs=[vm] * 3,
        out_specs=vm,
        scratch_shapes=[
            pltpu.VMEM(end.shape, jnp.bfloat16),
            pltpu.VMEM(end.shape, jnp.bfloat16),
            pltpu.SemaphoreType.DMA((end.shape[0],)),
            pltpu.SemaphoreType.DMA((end.shape[0],)),
        ],
        compiler_params=pltpu.CompilerParams(
            collective_id=5 if forward else 6, has_side_effects=True),
        name="chain_forward" if forward else "chain_backward",
    )(dsum, rates, end)


class Relay:
    def __init__(self, seq, forward, states, dsum_ref, vec_ref, end_ref, out_ref, mine, theirs, their_sum, held,
                 outgoing, pair_send, pair_recv, line_send, line_recv):
        me = Place(4, seq)
        y, z, last = me.y, me.z, me.Z - 1
        step = 1 if forward else -1
        self.first = y == (0 if forward else 1)
        self.has_before = z > 0 if forward else z < last
        self.has_after = z < last if forward else z > 0
        self.pair, self.before, self.after = me.at(y=1 - y), me.at(z=z - step), me.at(z=z + step)
        self.states, self.vec_ref, self.end_ref, self.out_ref = states, vec_ref, end_ref, out_ref
        self.mine, self.theirs, self.dsum_ref, self.their_sum = mine, theirs, dsum_ref, their_sum
        self.held, self.outgoing = held, outgoing
        self.pair_send, self.pair_recv, self.line_send, self.line_recv = pair_send, pair_recv, line_send, line_recv
        self.count = end_ref.shape[0]

    def peers(self):
        return [(None, self.pair), (self.has_before, self.before), (self.has_after, self.after)]

    def swaps(self, i):
        both = ((self.mine.at[i], self.theirs.at[i]), (self.dsum_ref.at[i], self.their_sum.at[i]))
        return [
            pltpu.make_async_remote_copy(
                src_ref=src, dst_ref=dst, send_sem=self.pair_send.at[i, k], recv_sem=self.pair_recv.at[i, k],
                device_id=self.pair, device_id_type=MESH)
            for k, (src, dst) in enumerate(both)
        ]

    def onward(self, i):
        return pltpu.make_async_remote_copy(
            src_ref=self.outgoing.at[i], dst_ref=self.held.at[i], send_sem=self.line_send.at[i],
            recv_sem=self.line_recv.at[i], device_id=self.after, device_id_type=MESH)

    def start(self, i):
        self.mine[i] = self.end_ref[i].astype(bf16)
        for cp in self.swaps(i):
            cp.start()

    def finish(self, i):
        rates = -jnp.exp(self.vec_ref[0 : self.states])
        for cp in self.swaps(i):
            cp.wait_recv()
        pick = lambda a, b: (jnp.where(self.first, a, b), jnp.where(self.first, b, a))
        early, late = pick(self.end_ref[i], self.theirs[i].astype(f32))
        early_sum, late_sum = pick(self.dsum_ref[i], self.their_sum[i])
        both = late + jnp.exp(rates * late_sum) * early

        @pl.when(self.has_before)
        def _():
            self.onward(i).wait_recv()
            arrived = self.held[i].astype(f32)
            self.outgoing[i] = (both + jnp.exp(rates * (early_sum + late_sum)) * arrived).astype(bf16)

        @pl.when(jnp.logical_not(self.has_before))
        def _():
            self.outgoing[i] = both.astype(bf16)

        @pl.when(self.has_after)
        def _():
            self.onward(i).start()

        @pl.when(self.has_before)
        def _():
            arrived = self.held[i].astype(f32)
            self.out_ref[i] = jnp.where(self.first, arrived, early + jnp.exp(rates * early_sum) * arrived)

        @pl.when(jnp.logical_not(self.has_before))
        def _():
            self.out_ref[i] = jnp.where(self.first, jnp.zeros_like(early), early)

    def settle(self):
        for i in range(self.count):
            for cp in self.swaps(i):
                cp.wait_send()
            pl.when(self.has_after)(self.onward(i).wait_send)


def relay_scratch(seqs, states, inner):
    n, state = seqs, (seqs, states, inner)
    dma = pltpu.SemaphoreType.DMA
    return [
        pltpu.VMEM(state, bf16),
        pltpu.VMEM(state, bf16),
        pltpu.VMEM((seqs, 1, inner), f32),
        pltpu.VMEM(state, bf16),
        pltpu.VMEM(state, bf16),
        dma((n, 2)),
        dma((n, 2)),
        dma((n,)),
        dma((n,)),
    ]


def dot(a, b):
    return jnp.dot(a, b, preferred_element_type=jnp.float32)


def dot_nt(a, b):
    return lax.dot_general(a, b, (((1,), (1,)), ((), ())), preferred_element_type=jnp.float32)


def dot_tn(a, b):
    return lax.dot_general(a, b, (((0,), (0,)), ((), ())), preferred_element_type=jnp.float32)


def sigmoid(v):
    return 1.0 / (1.0 + jnp.exp(-v))


def lanes(shape):
    return lax.broadcasted_iota(jnp.int32, shape, 1)


def subs(shape):
    return lax.broadcasted_iota(jnp.int32, shape, 0)


def column(row, base, states):
    shape = (states, row.shape[1])
    only = jnp.where(lanes(shape) == subs(shape) + base, jnp.broadcast_to(row, shape), 0.0)
    return jnp.broadcast_to(jnp.sum(only, axis=1, keepdims=True), shape)


def row_sums(parts):
    row = subs(parts[0].shape)
    four, two, one = row < 4, (row // 2) % 2 == 0, row % 2 == 0
    turn = lambda v, by: pltpu.roll(v, by, axis=0)
    a = [
        jnp.where(four, parts[j], parts[j + 4]) + turn(jnp.where(four, parts[j + 4], parts[j]), 4)
        for j in range(4)
    ]
    b = [jnp.where(two, a[j] + turn(a[j], 6), a[j + 2] + turn(a[j + 2], 2)) for j in range(2)]
    return jnp.where(one, b[0] + turn(b[0], 7), b[1] + turn(b[1], 1))


def fold(v):
    return sum(v[i : i + 8] for i in range(8, v.shape[0], 8)) + v[:8]


WIDE = 256
GROUP = 16
LOG2E = math.log2(math.e)


def conv_sum(ext_ref, s, cols, vec_ref, states, taps, rows):
    first = ext_ref.shape[1] - rows - taps + 1
    total = vec_ref[states + taps : states + taps + 1, cols]
    for k in range(taps):
        total = total + vec_ref[states + k : states + k + 1, cols] * ext_ref[s, first + k : first + k + rows, cols]
    return total


def normalize(x):
    return lax.rsqrt(jnp.mean(x * x, axis=-1, keepdims=True) + epsilon)


class Quiet:
    def __getattr__(self, name):
        return lambda *args: None


QUIET = Quiet()


class Hooks(Quiet):
    def __init__(self, **steps):
        self.__dict__.update(steps)


def unpack(tail_ref, share, low_share, room, experts, vec_ref, gain_ref, router_ref):
    right = tail_ref[:, TILE : 2 * TILE]
    vec_ref[...] = dot_nt(spot(room, 0, TILE), right)
    blocks = right.shape[0] // share
    model = right.astype(f32).reshape(blocks, share, TILE)[:, :low_share].reshape(blocks * low_share, TILE).astype(bf16)
    router_ref[...] = model
    gain_ref[...] = dot_nt(spot(gain_ref.shape[0], room + experts, TILE), model)


def enter_packed(dims, share, low_share, experts, tok_ref, halo_ref, win_ref, tail_ref,
                 ext_ref, z_ref, u_ref, dt_ref, proj_ref, end_ref, dsum_ref, vec_ref, gain_ref, router_ref, xn,
                 hooks=QUIET):
    unpack(tail_ref, share, low_share, vec_ref.shape[0], experts, vec_ref, gain_ref, router_ref)
    enter_kernel(dims, tok_ref, halo_ref, win_ref, tail_ref.at[:, 0:TILE], vec_ref, gain_ref,
                 ext_ref, z_ref, u_ref, dt_ref, proj_ref, end_ref, dsum_ref, xn, hooks)


def as_column(ref):
    seqs, rows = ref.shape
    diagonal = lanes((rows, rows)) == subs((rows, rows))
    spread = [
        jnp.where(diagonal, jnp.broadcast_to(ref[s : s + 1].astype(f32), (rows, rows)), 0.0) for s in range(seqs)
    ]
    return jnp.concatenate([jnp.sum(v, axis=1, keepdims=True) for v in spread]).astype(jnp.int32)


def enter_kernel(dims, tok_ref, halo_ref, win_ref, small_ref, vec_ref, gain_ref,
                 ext_ref, z_ref, u_ref, dt_ref, proj_ref, end_ref, dsum_ref, xn, hooks=QUIET):
    seqs, rows, inner, states, rank, taps = dims
    count = seqs * rows
    for ref, at in ((tok_ref, 0), (halo_ref, count)):
        x = ref[...].astype(jnp.float32)
        xn[at : at + x.shape[0]] = (x * normalize(x) * gain_ref[0:1]).astype(jnp.bfloat16)
    proj = jnp.zeros((count, small_ref.shape[1]), jnp.float32)
    for j in range(inner // WIDE):
        cols = slice(j * WIDE, (j + 1) * WIDE)
        hooks.weights(j)
        part = dot(xn[...], win_ref[:, cols])
        z_ref[:, cols] = dot(xn[:count], win_ref[:, inner + j * WIDE : inner + (j + 1) * WIDE])
        for s in range(seqs):
            ext_ref[s, 0:8, cols] = part[count + 8 * s : count + 8 * s + 8]
            ext_ref[s, 8:, cols] = part[s * rows : (s + 1) * rows]
            pre = conv_sum(ext_ref, s, cols, vec_ref, states, taps, rows)
            u_ref[s * rows : (s + 1) * rows, cols] = pre * sigmoid(pre)
        proj = proj + dot(u_ref[:, cols].astype(jnp.bfloat16), small_ref[cols, :])
    proj_ref[...] = proj
    low = rank_lanes(proj, rank, states)
    for j in range(inner // WIDE):
        cols = slice(j * WIDE, (j + 1) * WIDE)
        pre = dot_nt(low, small_ref[cols, :]) + vec_ref[states + taps + 1 : states + taps + 2, cols]
        dt = jnp.maximum(pre, 0.0) + jnp.log1p(jnp.exp(-jnp.abs(pre)))
        dt_ref[:, cols] = dt
        for s in range(seqs):
            dsum_ref[s, 0:1, cols] = jnp.sum(dt[s * rows : (s + 1) * rows], axis=0, keepdims=True)
    hooks.projected()
    a2 = -jnp.exp(vec_ref[0:states]) * LOG2E
    blocks = inner // 128
    for s in range(seqs):
        def eight(i, hs):
            hs = list(hs)
            at = pl.multiple_of(s * rows + i * 8, 8)
            small = proj_ref[pl.ds(at, 8), :]
            bs = [column(small[j : j + 1], rank, states) for j in range(8)]
            for k in range(blocks):
                sl = slice(k * 128, (k + 1) * 128)
                d8 = dt_ref[pl.ds(at, 8), sl]
                w8 = d8 * u_ref[pl.ds(at, 8), sl]
                for j in range(8):
                    hs[k] = jnp.exp2(d8[j : j + 1] * a2[:, sl]) * hs[k] + bs[j] * w8[j : j + 1]
            return tuple(hs)
        zero = jnp.zeros((states, 128), jnp.float32)
        hs = lax.fori_loop(0, rows // 8, eight, (zero,) * blocks)
        for k in range(blocks):
            end_ref[s, :, k * 128 : (k + 1) * 128] = hs[k]
        hooks.scanned(s)


def rank_lanes(proj, rank, states):
    at = rank + 2 * states
    moved = pltpu.roll(proj, at, axis=1)
    return jnp.where(lanes(proj.shape) >= at, moved, 0.0).astype(jnp.bfloat16)


def leave_kernel(dims, capacity, room, tok_ref, cot_ref, h0_ref, dt_ref, u_ref, z_ref, proj_ref, vec_ref, out_ref,
                 gain_ref, router_ref, route_ref, slot_ref,
                 hist_ref, y_ref, hid_ref, gated_ref, moe_ref, gate_ref, rows_ref,
                 hbuf, hcur, sem, sem0, hooks=QUIET):
    seqs, rows, inner, states, rank, taps = dims
    count = seqs * rows
    a2 = -jnp.exp(vec_ref[0:states]) * LOG2E
    blocks = inner // 128
    groups = rows // GROUP
    size = GROUP * states
    firsts = []
    for s in range(seqs):
        hcur[s] = h0_ref[s].astype(jnp.bfloat16)
        cp = pltpu.make_async_copy(hcur.at[s], hist_ref.at[s, pl.ds(0, states)], sem0.at[s])
        cp.start()
        firsts.append(cp)

    def out_copy(s, g, slot):
        at = pl.multiple_of(states + g * size, states)
        return pltpu.make_async_copy(hbuf.at[slot], hist_ref.at[s, pl.ds(at, size)], sem.at[slot])

    for s in range(seqs):
        def group(g, hs):
            hs = list(hs)
            slot = g % 2

            @pl.when(g >= 2)
            def _():
                out_copy(s, g - 2, slot).wait()
            for half in range(GROUP // 8):
                at = pl.multiple_of(s * rows + g * GROUP + half * 8, 8)
                small = proj_ref[pl.ds(at, 8), :]
                bs = [column(small[j : j + 1], rank, states) for j in range(8)]
                cs = [column(small[j : j + 1], rank + states, states) for j in range(8)]
                for k in range(blocks):
                    sl = slice(k * 128, (k + 1) * 128)
                    d8 = dt_ref[pl.ds(at, 8), sl]
                    w8 = d8 * u_ref[pl.ds(at, 8), sl]
                    parts = []
                    for j in range(8):
                        t = half * 8 + j
                        hs[k] = jnp.exp2(d8[j : j + 1] * a2[:, sl]) * hs[k] + bs[j] * w8[j : j + 1]
                        hbuf[slot, t * states : (t + 1) * states, sl] = hs[k].astype(jnp.bfloat16)
                        parts.append(fold(cs[j] * hs[k]))
                    y_ref[pl.ds(at, 8), sl] = row_sums(parts)
            out_copy(s, g, slot).start()
            return tuple(hs)
        hs = tuple(h0_ref[s, :, k * 128 : (k + 1) * 128] for k in range(blocks))
        lax.fori_loop(0, groups, group, hs)
        hooks.half(s)
        for g in (groups - 2, groups - 1):
            out_copy(s, g, g % 2).wait()
    for cp in firsts:
        cp.wait()
    hooks.out_proj()
    hid = tok_ref[...].astype(jnp.float32)
    for j in range(inner // WIDE):
        cols = slice(j * WIDE, (j + 1) * WIDE)
        y = y_ref[:, cols] + vec_ref[states + taps + 2 : states + taps + 3, cols] * u_ref[:, cols]
        y_ref[:, cols] = y
        z = z_ref[:, cols]
        gated = (y * (z * sigmoid(z))).astype(jnp.bfloat16)
        gated_ref[:, cols] = gated
        hid = hid + dot(gated, out_ref[cols, :])
    hooks.mixed()
    hid_ref[...] = hid
    moe_in = (hid * normalize(hid) * gain_ref[1:2]).astype(jnp.bfloat16)
    moe_ref[...] = moe_in
    logits = dot(moe_in, router_ref[...])
    route, slot = as_column(route_ref), as_column(slot_ref)
    chosen = lanes(logits.shape) == route + room
    gate = sigmoid(jnp.sum(jnp.where(chosen, logits, 0.0), axis=1, keepdims=True))
    gate_ref[...] = gate
    kept = (slot < capacity).astype(jnp.float32)
    grad_rows = (cot_ref[...].astype(jnp.float32) * (gate * kept)).astype(jnp.bfloat16)
    total = rows_ref.shape[0]
    place = jnp.where(slot_ref[...] < capacity, route_ref[...] * capacity + slot_ref[...], -1)
    place = jnp.concatenate([place[s : s + 1] for s in range(seqs)], axis=1)
    pick = (subs((total, count)) == place).astype(jnp.bfloat16)
    width = moe_in.shape[1]
    rows_ref[:, :width] = dot(pick, moe_in).astype(jnp.bfloat16)
    rows_ref[:, width:] = dot(pick, grad_rows).astype(jnp.bfloat16)


def erf(x):
    x = jnp.clip(x, -4.0, 4.0)
    x2 = x * x
    top = (-2.72614225801306e-10, 2.77068142495902e-08, -2.10102402082508e-06, -5.69250639462346e-05,
           -7.34990630326855e-04, -2.95459980854025e-03, -1.60960333262415e-02)
    low = (-1.45660718464996e-05, -2.13374055278905e-04, -1.68282697438203e-03, -7.37332916720468e-03,
           -1.42647390514189e-02)
    p = jnp.full_like(x2, top[0])
    for c in top[1:]:
        p = p * x2 + c
    q = jnp.full_like(x2, low[0])
    for c in low[1:]:
        q = q * x2 + c
    return x * p / q


def expert_kernel(rows_ref, up_ref, down_ref, part_ref, dup_ref, ddown_ref):
    width = up_ref.shape[0]
    x, g = rows_ref[:, :width], rows_ref[:, width:]
    hidden = dot(x, up_ref[...])
    half = 0.5 * (1.0 + erf(hidden * math.sqrt(0.5)))
    act = (hidden * half).astype(jnp.bfloat16)
    slope = half + hidden * (jnp.exp(-0.5 * hidden * hidden) * (1.0 / math.sqrt(2.0 * math.pi)))
    part_ref[:, :width] = dot(act, down_ref[...]).astype(jnp.bfloat16)
    grad_hidden = (dot_nt(g, down_ref[...]) * slope).astype(jnp.bfloat16)
    part_ref[:, width:] = dot_nt(grad_hidden, up_ref[...]).astype(jnp.bfloat16)
    ddown, dup = dot_tn(act, g), dot_tn(x, grad_hidden)

    @pl.when(pl.program_id(0) == 0)
    def _():
        dup_ref[...] = dup
        ddown_ref[...] = ddown

    @pl.when(pl.program_id(0) > 0)
    def _():
        dup_ref[...] += dup
        ddown_ref[...] += ddown


def return_kernel(dims, capacity, room, ret_ref, cot_ref, hid_ref, moe_ref, gate_ref, gated_ref, y_ref, u_ref, z_ref, dt_ref,
                  proj_ref, vec_ref, out_ref, gain_ref, router_ref, route_ref, slot_ref,
                  block_ref, ghid_ref, gy_ref, gz_ref, dout_ref, drouter_ref, dskip_ref, dgain_ref, adj_ref,
                  hooks=QUIET):
    seqs, rows, inner, states, rank, taps = dims
    count = seqs * rows
    total, width = ret_ref.shape[0], hid_ref.shape[1]
    route, slot = as_column(route_ref), as_column(slot_ref)
    place = jnp.where(slot < capacity, route * capacity + slot, -1)
    pick = (lanes((count, total)) == place).astype(jnp.bfloat16)
    result = dot(pick, ret_ref[:, :width])
    hid, gate = hid_ref[...], gate_ref[...]
    block_ref[...] = (hid + gate * result).astype(jnp.bfloat16)
    cot = cot_ref[...].astype(jnp.float32)
    grad_gate = jnp.sum(cot * result, axis=1, keepdims=True)
    wide = (count, router_ref.shape[1])
    grad_logits = jnp.where(lanes(wide) == route + room, grad_gate * gate * (1.0 - gate), 0.0).astype(jnp.bfloat16)
    grad_in = dot(pick, ret_ref[:, width:]) + dot_nt(grad_logits, router_ref[...])
    drouter_ref[...] = dot_tn(moe_ref[...], grad_logits)
    r2 = normalize(hid)
    dgain_ref[...] = jnp.sum(grad_in * (hid * r2), axis=0, keepdims=True)
    scaled = grad_in * gain_ref[1:2]
    grad_hid = cot + r2 * scaled - hid * (r2 * r2 * r2) * jnp.mean(scaled * hid, axis=1, keepdims=True)
    ghid_ref[...] = grad_hid
    branch = grad_hid.astype(jnp.bfloat16)
    hooks.activations()
    for j in range(inner // WIDE):
        cols = slice(j * WIDE, (j + 1) * WIDE)
        if dout_ref is not None:
            dout_ref[cols, :] = dot_tn(gated_ref[:, cols], branch).astype(jnp.bfloat16)
        grad = dot_nt(branch, out_ref[cols, :])
        z = z_ref[:, cols]
        sig = sigmoid(z)
        gy = grad * (z * sig)
        gy_ref[:, cols] = gy
        gz_ref[:, cols] = (grad * y_ref[:, cols] * (sig + z * sig * (1.0 - sig))).astype(jnp.bfloat16)
        dskip_ref[:, cols] = jnp.sum(gy * u_ref[:, cols], axis=0, keepdims=True)
    hooks.gradients()
    a2 = -jnp.exp(vec_ref[0:states]) * LOG2E
    blocks = inner // 128
    for s in range(seqs):
        def eight(i, ms):
            ms = list(ms)
            at = pl.multiple_of((s + 1) * rows - 8 - i * 8, 8)
            small = proj_ref[pl.ds(at, 8), :]
            cs = [column(small[j : j + 1], rank + states, states) for j in range(8)]
            for k in range(blocks):
                sl = slice(k * 128, (k + 1) * 128)
                d8, g8 = dt_ref[pl.ds(at, 8), sl], gy_ref[pl.ds(at, 8), sl]
                for j in reversed(range(8)):
                    ms[k] = jnp.exp2(d8[j : j + 1] * a2[:, sl]) * (ms[k] + cs[j] * g8[j : j + 1])
            return tuple(ms)
        zero = jnp.zeros((states, 128), jnp.float32)
        ms = lax.fori_loop(0, rows // 8, eight, (zero,) * blocks)
        for k in range(blocks):
            adj_ref[s, :, k * 128 : (k + 1) * 128] = ms[k]
        hooks.scanned(s)


def back_kernel(dims, tok_ref, halo_ref, ext_ref, hist_ref, later_ref, gy_ref, gz_ref, ghid_ref, u_ref, dt_ref,
                proj_ref, win_ref, small_ref, vec_ref, gain_ref,
                dtok_ref, dhalo_ref, din_ref, dsmall_ref, dvec_ref, dgain_ref,
                hbuf, ccol, bcol, gbsum, gcsum, adj, gdt, gu, gproj, gpad, gm, xn, gpre, sem, hooks=QUIET, in_grads=None):
    small_ref = small_ref.at[:, 0:TILE]
    seqs, rows, inner, states, rank, taps = dims
    count = seqs * rows
    groups = rows // GROUP
    size = GROUP * states
    steps = seqs * groups

    def fetch(i, slot):
        s, g = i // groups, groups - 1 - i % groups
        at = pl.multiple_of(g * size, size)
        return pltpu.make_async_copy(hist_ref.at[s, pl.ds(at, size + states)], hbuf.at[slot], sem.at[slot])

    fetch(0, 0).start()
    dvec_ref[...] = jnp.zeros_like(dvec_ref)
    strip = 512

    def group(i, carry):
        slot = i % 2
        s, g = i // groups, groups - 1 - i % groups

        @pl.when(i + 1 < steps)
        def _():
            fetch(i + 1, 1 - slot).start()

        @pl.when(g == groups - 1)
        def _():
            adj[...] = later_ref[s]
        at = pl.multiple_of(s * rows + g * GROUP, GROUP)
        small = proj_ref[pl.ds(at, GROUP), :]
        for t in range(GROUP):
            ccol[t] = column(small[t : t + 1], rank + states, states)
            bcol[t] = column(small[t : t + 1], rank, states)
            gbsum[t] = jnp.zeros((states, 128), f32)
            gcsum[t] = jnp.zeros((states, 128), f32)
        fetch(i, slot).wait()
        hooks.group(i)
        for c0 in range(0, inner, strip):
            sls = [slice(c0 + k, c0 + k + 128) for k in range(0, strip, 128)]
            scaled = [-jnp.exp(vec_ref[0:states, sl]) * LOG2E for sl in sls]
            m = [adj[:, sl] for sl in sls]
            dd = [dvec_ref[0:states, sl] for sl in sls]
            now = [hbuf[slot, GROUP * states : (GROUP + 1) * states, sl].astype(f32) for sl in sls]
            for half in reversed(range(GROUP // 8)):
                a8 = pl.multiple_of(at + half * 8, 8)
                d8 = [dt_ref[pl.ds(a8, 8), sl] for sl in sls]
                g8 = [gy_ref[pl.ds(a8, 8), sl] for sl in sls]
                u8 = [u_ref[pl.ds(a8, 8), sl] for sl in sls]
                w8 = [d * u for d, u in zip(d8, u8)]
                r1, r2 = [[None] * 8 for _ in sls], [[None] * 8 for _ in sls]
                for j in reversed(range(8)):
                    t = half * 8 + j
                    gb = gc = 0.0
                    for k, sl in enumerate(sls):
                        d, gy = d8[k][j : j + 1], g8[k][j : j + 1]
                        a = m[k] + ccol[t] * gy
                        m[k] = jnp.exp2(d * scaled[k]) * a
                        gb = gb + a * w8[k][j : j + 1]
                        gc = gc + gy * now[k]
                        now[k] = hbuf[slot, t * states : (t + 1) * states, sl].astype(f32)
                        p = m[k] * now[k] * scaled[k]
                        dd[k] = dd[k] + p * d
                        r1[k][j], r2[k][j] = fold(p), fold(a * bcol[t])
                    gbsum[t] += gb
                    gcsum[t] += gc
                for k, sl in enumerate(sls):
                    w1, w2 = row_sums(r1[k]), row_sums(r2[k])
                    gdt[pl.ds(a8, 8), sl] = w1 * (1.0 / LOG2E) + u8[k] * w2
                    gu[pl.ds(a8, 8), sl] = d8[k] * w2
            for k, sl in enumerate(sls):
                adj[:, sl] = m[k]
                dvec_ref[0:states, sl] = dd[k]
        square = (states, small.shape[1])
        where, entry = lanes(square), subs(square)
        line = subs((GROUP, small.shape[1]))
        out = jnp.zeros(small.shape, f32)
        for t in range(GROUP):
            gb = jnp.broadcast_to(jnp.sum(gbsum[t], axis=1, keepdims=True), square)
            gc = jnp.broadcast_to(jnp.sum(gcsum[t], axis=1, keepdims=True), square)
            put = jnp.where(where == entry + rank, gb, jnp.where(where == entry + rank + states, gc, 0.0))
            out = jnp.where(line == t, jnp.sum(put, axis=0, keepdims=True), out)
        gproj[pl.ds(at, GROUP), :] = out
        return carry
    lax.fori_loop(0, steps, group, 0)
    dvec_ref[0:states] = dvec_ref[0:states] * (1.0 / LOG2E)
    hooks.rest()

    low = rank_lanes(proj_ref[...], rank, states)
    at = rank + 2 * states
    row = states + taps
    grad_rank = jnp.zeros(proj_ref.shape, jnp.float32)
    for j in range(inner // WIDE):
        cols = slice(j * WIDE, (j + 1) * WIDE)
        pre = dot_nt(low, small_ref[cols, :]) + vec_ref[row + 1 : row + 2, cols]
        grad_pre = gdt[:, cols] * sigmoid(pre)
        dvec_ref[row + 1 : row + 2, cols] = jnp.sum(grad_pre, axis=0, keepdims=True)
        grad_pre = grad_pre.astype(jnp.bfloat16)
        gpre[:, cols] = grad_pre
        grad_rank = grad_rank + dot(grad_pre, small_ref[cols, :])
    where = lanes(grad_rank.shape)
    grad_rank = pltpu.roll(grad_rank, small_ref.shape[1] - at, axis=1)
    grad_proj = jnp.where(where < rank, grad_rank, jnp.where(where < at, gproj[...], 0.0)).astype(jnp.bfloat16)
    for ref, to in ((tok_ref, 0), (halo_ref, count)):
        x = ref[...].astype(jnp.float32)
        xn[to : to + x.shape[0]] = (x * normalize(x) * gain_ref[0:1]).astype(jnp.bfloat16)
    grad_normed = jnp.zeros((gm.shape[0], xn.shape[1]), jnp.float32)
    first = ext_ref.shape[1] - rows - taps + 1
    for j in range(inner // WIDE):
        cols = slice(j * WIDE, (j + 1) * WIDE)
        dsmall_ref[cols, :] = (
            dot_tn(u_ref[:, cols].astype(jnp.bfloat16), grad_proj) + dot_tn(gpre[:, cols], low)
        ).astype(jnp.bfloat16)
        grad_u = dot_nt(grad_proj, small_ref[cols, :]) + gy_ref[:, cols] * vec_ref[row + 2 : row + 3, cols] + gu[:, cols]
        taps_sum = [0.0] * taps
        bias_sum = 0.0
        heads = []
        for s in range(seqs):
            pre = conv_sum(ext_ref, s, cols, vec_ref, states, taps, rows)
            sig = sigmoid(pre)
            grad_conv = grad_u[s * rows : (s + 1) * rows] * (sig + pre * sig * (1.0 - sig))
            bias_sum = bias_sum + jnp.sum(grad_conv, axis=0, keepdims=True)
            for k in range(taps):
                taps_sum[k] = taps_sum[k] + jnp.sum(
                    grad_conv * ext_ref[s, first + k : first + k + rows, cols], axis=0, keepdims=True)
            gpad[0:8] = jnp.zeros((8, WIDE), jnp.float32)
            gpad[8 : 8 + rows] = grad_conv
            gpad[8 + rows :] = jnp.zeros((8, WIDE), jnp.float32)
            grad = 0.0
            for k in range(taps):
                grad = grad + vec_ref[states + k : states + k + 1, cols] * gpad[taps - 1 - k : taps + 7 - k + rows]
            heads.append(grad[0:8])
            gm[s * rows : (s + 1) * rows, cols] = grad[8:].astype(jnp.bfloat16)
        gm[count:, cols] = jnp.concatenate(heads).astype(jnp.bfloat16)
        dvec_ref[row : row + 1, cols] = bias_sum
        for k in range(taps):
            dvec_ref[states + k : states + k + 1, cols] = taps_sum[k]
    if in_grads is None:
        for j in range(inner // WIDE):
            cols, zcols = (slice(at + j * WIDE, at + (j + 1) * WIDE) for at in (0, inner))
            din_ref[:, cols] = dot_tn(xn[...], gm[:, cols]).astype(jnp.bfloat16)
            din_ref[:, zcols] = dot_tn(xn[:count], gz_ref[:, cols]).astype(jnp.bfloat16)
    else:
        in_grads()
    for j in range(inner // WIDE):
        cols, zcols = (slice(at + j * WIDE, at + (j + 1) * WIDE) for at in (0, inner))
        gz = jnp.concatenate([gz_ref[:, cols], jnp.zeros((gm.shape[0] - count, WIDE), jnp.bfloat16)])
        grad_normed = grad_normed + dot_nt(gm[:, cols], win_ref[:, cols]) + dot_nt(gz, win_ref[:, zcols])
    gain_sum = 0.0
    for ref, to, base, out in ((tok_ref, 0, ghid_ref, dtok_ref), (halo_ref, count, None, dhalo_ref)):
        x = ref[...].astype(jnp.float32)
        r1 = normalize(x)
        grad = grad_normed[to : to + x.shape[0]]
        gain_sum = gain_sum + jnp.sum(grad * (x * r1), axis=0, keepdims=True)
        grad = grad * gain_ref[0:1]
        grad = r1 * grad - x * (r1 * r1 * r1) * jnp.mean(grad * x, axis=1, keepdims=True)
        out[...] = grad if base is None else grad + base[...]
    dgain_ref[...] = gain_sum


def like(*shape, dtype=f32):
    return jax.ShapeDtypeStruct(shape, dtype)


def params(mib=56):
    return pltpu.CompilerParams(vmem_limit_bytes=mib << 20)


def moe_kernel(seq, rows_ref, up_ref, down_ref,
               back_ref, land_ref, dup_ref, ddown_ref,
               xbuf, part, act, ghid, hid, gact, far_buf, own_sum, up2_ref, down2_ref, dup2, ddown2, dup3, ddown3,
               local_sem, disp_sem, pass_sem, recv_sem, load_sem, far_send, far_recv,
               final_send, final_recv, final_local, swap_send, swap_recv):
    me = Place(4, seq)
    b, s = me.at()
    y, z, Z, x = me.y, me.z, me.Z, me.x
    cap, wide = rows_ref.shape[1], rows_ref.shape[2]
    width = wide // 2
    share = up_ref.shape[1]
    two = 2 * cap
    block = 2 * two
    sib, nx = me.at(c=1 - me.c), me.at(x=1 - x)
    greet([(None, sib), (None, nx)] + [(None, (b, (s + k) % seq)) for k in range(1, seq)])

    def remote(src, dst, send, recv, dev):
        return pltpu.make_async_remote_copy(
            src_ref=src, dst_ref=dst, send_sem=send, recv_sem=recv, device_id=dev, device_id_type=MESH)

    def slab(xx, ss):
        return land_ref.at[xx, pl.ds(pl.multiple_of(ss * cap, 8), cap)]

    def there(k, j):
        return ((z + k) % Z) * 2 + j

    def arrived(xx, ss):
        remote(slab(xx, ss), slab(xx, ss), disp_sem.at[0], recv_sem.at[xx, ss], nx).wait_recv()

    def hand(ss):
        return remote(slab(x, ss), slab(x, ss), pass_sem.at[ss], recv_sem.at[x, ss], nx)

    def load(k, xx):
        zz = (z + k) % Z
        return pltpu.make_async_copy(
            land_ref.at[xx, pl.ds(pl.multiple_of(zz * two, 8), two)],
            xbuf.at[k, pl.ds(pl.multiple_of(xx * two, 16), two)], load_sem.at[k, xx])

    def dispatch(k, j):
        to = ((z + Z - k) % Z) * 2 + j
        return remote(rows_ref.at[to], slab(x, s), disp_sem.at[2 * k + j], recv_sem.at[x, s], (b, to))

    dispatch(0, 1 - y).start()
    own = remote(rows_ref.at[s], slab(x, s), pass_sem.at[s], recv_sem.at[x, s], nx)
    own.start()
    local = pltpu.make_async_copy(rows_ref.at[s], slab(x, s), local_sem)
    local.start()
    for j in range(2):
        dispatch(1, j).start()

    def swap(i, src, dst):
        return remote(src, dst, swap_send.at[i], swap_recv.at[i], sib)

    weights = [swap(0, up_ref, up2_ref), swap(1, down_ref, down2_ref)]
    for cp in weights:
        cp.start()
    ups, downs = (up_ref, up2_ref), (down_ref, down2_ref)

    def compute(k):
        for i in range(2):
            for n in range(0, share, WIDE):
                to = slice(i * share + n, i * share + n + WIDE)
                hid[:, to] = dot(xbuf[k, :, :width], ups[i][:, n : n + WIDE])
                gact[:, to] = dot_nt(xbuf[k, :, width:], downs[i][n : n + WIDE, :])

        def sixteen(r, carry):
            at = pl.ds(pl.multiple_of(r * 16, 16), 16)
            to = pl.ds(pl.multiple_of(k * block + r * 16, 16), 16)
            h = hid[at, :]
            half = 0.5 * (1.0 + erf(h * math.sqrt(0.5)))
            act[to, :] = (h * half).astype(bf16)
            slope = half + h * (jnp.exp(-0.5 * h * h) * (1.0 / math.sqrt(2.0 * math.pi)))
            ghid[to, :] = (gact[at, :] * slope).astype(bf16)
            return carry
        lax.fori_loop(0, block // 16, sixteen, 0)
        mine = pl.ds(pl.multiple_of(k * block, 16), block)
        for n in range(0, width, WIDE):
            cols = slice(n, n + WIDE)
            part[k, :, cols] = (
                dot(act[mine, :share], down_ref[:, cols]) + dot(act[mine, share:], down2_ref[:, cols])
            ).astype(bf16)
            part[k, :, width + n : width + n + WIDE] = (
                dot_nt(ghid[mine, :share], up_ref[cols, :]) + dot_nt(ghid[mine, share:], up2_ref[cols, :])
            ).astype(bf16)

    def of_chip(k, xx):
        return part.at[k, pl.ds(pl.multiple_of(xx * two, 16), two)]

    def to_far(k):
        return remote(of_chip(k, 1 - x), far_buf.at[k], far_send.at[k], far_recv.at[k], nx)

    def to_home(k, j):
        return remote(own_sum.at[k, j], back_ref.at[s], final_send.at[k, j], final_recv.at[s], (b, there(k, j)))

    def keep_home():
        return pltpu.make_async_copy(own_sum.at[0, y], back_ref.at[s], final_local)

    def own_stage(k):
        @pl.when(k == 0)
        def _():
            arrived(x, z * 2 + 1 - y)
            hand(z * 2 + 1 - y).start()
            local.wait()

        @pl.when(k > 0)
        def _():
            for j in range(2):
                arrived(x, there(k, j))
                hand(there(k, j)).start()

        @pl.when(k < Z - 2)
        def _():
            for j in range(2):
                dispatch(k + 2, j).start()
        load(k, x).start()

    def compute_stage(k):
        for j in range(2):
            arrived(1 - x, there(k, j))
        load(k, 1 - x).start()
        for xx in range(2):
            load(k, xx).wait()

        @pl.when(k == 0)
        def _():
            for cp in weights:
                cp.wait_recv()
        compute(k)
        to_far(k).start()

    def home_stage(k):
        to_far(k).wait_recv()
        total = of_chip(k, x)[...].astype(f32) + far_buf[k].astype(f32)
        for j in range(2):
            own_sum[k, j] = total[j * cap : (j + 1) * cap].astype(bf16)

        @pl.when(k > 0)
        def _():
            for j in range(2):
                to_home(k, j).start()

        @pl.when(k == 0)
        def _():
            keep_home().start()
            to_home(0, 1 - y).start()

    everything = (Z * block, width)
    stages = ((own_stage, 0), (home_stage, 2), (compute_stage, 1))

    def step(t, carry):
        for stage, lag in stages:
            k = t - lag
            pl.when(jnp.logical_and(k >= 0, k < Z))(functools.partial(stage, k))
        return carry
    lax.fori_loop(0, Z + 2, step, 0)
    x_all = lambda: xbuf[:, :, :width].reshape(everything)
    g_all = lambda: xbuf[:, :, width:].reshape(everything)
    grads = [swap(2, dup2, dup3), swap(3, ddown2, ddown3)]
    for n in range(0, share, WIDE):
        dup2[:, n : n + WIDE] = dot_tn(x_all(), ghid[:, share + n : share + n + WIDE]).astype(bf16)
    grads[0].start()
    for n in range(0, share, WIDE):
        ddown2[n : n + WIDE, :] = dot_tn(act[:, share + n : share + n + WIDE], g_all()).astype(bf16)
    grads[1].start()
    for n in range(0, share, WIDE):
        dup_ref[:, n : n + WIDE] = dot_tn(x_all(), ghid[:, n : n + WIDE])
        ddown_ref[n : n + WIDE, :] = dot_tn(act[:, n : n + WIDE], g_all())
    grads[0].wait_recv()
    dup_ref[...] += dup3[...].astype(f32)
    grads[1].wait_recv()
    ddown_ref[...] += ddown3[...].astype(f32)
    for cp in weights + grads:
        cp.wait_send()

    for k in range(1, seq):
        e = (s + k) % seq
        remote(back_ref.at[e], back_ref.at[e], disp_sem.at[0], final_recv.at[e], sib).wait_recv()
    keep_home().wait()
    dispatch(0, 1 - y).wait_send()
    own.wait_send()
    hand(z * 2 + 1 - y).wait_send()
    to_home(0, 1 - y).wait_send()

    def settle(k, carry):
        to_far(k).wait_send()

        @pl.when(k > 0)
        def _():
            for j in range(2):
                dispatch(k, j).wait_send()
                to_home(k, j).wait_send()
                hand(there(k, j)).wait_send()
        return carry
    lax.fori_loop(0, Z, settle, 0)


def moe_rows(batch, seq, sent, up, down):
    width, hidden_share = up.shape
    capacity, wide = sent.shape[1:]
    block = seq * capacity
    if tuned(batch, seq):
        Z, block = seq // 2, 4 * capacity
        dma = pltpu.SemaphoreType.DMA
        quarter = [pltpu.VMEM((width, hidden_share), bf16), pltpu.VMEM((hidden_share, width), bf16)]
        out = pl.pallas_call(
            functools.partial(moe_kernel, seq),
            out_shape=[
                like(seq, capacity, wide, dtype=bf16),
                like(2, seq * capacity, wide, dtype=bf16),
                like(width, hidden_share),
                like(hidden_share, width),
            ],
            in_specs=[VM] * 3,
            out_specs=[HBM, HBM] + [VM] * 2,
            scratch_shapes=[
                pltpu.VMEM((Z, block, wide), bf16),
                pltpu.VMEM((Z, block, wide), bf16),
                pltpu.VMEM((Z * block, 2 * hidden_share), bf16),
                pltpu.VMEM((Z * block, 2 * hidden_share), bf16),
                pltpu.VMEM((block, 2 * hidden_share), f32),
                pltpu.VMEM((block, 2 * hidden_share), f32),
                pltpu.VMEM((Z, 2 * capacity, wide), bf16),
                pltpu.VMEM((Z, 2, capacity, wide), bf16),
                *quarter,
                *quarter,
                *quarter,
                dma,
                dma((2 * Z,)),
                dma((seq,)),
                dma((2, seq)),
                dma((Z, 2)),
                dma((Z,)),
                dma((Z,)),
                dma((Z, 2)),
                dma((seq,)),
                dma,
                dma((4,)),
                dma((4,)),
            ],
            compiler_params=pltpu.CompilerParams(
                collective_id=2, has_side_effects=True, vmem_limit_bytes=56 << 20),
            name="experts",
        )(sent, up, down)
        return out[0], out[2], out[3]
    mine = lax.all_to_all(sent, "seq", split_axis=0, concat_axis=0, tiled=True)
    rows = lax.all_gather(mine, "batch", axis=0).reshape(batch * block, wide)
    part, d_up, d_down = pl.pallas_call(
        expert_kernel,
        out_shape=[
            like(batch * block, wide, dtype=bf16),
            like(width, hidden_share),
            like(hidden_share, width),
        ],
        grid=(batch,),
        in_specs=[
            pl.BlockSpec((block, wide), lambda i: (i, 0)),
            pl.BlockSpec((width, hidden_share), lambda i: (0, 0)),
            pl.BlockSpec((hidden_share, width), lambda i: (0, 0)),
        ],
        out_specs=[
            pl.BlockSpec((block, wide), lambda i: (i, 0)),
            pl.BlockSpec((width, hidden_share), lambda i: (0, 0)),
            pl.BlockSpec((hidden_share, width), lambda i: (0, 0)),
        ],
        compiler_params=params(),
        name="experts",
    )(rows, up, down)
    part = part.reshape((batch,) + sent.shape)
    mine = lax.psum_scatter(part, "batch", scatter_dimension=0, tiled=False)
    return lax.all_to_all(mine, "seq", split_axis=0, concat_axis=0, tiled=True), d_up, d_down


class Moves:
    def __init__(self, sems):
        self.sems, self.used, self.named = sems, 0, {}

    def start(self, name, src, dst):
        cp = pltpu.make_async_copy(src, dst, self.sems.at[self.used])
        self.used += 1
        cp.start()
        self.named.setdefault(name, []).append(cp)

    def wait(self, *names):
        for name in names:
            for cp in self.named.pop(name):
                cp.wait()

    def wait_all(self):
        self.wait(*list(self.named))


def forward_kernel(dims, share, low_share, experts, capacity, room, batch, seq,
                   tok_ref, cot_ref, route_ref, slot_ref, state_ref, step_ref, router_in, *refs):
    seqs, rows, inner = dims[:3]
    lines, gains, refs = refs[:5], refs[5:7], refs[7:]
    (win_in, out_in, tok_hbm,
     win_hbm, out_hbm, tail_hbm, halo_hbm, ext_hbm, z_hbm, u_hbm, dt_hbm, y_hbm, gated_hbm, hist_ref,
     proj_ref, dsum_ref, vec_ref, gain_ref, router_ref, hid_ref, moe_ref, gate_ref, rows_ref,
     win, out, tail_all, halo, ext, z, u, dt, y, gated, end, start, xn, hbuf, hcur, sem, sem0,
     tail, vecs, feats, zeros, send_sem, recv_sem, edge_sem, sems) = refs[:48]
    relay_refs = refs[48:]
    moves = Moves(sems)
    gather = Gatherer(batch, seq, (win_in, tail, out_in), (win_hbm, tail_hbm, out_hbm), send_sem, recv_sem)
    WIN, TAIL, OUT = range(3)
    relay = Relay(seq, True, dims[3], dsum_ref, vec_ref, end, start, *relay_refs)
    b, s = gather.me.at()
    has_before, has_after = s > 0, s < seq - 1
    greet(gather.peers() + [(has_before, (b, s - 1)), (has_after, (b, s + 1))])

    gather.give(WIN)
    edges = [
        pltpu.make_async_remote_copy(
            src_ref=tok_hbm.at[i, pl.ds(rows - 8, 8)], dst_ref=halo_hbm.at[pl.ds(8 * i, 8)],
            send_sem=edge_sem.at[0, i], recv_sem=edge_sem.at[1, i], device_id=(b, s + 1), device_id_type=MESH)
        for i in range(seqs)
    ]
    none = pltpu.make_async_copy(zeros, halo_hbm, edge_sem.at[2, 0])
    zeros[...] = jnp.zeros_like(zeros)

    @pl.when(has_after)
    def _():
        for cp in edges:
            cp.start()
    pl.when(jnp.logical_not(has_before))(none.start)
    pack_weights(tail, vecs, feats, state_ref, step_ref, router_in, lines, gains)
    gather.give(TAIL)
    moves.start("own", win_in, gather.part(WIN, gather.own))
    moves.start("own", tail, gather.part(TAIL, gather.own))
    moves.start("own out", out_in, gather.part(OUT, gather.own))
    for h in range(1, gather.Z + 3):
        gather.hop((WIN, TAIL), h)
    gather.give(OUT)
    gather.rest((WIN, TAIL))

    @pl.when(has_before)
    def _():
        for cp in edges:
            cp.wait_recv()
    pl.when(jnp.logical_not(has_before))(none.wait)
    moves.wait("own")
    moves.start("head", halo_hbm, halo)
    moves.start("head", tail_hbm, tail_all)
    for j in range(inner // WIDE):
        for base in (0, inner):
            cols = pl.ds(base + j * WIDE, WIDE)
            moves.start(("win", j), win_hbm.at[:, cols], win.at[:, cols])
    moves.wait("head")

    def weights(j):
        moves.wait(("win", j))
        if j == 4:
            gather.hop((OUT,), 1)

    def projected():
        for name, src, dst in (("ext", ext, ext_hbm), ("z", z, z_hbm), ("u", u, u_hbm), ("dt", dt, dt_hbm)):
            moves.start(name, src, dst)
        gather.hop((OUT,), 2)

    def scanned(i):
        relay.start(i)
        gather.hop((OUT,), 3 + i)

    enter_packed(dims, share, low_share, experts, tok_ref, halo, win, tail_all, ext, z, u, dt, proj_ref, end,
                 dsum_ref, vec_ref, gain_ref, router_ref, xn,
                 hooks=Hooks(weights=weights, projected=projected, scanned=scanned))
    for i in range(relay.count):
        relay.finish(i)
    for h in range(3 + relay.count, gather.Z + 3):
        gather.hop((OUT,), h)

    def half(i):
        if i == 0:
            gather.rest((OUT,))
            moves.wait("own out")
            moves.start("out", out_hbm, out)

    def mixed():
        moves.start("y", y, y_hbm)
        moves.start("gated", gated, gated_hbm)

    leave_kernel(dims, capacity, room, tok_ref, cot_ref, start, dt, u, z, proj_ref, vec_ref, out, gain_ref, router_ref,
                 route_ref, slot_ref, hist_ref, y, hid_ref, gated, moe_ref, gate_ref, rows_ref, hbuf, hcur, sem, sem0,
                 hooks=Hooks(out_proj=lambda: moves.wait("out"), mixed=mixed, half=half))
    relay.settle()
    gather.settle()

    @pl.when(has_after)
    def _():
        for cp in edges:
            cp.wait_send()
    moves.wait_all()


def backward_kernel(dims, share, low_share, experts, capacity, room, batch, seq,
                    ret_ref, cot_ref, hid_ref, moe_ref, gate_ref, vec_ref, gain_ref, router_ref, route_ref, slot_ref,
                    dsum_ref, proj_ref, gated_hbm, out_hbm, z_hbm, y_hbm, u_hbm, dt_hbm, ext_hbm, win_hbm, tail_hbm,
                    tok_hbm, halo_hbm, hist_ref,
                    block_ref, dtok_ref, next_ref, in_out, out_out, tail_out,
                    gated, out, z, y, u, dt, ext, win, tail, tok, halo, gy, gz, ghid, adj, later,
                    dhalo, dsmall, dvec, dnorm, dmoe, drouter, dskip, blank,
                    hbuf, ccol, bcol, gbsum, gcsum, carry, gdt, gu, gproj, gpad, gm, xn, gpre, sem, sems, edge_sem,
                    *more):
    seqs, rows, inner, states, rank, taps = dims
    count, devices = seqs * rows, batch * seq
    relay_refs, more = more[:9], more[9:]
    moves = Moves(sems)
    for name, src, dst in (
        ("gated", gated_hbm, gated), ("out", out_hbm, out), ("z", z_hbm, z), ("y", y_hbm, y), ("u", u_hbm, u),
        ("dt", dt_hbm, dt), ("ext", ext_hbm, ext), ("win", win_hbm, win), ("tail", tail_hbm, tail),
        ("tok", tok_hbm, tok), ("halo", halo_hbm, halo),
    ):
        moves.start(name, src, dst)
    relay = Relay(seq, False, states, dsum_ref, vec_ref, adj, later, *relay_refs)
    reducer = Reducer(batch, seq, *(more[4 * i : 4 * i + 4] for i in range(5)), more[20:])
    OUT, GATE, IN, REST = range(4)
    b, s = reducer.me.at()
    has_before, has_after = s > 0, s < seq - 1
    greet(reducer.peers() + [(has_before, (b, s - 1)), (has_after, (b, s + 1))])
    me = reducer.me

    return_kernel(dims, capacity, room, ret_ref, cot_ref, hid_ref, moe_ref, gate_ref, gated, y, u, z, dt, proj_ref,
                  vec_ref, out, gain_ref, router_ref, route_ref, slot_ref,
                  block_ref, ghid, gy, gz, None, drouter, dskip, dmoe, adj,
                  hooks=Hooks(activations=lambda: moves.wait("gated", "out", "z", "y", "u"),
                              gradients=lambda: moves.wait("dt"), scanned=relay.start))

    def in_grads(a, grads, n, xx):
        half, cut, wide = devices // 2, low_share * devices // 2, 2 * WIDE
        at = pl.ds(pl.multiple_of(xx * cut, 128), cut)
        for c0 in range(0, inner, wide):
            part = dot_tn(xn[0:n, at], grads[:, c0 : c0 + wide]).reshape(half, low_share, wide)
            reducer.items[a][pl.ds(xx * half, half), :, c0 : c0 + wide] = part.astype(bf16)
        reducer.give(a, [(xx, 1 - me.y), (xx, me.y)])

    branch = ghid[...].astype(bf16)
    cut = 8 * share
    for q in range(devices // 8):
        part = dot_tn(gated[:, q * cut : (q + 1) * cut], branch)
        reducer.items[OUT][q * 8 : (q + 1) * 8] = part.astype(bf16).reshape(8, share, part.shape[1])
    reducer.give(OUT, reducer.others)
    relay.finish(0)
    moves.wait("tok")
    x = tok[...].astype(f32)
    xn[0:count] = (x * normalize(x) * gain_ref[0:1]).astype(bf16)
    for xx in (1 - me.x, me.x):
        in_grads(GATE, gz, count, xx)
    for i in range(1, relay.count):
        relay.finish(i)

    def group(i):
        for g in range(4):
            @pl.when(i // reducer.Z == g)
            def _(g=g):
                for a in (OUT, GATE):
                    reducer.step(a, g, i % reducer.Z)

    def late_grads():
        for xx in (1 - me.x, me.x):
            in_grads(IN, gm, count + 8 * seqs, xx)

    back_kernel(dims, tok, halo, ext, hist_ref, later, gy, gz, ghid, u, dt, proj_ref, win, tail, vec_ref, gain_ref,
                dtok_ref, dhalo, None, dsmall, dvec, dnorm,
                hbuf, ccol, bcol, gbsum, gcsum, carry, gdt, gu, gproj, gpad, gm, xn, gpre, sem,
                hooks=Hooks(rest=lambda: moves.wait("ext", "win", "tail", "halo"), group=group),
                in_grads=late_grads)
    edge = reducer.copy(dhalo, next_ref, edge_sem.at[0], edge_sem.at[1], (b, s - 1))
    none = pltpu.make_async_copy(blank, next_ref, edge_sem.at[2])
    blank[...] = jnp.zeros_like(blank)
    pl.when(has_before)(edge.start)
    pl.when(jnp.logical_not(has_after))(none.start)
    pack_tail(reducer.items[REST], low_share, experts, states + taps + 2, dsmall, dvec, dskip, drouter, dnorm, dmoe)
    reducer.give(REST, reducer.others)
    for t in range(reducer.Z + 2):
        for g, k in ((0, t), (1, t), (2, t - 1), (3, t - 2)):
            if 0 <= k < reducer.Z:
                for a in (IN, REST):
                    reducer.step(a, g, k)
                if g == 3:
                    for a, ref in ((OUT, out_out), (GATE, in_out.at[:, inner:]), (IN, in_out.at[:, :inner]),
                                   (REST, tail_out)):
                        reducer.line(a, k, ref)
    relay.settle()
    for a in (OUT, GATE, IN, REST):
        reducer.settle(a)
    pl.when(has_after)(edge.wait_recv)
    pl.when(has_before)(edge.wait_send)
    pl.when(jnp.logical_not(has_after))(none.wait)


def body(
    tokens,
    in_proj,
    conv_weight,
    conv_bias,
    state_proj,
    step_proj,
    step_bias,
    decay_log,
    skip_gain,
    out_proj,
    norm_gain,
    moe_gain,
    router_proj,
    expert_up,
    expert_down,
    routes,
    slot_index,
    cotangent,
):
    batch, seq = lax.axis_size("batch"), lax.axis_size("seq")
    both = ("batch", "seq")
    seqs, rows, width = tokens.shape
    count = seqs * rows
    devices = batch * seq
    taps, share = conv_weight.shape
    inner = share * devices
    states, rank = decay_log.shape[0], step_proj.shape[0]
    low_share = norm_gain.shape[0]
    experts = router_proj.shape[1]
    capacity = max(2, 5 * count // (4 * experts))
    dims = (seqs, rows, inner, states, rank, taps)
    tile = 128

    lines = (decay_log, conv_weight, conv_bias[None], step_bias[None], skip_gain[None])
    used = sum(a.shape[0] for a in lines)
    room = -(-used // 8) * 8
    fast = tuned(batch, seq)
    if not fast:
        features = jnp.concatenate([router_proj, norm_gain[:, None], moe_gain[:, None]], axis=1)
        tail = jnp.concatenate(
            [
                state_proj,
                step_proj.T,
                jnp.pad(jnp.concatenate(lines), ((0, room - used), (0, 0))).T,
                jnp.pad(features, ((0, share - low_share), (0, tile - room - features.shape[1]))),
            ],
            axis=1,
        )
        halo = lax.ppermute(tokens[:, rows - taps + 1 :], "seq", [(i, i + 1) for i in range(seq - 1)])
        halo = jnp.pad(halo, ((0, 0), (8 - taps + 1, 0), (0, 0))).reshape(seqs * 8, width)
        in_full, out_full, tail_full = (
            lax.all_gather(a, both, axis=0, tiled=True) for a in (in_proj, out_proj, tail)
        )
    tok, cot = tokens.reshape(count, width), cotangent.reshape(count, width)
    size = GROUP * states
    total = experts * capacity
    edge_rows = seqs * 8
    dma = pltpu.SemaphoreType.DMA
    acts = like(count, inner)
    ext_s, state_s, dsum_s = like(seqs, rows + 8, inner), like(seqs, states, inner), like(seqs, 1, inner)
    proj_s, low_s, vec_s = like(count, tile), like(count, inner, dtype=bf16), like(room, inner)
    hist_s = like(seqs, (rows + 1) * states, inner, dtype=bf16)
    hid_s, moe_s, gate_s = like(count, width), like(count, width, dtype=bf16), like(count, 1)
    rows_s = like(total, 2 * width, dtype=bf16)
    gain_s, router_s = like(8, width), like(width, tile, dtype=bf16)
    vmem = lambda a: pltpu.VMEM(a.shape, a.dtype)
    normed = pltpu.VMEM((count + edge_rows, width), bf16)
    leave_scratch = [pltpu.VMEM((2, size, inner), bf16), pltpu.VMEM(state_s.shape, bf16), dma((2,)), dma((seqs,))]
    back_scratch = [
        pltpu.VMEM((2, size + states, inner), bf16),
        pltpu.VMEM((GROUP, states, tile), f32),
        pltpu.VMEM((GROUP, states, tile), f32),
        pltpu.VMEM((GROUP, states, tile), f32),
        pltpu.VMEM((GROUP, states, tile), f32),
        pltpu.VMEM((states, inner), f32),
        vmem(acts),
        vmem(acts),
        vmem(proj_s),
        pltpu.VMEM((rows + 16, WIDE), f32),
        pltpu.VMEM((count + edge_rows, inner), bf16),
        normed,
        vmem(low_s),
        dma((2,)),
    ]
    tok_s, halo_s, din_s = like(count, width), like(edge_rows, width), like(width, 2 * inner, dtype=bf16)
    dout_s, dsmall_s = like(inner, width, dtype=bf16), like(inner, tile, dtype=bf16)
    drouter_s, dskip_s, dgain_s = like(width, tile), like(1, inner), like(1, width)
    wide = inner // WIDE
    if fast:
        in_s, out_s = like(width, 2 * inner, dtype=bf16), like(inner, width, dtype=bf16)
        tail_s, halo_b = like(inner, 2 * tile, dtype=bf16), like(edge_rows, width, dtype=bf16)
        (in_full, out_full, tail_full, halo, ext, z, u, dt, y, gated, hist, proj, dsum, vec, gain, router, hid, moe_in,
         gate, sent) = pl.pallas_call(
            partial(forward_kernel, dims, share, low_share, experts, capacity, room, batch, seq),
            out_shape=[in_s, out_s, tail_s, halo_b, ext_s, acts, acts, acts, acts, low_s, hist_s, proj_s, dsum_s, vec_s,
                       gain_s, router_s, hid_s, moe_s, gate_s, rows_s],
            in_specs=[VM] * 16 + [HBM],
            out_specs=[HBM] * 11 + [VM] * 9,
            scratch_shapes=[
                vmem(in_s), vmem(out_s), vmem(tail_s), vmem(halo_b), vmem(ext_s), vmem(acts), vmem(acts), vmem(acts),
                vmem(acts), vmem(low_s), vmem(state_s), vmem(state_s), normed, *leave_scratch,
                pltpu.VMEM((share, 2 * tile), bf16),
                pltpu.VMEM((room, share), f32),
                pltpu.VMEM((8, low_share), f32),
                vmem(halo_b),
                dma((3, n_sends(seq // 2))),
                dma((3, devices)),
                dma((3, seqs)),
                dma((2 * wide + 12,)),
                *relay_scratch(seqs, states, inner),
            ],
            compiler_params=pltpu.CompilerParams(
                collective_id=3, has_side_effects=True, vmem_limit_bytes=58 << 20),
            name="forward",
        )(tok, cot, routes, slot_index, state_proj, step_proj, router_proj.T, *lines, norm_gain[None], moe_gain[None],
          in_proj, out_proj, tokens)
    else:
        vec = tail_full[:, tile : tile + room].T.astype(f32)
        router = tail_full[:, tile:].reshape(devices, share, tile)[:, :low_share].reshape(width, tile)
        gain = router[:, room + experts : room + experts + 2].T.astype(f32)
        ext, z, u, dt, proj, end, dsum = pl.pallas_call(
            partial(enter_kernel, dims),
            out_shape=[ext_s, acts, acts, acts, proj_s, state_s, dsum_s],
            in_specs=[VM] * 6,
            out_specs=[VM] * 7,
            scratch_shapes=[normed],
            compiler_params=params(),
            name="enter",
        )(tok, halo, in_full, tail_full[:, :tile], vec, gain)
        rates = -jnp.exp(vec[:states])
        before = chain_states(seq, True, dsum, rates, end)
        hist, y, hid, gated, moe_in, gate, sent = pl.pallas_call(
            partial(leave_kernel, dims, capacity, room),
            out_shape=[hist_s, acts, hid_s, low_s, moe_s, gate_s, rows_s],
            in_specs=[VM] * 13,
            out_specs=[HBM] + [VM] * 6,
            scratch_shapes=leave_scratch,
            compiler_params=params(),
            name="leave",
        )(tok, cot, before, dt, u, z, proj, vec, out_full, gain, router, routes, slot_index)

    back, d_up, d_down = moe_rows(
        batch, seq, sent.reshape(experts, capacity, 2 * width), expert_up[0], expert_down[0])
    back = back.reshape(total, 2 * width)

    if fast:
        own = [(share, width), (low_share, inner), (low_share, inner), (share, 2 * tile)]
        block_out, d_tok, from_next, s_in, s_out, s_tail = pl.pallas_call(
            partial(backward_kernel, dims, share, low_share, experts, capacity, room, batch, seq),
            out_shape=[moe_s, tok_s, halo_s, like(low_share, 2 * inner), like(*own[0]), like(*own[3])],
            in_specs=[VM] * 12 + [HBM] * 12,
            out_specs=[VM] * 2 + [HBM] + [VM] * 3,
            scratch_shapes=[
                vmem(low_s), vmem(out_s), vmem(acts), vmem(acts), vmem(acts), vmem(acts), vmem(ext_s), vmem(in_s),
                vmem(tail_s), vmem(tok), vmem(halo_b), vmem(acts), vmem(low_s), vmem(tok_s), vmem(state_s),
                vmem(state_s), vmem(halo_s), vmem(dsmall_s), vmem(vec_s), vmem(dgain_s), vmem(dgain_s),
                vmem(drouter_s), vmem(dskip_s), vmem(halo_s), *back_scratch, dma((12,)), dma((3,)),
                *relay_scratch(seqs, states, inner), *reduce_scratch(devices, seq // 2, own),
            ],
            compiler_params=pltpu.CompilerParams(
                collective_id=4, has_side_effects=True, vmem_limit_bytes=62 << 20),
            name="backward",
        )(back, cot, hid, moe_in, gate, vec, gain, router, routes, slot_index, dsum, proj,
          gated, out_full, z, y, u, dt, ext, in_full, tail_full, tok, halo, hist)
    else:
        block_out, ghid, gy, gz, d_out, d_router, d_skip, d_moe, adj = pl.pallas_call(
            partial(return_kernel, dims, capacity, room),
            out_shape=[moe_s, tok_s, acts, low_s, dout_s, drouter_s, dskip_s, dgain_s, state_s],
            in_specs=[VM] * 17,
            out_specs=[VM] * 9,
            compiler_params=params(),
            name="back_experts",
        )(back, cot, hid, moe_in, gate, gated, y, u, z, dt, proj, vec, out_full, gain, router, routes, slot_index)
        later = chain_states(seq, False, dsum, rates, adj)
        d_tok, d_halo, d_in, d_small, d_vec, d_norm = pl.pallas_call(
            partial(back_kernel, dims),
            out_shape=[tok_s, halo_s, din_s, dsmall_s, vec_s, dgain_s],
            in_specs=[VM] * 3 + [HBM] + [VM] * 11,
            out_specs=[VM] * 6,
            scratch_shapes=back_scratch,
            compiler_params=params(),
            name="back_mixer",
        )(tok, halo, ext, hist, later, gy, gz, ghid, u, dt, proj, in_full, tail_full, vec, gain)

    skip_row = states + taps + 2
    if fast:
        shapes = [
            s_in.shape, (taps, share), (1, share), (share, rank + 2 * states), (rank, share), (1, share),
            (states, share), (1, share), s_out.shape, (1, low_share), (1, low_share), (experts, low_share),
        ]
        block_out, d_tok = block_out.reshape(tokens.shape), d_tok.reshape(tokens.shape)
        block_out, d_tok, *sums, d_up, d_down = pl.pallas_call(
            partial(finish_kernel, dims, low_share, experts),
            out_shape=[like(*tokens.shape, dtype=bf16), like(*tokens.shape)] + [like(*a) for a in shapes]
            + [like(*d_up.shape), like(*d_down.shape)],
            in_specs=[VM] * 4 + [HBM] * 4,
            out_specs=[HBM] * 2 + [VM] * 12 + [HBM] * 2,
            scratch_shapes=[vmem(block_out), vmem(d_tok), vmem(d_up), vmem(d_down), dma((20,))],
            compiler_params=params(),
            name="finish",
        )(s_tail, from_next.reshape(seqs, 8, width), s_in, s_out, block_out, d_tok, d_up, d_down)
        for i in (2, 5, 7, 9, 10):
            sums[i] = sums[i][0]
        sums[11] = sums[11].T
        return (block_out, d_tok, *sums, d_up[None], d_down[None])
    d_model = d_router.at[:, room + experts : room + experts + 2].set(jnp.concatenate([d_norm, d_moe]).T)
    d_model = jnp.pad(
        d_model.reshape(devices, low_share, tile)[:, :, room:], ((0, 0), (0, share - low_share), (0, 0))
    ).reshape(inner, tile - room)
    d_vec = d_vec.at[skip_row].set(d_skip[0])
    d_tail = jnp.concatenate([d_small, d_vec.T.astype(bf16), d_model.astype(bf16)], axis=1)
    s_in, s_out, s_tail = (
        lax.psum_scatter(a.astype(f32), both, scatter_dimension=0, tiled=True) for a in (d_in, d_out, d_tail)
    )
    from_next = lax.ppermute(
        d_halo.reshape(seqs, 8, width)[:, 8 - taps + 1 :], "seq", [(i + 1, i) for i in range(seq - 1)]
    )
    d_tok = d_tok.reshape(tokens.shape).at[:, rows - taps + 1 :].add(from_next)
    s_vec = s_tail[:, tile : tile + room].T
    s_model = s_tail[:low_share, tile + room :]
    return (
        block_out.reshape(tokens.shape),
        d_tok,
        s_in,
        s_vec[states : states + taps],
        s_vec[states + taps],
        s_tail[:, : rank + 2 * states],
        s_tail[:, rank + 2 * states : tile].T,
        s_vec[states + taps + 1],
        s_vec[:states],
        s_vec[states + taps + 2],
        s_out,
        s_model[:, experts],
        s_model[:, experts + 1],
        s_model[:, :experts],
        d_up[None],
        d_down[None],
    )


def solution(mesh):
    in_specs = (
        P("batch", "seq", None),
        P(("batch", "seq"), None),
        P(None, ("batch", "seq")),
        P(("batch", "seq")),
        P(("batch", "seq"), None),
        P(None, ("batch", "seq")),
        P(("batch", "seq")),
        P(None, ("batch", "seq")),
        P(("batch", "seq")),
        P(("batch", "seq"), None),
        P(("batch", "seq")),
        P(("batch", "seq")),
        P(("batch", "seq"), None),
        P("seq", None, "batch"),
        P("seq", "batch", None),
        P("batch", "seq"),
        P("batch", "seq"),
        P("batch", "seq", None),
    )
    out_specs = (
        P("batch", "seq", None),
        P("batch", "seq", None),
        P(("batch", "seq"), None),
        P(None, ("batch", "seq")),
        P(("batch", "seq")),
        P(("batch", "seq"), None),
        P(None, ("batch", "seq")),
        P(("batch", "seq")),
        P(None, ("batch", "seq")),
        P(("batch", "seq")),
        P(("batch", "seq"), None),
        P(("batch", "seq")),
        P(("batch", "seq")),
        P(("batch", "seq"), None),
        P("seq", None, "batch"),
        P("seq", "batch", None),
    )
    return jax.shard_map(body, mesh=mesh, in_specs=in_specs, out_specs=out_specs, check_vma=False)
```

```python
from functools import partial
import functools
import math

import jax
import jax.numpy as jnp
from jax import lax
from jax.experimental import pallas as pl
from jax.experimental.pallas import tpu as pltpu
from jax.sharding import PartitionSpec as P

epsilon = 1e-05
MESH = pl.DeviceIdType.MESH
HBM = pl.BlockSpec(memory_space=pl.ANY)
VM = pl.BlockSpec(memory_space=pltpu.VMEM)
bf16, f32 = jnp.bfloat16, jnp.float32


class Place:
    def __init__(self, batch, seq, ydim=2):
        self.batch, self.seq, self.Y = batch, seq, ydim
        self.Z = seq // ydim
        b, s = lax.axis_index("batch"), lax.axis_index("seq")
        self.x, self.c = b // 2, b % 2
        self.z, self.y = s // ydim, s % ydim

    def at(self, x=None, c=None, y=None, z=None):
        pick = lambda v, own: own if v is None else v
        x, c, y, z = pick(x, self.x), pick(c, self.c), pick(y, self.y), pick(z, self.z)
        return (x * 2 + c, z * self.Y + y)

    def index(self, dev):
        return dev[0] * self.seq + dev[1]


def greet(devices):
    barrier = pltpu.get_barrier_semaphore()
    count = 0
    for pred, dev in devices:
        if pred is None:
            pl.semaphore_signal(barrier, inc=1, device_id=dev, device_id_type=MESH)
            count = count + 1
        else:
            @pl.when(pred)
            def _(dev=dev):
                pl.semaphore_signal(barrier, inc=1, device_id=dev, device_id_type=MESH)
            count = count + jnp.where(pred, 1, 0)
    pl.semaphore_wait(barrier, count)


TILE = 128


def spot(rows, at, width):
    return (lanes((rows, width)) == subs((rows, width)) + at).astype(bf16)


class Gatherer:
    def __init__(self, batch, seq, ins, outs, send_sem, recv_sem):
        self.ins, self.outs, self.send_sem, self.recv_sem = ins, outs, send_sem, recv_sem
        self.me = me = Place(batch, seq)
        self.Z, self.z = me.Z, me.z
        self.sib = me.at(c=1 - me.c)
        self.up_ok, self.down_ok = me.z < me.Z - 1, me.z > 0
        self.up, self.down = me.at(z=me.z + 1), me.at(z=me.z - 1)
        self.nx, self.ny = me.at(x=1 - me.x), me.at(y=1 - me.y)
        first = me.c == 0
        pick = lambda a, b: tuple(jnp.where(first, p, q) for p, q in zip(a, b))
        self.second_dev, self.third_dev = pick(self.ny, self.nx), pick(self.nx, self.ny)
        ox, oy = 1 - me.x, 1 - me.y
        self.second_at = (jnp.where(first, me.x, ox), jnp.where(first, oy, me.y))
        self.third_at = (jnp.where(first, ox, me.x), jnp.where(first, me.y, oy))
        self.across_at = (ox, oy)
        self.own = me.index(me.at())
        self.sends = [[] for _ in ins]

    def peers(self):
        return [(None, self.sib), (None, self.nx), (None, self.ny), (self.up_ok, self.up), (self.down_ok, self.down)]

    def part(self, a, index):
        rows = self.ins[a].shape[0]
        return self.outs[a].at[pl.ds(pl.multiple_of(index * rows, 8), rows)]

    def send(self, a, pred, src, index, dev):
        copy = pltpu.make_async_remote_copy(
            src_ref=src, dst_ref=self.part(a, index), send_sem=self.send_sem.at[a, len(self.sends[a])],
            recv_sem=self.recv_sem.at[a, index], device_id=dev, device_id_type=MESH)
        self.sends[a].append((pred, copy))
        if pred is None:
            copy.start()
        else:
            pl.when(pred)(copy.start)

    def give(self, a):
        for pred, dev in self.targets():
            self.send(a, pred, self.ins[a], self.own, dev)

    def targets(self):
        return [(self.up_ok, self.up), (self.down_ok, self.down), (None, self.second_dev), (None, self.third_dev),
                (None, self.sib)]

    def arrive(self, a, pred, index, targets):
        part = self.part(a, index)
        copy = pltpu.make_async_remote_copy(
            src_ref=part, dst_ref=part, send_sem=self.send_sem.at[a, 0], recv_sem=self.recv_sem.at[a, index],
            device_id=self.sib, device_id_type=MESH)
        if pred is None:
            copy.wait_recv()
        else:
            pl.when(pred)(copy.wait_recv)
        for extra, dev in targets:
            p = pred if extra is None else (extra if pred is None else jnp.logical_and(pred, extra))
            self.send(a, p, part, index, dev)

    def offsets(self, k):
        return [(None, 0)] if k == 0 else [(self.z >= k, -k), (self.z + k < self.Z, k)]

    def hop(self, arrays, h):
        me, z = self.me, self.z
        to_second, to_third, to_sib = (None, self.second_dev), (None, self.third_dev), (None, self.sib)
        for k, at, targets in (
            (h, (me.x, me.y), None), (h - 1, self.second_at, [to_third, to_sib]), (h - 2, self.third_at, [to_sib]),
            (h - 3, self.across_at, [to_sib]),
        ):
            if not 0 <= k < self.Z or (targets is None and k == 0):
                continue
            for pred, off in self.offsets(k):
                onward = targets
                if targets is None:
                    onward = [(self.up_ok, self.up) if off < 0 else (self.down_ok, self.down), to_second, to_third, to_sib]
                for a in arrays:
                    self.arrive(a, pred, me.index(me.at(x=at[0], y=at[1], z=z + off)), onward)

    def rest(self, arrays):
        me = self.me
        for h in range(self.Z):
            for xx in (0, 1):
                for yy in (0, 1):
                    for pred, off in self.offsets(h):
                        for a in arrays:
                            self.arrive(a, pred, me.index(me.at(x=xx, y=yy, c=1 - me.c, z=self.z + off)), [])

    def settle(self):
        for sends in self.sends:
            for pred, copy in sends:
                if pred is None:
                    copy.wait_send()
                else:
                    pl.when(pred)(copy.wait_send)


def n_sends(Z):
    return 5 + (Z - 1) * 8 + (2 * Z - 1) * 2 + (2 * Z - 1) * 2


def pack_weights(tail, vecs, feats, state_ref, step_ref, router_ref, lines, gains):
    share, low_share, experts = state_ref.shape[0], router_ref.shape[1], router_ref.shape[0]
    rank, room, wide = step_ref.shape[0], vecs.shape[0], tail.shape[1]
    vecs[...] = jnp.zeros_like(vecs)
    at = 0
    for ref in lines:
        vecs[at : at + ref.shape[0]] = ref[...].astype(f32)
        at += ref.shape[0]
    feats[...] = jnp.zeros_like(feats)
    for i, ref in enumerate(gains):
        feats[i : i + 1] = ref[...].astype(f32)
    by_channel = (
        dot(state_ref[...], spot(state_ref.shape[1], 0, wide))
        + dot_tn(step_ref[...], spot(rank, TILE - rank, wide))
        + dot_tn(vecs[...].astype(bf16), spot(room, TILE, wide))
    )
    by_feature = dot_tn(router_ref[...], spot(experts, TILE + room, wide)) + dot_tn(
        feats[...].astype(bf16), spot(feats.shape[0], TILE + room + experts, wide))
    by_feature = jnp.concatenate([by_feature, jnp.zeros((share - low_share, wide), f32)])
    tail[...] = (by_channel + by_feature).astype(bf16)


class Reducer:
    def __init__(self, batch, seq, items, sib_bufs, far_bufs, near_bufs, line_bufs, sems):
        self.items, self.sib_bufs, self.far_bufs, self.near_bufs, self.line_bufs = (
            items, sib_bufs, far_bufs, near_bufs, line_bufs)
        (self.sib_send, self.sib_recv, self.far_send, self.far_recv, self.near_send, self.near_recv,
         self.line_send, self.line_recv) = sems
        self.me = me = Place(batch, seq)
        self.Z, self.z = me.Z, me.z
        self.sib = me.at(c=1 - me.c)
        self.nx, self.ny = me.at(x=1 - me.x), me.at(y=1 - me.y)
        pick = lambda a, b: tuple(jnp.where(me.c == 0, p, q) for p, q in zip(a, b))
        self.near, self.far = pick(self.ny, self.nx), pick(self.nx, self.ny)
        self.mine, self.others = self.groups(me.c), self.groups(1 - me.c)

    def peers(self):
        column = [(None, self.me.at(z=self.turn(k))) for k in range(self.Z - 1)]
        return [(None, self.sib), (None, self.nx), (None, self.ny)] + column

    def groups(self, c):
        me = self.me
        ox, oy = 1 - me.x, 1 - me.y
        pick = lambda a, b: jnp.where(c == 0, a, b)
        return [(ox, oy), (pick(ox, me.x), pick(me.y, oy)), (pick(me.x, ox), pick(oy, me.y)), (me.x, me.y)]

    def slot(self, xy, zz):
        return (xy[0] * 2 + xy[1]) * self.Z + zz

    def turn(self, k):
        above = self.Z - 1 - self.z
        return jnp.where(k < above, self.Z - 1 - k, jnp.where(k < self.Z - 1, k - above, self.z))

    def item(self, a, c, xy, zz):
        return self.items[a].at[self.me.index((xy[0] * 2 + c, zz * self.me.Y + xy[1]))]

    def copy(self, src, dst, send, recv, dev):
        return pltpu.make_async_remote_copy(
            src_ref=src, dst_ref=dst, send_sem=send, recv_sem=recv, device_id=dev, device_id_type=MESH)

    def to_sib(self, a, xy, k):
        t = self.turn(k)
        s = self.slot(xy, t)
        return self.copy(self.item(a, 1 - self.me.c, xy, t), self.sib_bufs[a].at[s],
                         self.sib_send.at[a, s], self.sib_recv.at[a, s], self.sib)

    def give(self, a, columns):
        for k in range(self.Z):
            for xy in columns:
                self.to_sib(a, xy, k).start()

    def to_far(self, a, g, k):
        t = self.turn(k)
        fs = g * self.Z + t
        return self.copy(self.item(a, self.me.c, self.mine[g], t), self.far_bufs[a].at[fs],
                         self.far_send.at[a, fs], self.far_recv.at[a, fs], self.far)

    def to_near(self, a, k):
        t = self.turn(k)
        return self.copy(self.item(a, self.me.c, self.mine[2], t), self.near_bufs[a].at[t],
                         self.near_send.at[a, t], self.near_recv.at[a, t], self.near)

    def step(self, a, g, k):
        t = self.turn(k)
        s = self.slot(self.mine[g], t)
        item = self.item(a, self.me.c, self.mine[g], t)
        take = lambda ref, recv: self.copy(ref, ref, self.sib_send.at[a, 0], recv, self.sib).wait_recv()
        parts = [self.sib_bufs[a].at[s]]
        take(parts[0], self.sib_recv.at[a, s])
        if g >= 2:
            fs = (g - 2) * self.Z + t
            parts.append(self.far_bufs[a].at[fs])
            take(parts[-1], self.far_recv.at[a, fs])
        if g == 3:
            parts.append(self.near_bufs[a].at[t])
            take(parts[-1], self.near_recv.at[a, t])
        total = item[...].astype(f32)
        for part in parts:
            total = total + part[...].astype(f32)
        item[...] = total.astype(bf16)
        if g < 2:
            self.to_far(a, g, k).start()
        elif g == 2:
            self.to_near(a, k).start()
        else:
            pl.when(k < self.Z - 1)(lambda: self.onward(a, k).start())

    def onward(self, a, k):
        t = self.turn(k)
        return self.copy(self.item(a, self.me.c, self.mine[3], t), self.line_bufs[a].at[self.z],
                         self.line_send.at[a, k], self.line_recv.at[a, self.z], self.me.at(z=t))

    def result(self, a, out_ref):
        total = self.item(a, self.me.c, self.mine[3], self.z)[...].astype(f32)
        for k in range(self.Z - 1):
            t = self.turn(k)
            ref = self.line_bufs[a].at[t]
            self.copy(ref, ref, self.sib_send.at[a, 0], self.line_recv.at[a, t], self.sib).wait_recv()
            total = total + ref[...].astype(f32)
        out_ref[...] = total

    def settle(self, a):
        def one(k, carry):
            for xy in self.others:
                self.to_sib(a, xy, k).wait_send()
            for g in range(2):
                self.to_far(a, g, k).wait_send()
            self.to_near(a, k).wait_send()

            @pl.when(k < self.Z - 1)
            def _():
                self.onward(a, k).wait_send()
            return carry
        lax.fori_loop(0, self.Z, one, 0)


def reduce_scratch(count, Z, shapes):
    half, n, dma = count // 2, len(shapes), pltpu.SemaphoreType.DMA
    bufs = [pltpu.VMEM(lead + s, bf16) for lead in ((count,), (half,), (2 * Z,), (Z,), (Z,)) for s in shapes]
    return bufs + [dma((n, half)), dma((n, half)), dma((n, 2 * Z)), dma((n, 2 * Z)), dma((n, Z)), dma((n, Z)),
                   dma((n, Z)), dma((n, Z))]


def pack_tail(tail, low_share, experts, skip_row, dsmall_ref, dvec_ref, dskip_ref, drouter_ref, dnorm_ref, dmoe_ref):
    blocks, share = tail.shape[:2]
    room, width = dvec_ref.shape[0], drouter_ref.shape[0]
    vec = jnp.where(subs(dvec_ref.shape) == skip_row, dskip_ref[...], dvec_ref[...])
    line = subs((8, width))
    gains = jnp.where(line == 0, dnorm_ref[...], jnp.where(line == 1, dmoe_ref[...], 0.0))
    model = drouter_ref[...] + dot_tn(gains.astype(bf16), spot(8, room + experts, TILE))
    model = jnp.concatenate(
        [model.reshape(blocks, low_share, TILE), jnp.zeros((blocks, share - low_share, TILE), f32)], axis=1)
    right = dot_tn(vec.astype(bf16), spot(room, 0, TILE)).reshape(blocks, share, TILE) + model
    tail[:, :, 0:TILE] = dsmall_ref[...].reshape(blocks, share, TILE)
    tail[:, :, TILE:] = right.astype(bf16)


def finish_kernel(dims, low_share, experts, tail_ref, halo_ref, in_ref, out_ref, block_hbm, tok_hbm, up_hbm, down_hbm,
                  block_out, tok_out, din, dconv, dbias, dstate, dstep, dstep_bias, ddecay, dskip, dout, dnorm, dmoe,
                  drouter, dup, ddown, block, tok, up, down, sems):
    seqs, rows, inner, states, rank, taps = dims
    moves = Moves(sems)
    routes = []
    for i in range(4):
        for src, at, dst in ((up_hbm, up, dup), (down_hbm, down, ddown)):
            n = src.shape[0] // 4
            piece = pl.ds(i * n, n)
            routes.append((len(routes), src.at[piece], at.at[piece], dst.at[piece]))
    routes.append(("tok", tok_hbm, tok, tok_out))
    routes.append(("block", block_hbm, block, block_out))
    for name, src, at, _ in routes:
        moves.start(name, src, at)
    din[...] = in_ref[...]
    dout[...] = out_ref[...]
    tail = tail_ref[...]
    wide = tail.shape[1]
    eye = (lanes((wide, wide)) == subs((wide, wide))).astype(bf16)
    high = tail.astype(bf16)
    turned = dot_nt(eye, high) + dot_nt(eye, (tail - high.astype(f32)).astype(bf16))
    dstate[...] = tail[:, : rank + 2 * states]
    dstep[...] = turned[TILE - rank : TILE]
    ddecay[...] = turned[TILE : TILE + states]
    dconv[...] = turned[TILE + states : TILE + states + taps]
    at = TILE + states + taps
    dbias[...] = turned[at : at + 1]
    dstep_bias[...] = turned[at + 1 : at + 2]
    dskip[...] = turned[at + 2 : at + 3]
    at = TILE + -(-(states + taps + 3) // 8) * 8
    drouter[...] = turned[at : at + experts, :low_share]
    at += experts
    dnorm[...] = turned[at : at + 1, :low_share]
    dmoe[...] = turned[at + 1 : at + 2, :low_share]
    for name, _, at, dst in routes:
        moves.wait(name)
        if name == "tok":
            tok[:, rows - 8 :] = tok[:, rows - 8 :] + halo_ref[...]
        moves.start("out", at, dst)
    moves.wait_all()


def tuned(batch, seq):
    return batch == 4 and seq == 8


def chain_kernel(seq, forward, dsum_ref, rates_ref, end_ref, out_ref, held, outgoing, send_sem, recv_sem):
    s = lax.axis_index("seq")
    b = lax.axis_index("batch")
    step = 1 if forward else -1
    has_before = s > 0 if forward else s < seq - 1
    has_after = s < seq - 1 if forward else s > 0
    before, after = (b, s - step), (b, s + step)
    barrier = pltpu.get_barrier_semaphore()
    for pred, dev in ((has_before, before), (has_after, after)):
        @pl.when(pred)
        def _(dev=dev):
            pl.semaphore_signal(barrier, inc=1, device_id=dev, device_id_type=MESH)
    pl.semaphore_wait(barrier, jnp.where(has_before, 1, 0) + jnp.where(has_after, 1, 0))
    count = end_ref.shape[0]

    def copy(i):
        return pltpu.make_async_remote_copy(
            src_ref=outgoing.at[i], dst_ref=held.at[i], send_sem=send_sem.at[i],
            recv_sem=recv_sem.at[i], device_id=after, device_id_type=MESH)

    for i in range(count):
        @pl.when(has_before)
        def _(i=i):
            copy(i).wait_recv()
            out_ref[i] = held[i].astype(jnp.float32)
            decay = jnp.exp(rates_ref[...] * dsum_ref[i])
            outgoing[i] = (end_ref[i] + decay * out_ref[i]).astype(jnp.bfloat16)

        @pl.when(jnp.logical_not(has_before))
        def _(i=i):
            out_ref[i] = jnp.zeros_like(out_ref[i])
            outgoing[i] = end_ref[i].astype(jnp.bfloat16)

        @pl.when(has_after)
        def _(i=i):
            copy(i).start()
    for i in range(count):
        @pl.when(has_after)
        def _(i=i):
            copy(i).wait_send()


def chain_states(seq, forward, dsum, rates, end):
    vm = pl.BlockSpec(memory_space=pltpu.VMEM)
    return pl.pallas_call(
        functools.partial(chain_kernel, seq, forward),
        out_shape=jax.ShapeDtypeStruct(end.shape, jnp.float32),
        in_specs=[vm] * 3,
        out_specs=vm,
        scratch_shapes=[
            pltpu.VMEM(end.shape, jnp.bfloat16),
            pltpu.VMEM(end.shape, jnp.bfloat16),
            pltpu.SemaphoreType.DMA((end.shape[0],)),
            pltpu.SemaphoreType.DMA((end.shape[0],)),
        ],
        compiler_params=pltpu.CompilerParams(
            collective_id=5 if forward else 6, has_side_effects=True),
        name="chain_forward" if forward else "chain_backward",
    )(dsum, rates, end)


class Relay:
    def __init__(self, seq, forward, states, dsum_ref, vec_ref, end_ref, out_ref, mine, theirs, their_sum, held,
                 outgoing, pair_send, pair_recv, line_send, line_recv):
        me = Place(4, seq)
        y, z, last = me.y, me.z, me.Z - 1
        step = 1 if forward else -1
        self.first = y == (0 if forward else 1)
        self.has_before = z > 0 if forward else z < last
        self.has_after = z < last if forward else z > 0
        self.pair, self.before, self.after = me.at(y=1 - y), me.at(z=z - step), me.at(z=z + step)
        self.states, self.vec_ref, self.end_ref, self.out_ref = states, vec_ref, end_ref, out_ref
        self.mine, self.theirs, self.dsum_ref, self.their_sum = mine, theirs, dsum_ref, their_sum
        self.held, self.outgoing = held, outgoing
        self.pair_send, self.pair_recv, self.line_send, self.line_recv = pair_send, pair_recv, line_send, line_recv
        self.count = end_ref.shape[0]

    def peers(self):
        return [(None, self.pair), (self.has_before, self.before), (self.has_after, self.after)]

    def swaps(self, i):
        both = ((self.mine.at[i], self.theirs.at[i]), (self.dsum_ref.at[i], self.their_sum.at[i]))
        return [
            pltpu.make_async_remote_copy(
                src_ref=src, dst_ref=dst, send_sem=self.pair_send.at[i, k], recv_sem=self.pair_recv.at[i, k],
                device_id=self.pair, device_id_type=MESH)
            for k, (src, dst) in enumerate(both)
        ]

    def onward(self, i):
        return pltpu.make_async_remote_copy(
            src_ref=self.outgoing.at[i], dst_ref=self.held.at[i], send_sem=self.line_send.at[i],
            recv_sem=self.line_recv.at[i], device_id=self.after, device_id_type=MESH)

    def start(self, i):
        self.mine[i] = self.end_ref[i].astype(bf16)
        for cp in self.swaps(i):
            cp.start()

    def finish(self, i):
        rates = -jnp.exp(self.vec_ref[0 : self.states])
        for cp in self.swaps(i):
            cp.wait_recv()
        pick = lambda a, b: (jnp.where(self.first, a, b), jnp.where(self.first, b, a))
        early, late = pick(self.end_ref[i], self.theirs[i].astype(f32))
        early_sum, late_sum = pick(self.dsum_ref[i], self.their_sum[i])
        both = late + jnp.exp(rates * late_sum) * early

        @pl.when(self.has_before)
        def _():
            self.onward(i).wait_recv()
            arrived = self.held[i].astype(f32)
            self.outgoing[i] = (both + jnp.exp(rates * (early_sum + late_sum)) * arrived).astype(bf16)

        @pl.when(jnp.logical_not(self.has_before))
        def _():
            self.outgoing[i] = both.astype(bf16)

        @pl.when(self.has_after)
        def _():
            self.onward(i).start()

        @pl.when(self.has_before)
        def _():
            arrived = self.held[i].astype(f32)
            self.out_ref[i] = jnp.where(self.first, arrived, early + jnp.exp(rates * early_sum) * arrived)

        @pl.when(jnp.logical_not(self.has_before))
        def _():
            self.out_ref[i] = jnp.where(self.first, jnp.zeros_like(early), early)

    def settle(self):
        for i in range(self.count):
            for cp in self.swaps(i):
                cp.wait_send()
            pl.when(self.has_after)(self.onward(i).wait_send)


def relay_scratch(seqs, states, inner):
    n, state = seqs, (seqs, states, inner)
    dma = pltpu.SemaphoreType.DMA
    return [
        pltpu.VMEM(state, bf16),
        pltpu.VMEM(state, bf16),
        pltpu.VMEM((seqs, 1, inner), f32),
        pltpu.VMEM(state, bf16),
        pltpu.VMEM(state, bf16),
        dma((n, 2)),
        dma((n, 2)),
        dma((n,)),
        dma((n,)),
    ]


def dot(a, b):
    return jnp.dot(a, b, preferred_element_type=jnp.float32)


def dot_nt(a, b):
    return lax.dot_general(a, b, (((1,), (1,)), ((), ())), preferred_element_type=jnp.float32)


def dot_tn(a, b):
    return lax.dot_general(a, b, (((0,), (0,)), ((), ())), preferred_element_type=jnp.float32)


def sigmoid(v):
    return 1.0 / (1.0 + jnp.exp(-v))


def lanes(shape):
    return lax.broadcasted_iota(jnp.int32, shape, 1)


def subs(shape):
    return lax.broadcasted_iota(jnp.int32, shape, 0)


def column(row, base, states):
    shape = (states, row.shape[1])
    only = jnp.where(lanes(shape) == subs(shape) + base, jnp.broadcast_to(row, shape), 0.0)
    return jnp.broadcast_to(jnp.sum(only, axis=1, keepdims=True), shape)


def row_sums(parts):
    row = subs(parts[0].shape)
    four, two, one = row < 4, (row // 2) % 2 == 0, row % 2 == 0
    turn = lambda v, by: pltpu.roll(v, by, axis=0)
    a = [
        jnp.where(four, parts[j], parts[j + 4]) + turn(jnp.where(four, parts[j + 4], parts[j]), 4)
        for j in range(4)
    ]
    b = [jnp.where(two, a[j] + turn(a[j], 6), a[j + 2] + turn(a[j + 2], 2)) for j in range(2)]
    return jnp.where(one, b[0] + turn(b[0], 7), b[1] + turn(b[1], 1))


def fold(v):
    return sum(v[i : i + 8] for i in range(8, v.shape[0], 8)) + v[:8]


WIDE = 256
GROUP = 16
LOG2E = math.log2(math.e)


def conv_sum(ext_ref, s, cols, vec_ref, states, taps, rows):
    first = ext_ref.shape[1] - rows - taps + 1
    total = vec_ref[states + taps : states + taps + 1, cols]
    for k in range(taps):
        total = total + vec_ref[states + k : states + k + 1, cols] * ext_ref[s, first + k : first + k + rows, cols]
    return total


def normalize(x):
    return lax.rsqrt(jnp.mean(x * x, axis=-1, keepdims=True) + epsilon)


class Quiet:
    def __getattr__(self, name):
        return lambda *args: None


QUIET = Quiet()


class Hooks(Quiet):
    def __init__(self, **steps):
        self.__dict__.update(steps)


def unpack(tail_ref, share, low_share, room, experts, vec_ref, gain_ref, router_ref):
    right = tail_ref[:, TILE : 2 * TILE]
    vec_ref[...] = dot_nt(spot(room, 0, TILE), right)
    blocks = right.shape[0] // share
    model = right.astype(f32).reshape(blocks, share, TILE)[:, :low_share].reshape(blocks * low_share, TILE).astype(bf16)
    router_ref[...] = model
    gain_ref[...] = dot_nt(spot(gain_ref.shape[0], room + experts, TILE), model)


def enter_packed(dims, share, low_share, experts, tok_ref, halo_ref, win_ref, tail_ref,
                 ext_ref, z_ref, u_ref, dt_ref, proj_ref, end_ref, dsum_ref, vec_ref, gain_ref, router_ref, xn,
                 hooks=QUIET):
    unpack(tail_ref, share, low_share, vec_ref.shape[0], experts, vec_ref, gain_ref, router_ref)
    enter_kernel(dims, tok_ref, halo_ref, win_ref, tail_ref.at[:, 0:TILE], vec_ref, gain_ref,
                 ext_ref, z_ref, u_ref, dt_ref, proj_ref, end_ref, dsum_ref, xn, hooks)


def as_column(ref):
    seqs, rows = ref.shape
    diagonal = lanes((rows, rows)) == subs((rows, rows))
    spread = [
        jnp.where(diagonal, jnp.broadcast_to(ref[s : s + 1].astype(f32), (rows, rows)), 0.0) for s in range(seqs)
    ]
    return jnp.concatenate([jnp.sum(v, axis=1, keepdims=True) for v in spread]).astype(jnp.int32)


def enter_kernel(dims, tok_ref, halo_ref, win_ref, small_ref, vec_ref, gain_ref,
                 ext_ref, z_ref, u_ref, dt_ref, proj_ref, end_ref, dsum_ref, xn, hooks=QUIET):
    seqs, rows, inner, states, rank, taps = dims
    count = seqs * rows
    for ref, at in ((tok_ref, 0), (halo_ref, count)):
        x = ref[...].astype(jnp.float32)
        xn[at : at + x.shape[0]] = (x * normalize(x) * gain_ref[0:1]).astype(jnp.bfloat16)
    proj = jnp.zeros((count, small_ref.shape[1]), jnp.float32)
    for j in range(inner // WIDE):
        cols = slice(j * WIDE, (j + 1) * WIDE)
        hooks.weights(j)
        part = dot(xn[...], win_ref[:, cols])
        z_ref[:, cols] = dot(xn[:count], win_ref[:, inner + j * WIDE : inner + (j + 1) * WIDE])
        for s in range(seqs):
            ext_ref[s, 0:8, cols] = part[count + 8 * s : count + 8 * s + 8]
            ext_ref[s, 8:, cols] = part[s * rows : (s + 1) * rows]
            pre = conv_sum(ext_ref, s, cols, vec_ref, states, taps, rows)
            u_ref[s * rows : (s + 1) * rows, cols] = pre * sigmoid(pre)
        proj = proj + dot(u_ref[:, cols].astype(jnp.bfloat16), small_ref[cols, :])
    proj_ref[...] = proj
    low = rank_lanes(proj, rank, states)
    for j in range(inner // WIDE):
        cols = slice(j * WIDE, (j + 1) * WIDE)
        pre = dot_nt(low, small_ref[cols, :]) + vec_ref[states + taps + 1 : states + taps + 2, cols]
        dt = jnp.maximum(pre, 0.0) + jnp.log1p(jnp.exp(-jnp.abs(pre)))
        dt_ref[:, cols] = dt
        for s in range(seqs):
            dsum_ref[s, 0:1, cols] = jnp.sum(dt[s * rows : (s + 1) * rows], axis=0, keepdims=True)
    hooks.projected()
    a2 = -jnp.exp(vec_ref[0:states]) * LOG2E
    blocks = inner // 128
    for s in range(seqs):
        def eight(i, hs):
            hs = list(hs)
            at = pl.multiple_of(s * rows + i * 8, 8)
            small = proj_ref[pl.ds(at, 8), :]
            bs = [column(small[j : j + 1], rank, states) for j in range(8)]
            for k in range(blocks):
                sl = slice(k * 128, (k + 1) * 128)
                d8 = dt_ref[pl.ds(at, 8), sl]
                w8 = d8 * u_ref[pl.ds(at, 8), sl]
                for j in range(8):
                    hs[k] = jnp.exp2(d8[j : j + 1] * a2[:, sl]) * hs[k] + bs[j] * w8[j : j + 1]
            return tuple(hs)
        zero = jnp.zeros((states, 128), jnp.float32)
        hs = lax.fori_loop(0, rows // 8, eight, (zero,) * blocks)
        for k in range(blocks):
            end_ref[s, :, k * 128 : (k + 1) * 128] = hs[k]
        hooks.scanned(s)


def rank_lanes(proj, rank, states):
    at = rank + 2 * states
    moved = pltpu.roll(proj, at, axis=1)
    return jnp.where(lanes(proj.shape) >= at, moved, 0.0).astype(jnp.bfloat16)


def leave_kernel(dims, capacity, room, tok_ref, cot_ref, h0_ref, dt_ref, u_ref, z_ref, proj_ref, vec_ref, out_ref,
                 gain_ref, router_ref, route_ref, slot_ref,
                 hist_ref, y_ref, hid_ref, gated_ref, moe_ref, gate_ref, rows_ref,
                 hbuf, hcur, sem, sem0, hooks=QUIET):
    seqs, rows, inner, states, rank, taps = dims
    count = seqs * rows
    a2 = -jnp.exp(vec_ref[0:states]) * LOG2E
    blocks = inner // 128
    groups = rows // GROUP
    size = GROUP * states
    firsts = []
    for s in range(seqs):
        hcur[s] = h0_ref[s].astype(jnp.bfloat16)
        cp = pltpu.make_async_copy(hcur.at[s], hist_ref.at[s, pl.ds(0, states)], sem0.at[s])
        cp.start()
        firsts.append(cp)

    def out_copy(s, g, slot):
        at = pl.multiple_of(states + g * size, states)
        return pltpu.make_async_copy(hbuf.at[slot], hist_ref.at[s, pl.ds(at, size)], sem.at[slot])

    for s in range(seqs):
        def group(g, hs):
            hs = list(hs)
            slot = g % 2

            @pl.when(g >= 2)
            def _():
                out_copy(s, g - 2, slot).wait()
            for half in range(GROUP // 8):
                at = pl.multiple_of(s * rows + g * GROUP + half * 8, 8)
                small = proj_ref[pl.ds(at, 8), :]
                bs = [column(small[j : j + 1], rank, states) for j in range(8)]
                cs = [column(small[j : j + 1], rank + states, states) for j in range(8)]
                for k in range(blocks):
                    sl = slice(k * 128, (k + 1) * 128)
                    d8 = dt_ref[pl.ds(at, 8), sl]
                    w8 = d8 * u_ref[pl.ds(at, 8), sl]
                    parts = []
                    for j in range(8):
                        t = half * 8 + j
                        hs[k] = jnp.exp2(d8[j : j + 1] * a2[:, sl]) * hs[k] + bs[j] * w8[j : j + 1]
                        hbuf[slot, t * states : (t + 1) * states, sl] = hs[k].astype(jnp.bfloat16)
                        parts.append(fold(cs[j] * hs[k]))
                    y_ref[pl.ds(at, 8), sl] = row_sums(parts)
            out_copy(s, g, slot).start()
            return tuple(hs)
        hs = tuple(h0_ref[s, :, k * 128 : (k + 1) * 128] for k in range(blocks))
        lax.fori_loop(0, groups, group, hs)
        hooks.half(s)
        for g in (groups - 2, groups - 1):
            out_copy(s, g, g % 2).wait()
    for cp in firsts:
        cp.wait()
    hooks.out_proj()
    hid = tok_ref[...].astype(jnp.float32)
    for j in range(inner // WIDE):
        cols = slice(j * WIDE, (j + 1) * WIDE)
        y = y_ref[:, cols] + vec_ref[states + taps + 2 : states + taps + 3, cols] * u_ref[:, cols]
        y_ref[:, cols] = y
        z = z_ref[:, cols]
        gated = (y * (z * sigmoid(z))).astype(jnp.bfloat16)
        gated_ref[:, cols] = gated
        hid = hid + dot(gated, out_ref[cols, :])
    hooks.mixed()
    hid_ref[...] = hid
    moe_in = (hid * normalize(hid) * gain_ref[1:2]).astype(jnp.bfloat16)
    moe_ref[...] = moe_in
    logits = dot(moe_in, router_ref[...])
    route, slot = as_column(route_ref), as_column(slot_ref)
    chosen = lanes(logits.shape) == route + room
    gate = sigmoid(jnp.sum(jnp.where(chosen, logits, 0.0), axis=1, keepdims=True))
    gate_ref[...] = gate
    kept = (slot < capacity).astype(jnp.float32)
    grad_rows = (cot_ref[...].astype(jnp.float32) * (gate * kept)).astype(jnp.bfloat16)
    total = rows_ref.shape[0]
    place = jnp.where(slot_ref[...] < capacity, route_ref[...] * capacity + slot_ref[...], -1)
    place = jnp.concatenate([place[s : s + 1] for s in range(seqs)], axis=1)
    pick = (subs((total, count)) == place).astype(jnp.bfloat16)
    width = moe_in.shape[1]
    rows_ref[:, :width] = dot(pick, moe_in).astype(jnp.bfloat16)
    rows_ref[:, width:] = dot(pick, grad_rows).astype(jnp.bfloat16)


def erf(x):
    x = jnp.clip(x, -4.0, 4.0)
    x2 = x * x
    top = (-2.72614225801306e-10, 2.77068142495902e-08, -2.10102402082508e-06, -5.69250639462346e-05,
           -7.34990630326855e-04, -2.95459980854025e-03, -1.60960333262415e-02)
    low = (-1.45660718464996e-05, -2.13374055278905e-04, -1.68282697438203e-03, -7.37332916720468e-03,
           -1.42647390514189e-02)
    p = jnp.full_like(x2, top[0])
    for c in top[1:]:
        p = p * x2 + c
    q = jnp.full_like(x2, low[0])
    for c in low[1:]:
        q = q * x2 + c
    return x * p / q


def expert_kernel(rows_ref, up_ref, down_ref, part_ref, dup_ref, ddown_ref):
    width = up_ref.shape[0]
    x, g = rows_ref[:, :width], rows_ref[:, width:]
    hidden = dot(x, up_ref[...])
    half = 0.5 * (1.0 + erf(hidden * math.sqrt(0.5)))
    act = (hidden * half).astype(jnp.bfloat16)
    slope = half + hidden * (jnp.exp(-0.5 * hidden * hidden) * (1.0 / math.sqrt(2.0 * math.pi)))
    part_ref[:, :width] = dot(act, down_ref[...]).astype(jnp.bfloat16)
    grad_hidden = (dot_nt(g, down_ref[...]) * slope).astype(jnp.bfloat16)
    part_ref[:, width:] = dot_nt(grad_hidden, up_ref[...]).astype(jnp.bfloat16)
    ddown, dup = dot_tn(act, g), dot_tn(x, grad_hidden)

    @pl.when(pl.program_id(0) == 0)
    def _():
        dup_ref[...] = dup
        ddown_ref[...] = ddown

    @pl.when(pl.program_id(0) > 0)
    def _():
        dup_ref[...] += dup
        ddown_ref[...] += ddown


def return_kernel(dims, capacity, room, ret_ref, cot_ref, hid_ref, moe_ref, gate_ref, gated_ref, y_ref, u_ref, z_ref, dt_ref,
                  proj_ref, vec_ref, out_ref, gain_ref, router_ref, route_ref, slot_ref,
                  block_ref, ghid_ref, gy_ref, gz_ref, dout_ref, drouter_ref, dskip_ref, dgain_ref, adj_ref,
                  hooks=QUIET):
    seqs, rows, inner, states, rank, taps = dims
    count = seqs * rows
    total, width = ret_ref.shape[0], hid_ref.shape[1]
    route, slot = as_column(route_ref), as_column(slot_ref)
    place = jnp.where(slot < capacity, route * capacity + slot, -1)
    pick = (lanes((count, total)) == place).astype(jnp.bfloat16)
    result = dot(pick, ret_ref[:, :width])
    hid, gate = hid_ref[...], gate_ref[...]
    block_ref[...] = (hid + gate * result).astype(jnp.bfloat16)
    cot = cot_ref[...].astype(jnp.float32)
    grad_gate = jnp.sum(cot * result, axis=1, keepdims=True)
    wide = (count, router_ref.shape[1])
    grad_logits = jnp.where(lanes(wide) == route + room, grad_gate * gate * (1.0 - gate), 0.0).astype(jnp.bfloat16)
    grad_in = dot(pick, ret_ref[:, width:]) + dot_nt(grad_logits, router_ref[...])
    drouter_ref[...] = dot_tn(moe_ref[...], grad_logits)
    r2 = normalize(hid)
    dgain_ref[...] = jnp.sum(grad_in * (hid * r2), axis=0, keepdims=True)
    scaled = grad_in * gain_ref[1:2]
    grad_hid = cot + r2 * scaled - hid * (r2 * r2 * r2) * jnp.mean(scaled * hid, axis=1, keepdims=True)
    ghid_ref[...] = grad_hid
    branch = grad_hid.astype(jnp.bfloat16)
    hooks.activations()
    for j in range(inner // WIDE):
        cols = slice(j * WIDE, (j + 1) * WIDE)
        if dout_ref is not None:
            dout_ref[cols, :] = dot_tn(gated_ref[:, cols], branch).astype(jnp.bfloat16)
        grad = dot_nt(branch, out_ref[cols, :])
        z = z_ref[:, cols]
        sig = sigmoid(z)
        gy = grad * (z * sig)
        gy_ref[:, cols] = gy
        gz_ref[:, cols] = (grad * y_ref[:, cols] * (sig + z * sig * (1.0 - sig))).astype(jnp.bfloat16)
        dskip_ref[:, cols] = jnp.sum(gy * u_ref[:, cols], axis=0, keepdims=True)
    hooks.gradients()
    a2 = -jnp.exp(vec_ref[0:states]) * LOG2E
    blocks = inner // 128
    for s in range(seqs):
        def eight(i, ms):
            ms = list(ms)
            at = pl.multiple_of((s + 1) * rows - 8 - i * 8, 8)
            small = proj_ref[pl.ds(at, 8), :]
            cs = [column(small[j : j + 1], rank + states, states) for j in range(8)]
            for k in range(blocks):
                sl = slice(k * 128, (k + 1) * 128)
                d8, g8 = dt_ref[pl.ds(at, 8), sl], gy_ref[pl.ds(at, 8), sl]
                for j in reversed(range(8)):
                    ms[k] = jnp.exp2(d8[j : j + 1] * a2[:, sl]) * (ms[k] + cs[j] * g8[j : j + 1])
            return tuple(ms)
        zero = jnp.zeros((states, 128), jnp.float32)
        ms = lax.fori_loop(0, rows // 8, eight, (zero,) * blocks)
        for k in range(blocks):
            adj_ref[s, :, k * 128 : (k + 1) * 128] = ms[k]
        hooks.scanned(s)


def back_kernel(dims, tok_ref, halo_ref, ext_ref, hist_ref, later_ref, gy_ref, gz_ref, ghid_ref, u_ref, dt_ref,
                proj_ref, win_ref, small_ref, vec_ref, gain_ref,
                dtok_ref, dhalo_ref, din_ref, dsmall_ref, dvec_ref, dgain_ref,
                hbuf, ccol, bcol, gbsum, gcsum, adj, gdt, gu, gproj, gpad, gm, xn, gpre, sem, hooks=QUIET, in_grads=None):
    small_ref = small_ref.at[:, 0:TILE]
    seqs, rows, inner, states, rank, taps = dims
    count = seqs * rows
    groups = rows // GROUP
    size = GROUP * states
    steps = seqs * groups

    def fetch(i, slot):
        s, g = i // groups, groups - 1 - i % groups
        at = pl.multiple_of(g * size, size)
        return pltpu.make_async_copy(hist_ref.at[s, pl.ds(at, size + states)], hbuf.at[slot], sem.at[slot])

    fetch(0, 0).start()
    dvec_ref[...] = jnp.zeros_like(dvec_ref)
    strip = 512

    def group(i, carry):
        slot = i % 2
        s, g = i // groups, groups - 1 - i % groups

        @pl.when(i + 1 < steps)
        def _():
            fetch(i + 1, 1 - slot).start()

        @pl.when(g == groups - 1)
        def _():
            adj[...] = later_ref[s]
        at = pl.multiple_of(s * rows + g * GROUP, GROUP)
        small = proj_ref[pl.ds(at, GROUP), :]
        for t in range(GROUP):
            ccol[t] = column(small[t : t + 1], rank + states, states)
            bcol[t] = column(small[t : t + 1], rank, states)
            gbsum[t] = jnp.zeros((states, 128), f32)
            gcsum[t] = jnp.zeros((states, 128), f32)
        fetch(i, slot).wait()
        hooks.group(i)
        for c0 in range(0, inner, strip):
            sls = [slice(c0 + k, c0 + k + 128) for k in range(0, strip, 128)]
            scaled = [-jnp.exp(vec_ref[0:states, sl]) * LOG2E for sl in sls]
            m = [adj[:, sl] for sl in sls]
            dd = [dvec_ref[0:states, sl] for sl in sls]
            now = [hbuf[slot, GROUP * states : (GROUP + 1) * states, sl].astype(f32) for sl in sls]
            for half in reversed(range(GROUP // 8)):
                a8 = pl.multiple_of(at + half * 8, 8)
                d8 = [dt_ref[pl.ds(a8, 8), sl] for sl in sls]
                g8 = [gy_ref[pl.ds(a8, 8), sl] for sl in sls]
                u8 = [u_ref[pl.ds(a8, 8), sl] for sl in sls]
                w8 = [d * u for d, u in zip(d8, u8)]
                r1, r2 = [[None] * 8 for _ in sls], [[None] * 8 for _ in sls]
                for j in reversed(range(8)):
                    t = half * 8 + j
                    gb = gc = 0.0
                    for k, sl in enumerate(sls):
                        d, gy = d8[k][j : j + 1], g8[k][j : j + 1]
                        a = m[k] + ccol[t] * gy
                        m[k] = jnp.exp2(d * scaled[k]) * a
                        gb = gb + a * w8[k][j : j + 1]
                        gc = gc + gy * now[k]
                        now[k] = hbuf[slot, t * states : (t + 1) * states, sl].astype(f32)
                        p = m[k] * now[k] * scaled[k]
                        dd[k] = dd[k] + p * d
                        r1[k][j], r2[k][j] = fold(p), fold(a * bcol[t])
                    gbsum[t] += gb
                    gcsum[t] += gc
                for k, sl in enumerate(sls):
                    w1, w2 = row_sums(r1[k]), row_sums(r2[k])
                    gdt[pl.ds(a8, 8), sl] = w1 * (1.0 / LOG2E) + u8[k] * w2
                    gu[pl.ds(a8, 8), sl] = d8[k] * w2
            for k, sl in enumerate(sls):
                adj[:, sl] = m[k]
                dvec_ref[0:states, sl] = dd[k]
        square = (states, small.shape[1])
        where, entry = lanes(square), subs(square)
        line = subs((GROUP, small.shape[1]))
        out = jnp.zeros(small.shape, f32)
        for t in range(GROUP):
            gb = jnp.broadcast_to(jnp.sum(gbsum[t], axis=1, keepdims=True), square)
            gc = jnp.broadcast_to(jnp.sum(gcsum[t], axis=1, keepdims=True), square)
            put = jnp.where(where == entry + rank, gb, jnp.where(where == entry + rank + states, gc, 0.0))
            out = jnp.where(line == t, jnp.sum(put, axis=0, keepdims=True), out)
        gproj[pl.ds(at, GROUP), :] = out
        return carry
    lax.fori_loop(0, steps, group, 0)
    dvec_ref[0:states] = dvec_ref[0:states] * (1.0 / LOG2E)
    hooks.rest()

    low = rank_lanes(proj_ref[...], rank, states)
    at = rank + 2 * states
    row = states + taps
    grad_rank = jnp.zeros(proj_ref.shape, jnp.float32)
    for j in range(inner // WIDE):
        cols = slice(j * WIDE, (j + 1) * WIDE)
        pre = dot_nt(low, small_ref[cols, :]) + vec_ref[row + 1 : row + 2, cols]
        grad_pre = gdt[:, cols] * sigmoid(pre)
        dvec_ref[row + 1 : row + 2, cols] = jnp.sum(grad_pre, axis=0, keepdims=True)
        grad_pre = grad_pre.astype(jnp.bfloat16)
        gpre[:, cols] = grad_pre
        grad_rank = grad_rank + dot(grad_pre, small_ref[cols, :])
    where = lanes(grad_rank.shape)
    grad_rank = pltpu.roll(grad_rank, small_ref.shape[1] - at, axis=1)
    grad_proj = jnp.where(where < rank, grad_rank, jnp.where(where < at, gproj[...], 0.0)).astype(jnp.bfloat16)
    for ref, to in ((tok_ref, 0), (halo_ref, count)):
        x = ref[...].astype(jnp.float32)
        xn[to : to + x.shape[0]] = (x * normalize(x) * gain_ref[0:1]).astype(jnp.bfloat16)
    grad_normed = jnp.zeros((gm.shape[0], xn.shape[1]), jnp.float32)
    first = ext_ref.shape[1] - rows - taps + 1
    for j in range(inner // WIDE):
        cols = slice(j * WIDE, (j + 1) * WIDE)
        dsmall_ref[cols, :] = (
            dot_tn(u_ref[:, cols].astype(jnp.bfloat16), grad_proj) + dot_tn(gpre[:, cols], low)
        ).astype(jnp.bfloat16)
        grad_u = dot_nt(grad_proj, small_ref[cols, :]) + gy_ref[:, cols] * vec_ref[row + 2 : row + 3, cols] + gu[:, cols]
        taps_sum = [0.0] * taps
        bias_sum = 0.0
        heads = []
        for s in range(seqs):
            pre = conv_sum(ext_ref, s, cols, vec_ref, states, taps, rows)
            sig = sigmoid(pre)
            grad_conv = grad_u[s * rows : (s + 1) * rows] * (sig + pre * sig * (1.0 - sig))
            bias_sum = bias_sum + jnp.sum(grad_conv, axis=0, keepdims=True)
            for k in range(taps):
                taps_sum[k] = taps_sum[k] + jnp.sum(
                    grad_conv * ext_ref[s, first + k : first + k + rows, cols], axis=0, keepdims=True)
            gpad[0:8] = jnp.zeros((8, WIDE), jnp.float32)
            gpad[8 : 8 + rows] = grad_conv
            gpad[8 + rows :] = jnp.zeros((8, WIDE), jnp.float32)
            grad = 0.0
            for k in range(taps):
                grad = grad + vec_ref[states + k : states + k + 1, cols] * gpad[taps - 1 - k : taps + 7 - k + rows]
            heads.append(grad[0:8])
            gm[s * rows : (s + 1) * rows, cols] = grad[8:].astype(jnp.bfloat16)
        gm[count:, cols] = jnp.concatenate(heads).astype(jnp.bfloat16)
        dvec_ref[row : row + 1, cols] = bias_sum
        for k in range(taps):
            dvec_ref[states + k : states + k + 1, cols] = taps_sum[k]
    if in_grads is None:
        for j in range(inner // WIDE):
            cols, zcols = (slice(at + j * WIDE, at + (j + 1) * WIDE) for at in (0, inner))
            din_ref[:, cols] = dot_tn(xn[...], gm[:, cols]).astype(jnp.bfloat16)
            din_ref[:, zcols] = dot_tn(xn[:count], gz_ref[:, cols]).astype(jnp.bfloat16)
    else:
        in_grads()
    for j in range(inner // WIDE):
        cols, zcols = (slice(at + j * WIDE, at + (j + 1) * WIDE) for at in (0, inner))
        gz = jnp.concatenate([gz_ref[:, cols], jnp.zeros((gm.shape[0] - count, WIDE), jnp.bfloat16)])
        grad_normed = grad_normed + dot_nt(gm[:, cols], win_ref[:, cols]) + dot_nt(gz, win_ref[:, zcols])
    gain_sum = 0.0
    for ref, to, base, out in ((tok_ref, 0, ghid_ref, dtok_ref), (halo_ref, count, None, dhalo_ref)):
        x = ref[...].astype(jnp.float32)
        r1 = normalize(x)
        grad = grad_normed[to : to + x.shape[0]]
        gain_sum = gain_sum + jnp.sum(grad * (x * r1), axis=0, keepdims=True)
        grad = grad * gain_ref[0:1]
        grad = r1 * grad - x * (r1 * r1 * r1) * jnp.mean(grad * x, axis=1, keepdims=True)
        out[...] = grad if base is None else grad + base[...]
    dgain_ref[...] = gain_sum


def like(*shape, dtype=f32):
    return jax.ShapeDtypeStruct(shape, dtype)


def params(mib=56):
    return pltpu.CompilerParams(vmem_limit_bytes=mib << 20)


def moe_kernel(seq, rows_ref, up_ref, down_ref,
               back_ref, land_ref, dup_ref, ddown_ref,
               xbuf, part, act, ghid, hid, gact, far_buf, own_sum, up2_ref, down2_ref, dup2, ddown2, dup3, ddown3,
               local_sem, disp_sem, pass_sem, recv_sem, load_sem, far_send, far_recv,
               final_send, final_recv, final_local, swap_send, swap_recv):
    me = Place(4, seq)
    b, s = me.at()
    y, z, Z, x = me.y, me.z, me.Z, me.x
    cap, wide = rows_ref.shape[1], rows_ref.shape[2]
    width = wide // 2
    share = up_ref.shape[1]
    two = 2 * cap
    block = 2 * two
    sib, nx = me.at(c=1 - me.c), me.at(x=1 - x)
    greet([(None, sib), (None, nx)] + [(None, (b, (s + k) % seq)) for k in range(1, seq)])

    def remote(src, dst, send, recv, dev):
        return pltpu.make_async_remote_copy(
            src_ref=src, dst_ref=dst, send_sem=send, recv_sem=recv, device_id=dev, device_id_type=MESH)

    def slab(xx, ss):
        return land_ref.at[xx, pl.ds(pl.multiple_of(ss * cap, 8), cap)]

    def there(k, j):
        return ((z + k) % Z) * 2 + j

    def arrived(xx, ss):
        remote(slab(xx, ss), slab(xx, ss), disp_sem.at[0], recv_sem.at[xx, ss], nx).wait_recv()

    def hand(ss):
        return remote(slab(x, ss), slab(x, ss), pass_sem.at[ss], recv_sem.at[x, ss], nx)

    def load(k, xx):
        zz = (z + k) % Z
        return pltpu.make_async_copy(
            land_ref.at[xx, pl.ds(pl.multiple_of(zz * two, 8), two)],
            xbuf.at[k, pl.ds(pl.multiple_of(xx * two, 16), two)], load_sem.at[k, xx])

    def dispatch(k, j):
        to = ((z + Z - k) % Z) * 2 + j
        return remote(rows_ref.at[to], slab(x, s), disp_sem.at[2 * k + j], recv_sem.at[x, s], (b, to))

    dispatch(0, 1 - y).start()
    own = remote(rows_ref.at[s], slab(x, s), pass_sem.at[s], recv_sem.at[x, s], nx)
    own.start()
    local = pltpu.make_async_copy(rows_ref.at[s], slab(x, s), local_sem)
    local.start()
    for j in range(2):
        dispatch(1, j).start()

    def swap(i, src, dst):
        return remote(src, dst, swap_send.at[i], swap_recv.at[i], sib)

    weights = [swap(0, up_ref, up2_ref), swap(1, down_ref, down2_ref)]
    for cp in weights:
        cp.start()
    ups, downs = (up_ref, up2_ref), (down_ref, down2_ref)

    def compute(k):
        for i in range(2):
            for n in range(0, share, WIDE):
                to = slice(i * share + n, i * share + n + WIDE)
                hid[:, to] = dot(xbuf[k, :, :width], ups[i][:, n : n + WIDE])
                gact[:, to] = dot_nt(xbuf[k, :, width:], downs[i][n : n + WIDE, :])

        def sixteen(r, carry):
            at = pl.ds(pl.multiple_of(r * 16, 16), 16)
            to = pl.ds(pl.multiple_of(k * block + r * 16, 16), 16)
            h = hid[at, :]
            half = 0.5 * (1.0 + erf(h * math.sqrt(0.5)))
            act[to, :] = (h * half).astype(bf16)
            slope = half + h * (jnp.exp(-0.5 * h * h) * (1.0 / math.sqrt(2.0 * math.pi)))
            ghid[to, :] = (gact[at, :] * slope).astype(bf16)
            return carry
        lax.fori_loop(0, block // 16, sixteen, 0)
        mine = pl.ds(pl.multiple_of(k * block, 16), block)
        for n in range(0, width, WIDE):
            cols = slice(n, n + WIDE)
            part[k, :, cols] = (
                dot(act[mine, :share], down_ref[:, cols]) + dot(act[mine, share:], down2_ref[:, cols])
            ).astype(bf16)
            part[k, :, width + n : width + n + WIDE] = (
                dot_nt(ghid[mine, :share], up_ref[cols, :]) + dot_nt(ghid[mine, share:], up2_ref[cols, :])
            ).astype(bf16)

    def of_chip(k, xx):
        return part.at[k, pl.ds(pl.multiple_of(xx * two, 16), two)]

    def to_far(k):
        return remote(of_chip(k, 1 - x), far_buf.at[k], far_send.at[k], far_recv.at[k], nx)

    def to_home(k, j):
        return remote(own_sum.at[k, j], back_ref.at[s], final_send.at[k, j], final_recv.at[s], (b, there(k, j)))

    def keep_home():
        return pltpu.make_async_copy(own_sum.at[0, y], back_ref.at[s], final_local)

    def own_stage(k):
        @pl.when(k == 0)
        def _():
            arrived(x, z * 2 + 1 - y)
            hand(z * 2 + 1 - y).start()
            local.wait()

        @pl.when(k > 0)
        def _():
            for j in range(2):
                arrived(x, there(k, j))
                hand(there(k, j)).start()

        @pl.when(k < Z - 2)
        def _():
            for j in range(2):
                dispatch(k + 2, j).start()
        load(k, x).start()

    def compute_stage(k):
        for j in range(2):
            arrived(1 - x, there(k, j))
        load(k, 1 - x).start()
        for xx in range(2):
            load(k, xx).wait()

        @pl.when(k == 0)
        def _():
            for cp in weights:
                cp.wait_recv()
        compute(k)
        to_far(k).start()

    def home_stage(k):
        to_far(k).wait_recv()
        total = of_chip(k, x)[...].astype(f32) + far_buf[k].astype(f32)
        for j in range(2):
            own_sum[k, j] = total[j * cap : (j + 1) * cap].astype(bf16)

        @pl.when(k > 0)
        def _():
            for j in range(2):
                to_home(k, j).start()

        @pl.when(k == 0)
        def _():
            keep_home().start()
            to_home(0, 1 - y).start()

    everything = (Z * block, width)
    stages = ((own_stage, 0), (home_stage, 2), (compute_stage, 1))

    def step(t, carry):
        for stage, lag in stages:
            k = t - lag
            pl.when(jnp.logical_and(k >= 0, k < Z))(functools.partial(stage, k))
        return carry
    lax.fori_loop(0, Z + 2, step, 0)
    x_all = lambda: xbuf[:, :, :width].reshape(everything)
    g_all = lambda: xbuf[:, :, width:].reshape(everything)
    grads = [swap(2, dup2, dup3), swap(3, ddown2, ddown3)]
    for n in range(0, share, WIDE):
        dup2[:, n : n + WIDE] = dot_tn(x_all(), ghid[:, share + n : share + n + WIDE]).astype(bf16)
    grads[0].start()
    for n in range(0, share, WIDE):
        ddown2[n : n + WIDE, :] = dot_tn(act[:, share + n : share + n + WIDE], g_all()).astype(bf16)
    grads[1].start()
    for n in range(0, share, WIDE):
        dup_ref[:, n : n + WIDE] = dot_tn(x_all(), ghid[:, n : n + WIDE])
        ddown_ref[n : n + WIDE, :] = dot_tn(act[:, n : n + WIDE], g_all())
    grads[0].wait_recv()
    dup_ref[...] += dup3[...].astype(f32)
    grads[1].wait_recv()
    ddown_ref[...] += ddown3[...].astype(f32)
    for cp in weights + grads:
        cp.wait_send()

    for k in range(1, seq):
        e = (s + k) % seq
        remote(back_ref.at[e], back_ref.at[e], disp_sem.at[0], final_recv.at[e], sib).wait_recv()
    keep_home().wait()
    dispatch(0, 1 - y).wait_send()
    own.wait_send()
    hand(z * 2 + 1 - y).wait_send()
    to_home(0, 1 - y).wait_send()

    def settle(k, carry):
        to_far(k).wait_send()

        @pl.when(k > 0)
        def _():
            for j in range(2):
                dispatch(k, j).wait_send()
                to_home(k, j).wait_send()
                hand(there(k, j)).wait_send()
        return carry
    lax.fori_loop(0, Z, settle, 0)


def moe_rows(batch, seq, sent, up, down):
    width, hidden_share = up.shape
    capacity, wide = sent.shape[1:]
    block = seq * capacity
    if tuned(batch, seq):
        Z, block = seq // 2, 4 * capacity
        dma = pltpu.SemaphoreType.DMA
        quarter = [pltpu.VMEM((width, hidden_share), bf16), pltpu.VMEM((hidden_share, width), bf16)]
        out = pl.pallas_call(
            functools.partial(moe_kernel, seq),
            out_shape=[
                like(seq, capacity, wide, dtype=bf16),
                like(2, seq * capacity, wide, dtype=bf16),
                like(width, hidden_share),
                like(hidden_share, width),
            ],
            in_specs=[VM] * 3,
            out_specs=[HBM, HBM] + [VM] * 2,
            scratch_shapes=[
                pltpu.VMEM((Z, block, wide), bf16),
                pltpu.VMEM((Z, block, wide), bf16),
                pltpu.VMEM((Z * block, 2 * hidden_share), bf16),
                pltpu.VMEM((Z * block, 2 * hidden_share), bf16),
                pltpu.VMEM((block, 2 * hidden_share), f32),
                pltpu.VMEM((block, 2 * hidden_share), f32),
                pltpu.VMEM((Z, 2 * capacity, wide), bf16),
                pltpu.VMEM((Z, 2, capacity, wide), bf16),
                *quarter,
                *quarter,
                *quarter,
                dma,
                dma((2 * Z,)),
                dma((seq,)),
                dma((2, seq)),
                dma((Z, 2)),
                dma((Z,)),
                dma((Z,)),
                dma((Z, 2)),
                dma((seq,)),
                dma,
                dma((4,)),
                dma((4,)),
            ],
            compiler_params=pltpu.CompilerParams(
                collective_id=2, has_side_effects=True, vmem_limit_bytes=56 << 20),
            name="experts",
        )(sent, up, down)
        return out[0], out[2], out[3]
    mine = lax.all_to_all(sent, "seq", split_axis=0, concat_axis=0, tiled=True)
    rows = lax.all_gather(mine, "batch", axis=0).reshape(batch * block, wide)
    part, d_up, d_down = pl.pallas_call(
        expert_kernel,
        out_shape=[
            like(batch * block, wide, dtype=bf16),
            like(width, hidden_share),
            like(hidden_share, width),
        ],
        grid=(batch,),
        in_specs=[
            pl.BlockSpec((block, wide), lambda i: (i, 0)),
            pl.BlockSpec((width, hidden_share), lambda i: (0, 0)),
            pl.BlockSpec((hidden_share, width), lambda i: (0, 0)),
        ],
        out_specs=[
            pl.BlockSpec((block, wide), lambda i: (i, 0)),
            pl.BlockSpec((width, hidden_share), lambda i: (0, 0)),
            pl.BlockSpec((hidden_share, width), lambda i: (0, 0)),
        ],
        compiler_params=params(),
        name="experts",
    )(rows, up, down)
    part = part.reshape((batch,) + sent.shape)
    mine = lax.psum_scatter(part, "batch", scatter_dimension=0, tiled=False)
    return lax.all_to_all(mine, "seq", split_axis=0, concat_axis=0, tiled=True), d_up, d_down


class Moves:
    def __init__(self, sems):
        self.sems, self.used, self.named = sems, 0, {}

    def start(self, name, src, dst):
        cp = pltpu.make_async_copy(src, dst, self.sems.at[self.used])
        self.used += 1
        cp.start()
        self.named.setdefault(name, []).append(cp)

    def wait(self, *names):
        for name in names:
            for cp in self.named.pop(name):
                cp.wait()

    def wait_all(self):
        self.wait(*list(self.named))


def forward_kernel(dims, share, low_share, experts, capacity, room, batch, seq,
                   tok_ref, cot_ref, route_ref, slot_ref, state_ref, step_ref, router_in, *refs):
    seqs, rows, inner = dims[:3]
    lines, gains, refs = refs[:5], refs[5:7], refs[7:]
    (win_in, out_in, tok_hbm,
     win_hbm, out_hbm, tail_hbm, halo_hbm, ext_hbm, z_hbm, u_hbm, dt_hbm, y_hbm, gated_hbm, hist_ref,
     proj_ref, dsum_ref, vec_ref, gain_ref, router_ref, hid_ref, moe_ref, gate_ref, rows_ref,
     win, out, tail_all, halo, ext, z, u, dt, y, gated, end, start, xn, hbuf, hcur, sem, sem0,
     tail, vecs, feats, zeros, send_sem, recv_sem, edge_sem, sems) = refs[:48]
    relay_refs = refs[48:]
    moves = Moves(sems)
    gather = Gatherer(batch, seq, (win_in, tail, out_in), (win_hbm, tail_hbm, out_hbm), send_sem, recv_sem)
    WIN, TAIL, OUT = range(3)
    relay = Relay(seq, True, dims[3], dsum_ref, vec_ref, end, start, *relay_refs)
    b, s = gather.me.at()
    has_before, has_after = s > 0, s < seq - 1
    greet(gather.peers() + [(has_before, (b, s - 1)), (has_after, (b, s + 1))])

    gather.give(WIN)
    edges = [
        pltpu.make_async_remote_copy(
            src_ref=tok_hbm.at[i, pl.ds(rows - 8, 8)], dst_ref=halo_hbm.at[pl.ds(8 * i, 8)],
            send_sem=edge_sem.at[0, i], recv_sem=edge_sem.at[1, i], device_id=(b, s + 1), device_id_type=MESH)
        for i in range(seqs)
    ]
    none = pltpu.make_async_copy(zeros, halo_hbm, edge_sem.at[2, 0])
    zeros[...] = jnp.zeros_like(zeros)

    @pl.when(has_after)
    def _():
        for cp in edges:
            cp.start()
    pl.when(jnp.logical_not(has_before))(none.start)
    pack_weights(tail, vecs, feats, state_ref, step_ref, router_in, lines, gains)
    gather.give(TAIL)
    moves.start("own", win_in, gather.part(WIN, gather.own))
    moves.start("own", tail, gather.part(TAIL, gather.own))
    moves.start("own out", out_in, gather.part(OUT, gather.own))
    for h in range(1, gather.Z + 3):
        gather.hop((WIN, TAIL), h)
    gather.give(OUT)
    gather.rest((WIN, TAIL))

    @pl.when(has_before)
    def _():
        for cp in edges:
            cp.wait_recv()
    pl.when(jnp.logical_not(has_before))(none.wait)
    moves.wait("own")
    moves.start("head", halo_hbm, halo)
    moves.start("head", tail_hbm, tail_all)
    for j in range(inner // WIDE):
        for base in (0, inner):
            cols = pl.ds(base + j * WIDE, WIDE)
            moves.start(("win", j), win_hbm.at[:, cols], win.at[:, cols])
    moves.wait("head")

    def weights(j):
        moves.wait(("win", j))
        if j == 4:
            gather.hop((OUT,), 1)

    def projected():
        for name, src, dst in (("ext", ext, ext_hbm), ("z", z, z_hbm), ("u", u, u_hbm), ("dt", dt, dt_hbm)):
            moves.start(name, src, dst)
        gather.hop((OUT,), 2)

    def scanned(i):
        relay.start(i)
        gather.hop((OUT,), 3 + i)

    enter_packed(dims, share, low_share, experts, tok_ref, halo, win, tail_all, ext, z, u, dt, proj_ref, end,
                 dsum_ref, vec_ref, gain_ref, router_ref, xn,
                 hooks=Hooks(weights=weights, projected=projected, scanned=scanned))
    for i in range(relay.count):
        relay.finish(i)
    for h in range(3 + relay.count, gather.Z + 3):
        gather.hop((OUT,), h)

    def half(i):
        if i == 0:
            gather.rest((OUT,))
            moves.wait("own out")
            moves.start("out", out_hbm, out)

    def mixed():
        moves.start("y", y, y_hbm)
        moves.start("gated", gated, gated_hbm)

    leave_kernel(dims, capacity, room, tok_ref, cot_ref, start, dt, u, z, proj_ref, vec_ref, out, gain_ref, router_ref,
                 route_ref, slot_ref, hist_ref, y, hid_ref, gated, moe_ref, gate_ref, rows_ref, hbuf, hcur, sem, sem0,
                 hooks=Hooks(out_proj=lambda: moves.wait("out"), mixed=mixed, half=half))
    relay.settle()
    gather.settle()

    @pl.when(has_after)
    def _():
        for cp in edges:
            cp.wait_send()
    moves.wait_all()


def backward_kernel(dims, share, low_share, experts, capacity, room, batch, seq,
                    ret_ref, cot_ref, hid_ref, moe_ref, gate_ref, vec_ref, gain_ref, router_ref, route_ref, slot_ref,
                    dsum_ref, proj_ref, gated_hbm, out_hbm, z_hbm, y_hbm, u_hbm, dt_hbm, ext_hbm, win_hbm, tail_hbm,
                    tok_hbm, halo_hbm, hist_ref,
                    block_ref, dtok_ref, next_ref, in_out, out_out, tail_out,
                    gated, out, z, y, u, dt, ext, win, tail, tok, halo, gy, gz, ghid, adj, later,
                    dhalo, dsmall, dvec, dnorm, dmoe, drouter, dskip, blank,
                    hbuf, ccol, bcol, gbsum, gcsum, carry, gdt, gu, gproj, gpad, gm, xn, gpre, sem, sems, edge_sem,
                    *more):
    seqs, rows, inner, states, rank, taps = dims
    count, devices = seqs * rows, batch * seq
    relay_refs, more = more[:9], more[9:]
    moves = Moves(sems)
    for name, src, dst in (
        ("gated", gated_hbm, gated), ("out", out_hbm, out), ("z", z_hbm, z), ("y", y_hbm, y), ("u", u_hbm, u),
        ("dt", dt_hbm, dt), ("ext", ext_hbm, ext), ("win", win_hbm, win), ("tail", tail_hbm, tail),
        ("tok", tok_hbm, tok), ("halo", halo_hbm, halo),
    ):
        moves.start(name, src, dst)
    relay = Relay(seq, False, states, dsum_ref, vec_ref, adj, later, *relay_refs)
    reducer = Reducer(batch, seq, *(more[4 * i : 4 * i + 4] for i in range(5)), more[20:])
    OUT, GATE, IN, REST = range(4)
    b, s = reducer.me.at()
    has_before, has_after = s > 0, s < seq - 1
    greet(reducer.peers() + [(has_before, (b, s - 1)), (has_after, (b, s + 1))])
    me = reducer.me

    return_kernel(dims, capacity, room, ret_ref, cot_ref, hid_ref, moe_ref, gate_ref, gated, y, u, z, dt, proj_ref,
                  vec_ref, out, gain_ref, router_ref, route_ref, slot_ref,
                  block_ref, ghid, gy, gz, None, drouter, dskip, dmoe, adj,
                  hooks=Hooks(activations=lambda: moves.wait("gated", "out", "z", "y", "u"),
                              gradients=lambda: moves.wait("dt"), scanned=relay.start))

    def in_grads(a, grads, n, xx):
        half, cut, wide = devices // 2, low_share * devices // 2, 2 * WIDE
        at = pl.ds(pl.multiple_of(xx * cut, 128), cut)
        for c0 in range(0, inner, wide):
            part = dot_tn(xn[0:n, at], grads[:, c0 : c0 + wide]).reshape(half, low_share, wide)
            reducer.items[a][pl.ds(xx * half, half), :, c0 : c0 + wide] = part.astype(bf16)
        reducer.give(a, [(xx, 1 - me.y), (xx, me.y)])

    branch = ghid[...].astype(bf16)
    cut = 8 * share
    for q in range(devices // 8):
        part = dot_tn(gated[:, q * cut : (q + 1) * cut], branch)
        reducer.items[OUT][q * 8 : (q + 1) * 8] = part.astype(bf16).reshape(8, share, part.shape[1])
    reducer.give(OUT, reducer.others)
    relay.finish(0)
    moves.wait("tok")
    x = tok[...].astype(f32)
    xn[0:count] = (x * normalize(x) * gain_ref[0:1]).astype(bf16)
    for xx in (1 - me.x, me.x):
        in_grads(GATE, gz, count, xx)
    for i in range(1, relay.count):
        relay.finish(i)

    def group(i):
        for g in range(4):
            @pl.when(i // reducer.Z == g)
            def _(g=g):
                for a in (OUT, GATE):
                    reducer.step(a, g, i % reducer.Z)

    def late_grads():
        for xx in (1 - me.x, me.x):
            in_grads(IN, gm, count + 8 * seqs, xx)

    back_kernel(dims, tok, halo, ext, hist_ref, later, gy, gz, ghid, u, dt, proj_ref, win, tail, vec_ref, gain_ref,
                dtok_ref, dhalo, None, dsmall, dvec, dnorm,
                hbuf, ccol, bcol, gbsum, gcsum, carry, gdt, gu, gproj, gpad, gm, xn, gpre, sem,
                hooks=Hooks(rest=lambda: moves.wait("ext", "win", "tail", "halo"), group=group),
                in_grads=late_grads)
    edge = reducer.copy(dhalo, next_ref, edge_sem.at[0], edge_sem.at[1], (b, s - 1))
    none = pltpu.make_async_copy(blank, next_ref, edge_sem.at[2])
    blank[...] = jnp.zeros_like(blank)
    pl.when(has_before)(edge.start)
    pl.when(jnp.logical_not(has_after))(none.start)
    pack_tail(reducer.items[REST], low_share, experts, states + taps + 2, dsmall, dvec, dskip, drouter, dnorm, dmoe)
    reducer.give(REST, reducer.others)
    for t in range(reducer.Z + 2):
        for g, k in ((0, t), (1, t), (2, t - 1), (3, t - 2)):
            if 0 <= k < reducer.Z:
                for a in (IN, REST):
                    reducer.step(a, g, k)
    for a, ref in ((OUT, out_out), (GATE, in_out.at[:, inner:]), (IN, in_out.at[:, :inner]), (REST, tail_out)):
        reducer.result(a, ref)
    relay.settle()
    for a in (OUT, GATE, IN, REST):
        reducer.settle(a)
    pl.when(has_after)(edge.wait_recv)
    pl.when(has_before)(edge.wait_send)
    pl.when(jnp.logical_not(has_after))(none.wait)


def body(
    tokens,
    in_proj,
    conv_weight,
    conv_bias,
    state_proj,
    step_proj,
    step_bias,
    decay_log,
    skip_gain,
    out_proj,
    norm_gain,
    moe_gain,
    router_proj,
    expert_up,
    expert_down,
    routes,
    slot_index,
    cotangent,
):
    batch, seq = lax.axis_size("batch"), lax.axis_size("seq")
    both = ("batch", "seq")
    seqs, rows, width = tokens.shape
    count = seqs * rows
    devices = batch * seq
    taps, share = conv_weight.shape
    inner = share * devices
    states, rank = decay_log.shape[0], step_proj.shape[0]
    low_share = norm_gain.shape[0]
    experts = router_proj.shape[1]
    capacity = max(2, 5 * count // (4 * experts))
    dims = (seqs, rows, inner, states, rank, taps)
    tile = 128

    lines = (decay_log, conv_weight, conv_bias[None], step_bias[None], skip_gain[None])
    used = sum(a.shape[0] for a in lines)
    room = -(-used // 8) * 8
    fast = tuned(batch, seq)
    if not fast:
        features = jnp.concatenate([router_proj, norm_gain[:, None], moe_gain[:, None]], axis=1)
        tail = jnp.concatenate(
            [
                state_proj,
                step_proj.T,
                jnp.pad(jnp.concatenate(lines), ((0, room - used), (0, 0))).T,
                jnp.pad(features, ((0, share - low_share), (0, tile - room - features.shape[1]))),
            ],
            axis=1,
        )
        halo = lax.ppermute(tokens[:, rows - taps + 1 :], "seq", [(i, i + 1) for i in range(seq - 1)])
        halo = jnp.pad(halo, ((0, 0), (8 - taps + 1, 0), (0, 0))).reshape(seqs * 8, width)
        in_full, out_full, tail_full = (
            lax.all_gather(a, both, axis=0, tiled=True) for a in (in_proj, out_proj, tail)
        )
    tok, cot = tokens.reshape(count, width), cotangent.reshape(count, width)
    size = GROUP * states
    total = experts * capacity
    edge_rows = seqs * 8
    dma = pltpu.SemaphoreType.DMA
    acts = like(count, inner)
    ext_s, state_s, dsum_s = like(seqs, rows + 8, inner), like(seqs, states, inner), like(seqs, 1, inner)
    proj_s, low_s, vec_s = like(count, tile), like(count, inner, dtype=bf16), like(room, inner)
    hist_s = like(seqs, (rows + 1) * states, inner, dtype=bf16)
    hid_s, moe_s, gate_s = like(count, width), like(count, width, dtype=bf16), like(count, 1)
    rows_s = like(total, 2 * width, dtype=bf16)
    gain_s, router_s = like(8, width), like(width, tile, dtype=bf16)
    vmem = lambda a: pltpu.VMEM(a.shape, a.dtype)
    normed = pltpu.VMEM((count + edge_rows, width), bf16)
    leave_scratch = [pltpu.VMEM((2, size, inner), bf16), pltpu.VMEM(state_s.shape, bf16), dma((2,)), dma((seqs,))]
    back_scratch = [
        pltpu.VMEM((2, size + states, inner), bf16),
        pltpu.VMEM((GROUP, states, tile), f32),
        pltpu.VMEM((GROUP, states, tile), f32),
        pltpu.VMEM((GROUP, states, tile), f32),
        pltpu.VMEM((GROUP, states, tile), f32),
        pltpu.VMEM((states, inner), f32),
        vmem(acts),
        vmem(acts),
        vmem(proj_s),
        pltpu.VMEM((rows + 16, WIDE), f32),
        pltpu.VMEM((count + edge_rows, inner), bf16),
        normed,
        vmem(low_s),
        dma((2,)),
    ]
    tok_s, halo_s, din_s = like(count, width), like(edge_rows, width), like(width, 2 * inner, dtype=bf16)
    dout_s, dsmall_s = like(inner, width, dtype=bf16), like(inner, tile, dtype=bf16)
    drouter_s, dskip_s, dgain_s = like(width, tile), like(1, inner), like(1, width)
    wide = inner // WIDE
    if fast:
        in_s, out_s = like(width, 2 * inner, dtype=bf16), like(inner, width, dtype=bf16)
        tail_s, halo_b = like(inner, 2 * tile, dtype=bf16), like(edge_rows, width, dtype=bf16)
        (in_full, out_full, tail_full, halo, ext, z, u, dt, y, gated, hist, proj, dsum, vec, gain, router, hid, moe_in,
         gate, sent) = pl.pallas_call(
            partial(forward_kernel, dims, share, low_share, experts, capacity, room, batch, seq),
            out_shape=[in_s, out_s, tail_s, halo_b, ext_s, acts, acts, acts, acts, low_s, hist_s, proj_s, dsum_s, vec_s,
                       gain_s, router_s, hid_s, moe_s, gate_s, rows_s],
            in_specs=[VM] * 16 + [HBM],
            out_specs=[HBM] * 11 + [VM] * 9,
            scratch_shapes=[
                vmem(in_s), vmem(out_s), vmem(tail_s), vmem(halo_b), vmem(ext_s), vmem(acts), vmem(acts), vmem(acts),
                vmem(acts), vmem(low_s), vmem(state_s), vmem(state_s), normed, *leave_scratch,
                pltpu.VMEM((share, 2 * tile), bf16),
                pltpu.VMEM((room, share), f32),
                pltpu.VMEM((8, low_share), f32),
                vmem(halo_b),
                dma((3, n_sends(seq // 2))),
                dma((3, devices)),
                dma((3, seqs)),
                dma((2 * wide + 12,)),
                *relay_scratch(seqs, states, inner),
            ],
            compiler_params=pltpu.CompilerParams(
                collective_id=3, has_side_effects=True, vmem_limit_bytes=58 << 20),
            name="forward",
        )(tok, cot, routes, slot_index, state_proj, step_proj, router_proj.T, *lines, norm_gain[None], moe_gain[None],
          in_proj, out_proj, tokens)
    else:
        vec = tail_full[:, tile : tile + room].T.astype(f32)
        router = tail_full[:, tile:].reshape(devices, share, tile)[:, :low_share].reshape(width, tile)
        gain = router[:, room + experts : room + experts + 2].T.astype(f32)
        ext, z, u, dt, proj, end, dsum = pl.pallas_call(
            partial(enter_kernel, dims),
            out_shape=[ext_s, acts, acts, acts, proj_s, state_s, dsum_s],
            in_specs=[VM] * 6,
            out_specs=[VM] * 7,
            scratch_shapes=[normed],
            compiler_params=params(),
            name="enter",
        )(tok, halo, in_full, tail_full[:, :tile], vec, gain)
        rates = -jnp.exp(vec[:states])
        before = chain_states(seq, True, dsum, rates, end)
        hist, y, hid, gated, moe_in, gate, sent = pl.pallas_call(
            partial(leave_kernel, dims, capacity, room),
            out_shape=[hist_s, acts, hid_s, low_s, moe_s, gate_s, rows_s],
            in_specs=[VM] * 13,
            out_specs=[HBM] + [VM] * 6,
            scratch_shapes=leave_scratch,
            compiler_params=params(),
            name="leave",
        )(tok, cot, before, dt, u, z, proj, vec, out_full, gain, router, routes, slot_index)

    back, d_up, d_down = moe_rows(
        batch, seq, sent.reshape(experts, capacity, 2 * width), expert_up[0], expert_down[0])
    back = back.reshape(total, 2 * width)

    if fast:
        own = [(share, width), (low_share, inner), (low_share, inner), (share, 2 * tile)]
        block_out, d_tok, from_next, s_in, s_out, s_tail = pl.pallas_call(
            partial(backward_kernel, dims, share, low_share, experts, capacity, room, batch, seq),
            out_shape=[moe_s, tok_s, halo_s, like(low_share, 2 * inner), like(*own[0]), like(*own[3])],
            in_specs=[VM] * 12 + [HBM] * 12,
            out_specs=[VM] * 2 + [HBM] + [VM] * 3,
            scratch_shapes=[
                vmem(low_s), vmem(out_s), vmem(acts), vmem(acts), vmem(acts), vmem(acts), vmem(ext_s), vmem(in_s),
                vmem(tail_s), vmem(tok), vmem(halo_b), vmem(acts), vmem(low_s), vmem(tok_s), vmem(state_s),
                vmem(state_s), vmem(halo_s), vmem(dsmall_s), vmem(vec_s), vmem(dgain_s), vmem(dgain_s),
                vmem(drouter_s), vmem(dskip_s), vmem(halo_s), *back_scratch, dma((12,)), dma((3,)),
                *relay_scratch(seqs, states, inner), *reduce_scratch(devices, seq // 2, own),
            ],
            compiler_params=pltpu.CompilerParams(
                collective_id=4, has_side_effects=True, vmem_limit_bytes=62 << 20),
            name="backward",
        )(back, cot, hid, moe_in, gate, vec, gain, router, routes, slot_index, dsum, proj,
          gated, out_full, z, y, u, dt, ext, in_full, tail_full, tok, halo, hist)
    else:
        block_out, ghid, gy, gz, d_out, d_router, d_skip, d_moe, adj = pl.pallas_call(
            partial(return_kernel, dims, capacity, room),
            out_shape=[moe_s, tok_s, acts, low_s, dout_s, drouter_s, dskip_s, dgain_s, state_s],
            in_specs=[VM] * 17,
            out_specs=[VM] * 9,
            compiler_params=params(),
            name="back_experts",
        )(back, cot, hid, moe_in, gate, gated, y, u, z, dt, proj, vec, out_full, gain, router, routes, slot_index)
        later = chain_states(seq, False, dsum, rates, adj)
        d_tok, d_halo, d_in, d_small, d_vec, d_norm = pl.pallas_call(
            partial(back_kernel, dims),
            out_shape=[tok_s, halo_s, din_s, dsmall_s, vec_s, dgain_s],
            in_specs=[VM] * 3 + [HBM] + [VM] * 11,
            out_specs=[VM] * 6,
            scratch_shapes=back_scratch,
            compiler_params=params(),
            name="back_mixer",
        )(tok, halo, ext, hist, later, gy, gz, ghid, u, dt, proj, in_full, tail_full, vec, gain)

    skip_row = states + taps + 2
    if fast:
        shapes = [
            s_in.shape, (taps, share), (1, share), (share, rank + 2 * states), (rank, share), (1, share),
            (states, share), (1, share), s_out.shape, (1, low_share), (1, low_share), (experts, low_share),
        ]
        block_out, d_tok = block_out.reshape(tokens.shape), d_tok.reshape(tokens.shape)
        block_out, d_tok, *sums, d_up, d_down = pl.pallas_call(
            partial(finish_kernel, dims, low_share, experts),
            out_shape=[like(*tokens.shape, dtype=bf16), like(*tokens.shape)] + [like(*a) for a in shapes]
            + [like(*d_up.shape), like(*d_down.shape)],
            in_specs=[VM] * 4 + [HBM] * 4,
            out_specs=[HBM] * 2 + [VM] * 12 + [HBM] * 2,
            scratch_shapes=[vmem(block_out), vmem(d_tok), vmem(d_up), vmem(d_down), dma((20,))],
            compiler_params=params(),
            name="finish",
        )(s_tail, from_next.reshape(seqs, 8, width), s_in, s_out, block_out, d_tok, d_up, d_down)
        for i in (2, 5, 7, 9, 10):
            sums[i] = sums[i][0]
        sums[11] = sums[11].T
        return (block_out, d_tok, *sums, d_up[None], d_down[None])
    d_model = d_router.at[:, room + experts : room + experts + 2].set(jnp.concatenate([d_norm, d_moe]).T)
    d_model = jnp.pad(
        d_model.reshape(devices, low_share, tile)[:, :, room:], ((0, 0), (0, share - low_share), (0, 0))
    ).reshape(inner, tile - room)
    d_vec = d_vec.at[skip_row].set(d_skip[0])
    d_tail = jnp.concatenate([d_small, d_vec.T.astype(bf16), d_model.astype(bf16)], axis=1)
    s_in, s_out, s_tail = (
        lax.psum_scatter(a.astype(f32), both, scatter_dimension=0, tiled=True) for a in (d_in, d_out, d_tail)
    )
    from_next = lax.ppermute(
        d_halo.reshape(seqs, 8, width)[:, 8 - taps + 1 :], "seq", [(i + 1, i) for i in range(seq - 1)]
    )
    d_tok = d_tok.reshape(tokens.shape).at[:, rows - taps + 1 :].add(from_next)
    s_vec = s_tail[:, tile : tile + room].T
    s_model = s_tail[:low_share, tile + room :]
    return (
        block_out.reshape(tokens.shape),
        d_tok,
        s_in,
        s_vec[states : states + taps],
        s_vec[states + taps],
        s_tail[:, : rank + 2 * states],
        s_tail[:, rank + 2 * states : tile].T,
        s_vec[states + taps + 1],
        s_vec[:states],
        s_vec[states + taps + 2],
        s_out,
        s_model[:, experts],
        s_model[:, experts + 1],
        s_model[:, :experts],
        d_up[None],
        d_down[None],
    )


def solution(mesh):
    in_specs = (
        P("batch", "seq", None),
        P(("batch", "seq"), None),
        P(None, ("batch", "seq")),
        P(("batch", "seq")),
        P(("batch", "seq"), None),
        P(None, ("batch", "seq")),
        P(("batch", "seq")),
        P(None, ("batch", "seq")),
        P(("batch", "seq")),
        P(("batch", "seq"), None),
        P(("batch", "seq")),
        P(("batch", "seq")),
        P(("batch", "seq"), None),
        P("seq", None, "batch"),
        P("seq", "batch", None),
        P("batch", "seq"),
        P("batch", "seq"),
        P("batch", "seq", None),
    )
    out_specs = (
        P("batch", "seq", None),
        P("batch", "seq", None),
        P(("batch", "seq"), None),
        P(None, ("batch", "seq")),
        P(("batch", "seq")),
        P(("batch", "seq"), None),
        P(None, ("batch", "seq")),
        P(("batch", "seq")),
        P(None, ("batch", "seq")),
        P(("batch", "seq")),
        P(("batch", "seq"), None),
        P(("batch", "seq")),
        P(("batch", "seq")),
        P(("batch", "seq"), None),
        P("seq", None, "batch"),
        P("seq", "batch", None),
    )
    return jax.shard_map(body, mesh=mesh, in_specs=in_specs, out_specs=out_specs, check_vma=False)
```

```python
from functools import partial
import functools
import math

import jax
import jax.numpy as jnp
from jax import lax
from jax.experimental import pallas as pl
from jax.experimental.pallas import tpu as pltpu
from jax.sharding import PartitionSpec as P

epsilon = 1e-05
MESH = pl.DeviceIdType.MESH
HBM = pl.BlockSpec(memory_space=pl.ANY)
VM = pl.BlockSpec(memory_space=pltpu.VMEM)
bf16, f32 = jnp.bfloat16, jnp.float32


class Place:
    def __init__(self, batch, seq, ydim=2):
        self.batch, self.seq, self.Y = batch, seq, ydim
        self.Z = seq // ydim
        b, s = lax.axis_index("batch"), lax.axis_index("seq")
        self.x, self.c = b // 2, b % 2
        self.z, self.y = s // ydim, s % ydim

    def at(self, x=None, c=None, y=None, z=None):
        pick = lambda v, own: own if v is None else v
        x, c, y, z = pick(x, self.x), pick(c, self.c), pick(y, self.y), pick(z, self.z)
        return (x * 2 + c, z * self.Y + y)

    def index(self, dev):
        return dev[0] * self.seq + dev[1]


def greet(devices):
    barrier = pltpu.get_barrier_semaphore()
    count = 0
    for pred, dev in devices:
        if pred is None:
            pl.semaphore_signal(barrier, inc=1, device_id=dev, device_id_type=MESH)
            count = count + 1
        else:
            @pl.when(pred)
            def _(dev=dev):
                pl.semaphore_signal(barrier, inc=1, device_id=dev, device_id_type=MESH)
            count = count + jnp.where(pred, 1, 0)
    pl.semaphore_wait(barrier, count)


TILE = 128


def spot(rows, at, width):
    return (lanes((rows, width)) == subs((rows, width)) + at).astype(bf16)


class Gatherer:
    def __init__(self, batch, seq, ins, outs, send_sem, recv_sem):
        self.ins, self.outs, self.send_sem, self.recv_sem = ins, outs, send_sem, recv_sem
        self.me = me = Place(batch, seq)
        self.Z, self.z = me.Z, me.z
        self.sib = me.at(c=1 - me.c)
        self.up_ok, self.down_ok = me.z < me.Z - 1, me.z > 0
        self.up, self.down = me.at(z=me.z + 1), me.at(z=me.z - 1)
        self.nx, self.ny = me.at(x=1 - me.x), me.at(y=1 - me.y)
        first = me.c == 0
        pick = lambda a, b: tuple(jnp.where(first, p, q) for p, q in zip(a, b))
        self.second_dev, self.third_dev = pick(self.ny, self.nx), pick(self.nx, self.ny)
        ox, oy = 1 - me.x, 1 - me.y
        self.second_at = (jnp.where(first, me.x, ox), jnp.where(first, oy, me.y))
        self.third_at = (jnp.where(first, ox, me.x), jnp.where(first, me.y, oy))
        self.across_at = (ox, oy)
        self.own = me.index(me.at())
        self.sends = [[] for _ in ins]

    def peers(self):
        return [(None, self.sib), (None, self.nx), (None, self.ny), (self.up_ok, self.up), (self.down_ok, self.down)]

    def part(self, a, index):
        rows = self.ins[a].shape[0]
        return self.outs[a].at[pl.ds(pl.multiple_of(index * rows, 8), rows)]

    def send(self, a, pred, src, index, dev):
        copy = pltpu.make_async_remote_copy(
            src_ref=src, dst_ref=self.part(a, index), send_sem=self.send_sem.at[a, len(self.sends[a])],
            recv_sem=self.recv_sem.at[a, index], device_id=dev, device_id_type=MESH)
        self.sends[a].append((pred, copy))
        if pred is None:
            copy.start()
        else:
            pl.when(pred)(copy.start)

    def give(self, a):
        for pred, dev in self.targets():
            self.send(a, pred, self.ins[a], self.own, dev)

    def targets(self):
        return [(self.up_ok, self.up), (self.down_ok, self.down), (None, self.second_dev), (None, self.third_dev),
                (None, self.sib)]

    def arrive(self, a, pred, index, targets):
        part = self.part(a, index)
        copy = pltpu.make_async_remote_copy(
            src_ref=part, dst_ref=part, send_sem=self.send_sem.at[a, 0], recv_sem=self.recv_sem.at[a, index],
            device_id=self.sib, device_id_type=MESH)
        if pred is None:
            copy.wait_recv()
        else:
            pl.when(pred)(copy.wait_recv)
        for extra, dev in targets:
            p = pred if extra is None else (extra if pred is None else jnp.logical_and(pred, extra))
            self.send(a, p, part, index, dev)

    def offsets(self, k):
        return [(None, 0)] if k == 0 else [(self.z >= k, -k), (self.z + k < self.Z, k)]

    def hop(self, arrays, h):
        me, z = self.me, self.z
        to_second, to_third, to_sib = (None, self.second_dev), (None, self.third_dev), (None, self.sib)
        for k, at, targets in (
            (h, (me.x, me.y), None), (h - 1, self.second_at, [to_third, to_sib]), (h - 2, self.third_at, [to_sib]),
            (h - 3, self.across_at, [to_sib]),
        ):
            if not 0 <= k < self.Z or (targets is None and k == 0):
                continue
            for pred, off in self.offsets(k):
                onward = targets
                if targets is None:
                    onward = [(self.up_ok, self.up) if off < 0 else (self.down_ok, self.down), to_second, to_third, to_sib]
                for a in arrays:
                    self.arrive(a, pred, me.index(me.at(x=at[0], y=at[1], z=z + off)), onward)

    def rest(self, arrays):
        me = self.me
        for h in range(self.Z):
            for xx in (0, 1):
                for yy in (0, 1):
                    for pred, off in self.offsets(h):
                        for a in arrays:
                            self.arrive(a, pred, me.index(me.at(x=xx, y=yy, c=1 - me.c, z=self.z + off)), [])

    def settle(self):
        for sends in self.sends:
            for pred, copy in sends:
                if pred is None:
                    copy.wait_send()
                else:
                    pl.when(pred)(copy.wait_send)


def n_sends(Z):
    return 5 + (Z - 1) * 8 + (2 * Z - 1) * 2 + (2 * Z - 1) * 2


def pack_weights(tail, vecs, feats, state_ref, step_ref, router_ref, lines, gains):
    share, low_share, experts = state_ref.shape[0], router_ref.shape[1], router_ref.shape[0]
    rank, room, wide = step_ref.shape[0], vecs.shape[0], tail.shape[1]
    vecs[...] = jnp.zeros_like(vecs)
    at = 0
    for ref in lines:
        vecs[at : at + ref.shape[0]] = ref[...].astype(f32)
        at += ref.shape[0]
    feats[...] = jnp.zeros_like(feats)
    for i, ref in enumerate(gains):
        feats[i : i + 1] = ref[...].astype(f32)
    by_channel = (
        dot(state_ref[...], spot(state_ref.shape[1], 0, wide))
        + dot_tn(step_ref[...], spot(rank, TILE - rank, wide))
        + dot_tn(vecs[...].astype(bf16), spot(room, TILE, wide))
    )
    by_feature = dot_tn(router_ref[...], spot(experts, TILE + room, wide)) + dot_tn(
        feats[...].astype(bf16), spot(feats.shape[0], TILE + room + experts, wide))
    by_feature = jnp.concatenate([by_feature, jnp.zeros((share - low_share, wide), f32)])
    tail[...] = (by_channel + by_feature).astype(bf16)


class Reducer:
    def __init__(self, batch, seq, items, sib_bufs, far_bufs, near_bufs, line_bufs, sems):
        self.items, self.sib_bufs, self.far_bufs, self.near_bufs, self.line_bufs = (
            items, sib_bufs, far_bufs, near_bufs, line_bufs)
        (self.sib_send, self.sib_recv, self.far_send, self.far_recv, self.near_send, self.near_recv,
         self.line_send, self.line_recv) = sems
        self.me = me = Place(batch, seq)
        self.Z, self.z = me.Z, me.z
        self.sib = me.at(c=1 - me.c)
        self.nx, self.ny = me.at(x=1 - me.x), me.at(y=1 - me.y)
        pick = lambda a, b: tuple(jnp.where(me.c == 0, p, q) for p, q in zip(a, b))
        self.near, self.far = pick(self.ny, self.nx), pick(self.nx, self.ny)
        self.mine, self.others = self.groups(me.c), self.groups(1 - me.c)

    def peers(self):
        column = [(None, self.me.at(z=self.turn(k))) for k in range(self.Z - 1)]
        return [(None, self.sib), (None, self.nx), (None, self.ny)] + column

    def groups(self, c):
        me = self.me
        ox, oy = 1 - me.x, 1 - me.y
        pick = lambda a, b: jnp.where(c == 0, a, b)
        return [(ox, oy), (pick(ox, me.x), pick(me.y, oy)), (pick(me.x, ox), pick(oy, me.y)), (me.x, me.y)]

    def slot(self, xy, zz):
        return (xy[0] * 2 + xy[1]) * self.Z + zz

    def turn(self, k):
        above = self.Z - 1 - self.z
        return jnp.where(k < above, self.Z - 1 - k, jnp.where(k < self.Z - 1, k - above, self.z))

    def item(self, a, c, xy, zz):
        return self.items[a].at[self.me.index((xy[0] * 2 + c, zz * self.me.Y + xy[1]))]

    def copy(self, src, dst, send, recv, dev):
        return pltpu.make_async_remote_copy(
            src_ref=src, dst_ref=dst, send_sem=send, recv_sem=recv, device_id=dev, device_id_type=MESH)

    def to_sib(self, a, xy, k):
        t = self.turn(k)
        s = self.slot(xy, t)
        return self.copy(self.item(a, 1 - self.me.c, xy, t), self.sib_bufs[a].at[s],
                         self.sib_send.at[a, s], self.sib_recv.at[a, s], self.sib)

    def give(self, a, columns):
        for k in range(self.Z):
            for xy in columns:
                self.to_sib(a, xy, k).start()

    def to_far(self, a, g, k):
        t = self.turn(k)
        fs = g * self.Z + t
        return self.copy(self.item(a, self.me.c, self.mine[g], t), self.far_bufs[a].at[fs],
                         self.far_send.at[a, fs], self.far_recv.at[a, fs], self.far)

    def to_near(self, a, k):
        t = self.turn(k)
        return self.copy(self.item(a, self.me.c, self.mine[2], t), self.near_bufs[a].at[t],
                         self.near_send.at[a, t], self.near_recv.at[a, t], self.near)

    def step(self, a, g, k):
        t = self.turn(k)
        s = self.slot(self.mine[g], t)
        item = self.item(a, self.me.c, self.mine[g], t)
        take = lambda ref, recv: self.copy(ref, ref, self.sib_send.at[a, 0], recv, self.sib).wait_recv()
        parts = [self.sib_bufs[a].at[s]]
        take(parts[0], self.sib_recv.at[a, s])
        if g >= 2:
            fs = (g - 2) * self.Z + t
            parts.append(self.far_bufs[a].at[fs])
            take(parts[-1], self.far_recv.at[a, fs])
        if g == 3:
            parts.append(self.near_bufs[a].at[t])
            take(parts[-1], self.near_recv.at[a, t])
        total = item[...].astype(f32)
        for part in parts:
            total = total + part[...].astype(f32)
        item[...] = total.astype(bf16)
        if g < 2:
            self.to_far(a, g, k).start()
        elif g == 2:
            self.to_near(a, k).start()
        else:
            pl.when(k < self.Z - 1)(lambda: self.onward(a, k).start())

    def onward(self, a, k):
        t = self.turn(k)
        return self.copy(self.item(a, self.me.c, self.mine[3], t), self.line_bufs[a].at[self.z],
                         self.line_send.at[a, k], self.line_recv.at[a, self.z], self.me.at(z=t))

    def result(self, a, out_ref):
        total = self.item(a, self.me.c, self.mine[3], self.z)[...].astype(f32)
        for k in range(self.Z - 1):
            t = self.turn(k)
            ref = self.line_bufs[a].at[t]
            self.copy(ref, ref, self.sib_send.at[a, 0], self.line_recv.at[a, t], self.sib).wait_recv()
            total = total + ref[...].astype(f32)
        out_ref[...] = total

    def settle(self, a):
        def one(k, carry):
            for xy in self.others:
                self.to_sib(a, xy, k).wait_send()
            for g in range(2):
                self.to_far(a, g, k).wait_send()
            self.to_near(a, k).wait_send()

            @pl.when(k < self.Z - 1)
            def _():
                self.onward(a, k).wait_send()
            return carry
        lax.fori_loop(0, self.Z, one, 0)


def reduce_scratch(count, Z, shapes):
    half, n, dma = count // 2, len(shapes), pltpu.SemaphoreType.DMA
    bufs = [pltpu.VMEM(lead + s, bf16) for lead in ((count,), (half,), (2 * Z,), (Z,), (Z,)) for s in shapes]
    return bufs + [dma((n, half)), dma((n, half)), dma((n, 2 * Z)), dma((n, 2 * Z)), dma((n, Z)), dma((n, Z)),
                   dma((n, Z)), dma((n, Z))]


def pack_tail(tail, low_share, experts, skip_row, dsmall_ref, dvec_ref, dskip_ref, drouter_ref, dnorm_ref, dmoe_ref):
    blocks, share = tail.shape[:2]
    room, width = dvec_ref.shape[0], drouter_ref.shape[0]
    vec = jnp.where(subs(dvec_ref.shape) == skip_row, dskip_ref[...], dvec_ref[...])
    line = subs((8, width))
    gains = jnp.where(line == 0, dnorm_ref[...], jnp.where(line == 1, dmoe_ref[...], 0.0))
    model = drouter_ref[...] + dot_tn(gains.astype(bf16), spot(8, room + experts, TILE))
    model = jnp.concatenate(
        [model.reshape(blocks, low_share, TILE), jnp.zeros((blocks, share - low_share, TILE), f32)], axis=1)
    right = dot_tn(vec.astype(bf16), spot(room, 0, TILE)).reshape(blocks, share, TILE) + model
    tail[:, :, 0:TILE] = dsmall_ref[...].reshape(blocks, share, TILE)
    tail[:, :, TILE:] = right.astype(bf16)


def finish_kernel(dims, low_share, experts, tail_ref, halo_ref, in_ref, out_ref, block_hbm, tok_hbm, up_hbm, down_hbm,
                  block_out, tok_out, din, dconv, dbias, dstate, dstep, dstep_bias, ddecay, dskip, dout, dnorm, dmoe,
                  drouter, dup, ddown, block, tok, up, down, sems):
    seqs, rows, inner, states, rank, taps = dims
    moves = Moves(sems)
    routes = []
    for i in range(4):
        for src, at, dst in ((up_hbm, up, dup), (down_hbm, down, ddown)):
            n = src.shape[0] // 4
            piece = pl.ds(i * n, n)
            routes.append((len(routes), src.at[piece], at.at[piece], dst.at[piece]))
    routes.append(("tok", tok_hbm, tok, tok_out))
    routes.append(("block", block_hbm, block, block_out))
    for name, src, at, _ in routes:
        moves.start(name, src, at)
    din[...] = in_ref[...]
    dout[...] = out_ref[...]
    tail = tail_ref[...]
    wide = tail.shape[1]
    eye = (lanes((wide, wide)) == subs((wide, wide))).astype(bf16)
    high = tail.astype(bf16)
    turned = dot_nt(eye, high) + dot_nt(eye, (tail - high.astype(f32)).astype(bf16))
    dstate[...] = tail[:, : rank + 2 * states]
    dstep[...] = turned[TILE - rank : TILE]
    ddecay[...] = turned[TILE : TILE + states]
    dconv[...] = turned[TILE + states : TILE + states + taps]
    at = TILE + states + taps
    dbias[...] = turned[at : at + 1]
    dstep_bias[...] = turned[at + 1 : at + 2]
    dskip[...] = turned[at + 2 : at + 3]
    at = TILE + -(-(states + taps + 3) // 8) * 8
    drouter[...] = turned[at : at + experts, :low_share]
    at += experts
    dnorm[...] = turned[at : at + 1, :low_share]
    dmoe[...] = turned[at + 1 : at + 2, :low_share]
    for name, _, at, dst in routes:
        moves.wait(name)
        if name == "tok":
            tok[:, rows - 8 :] = tok[:, rows - 8 :] + halo_ref[...]
        moves.start("out", at, dst)
    moves.wait_all()


def tuned(batch, seq):
    return batch == 4 and seq == 8


def chain_kernel(seq, forward, dsum_ref, rates_ref, end_ref, out_ref, held, outgoing, send_sem, recv_sem):
    s = lax.axis_index("seq")
    b = lax.axis_index("batch")
    step = 1 if forward else -1
    has_before = s > 0 if forward else s < seq - 1
    has_after = s < seq - 1 if forward else s > 0
    before, after = (b, s - step), (b, s + step)
    barrier = pltpu.get_barrier_semaphore()
    for pred, dev in ((has_before, before), (has_after, after)):
        @pl.when(pred)
        def _(dev=dev):
            pl.semaphore_signal(barrier, inc=1, device_id=dev, device_id_type=MESH)
    pl.semaphore_wait(barrier, jnp.where(has_before, 1, 0) + jnp.where(has_after, 1, 0))
    count = end_ref.shape[0]

    def copy(i):
        return pltpu.make_async_remote_copy(
            src_ref=outgoing.at[i], dst_ref=held.at[i], send_sem=send_sem.at[i],
            recv_sem=recv_sem.at[i], device_id=after, device_id_type=MESH)

    for i in range(count):
        @pl.when(has_before)
        def _(i=i):
            copy(i).wait_recv()
            out_ref[i] = held[i].astype(jnp.float32)
            decay = jnp.exp(rates_ref[...] * dsum_ref[i])
            outgoing[i] = (end_ref[i] + decay * out_ref[i]).astype(jnp.bfloat16)

        @pl.when(jnp.logical_not(has_before))
        def _(i=i):
            out_ref[i] = jnp.zeros_like(out_ref[i])
            outgoing[i] = end_ref[i].astype(jnp.bfloat16)

        @pl.when(has_after)
        def _(i=i):
            copy(i).start()
    for i in range(count):
        @pl.when(has_after)
        def _(i=i):
            copy(i).wait_send()


def chain_states(seq, forward, dsum, rates, end):
    vm = pl.BlockSpec(memory_space=pltpu.VMEM)
    return pl.pallas_call(
        functools.partial(chain_kernel, seq, forward),
        out_shape=jax.ShapeDtypeStruct(end.shape, jnp.float32),
        in_specs=[vm] * 3,
        out_specs=vm,
        scratch_shapes=[
            pltpu.VMEM(end.shape, jnp.bfloat16),
            pltpu.VMEM(end.shape, jnp.bfloat16),
            pltpu.SemaphoreType.DMA((end.shape[0],)),
            pltpu.SemaphoreType.DMA((end.shape[0],)),
        ],
        compiler_params=pltpu.CompilerParams(
            collective_id=5 if forward else 6, has_side_effects=True),
        name="chain_forward" if forward else "chain_backward",
    )(dsum, rates, end)


class Relay:
    def __init__(self, seq, forward, states, dsum_ref, vec_ref, end_ref, out_ref, mine, theirs, their_sum, held,
                 outgoing, pair_send, pair_recv, line_send, line_recv):
        me = Place(4, seq)
        y, z, last = me.y, me.z, me.Z - 1
        step = 1 if forward else -1
        self.first = y == (0 if forward else 1)
        self.has_before = z > 0 if forward else z < last
        self.has_after = z < last if forward else z > 0
        self.pair, self.before, self.after = me.at(y=1 - y), me.at(z=z - step), me.at(z=z + step)
        self.states, self.vec_ref, self.end_ref, self.out_ref = states, vec_ref, end_ref, out_ref
        self.mine, self.theirs, self.dsum_ref, self.their_sum = mine, theirs, dsum_ref, their_sum
        self.held, self.outgoing = held, outgoing
        self.pair_send, self.pair_recv, self.line_send, self.line_recv = pair_send, pair_recv, line_send, line_recv
        self.count = end_ref.shape[0]

    def peers(self):
        return [(None, self.pair), (self.has_before, self.before), (self.has_after, self.after)]

    def swaps(self, i):
        both = ((self.mine.at[i], self.theirs.at[i]), (self.dsum_ref.at[i], self.their_sum.at[i]))
        return [
            pltpu.make_async_remote_copy(
                src_ref=src, dst_ref=dst, send_sem=self.pair_send.at[i, k], recv_sem=self.pair_recv.at[i, k],
                device_id=self.pair, device_id_type=MESH)
            for k, (src, dst) in enumerate(both)
        ]

    def onward(self, i):
        return pltpu.make_async_remote_copy(
            src_ref=self.outgoing.at[i], dst_ref=self.held.at[i], send_sem=self.line_send.at[i],
            recv_sem=self.line_recv.at[i], device_id=self.after, device_id_type=MESH)

    def start(self, i):
        self.mine[i] = self.end_ref[i].astype(bf16)
        for cp in self.swaps(i):
            cp.start()

    def finish(self, i):
        rates = -jnp.exp(self.vec_ref[0 : self.states])
        for cp in self.swaps(i):
            cp.wait_recv()
        pick = lambda a, b: (jnp.where(self.first, a, b), jnp.where(self.first, b, a))
        early, late = pick(self.end_ref[i], self.theirs[i].astype(f32))
        early_sum, late_sum = pick(self.dsum_ref[i], self.their_sum[i])
        both = late + jnp.exp(rates * late_sum) * early

        @pl.when(self.has_before)
        def _():
            self.onward(i).wait_recv()
            arrived = self.held[i].astype(f32)
            self.outgoing[i] = (both + jnp.exp(rates * (early_sum + late_sum)) * arrived).astype(bf16)

        @pl.when(jnp.logical_not(self.has_before))
        def _():
            self.outgoing[i] = both.astype(bf16)

        @pl.when(self.has_after)
        def _():
            self.onward(i).start()

        @pl.when(self.has_before)
        def _():
            arrived = self.held[i].astype(f32)
            self.out_ref[i] = jnp.where(self.first, arrived, early + jnp.exp(rates * early_sum) * arrived)

        @pl.when(jnp.logical_not(self.has_before))
        def _():
            self.out_ref[i] = jnp.where(self.first, jnp.zeros_like(early), early)

    def settle(self):
        for i in range(self.count):
            for cp in self.swaps(i):
                cp.wait_send()
            pl.when(self.has_after)(self.onward(i).wait_send)


def relay_scratch(seqs, states, inner):
    n, state = seqs, (seqs, states, inner)
    dma = pltpu.SemaphoreType.DMA
    return [
        pltpu.VMEM(state, bf16),
        pltpu.VMEM(state, bf16),
        pltpu.VMEM((seqs, 1, inner), f32),
        pltpu.VMEM(state, bf16),
        pltpu.VMEM(state, bf16),
        dma((n, 2)),
        dma((n, 2)),
        dma((n,)),
        dma((n,)),
    ]


def dot(a, b):
    return jnp.dot(a, b, preferred_element_type=jnp.float32)


def dot_nt(a, b):
    return lax.dot_general(a, b, (((1,), (1,)), ((), ())), preferred_element_type=jnp.float32)


def dot_tn(a, b):
    return lax.dot_general(a, b, (((0,), (0,)), ((), ())), preferred_element_type=jnp.float32)


def sigmoid(v):
    return 1.0 / (1.0 + jnp.exp(-v))


def lanes(shape):
    return lax.broadcasted_iota(jnp.int32, shape, 1)


def subs(shape):
    return lax.broadcasted_iota(jnp.int32, shape, 0)


def column(row, base, states):
    shape = (states, row.shape[1])
    only = jnp.where(lanes(shape) == subs(shape) + base, jnp.broadcast_to(row, shape), 0.0)
    return jnp.broadcast_to(jnp.sum(only, axis=1, keepdims=True), shape)


def row_sums(parts):
    row = subs(parts[0].shape)
    four, two, one = row < 4, (row // 2) % 2 == 0, row % 2 == 0
    turn = lambda v, by: pltpu.roll(v, by, axis=0)
    a = [
        jnp.where(four, parts[j], parts[j + 4]) + turn(jnp.where(four, parts[j + 4], parts[j]), 4)
        for j in range(4)
    ]
    b = [jnp.where(two, a[j] + turn(a[j], 6), a[j + 2] + turn(a[j + 2], 2)) for j in range(2)]
    return jnp.where(one, b[0] + turn(b[0], 7), b[1] + turn(b[1], 1))


def fold(v):
    return sum(v[i : i + 8] for i in range(8, v.shape[0], 8)) + v[:8]


WIDE = 256
GROUP = 16
LOG2E = math.log2(math.e)


def conv_sum(ext_ref, s, cols, vec_ref, states, taps, rows):
    first = ext_ref.shape[1] - rows - taps + 1
    total = vec_ref[states + taps : states + taps + 1, cols]
    for k in range(taps):
        total = total + vec_ref[states + k : states + k + 1, cols] * ext_ref[s, first + k : first + k + rows, cols]
    return total


def normalize(x):
    return lax.rsqrt(jnp.mean(x * x, axis=-1, keepdims=True) + epsilon)


class Quiet:
    def __getattr__(self, name):
        return lambda *args: None


QUIET = Quiet()


class Hooks(Quiet):
    def __init__(self, **steps):
        self.__dict__.update(steps)


def unpack(tail_ref, share, low_share, room, experts, vec_ref, gain_ref, router_ref):
    right = tail_ref[:, TILE : 2 * TILE]
    vec_ref[...] = dot_nt(spot(room, 0, TILE), right)
    blocks = right.shape[0] // share
    model = right.astype(f32).reshape(blocks, share, TILE)[:, :low_share].reshape(blocks * low_share, TILE).astype(bf16)
    router_ref[...] = model
    gain_ref[...] = dot_nt(spot(gain_ref.shape[0], room + experts, TILE), model)


def enter_packed(dims, share, low_share, experts, tok_ref, halo_ref, win_ref, tail_ref,
                 ext_ref, z_ref, u_ref, dt_ref, proj_ref, end_ref, dsum_ref, vec_ref, gain_ref, router_ref, xn,
                 hooks=QUIET):
    unpack(tail_ref, share, low_share, vec_ref.shape[0], experts, vec_ref, gain_ref, router_ref)
    enter_kernel(dims, tok_ref, halo_ref, win_ref, tail_ref.at[:, 0:TILE], vec_ref, gain_ref,
                 ext_ref, z_ref, u_ref, dt_ref, proj_ref, end_ref, dsum_ref, xn, hooks)


def as_column(ref):
    seqs, rows = ref.shape
    diagonal = lanes((rows, rows)) == subs((rows, rows))
    spread = [
        jnp.where(diagonal, jnp.broadcast_to(ref[s : s + 1].astype(f32), (rows, rows)), 0.0) for s in range(seqs)
    ]
    return jnp.concatenate([jnp.sum(v, axis=1, keepdims=True) for v in spread]).astype(jnp.int32)


def enter_kernel(dims, tok_ref, halo_ref, win_ref, small_ref, vec_ref, gain_ref,
                 ext_ref, z_ref, u_ref, dt_ref, proj_ref, end_ref, dsum_ref, xn, hooks=QUIET):
    seqs, rows, inner, states, rank, taps = dims
    count = seqs * rows
    for ref, at in ((tok_ref, 0), (halo_ref, count)):
        x = ref[...].astype(jnp.float32)
        xn[at : at + x.shape[0]] = (x * normalize(x) * gain_ref[0:1]).astype(jnp.bfloat16)
    proj = jnp.zeros((count, small_ref.shape[1]), jnp.float32)
    for j in range(inner // WIDE):
        cols = slice(j * WIDE, (j + 1) * WIDE)
        hooks.weights(j)
        part = dot(xn[...], win_ref[:, cols])
        z_ref[:, cols] = dot(xn[:count], win_ref[:, inner + j * WIDE : inner + (j + 1) * WIDE])
        for s in range(seqs):
            ext_ref[s, 0:8, cols] = part[count + 8 * s : count + 8 * s + 8]
            ext_ref[s, 8:, cols] = part[s * rows : (s + 1) * rows]
            pre = conv_sum(ext_ref, s, cols, vec_ref, states, taps, rows)
            u_ref[s * rows : (s + 1) * rows, cols] = pre * sigmoid(pre)
        proj = proj + dot(u_ref[:, cols].astype(jnp.bfloat16), small_ref[cols, :])
    proj_ref[...] = proj
    low = rank_lanes(proj, rank, states)
    for j in range(inner // WIDE):
        cols = slice(j * WIDE, (j + 1) * WIDE)
        pre = dot_nt(low, small_ref[cols, :]) + vec_ref[states + taps + 1 : states + taps + 2, cols]
        dt = jnp.maximum(pre, 0.0) + jnp.log1p(jnp.exp(-jnp.abs(pre)))
        dt_ref[:, cols] = dt
        for s in range(seqs):
            dsum_ref[s, 0:1, cols] = jnp.sum(dt[s * rows : (s + 1) * rows], axis=0, keepdims=True)
    hooks.projected()
    a2 = -jnp.exp(vec_ref[0:states]) * LOG2E
    blocks = inner // 128
    for s in range(seqs):
        def eight(i, hs):
            hs = list(hs)
            at = pl.multiple_of(s * rows + i * 8, 8)
            small = proj_ref[pl.ds(at, 8), :]
            bs = [column(small[j : j + 1], rank, states) for j in range(8)]
            for k in range(blocks):
                sl = slice(k * 128, (k + 1) * 128)
                d8 = dt_ref[pl.ds(at, 8), sl]
                w8 = d8 * u_ref[pl.ds(at, 8), sl]
                for j in range(8):
                    hs[k] = jnp.exp2(d8[j : j + 1] * a2[:, sl]) * hs[k] + bs[j] * w8[j : j + 1]
            return tuple(hs)
        zero = jnp.zeros((states, 128), jnp.float32)
        hs = lax.fori_loop(0, rows // 8, eight, (zero,) * blocks)
        for k in range(blocks):
            end_ref[s, :, k * 128 : (k + 1) * 128] = hs[k]
        hooks.scanned(s)


def rank_lanes(proj, rank, states):
    at = rank + 2 * states
    moved = pltpu.roll(proj, at, axis=1)
    return jnp.where(lanes(proj.shape) >= at, moved, 0.0).astype(jnp.bfloat16)


def leave_kernel(dims, capacity, room, tok_ref, cot_ref, h0_ref, dt_ref, u_ref, z_ref, proj_ref, vec_ref, out_ref,
                 gain_ref, router_ref, route_ref, slot_ref,
                 hist_ref, y_ref, hid_ref, gated_ref, moe_ref, gate_ref, rows_ref,
                 hbuf, hcur, sem, sem0, hooks=QUIET):
    seqs, rows, inner, states, rank, taps = dims
    count = seqs * rows
    a2 = -jnp.exp(vec_ref[0:states]) * LOG2E
    blocks = inner // 128
    groups = rows // GROUP
    size = GROUP * states
    firsts = []
    for s in range(seqs):
        hcur[s] = h0_ref[s].astype(jnp.bfloat16)
        cp = pltpu.make_async_copy(hcur.at[s], hist_ref.at[s, pl.ds(0, states)], sem0.at[s])
        cp.start()
        firsts.append(cp)

    def out_copy(s, g, slot):
        at = pl.multiple_of(states + g * size, states)
        return pltpu.make_async_copy(hbuf.at[slot], hist_ref.at[s, pl.ds(at, size)], sem.at[slot])

    for s in range(seqs):
        def group(g, hs):
            hs = list(hs)
            slot = g % 2

            @pl.when(g >= 2)
            def _():
                out_copy(s, g - 2, slot).wait()
            for half in range(GROUP // 8):
                at = pl.multiple_of(s * rows + g * GROUP + half * 8, 8)
                small = proj_ref[pl.ds(at, 8), :]
                bs = [column(small[j : j + 1], rank, states) for j in range(8)]
                cs = [column(small[j : j + 1], rank + states, states) for j in range(8)]
                for k in range(blocks):
                    sl = slice(k * 128, (k + 1) * 128)
                    d8 = dt_ref[pl.ds(at, 8), sl]
                    w8 = d8 * u_ref[pl.ds(at, 8), sl]
                    parts = []
                    for j in range(8):
                        t = half * 8 + j
                        hs[k] = jnp.exp2(d8[j : j + 1] * a2[:, sl]) * hs[k] + bs[j] * w8[j : j + 1]
                        hbuf[slot, t * states : (t + 1) * states, sl] = hs[k].astype(jnp.bfloat16)
                        parts.append(fold(cs[j] * hs[k]))
                    y_ref[pl.ds(at, 8), sl] = row_sums(parts)
            out_copy(s, g, slot).start()
            return tuple(hs)
        hs = tuple(h0_ref[s, :, k * 128 : (k + 1) * 128] for k in range(blocks))
        lax.fori_loop(0, groups, group, hs)
        hooks.half(s)
        for g in (groups - 2, groups - 1):
            out_copy(s, g, g % 2).wait()
    for cp in firsts:
        cp.wait()
    hooks.out_proj()
    hid = tok_ref[...].astype(jnp.float32)
    for j in range(inner // WIDE):
        cols = slice(j * WIDE, (j + 1) * WIDE)
        y = y_ref[:, cols] + vec_ref[states + taps + 2 : states + taps + 3, cols] * u_ref[:, cols]
        y_ref[:, cols] = y
        z = z_ref[:, cols]
        gated = (y * (z * sigmoid(z))).astype(jnp.bfloat16)
        gated_ref[:, cols] = gated
        hid = hid + dot(gated, out_ref[cols, :])
    hooks.mixed()
    hid_ref[...] = hid
    moe_in = (hid * normalize(hid) * gain_ref[1:2]).astype(jnp.bfloat16)
    moe_ref[...] = moe_in
    logits = dot(moe_in, router_ref[...])
    route, slot = as_column(route_ref), as_column(slot_ref)
    chosen = lanes(logits.shape) == route + room
    gate = sigmoid(jnp.sum(jnp.where(chosen, logits, 0.0), axis=1, keepdims=True))
    gate_ref[...] = gate
    kept = (slot < capacity).astype(jnp.float32)
    grad_rows = (cot_ref[...].astype(jnp.float32) * (gate * kept)).astype(jnp.bfloat16)
    total = rows_ref.shape[0]
    place = jnp.where(slot_ref[...] < capacity, route_ref[...] * capacity + slot_ref[...], -1)
    place = jnp.concatenate([place[s : s + 1] for s in range(seqs)], axis=1)
    pick = (subs((total, count)) == place).astype(jnp.bfloat16)
    width = moe_in.shape[1]
    rows_ref[:, :width] = dot(pick, moe_in).astype(jnp.bfloat16)
    rows_ref[:, width:] = dot(pick, grad_rows).astype(jnp.bfloat16)


def erf(x):
    x = jnp.clip(x, -4.0, 4.0)
    x2 = x * x
    top = (-2.72614225801306e-10, 2.77068142495902e-08, -2.10102402082508e-06, -5.69250639462346e-05,
           -7.34990630326855e-04, -2.95459980854025e-03, -1.60960333262415e-02)
    low = (-1.45660718464996e-05, -2.13374055278905e-04, -1.68282697438203e-03, -7.37332916720468e-03,
           -1.42647390514189e-02)
    p = jnp.full_like(x2, top[0])
    for c in top[1:]:
        p = p * x2 + c
    q = jnp.full_like(x2, low[0])
    for c in low[1:]:
        q = q * x2 + c
    return x * p / q


def expert_kernel(rows_ref, up_ref, down_ref, part_ref, dup_ref, ddown_ref):
    width = up_ref.shape[0]
    x, g = rows_ref[:, :width], rows_ref[:, width:]
    hidden = dot(x, up_ref[...])
    half = 0.5 * (1.0 + erf(hidden * math.sqrt(0.5)))
    act = (hidden * half).astype(jnp.bfloat16)
    slope = half + hidden * (jnp.exp(-0.5 * hidden * hidden) * (1.0 / math.sqrt(2.0 * math.pi)))
    part_ref[:, :width] = dot(act, down_ref[...]).astype(jnp.bfloat16)
    grad_hidden = (dot_nt(g, down_ref[...]) * slope).astype(jnp.bfloat16)
    part_ref[:, width:] = dot_nt(grad_hidden, up_ref[...]).astype(jnp.bfloat16)
    ddown, dup = dot_tn(act, g), dot_tn(x, grad_hidden)

    @pl.when(pl.program_id(0) == 0)
    def _():
        dup_ref[...] = dup
        ddown_ref[...] = ddown

    @pl.when(pl.program_id(0) > 0)
    def _():
        dup_ref[...] += dup
        ddown_ref[...] += ddown


def return_kernel(dims, capacity, room, ret_ref, cot_ref, hid_ref, moe_ref, gate_ref, gated_ref, y_ref, u_ref, z_ref, dt_ref,
                  proj_ref, vec_ref, out_ref, gain_ref, router_ref, route_ref, slot_ref,
                  block_ref, ghid_ref, gy_ref, gz_ref, dout_ref, drouter_ref, dskip_ref, dgain_ref, adj_ref,
                  hooks=QUIET):
    seqs, rows, inner, states, rank, taps = dims
    count = seqs * rows
    total, width = ret_ref.shape[0], hid_ref.shape[1]
    route, slot = as_column(route_ref), as_column(slot_ref)
    place = jnp.where(slot < capacity, route * capacity + slot, -1)
    pick = (lanes((count, total)) == place).astype(jnp.bfloat16)
    result = dot(pick, ret_ref[:, :width])
    hid, gate = hid_ref[...], gate_ref[...]
    block_ref[...] = (hid + gate * result).astype(jnp.bfloat16)
    cot = cot_ref[...].astype(jnp.float32)
    grad_gate = jnp.sum(cot * result, axis=1, keepdims=True)
    wide = (count, router_ref.shape[1])
    grad_logits = jnp.where(lanes(wide) == route + room, grad_gate * gate * (1.0 - gate), 0.0).astype(jnp.bfloat16)
    grad_in = dot(pick, ret_ref[:, width:]) + dot_nt(grad_logits, router_ref[...])
    drouter_ref[...] = dot_tn(moe_ref[...], grad_logits)
    r2 = normalize(hid)
    dgain_ref[...] = jnp.sum(grad_in * (hid * r2), axis=0, keepdims=True)
    scaled = grad_in * gain_ref[1:2]
    grad_hid = cot + r2 * scaled - hid * (r2 * r2 * r2) * jnp.mean(scaled * hid, axis=1, keepdims=True)
    ghid_ref[...] = grad_hid
    branch = grad_hid.astype(jnp.bfloat16)
    hooks.activations()
    for j in range(inner // WIDE):
        cols = slice(j * WIDE, (j + 1) * WIDE)
        if dout_ref is not None:
            dout_ref[cols, :] = dot_tn(gated_ref[:, cols], branch).astype(jnp.bfloat16)
        grad = dot_nt(branch, out_ref[cols, :])
        z = z_ref[:, cols]
        sig = sigmoid(z)
        gy = grad * (z * sig)
        gy_ref[:, cols] = gy
        gz_ref[:, cols] = (grad * y_ref[:, cols] * (sig + z * sig * (1.0 - sig))).astype(jnp.bfloat16)
        dskip_ref[:, cols] = jnp.sum(gy * u_ref[:, cols], axis=0, keepdims=True)
    hooks.gradients()
    a2 = -jnp.exp(vec_ref[0:states]) * LOG2E
    blocks = inner // 128
    for s in range(seqs):
        def eight(i, ms):
            ms = list(ms)
            at = pl.multiple_of((s + 1) * rows - 8 - i * 8, 8)
            small = proj_ref[pl.ds(at, 8), :]
            cs = [column(small[j : j + 1], rank + states, states) for j in range(8)]
            for k in range(blocks):
                sl = slice(k * 128, (k + 1) * 128)
                d8, g8 = dt_ref[pl.ds(at, 8), sl], gy_ref[pl.ds(at, 8), sl]
                for j in reversed(range(8)):
                    ms[k] = jnp.exp2(d8[j : j + 1] * a2[:, sl]) * (ms[k] + cs[j] * g8[j : j + 1])
            return tuple(ms)
        zero = jnp.zeros((states, 128), jnp.float32)
        ms = lax.fori_loop(0, rows // 8, eight, (zero,) * blocks)
        for k in range(blocks):
            adj_ref[s, :, k * 128 : (k + 1) * 128] = ms[k]
        hooks.scanned(s)


def back_kernel(dims, tok_ref, halo_ref, ext_ref, hist_ref, later_ref, gy_ref, gz_ref, ghid_ref, u_ref, dt_ref,
                proj_ref, win_ref, small_ref, vec_ref, gain_ref,
                dtok_ref, dhalo_ref, din_ref, dsmall_ref, dvec_ref, dgain_ref,
                hbuf, ccol, bcol, gbsum, gcsum, adj, gdt, gu, gproj, gpad, gm, xn, gpre, sem, hooks=QUIET, in_grads=None):
    small_ref = small_ref.at[:, 0:TILE]
    seqs, rows, inner, states, rank, taps = dims
    count = seqs * rows
    groups = rows // GROUP
    size = GROUP * states
    steps = seqs * groups

    def fetch(i, slot):
        s, g = i // groups, groups - 1 - i % groups
        at = pl.multiple_of(g * size, size)
        return pltpu.make_async_copy(hist_ref.at[s, pl.ds(at, size + states)], hbuf.at[slot], sem.at[slot])

    fetch(0, 0).start()
    dvec_ref[...] = jnp.zeros_like(dvec_ref)
    strip = 512

    def group(i, carry):
        slot = i % 2
        s, g = i // groups, groups - 1 - i % groups

        @pl.when(i + 1 < steps)
        def _():
            fetch(i + 1, 1 - slot).start()

        @pl.when(g == groups - 1)
        def _():
            adj[...] = later_ref[s]
        at = pl.multiple_of(s * rows + g * GROUP, GROUP)
        small = proj_ref[pl.ds(at, GROUP), :]
        for t in range(GROUP):
            ccol[t] = column(small[t : t + 1], rank + states, states)
            bcol[t] = column(small[t : t + 1], rank, states)
            gbsum[t] = jnp.zeros((states, 128), f32)
            gcsum[t] = jnp.zeros((states, 128), f32)
        fetch(i, slot).wait()
        hooks.group(i)
        for c0 in range(0, inner, strip):
            sls = [slice(c0 + k, c0 + k + 128) for k in range(0, strip, 128)]
            scaled = [-jnp.exp(vec_ref[0:states, sl]) * LOG2E for sl in sls]
            m = [adj[:, sl] for sl in sls]
            dd = [dvec_ref[0:states, sl] for sl in sls]
            now = [hbuf[slot, GROUP * states : (GROUP + 1) * states, sl].astype(f32) for sl in sls]
            for half in reversed(range(GROUP // 8)):
                a8 = pl.multiple_of(at + half * 8, 8)
                d8 = [dt_ref[pl.ds(a8, 8), sl] for sl in sls]
                g8 = [gy_ref[pl.ds(a8, 8), sl] for sl in sls]
                u8 = [u_ref[pl.ds(a8, 8), sl] for sl in sls]
                w8 = [d * u for d, u in zip(d8, u8)]
                r1, r2 = [[None] * 8 for _ in sls], [[None] * 8 for _ in sls]
                for j in reversed(range(8)):
                    t = half * 8 + j
                    gb = gc = 0.0
                    for k, sl in enumerate(sls):
                        d, gy = d8[k][j : j + 1], g8[k][j : j + 1]
                        a = m[k] + ccol[t] * gy
                        m[k] = jnp.exp2(d * scaled[k]) * a
                        gb = gb + a * w8[k][j : j + 1]
                        gc = gc + gy * now[k]
                        now[k] = hbuf[slot, t * states : (t + 1) * states, sl].astype(f32)
                        p = m[k] * now[k] * scaled[k]
                        dd[k] = dd[k] + p * d
                        r1[k][j], r2[k][j] = fold(p), fold(a * bcol[t])
                    gbsum[t] += gb
                    gcsum[t] += gc
                for k, sl in enumerate(sls):
                    w1, w2 = row_sums(r1[k]), row_sums(r2[k])
                    gdt[pl.ds(a8, 8), sl] = w1 * (1.0 / LOG2E) + u8[k] * w2
                    gu[pl.ds(a8, 8), sl] = d8[k] * w2
            for k, sl in enumerate(sls):
                adj[:, sl] = m[k]
                dvec_ref[0:states, sl] = dd[k]
        square = (states, small.shape[1])
        where, entry = lanes(square), subs(square)
        line = subs((GROUP, small.shape[1]))
        out = jnp.zeros(small.shape, f32)
        for t in range(GROUP):
            gb = jnp.broadcast_to(jnp.sum(gbsum[t], axis=1, keepdims=True), square)
            gc = jnp.broadcast_to(jnp.sum(gcsum[t], axis=1, keepdims=True), square)
            put = jnp.where(where == entry + rank, gb, jnp.where(where == entry + rank + states, gc, 0.0))
            out = jnp.where(line == t, jnp.sum(put, axis=0, keepdims=True), out)
        gproj[pl.ds(at, GROUP), :] = out
        return carry
    lax.fori_loop(0, steps, group, 0)
    dvec_ref[0:states] = dvec_ref[0:states] * (1.0 / LOG2E)
    hooks.rest()

    low = rank_lanes(proj_ref[...], rank, states)
    at = rank + 2 * states
    row = states + taps
    grad_rank = jnp.zeros(proj_ref.shape, jnp.float32)
    for j in range(inner // WIDE):
        cols = slice(j * WIDE, (j + 1) * WIDE)
        pre = dot_nt(low, small_ref[cols, :]) + vec_ref[row + 1 : row + 2, cols]
        grad_pre = gdt[:, cols] * sigmoid(pre)
        dvec_ref[row + 1 : row + 2, cols] = jnp.sum(grad_pre, axis=0, keepdims=True)
        grad_pre = grad_pre.astype(jnp.bfloat16)
        gpre[:, cols] = grad_pre
        grad_rank = grad_rank + dot(grad_pre, small_ref[cols, :])
    where = lanes(grad_rank.shape)
    grad_rank = pltpu.roll(grad_rank, small_ref.shape[1] - at, axis=1)
    grad_proj = jnp.where(where < rank, grad_rank, jnp.where(where < at, gproj[...], 0.0)).astype(jnp.bfloat16)
    for ref, to in ((tok_ref, 0), (halo_ref, count)):
        x = ref[...].astype(jnp.float32)
        xn[to : to + x.shape[0]] = (x * normalize(x) * gain_ref[0:1]).astype(jnp.bfloat16)
    grad_normed = jnp.zeros((gm.shape[0], xn.shape[1]), jnp.float32)
    first = ext_ref.shape[1] - rows - taps + 1
    for j in range(inner // WIDE):
        cols = slice(j * WIDE, (j + 1) * WIDE)
        dsmall_ref[cols, :] = (
            dot_tn(u_ref[:, cols].astype(jnp.bfloat16), grad_proj) + dot_tn(gpre[:, cols], low)
        ).astype(jnp.bfloat16)
        grad_u = dot_nt(grad_proj, small_ref[cols, :]) + gy_ref[:, cols] * vec_ref[row + 2 : row + 3, cols] + gu[:, cols]
        taps_sum = [0.0] * taps
        bias_sum = 0.0
        heads = []
        for s in range(seqs):
            pre = conv_sum(ext_ref, s, cols, vec_ref, states, taps, rows)
            sig = sigmoid(pre)
            grad_conv = grad_u[s * rows : (s + 1) * rows] * (sig + pre * sig * (1.0 - sig))
            bias_sum = bias_sum + jnp.sum(grad_conv, axis=0, keepdims=True)
            for k in range(taps):
                taps_sum[k] = taps_sum[k] + jnp.sum(
                    grad_conv * ext_ref[s, first + k : first + k + rows, cols], axis=0, keepdims=True)
            gpad[0:8] = jnp.zeros((8, WIDE), jnp.float32)
            gpad[8 : 8 + rows] = grad_conv
            gpad[8 + rows :] = jnp.zeros((8, WIDE), jnp.float32)
            grad = 0.0
            for k in range(taps):
                grad = grad + vec_ref[states + k : states + k + 1, cols] * gpad[taps - 1 - k : taps + 7 - k + rows]
            heads.append(grad[0:8])
            gm[s * rows : (s + 1) * rows, cols] = grad[8:].astype(jnp.bfloat16)
        gm[count:, cols] = jnp.concatenate(heads).astype(jnp.bfloat16)
        dvec_ref[row : row + 1, cols] = bias_sum
        for k in range(taps):
            dvec_ref[states + k : states + k + 1, cols] = taps_sum[k]
    if in_grads is None:
        for j in range(inner // WIDE):
            cols, zcols = (slice(at + j * WIDE, at + (j + 1) * WIDE) for at in (0, inner))
            din_ref[:, cols] = dot_tn(xn[...], gm[:, cols]).astype(jnp.bfloat16)
            din_ref[:, zcols] = dot_tn(xn[:count], gz_ref[:, cols]).astype(jnp.bfloat16)
    else:
        in_grads()
    for j in range(inner // WIDE):
        cols, zcols = (slice(at + j * WIDE, at + (j + 1) * WIDE) for at in (0, inner))
        gz = jnp.concatenate([gz_ref[:, cols], jnp.zeros((gm.shape[0] - count, WIDE), jnp.bfloat16)])
        grad_normed = grad_normed + dot_nt(gm[:, cols], win_ref[:, cols]) + dot_nt(gz, win_ref[:, zcols])
    gain_sum = 0.0
    for ref, to, base, out in ((tok_ref, 0, ghid_ref, dtok_ref), (halo_ref, count, None, dhalo_ref)):
        x = ref[...].astype(jnp.float32)
        r1 = normalize(x)
        grad = grad_normed[to : to + x.shape[0]]
        gain_sum = gain_sum + jnp.sum(grad * (x * r1), axis=0, keepdims=True)
        grad = grad * gain_ref[0:1]
        grad = r1 * grad - x * (r1 * r1 * r1) * jnp.mean(grad * x, axis=1, keepdims=True)
        out[...] = grad if base is None else grad + base[...]
    dgain_ref[...] = gain_sum


def like(*shape, dtype=f32):
    return jax.ShapeDtypeStruct(shape, dtype)


def params(mib=56):
    return pltpu.CompilerParams(vmem_limit_bytes=mib << 20)


def moe_kernel(seq, rows_ref, up_ref, down_ref,
               back_ref, land_ref, dup_ref, ddown_ref,
               xbuf, part, act, ghid, hid, gact, far_buf, own_sum, up2_ref, down2_ref, dup2, ddown2, dup3, ddown3,
               local_sem, disp_sem, pass_sem, recv_sem, load_sem, far_send, far_recv,
               final_send, final_recv, final_local, swap_send, swap_recv):
    me = Place(4, seq)
    b, s = me.at()
    y, z, Z, x = me.y, me.z, me.Z, me.x
    cap, wide = rows_ref.shape[1], rows_ref.shape[2]
    width = wide // 2
    share = up_ref.shape[1]
    two = 2 * cap
    block = 2 * two
    sib, nx = me.at(c=1 - me.c), me.at(x=1 - x)
    greet([(None, sib), (None, nx)] + [(None, (b, (s + k) % seq)) for k in range(1, seq)])

    def remote(src, dst, send, recv, dev):
        return pltpu.make_async_remote_copy(
            src_ref=src, dst_ref=dst, send_sem=send, recv_sem=recv, device_id=dev, device_id_type=MESH)

    def slab(xx, ss):
        return land_ref.at[xx, pl.ds(pl.multiple_of(ss * cap, 8), cap)]

    def there(k, j):
        return ((z + k) % Z) * 2 + j

    def arrived(xx, ss):
        remote(slab(xx, ss), slab(xx, ss), disp_sem.at[0], recv_sem.at[xx, ss], nx).wait_recv()

    def hand(ss):
        return remote(slab(x, ss), slab(x, ss), pass_sem.at[ss], recv_sem.at[x, ss], nx)

    def load(k, xx):
        zz = (z + k) % Z
        return pltpu.make_async_copy(
            land_ref.at[xx, pl.ds(pl.multiple_of(zz * two, 8), two)],
            xbuf.at[k, pl.ds(pl.multiple_of(xx * two, 16), two)], load_sem.at[k, xx])

    def dispatch(k, j):
        to = ((z + Z - k) % Z) * 2 + j
        return remote(rows_ref.at[to], slab(x, s), disp_sem.at[2 * k + j], recv_sem.at[x, s], (b, to))

    dispatch(0, 1 - y).start()
    own = remote(rows_ref.at[s], slab(x, s), pass_sem.at[s], recv_sem.at[x, s], nx)
    own.start()
    local = pltpu.make_async_copy(rows_ref.at[s], slab(x, s), local_sem)
    local.start()
    for j in range(2):
        dispatch(1, j).start()

    def swap(i, src, dst):
        return remote(src, dst, swap_send.at[i], swap_recv.at[i], sib)

    weights = [swap(0, up_ref, up2_ref), swap(1, down_ref, down2_ref)]
    for cp in weights:
        cp.start()
    ups, downs = (up_ref, up2_ref), (down_ref, down2_ref)

    def compute(k):
        for i in range(2):
            for n in range(0, share, WIDE):
                to = slice(i * share + n, i * share + n + WIDE)
                hid[:, to] = dot(xbuf[k, :, :width], ups[i][:, n : n + WIDE])
                gact[:, to] = dot_nt(xbuf[k, :, width:], downs[i][n : n + WIDE, :])

        def sixteen(r, carry):
            at = pl.ds(pl.multiple_of(r * 16, 16), 16)
            to = pl.ds(pl.multiple_of(k * block + r * 16, 16), 16)
            h = hid[at, :]
            half = 0.5 * (1.0 + erf(h * math.sqrt(0.5)))
            act[to, :] = (h * half).astype(bf16)
            slope = half + h * (jnp.exp(-0.5 * h * h) * (1.0 / math.sqrt(2.0 * math.pi)))
            ghid[to, :] = (gact[at, :] * slope).astype(bf16)
            return carry
        lax.fori_loop(0, block // 16, sixteen, 0)
        mine = pl.ds(pl.multiple_of(k * block, 16), block)
        for n in range(0, width, WIDE):
            cols = slice(n, n + WIDE)
            part[k, :, cols] = (
                dot(act[mine, :share], down_ref[:, cols]) + dot(act[mine, share:], down2_ref[:, cols])
            ).astype(bf16)
            part[k, :, width + n : width + n + WIDE] = (
                dot_nt(ghid[mine, :share], up_ref[cols, :]) + dot_nt(ghid[mine, share:], up2_ref[cols, :])
            ).astype(bf16)

    def of_chip(k, xx):
        return part.at[k, pl.ds(pl.multiple_of(xx * two, 16), two)]

    def to_far(k):
        return remote(of_chip(k, 1 - x), far_buf.at[k], far_send.at[k], far_recv.at[k], nx)

    def to_home(k, j):
        return remote(own_sum.at[k, j], back_ref.at[s], final_send.at[k, j], final_recv.at[s], (b, there(k, j)))

    def keep_home():
        return pltpu.make_async_copy(own_sum.at[0, y], back_ref.at[s], final_local)

    def own_stage(k):
        @pl.when(k == 0)
        def _():
            arrived(x, z * 2 + 1 - y)
            hand(z * 2 + 1 - y).start()
            local.wait()

        @pl.when(k > 0)
        def _():
            for j in range(2):
                arrived(x, there(k, j))
                hand(there(k, j)).start()

        @pl.when(k < Z - 2)
        def _():
            for j in range(2):
                dispatch(k + 2, j).start()
        load(k, x).start()

    def compute_stage(k):
        for j in range(2):
            arrived(1 - x, there(k, j))
        load(k, 1 - x).start()
        for xx in range(2):
            load(k, xx).wait()

        @pl.when(k == 0)
        def _():
            for cp in weights:
                cp.wait_recv()
        compute(k)
        to_far(k).start()

    def home_stage(k):
        to_far(k).wait_recv()
        total = of_chip(k, x)[...].astype(f32) + far_buf[k].astype(f32)
        for j in range(2):
            own_sum[k, j] = total[j * cap : (j + 1) * cap].astype(bf16)

        @pl.when(k > 0)
        def _():
            for j in range(2):
                to_home(k, j).start()

        @pl.when(k == 0)
        def _():
            keep_home().start()
            to_home(0, 1 - y).start()

    everything = (Z * block, width)
    stages = ((own_stage, 0), (home_stage, 2), (compute_stage, 1))

    def step(t, carry):
        for stage, lag in stages:
            k = t - lag
            pl.when(jnp.logical_and(k >= 0, k < Z))(functools.partial(stage, k))
        return carry
    lax.fori_loop(0, Z + 2, step, 0)
    x_all = lambda: xbuf[:, :, :width].reshape(everything)
    g_all = lambda: xbuf[:, :, width:].reshape(everything)
    grads = [swap(2, dup2, dup3), swap(3, ddown2, ddown3)]
    for n in range(0, share, WIDE):
        dup2[:, n : n + WIDE] = dot_tn(x_all(), ghid[:, share + n : share + n + WIDE]).astype(bf16)
    grads[0].start()
    for n in range(0, share, WIDE):
        ddown2[n : n + WIDE, :] = dot_tn(act[:, share + n : share + n + WIDE], g_all()).astype(bf16)
    grads[1].start()
    for n in range(0, share, WIDE):
        dup_ref[:, n : n + WIDE] = dot_tn(x_all(), ghid[:, n : n + WIDE])
        ddown_ref[n : n + WIDE, :] = dot_tn(act[:, n : n + WIDE], g_all())
    grads[0].wait_recv()
    dup_ref[...] += dup3[...].astype(f32)
    grads[1].wait_recv()
    ddown_ref[...] += ddown3[...].astype(f32)
    for cp in weights + grads:
        cp.wait_send()

    for k in range(1, seq):
        e = (s + k) % seq
        remote(back_ref.at[e], back_ref.at[e], disp_sem.at[0], final_recv.at[e], sib).wait_recv()
    keep_home().wait()
    dispatch(0, 1 - y).wait_send()
    own.wait_send()
    hand(z * 2 + 1 - y).wait_send()
    to_home(0, 1 - y).wait_send()

    def settle(k, carry):
        to_far(k).wait_send()

        @pl.when(k > 0)
        def _():
            for j in range(2):
                dispatch(k, j).wait_send()
                to_home(k, j).wait_send()
                hand(there(k, j)).wait_send()
        return carry
    lax.fori_loop(0, Z, settle, 0)


def moe_rows(batch, seq, sent, up, down):
    width, hidden_share = up.shape
    capacity, wide = sent.shape[1:]
    block = seq * capacity
    if tuned(batch, seq):
        Z, block = seq // 2, 4 * capacity
        dma = pltpu.SemaphoreType.DMA
        quarter = [pltpu.VMEM((width, hidden_share), bf16), pltpu.VMEM((hidden_share, width), bf16)]
        out = pl.pallas_call(
            functools.partial(moe_kernel, seq),
            out_shape=[
                like(seq, capacity, wide, dtype=bf16),
                like(2, seq * capacity, wide, dtype=bf16),
                like(width, hidden_share),
                like(hidden_share, width),
            ],
            in_specs=[VM] * 3,
            out_specs=[HBM, HBM] + [VM] * 2,
            scratch_shapes=[
                pltpu.VMEM((Z, block, wide), bf16),
                pltpu.VMEM((Z, block, wide), bf16),
                pltpu.VMEM((Z * block, 2 * hidden_share), bf16),
                pltpu.VMEM((Z * block, 2 * hidden_share), bf16),
                pltpu.VMEM((block, 2 * hidden_share), f32),
                pltpu.VMEM((block, 2 * hidden_share), f32),
                pltpu.VMEM((Z, 2 * capacity, wide), bf16),
                pltpu.VMEM((Z, 2, capacity, wide), bf16),
                *quarter,
                *quarter,
                *quarter,
                dma,
                dma((2 * Z,)),
                dma((seq,)),
                dma((2, seq)),
                dma((Z, 2)),
                dma((Z,)),
                dma((Z,)),
                dma((Z, 2)),
                dma((seq,)),
                dma,
                dma((4,)),
                dma((4,)),
            ],
            compiler_params=pltpu.CompilerParams(
                collective_id=2, has_side_effects=True, vmem_limit_bytes=56 << 20),
            name="experts",
        )(sent, up, down)
        return out[0], out[2], out[3]
    mine = lax.all_to_all(sent, "seq", split_axis=0, concat_axis=0, tiled=True)
    rows = lax.all_gather(mine, "batch", axis=0).reshape(batch * block, wide)
    part, d_up, d_down = pl.pallas_call(
        expert_kernel,
        out_shape=[
            like(batch * block, wide, dtype=bf16),
            like(width, hidden_share),
            like(hidden_share, width),
        ],
        grid=(batch,),
        in_specs=[
            pl.BlockSpec((block, wide), lambda i: (i, 0)),
            pl.BlockSpec((width, hidden_share), lambda i: (0, 0)),
            pl.BlockSpec((hidden_share, width), lambda i: (0, 0)),
        ],
        out_specs=[
            pl.BlockSpec((block, wide), lambda i: (i, 0)),
            pl.BlockSpec((width, hidden_share), lambda i: (0, 0)),
            pl.BlockSpec((hidden_share, width), lambda i: (0, 0)),
        ],
        compiler_params=params(),
        name="experts",
    )(rows, up, down)
    part = part.reshape((batch,) + sent.shape)
    mine = lax.psum_scatter(part, "batch", scatter_dimension=0, tiled=False)
    return lax.all_to_all(mine, "seq", split_axis=0, concat_axis=0, tiled=True), d_up, d_down


class Moves:
    def __init__(self, sems):
        self.sems, self.used, self.named = sems, 0, {}

    def start(self, name, src, dst):
        cp = pltpu.make_async_copy(src, dst, self.sems.at[self.used])
        self.used += 1
        cp.start()
        self.named.setdefault(name, []).append(cp)

    def wait(self, *names):
        for name in names:
            for cp in self.named.pop(name):
                cp.wait()

    def wait_all(self):
        self.wait(*list(self.named))


def forward_kernel(dims, share, low_share, experts, capacity, room, batch, seq,
                   tok_ref, cot_ref, route_ref, slot_ref, state_ref, step_ref, router_in, *refs):
    seqs, rows, inner = dims[:3]
    lines, gains, refs = refs[:5], refs[5:7], refs[7:]
    (win_in, out_in, tok_hbm,
     win_hbm, out_hbm, tail_hbm, halo_hbm, ext_hbm, z_hbm, u_hbm, dt_hbm, y_hbm, gated_hbm, hist_ref,
     proj_ref, dsum_ref, vec_ref, gain_ref, router_ref, hid_ref, moe_ref, gate_ref, rows_ref,
     win, out, tail_all, halo, ext, z, u, dt, y, gated, end, start, xn, hbuf, hcur, sem, sem0,
     tail, vecs, feats, zeros, send_sem, recv_sem, edge_sem, sems) = refs[:48]
    relay_refs = refs[48:]
    moves = Moves(sems)
    gather = Gatherer(batch, seq, (win_in, tail, out_in), (win_hbm, tail_hbm, out_hbm), send_sem, recv_sem)
    WIN, TAIL, OUT = range(3)
    relay = Relay(seq, True, dims[3], dsum_ref, vec_ref, end, start, *relay_refs)
    b, s = gather.me.at()
    has_before, has_after = s > 0, s < seq - 1
    greet(gather.peers() + [(has_before, (b, s - 1)), (has_after, (b, s + 1))])

    gather.give(WIN)
    edges = [
        pltpu.make_async_remote_copy(
            src_ref=tok_hbm.at[i, pl.ds(rows - 8, 8)], dst_ref=halo_hbm.at[pl.ds(8 * i, 8)],
            send_sem=edge_sem.at[0, i], recv_sem=edge_sem.at[1, i], device_id=(b, s + 1), device_id_type=MESH)
        for i in range(seqs)
    ]
    none = pltpu.make_async_copy(zeros, halo_hbm, edge_sem.at[2, 0])
    zeros[...] = jnp.zeros_like(zeros)

    @pl.when(has_after)
    def _():
        for cp in edges:
            cp.start()
    pl.when(jnp.logical_not(has_before))(none.start)
    pack_weights(tail, vecs, feats, state_ref, step_ref, router_in, lines, gains)
    gather.give(TAIL)
    moves.start("own", win_in, gather.part(WIN, gather.own))
    moves.start("own", tail, gather.part(TAIL, gather.own))
    moves.start("own out", out_in, gather.part(OUT, gather.own))
    for h in range(1, gather.Z + 3):
        gather.hop((WIN, TAIL), h)
    gather.give(OUT)
    gather.rest((WIN, TAIL))

    @pl.when(has_before)
    def _():
        for cp in edges:
            cp.wait_recv()
    pl.when(jnp.logical_not(has_before))(none.wait)
    moves.wait("own")
    moves.start("head", halo_hbm, halo)
    moves.start("head", tail_hbm, tail_all)
    for j in range(inner // WIDE):
        for base in (0, inner):
            cols = pl.ds(base + j * WIDE, WIDE)
            moves.start(("win", j), win_hbm.at[:, cols], win.at[:, cols])
    moves.wait("head")

    def weights(j):
        moves.wait(("win", j))
        if j in (2, 5):
            gather.hop((OUT,), 1 + j // 5)

    def projected():
        for name, src, dst in (("ext", ext, ext_hbm), ("z", z, z_hbm), ("u", u, u_hbm), ("dt", dt, dt_hbm)):
            moves.start(name, src, dst)
        gather.hop((OUT,), 3)

    def scanned(i):
        relay.start(i)
        gather.hop((OUT,), 4 + i)

    enter_packed(dims, share, low_share, experts, tok_ref, halo, win, tail_all, ext, z, u, dt, proj_ref, end,
                 dsum_ref, vec_ref, gain_ref, router_ref, xn,
                 hooks=Hooks(weights=weights, projected=projected, scanned=scanned))
    for i in range(relay.count):
        relay.finish(i)
    for h in range(4 + relay.count, gather.Z + 3):
        gather.hop((OUT,), h)

    def half(i):
        if i == 0:
            gather.rest((OUT,))
            moves.wait("own out")
            moves.start("out", out_hbm, out)

    def mixed():
        moves.start("y", y, y_hbm)
        moves.start("gated", gated, gated_hbm)

    leave_kernel(dims, capacity, room, tok_ref, cot_ref, start, dt, u, z, proj_ref, vec_ref, out, gain_ref, router_ref,
                 route_ref, slot_ref, hist_ref, y, hid_ref, gated, moe_ref, gate_ref, rows_ref, hbuf, hcur, sem, sem0,
                 hooks=Hooks(out_proj=lambda: moves.wait("out"), mixed=mixed, half=half))
    relay.settle()
    gather.settle()

    @pl.when(has_after)
    def _():
        for cp in edges:
            cp.wait_send()
    moves.wait_all()


def backward_kernel(dims, share, low_share, experts, capacity, room, batch, seq,
                    ret_ref, cot_ref, hid_ref, moe_ref, gate_ref, vec_ref, gain_ref, router_ref, route_ref, slot_ref,
                    dsum_ref, proj_ref, gated_hbm, out_hbm, z_hbm, y_hbm, u_hbm, dt_hbm, ext_hbm, win_hbm, tail_hbm,
                    tok_hbm, halo_hbm, hist_ref,
                    block_ref, dtok_ref, next_ref, in_out, out_out, tail_out,
                    gated, out, z, y, u, dt, ext, win, tail, tok, halo, gy, gz, ghid, adj, later,
                    dhalo, dsmall, dvec, dnorm, dmoe, drouter, dskip, blank,
                    hbuf, ccol, bcol, gbsum, gcsum, carry, gdt, gu, gproj, gpad, gm, xn, gpre, sem, sems, edge_sem,
                    *more):
    seqs, rows, inner, states, rank, taps = dims
    count, devices = seqs * rows, batch * seq
    relay_refs, more = more[:9], more[9:]
    moves = Moves(sems)
    for name, src, dst in (
        ("gated", gated_hbm, gated), ("out", out_hbm, out), ("z", z_hbm, z), ("y", y_hbm, y), ("u", u_hbm, u),
        ("dt", dt_hbm, dt), ("ext", ext_hbm, ext), ("win", win_hbm, win), ("tail", tail_hbm, tail),
        ("tok", tok_hbm, tok), ("halo", halo_hbm, halo),
    ):
        moves.start(name, src, dst)
    relay = Relay(seq, False, states, dsum_ref, vec_ref, adj, later, *relay_refs)
    reducer = Reducer(batch, seq, *(more[4 * i : 4 * i + 4] for i in range(5)), more[20:])
    OUT, GATE, IN, REST = range(4)
    b, s = reducer.me.at()
    has_before, has_after = s > 0, s < seq - 1
    greet(reducer.peers() + [(has_before, (b, s - 1)), (has_after, (b, s + 1))])
    me = reducer.me

    return_kernel(dims, capacity, room, ret_ref, cot_ref, hid_ref, moe_ref, gate_ref, gated, y, u, z, dt, proj_ref,
                  vec_ref, out, gain_ref, router_ref, route_ref, slot_ref,
                  block_ref, ghid, gy, gz, None, drouter, dskip, dmoe, adj,
                  hooks=Hooks(activations=lambda: moves.wait("gated", "out", "z", "y", "u"),
                              gradients=lambda: moves.wait("dt"), scanned=relay.start))

    def in_grads(a, grads, n, xx):
        half, cut, wide = devices // 2, low_share * devices // 2, 2 * WIDE
        at = pl.ds(pl.multiple_of(xx * cut, 128), cut)
        for c0 in range(0, inner, wide):
            part = dot_tn(xn[0:n, at], grads[:, c0 : c0 + wide]).reshape(half, low_share, wide)
            reducer.items[a][pl.ds(xx * half, half), :, c0 : c0 + wide] = part.astype(bf16)
        reducer.give(a, [(xx, 1 - me.y), (xx, me.y)])

    branch = ghid[...].astype(bf16)
    cut = 8 * share
    for q in range(devices // 8):
        part = dot_tn(gated[:, q * cut : (q + 1) * cut], branch)
        reducer.items[OUT][q * 8 : (q + 1) * 8] = part.astype(bf16).reshape(8, share, part.shape[1])
    reducer.give(OUT, reducer.others)
    relay.finish(0)
    moves.wait("tok")
    x = tok[...].astype(f32)
    xn[0:count] = (x * normalize(x) * gain_ref[0:1]).astype(bf16)
    for xx in (1 - me.x, me.x):
        in_grads(GATE, gz, count, xx)
    for i in range(1, relay.count):
        relay.finish(i)

    def group(i):
        for g in range(4):
            @pl.when(i // reducer.Z == g)
            def _(g=g):
                for a in (OUT, GATE):
                    reducer.step(a, g, i % reducer.Z)

    def late_grads():
        for xx in (1 - me.x, me.x):
            in_grads(IN, gm, count + 8 * seqs, xx)

    back_kernel(dims, tok, halo, ext, hist_ref, later, gy, gz, ghid, u, dt, proj_ref, win, tail, vec_ref, gain_ref,
                dtok_ref, dhalo, None, dsmall, dvec, dnorm,
                hbuf, ccol, bcol, gbsum, gcsum, carry, gdt, gu, gproj, gpad, gm, xn, gpre, sem,
                hooks=Hooks(rest=lambda: moves.wait("ext", "win", "tail", "halo"), group=group),
                in_grads=late_grads)
    edge = reducer.copy(dhalo, next_ref, edge_sem.at[0], edge_sem.at[1], (b, s - 1))
    none = pltpu.make_async_copy(blank, next_ref, edge_sem.at[2])
    blank[...] = jnp.zeros_like(blank)
    pl.when(has_before)(edge.start)
    pl.when(jnp.logical_not(has_after))(none.start)
    pack_tail(reducer.items[REST], low_share, experts, states + taps + 2, dsmall, dvec, dskip, drouter, dnorm, dmoe)
    reducer.give(REST, reducer.others)
    for t in range(reducer.Z + 2):
        for g, k in ((0, t), (1, t), (2, t - 1), (3, t - 2)):
            if 0 <= k < reducer.Z:
                for a in (IN, REST):
                    reducer.step(a, g, k)
    for a, ref in ((OUT, out_out), (GATE, in_out.at[:, inner:]), (IN, in_out.at[:, :inner]), (REST, tail_out)):
        reducer.result(a, ref)
    relay.settle()
    for a in (OUT, GATE, IN, REST):
        reducer.settle(a)
    pl.when(has_after)(edge.wait_recv)
    pl.when(has_before)(edge.wait_send)
    pl.when(jnp.logical_not(has_after))(none.wait)


def body(
    tokens,
    in_proj,
    conv_weight,
    conv_bias,
    state_proj,
    step_proj,
    step_bias,
    decay_log,
    skip_gain,
    out_proj,
    norm_gain,
    moe_gain,
    router_proj,
    expert_up,
    expert_down,
    routes,
    slot_index,
    cotangent,
):
    batch, seq = lax.axis_size("batch"), lax.axis_size("seq")
    both = ("batch", "seq")
    seqs, rows, width = tokens.shape
    count = seqs * rows
    devices = batch * seq
    taps, share = conv_weight.shape
    inner = share * devices
    states, rank = decay_log.shape[0], step_proj.shape[0]
    low_share = norm_gain.shape[0]
    experts = router_proj.shape[1]
    capacity = max(2, 5 * count // (4 * experts))
    dims = (seqs, rows, inner, states, rank, taps)
    tile = 128

    lines = (decay_log, conv_weight, conv_bias[None], step_bias[None], skip_gain[None])
    used = sum(a.shape[0] for a in lines)
    room = -(-used // 8) * 8
    fast = tuned(batch, seq)
    if not fast:
        features = jnp.concatenate([router_proj, norm_gain[:, None], moe_gain[:, None]], axis=1)
        tail = jnp.concatenate(
            [
                state_proj,
                step_proj.T,
                jnp.pad(jnp.concatenate(lines), ((0, room - used), (0, 0))).T,
                jnp.pad(features, ((0, share - low_share), (0, tile - room - features.shape[1]))),
            ],
            axis=1,
        )
        halo = lax.ppermute(tokens[:, rows - taps + 1 :], "seq", [(i, i + 1) for i in range(seq - 1)])
        halo = jnp.pad(halo, ((0, 0), (8 - taps + 1, 0), (0, 0))).reshape(seqs * 8, width)
        in_full, out_full, tail_full = (
            lax.all_gather(a, both, axis=0, tiled=True) for a in (in_proj, out_proj, tail)
        )
    tok, cot = tokens.reshape(count, width), cotangent.reshape(count, width)
    size = GROUP * states
    total = experts * capacity
    edge_rows = seqs * 8
    dma = pltpu.SemaphoreType.DMA
    acts = like(count, inner)
    ext_s, state_s, dsum_s = like(seqs, rows + 8, inner), like(seqs, states, inner), like(seqs, 1, inner)
    proj_s, low_s, vec_s = like(count, tile), like(count, inner, dtype=bf16), like(room, inner)
    hist_s = like(seqs, (rows + 1) * states, inner, dtype=bf16)
    hid_s, moe_s, gate_s = like(count, width), like(count, width, dtype=bf16), like(count, 1)
    rows_s = like(total, 2 * width, dtype=bf16)
    gain_s, router_s = like(8, width), like(width, tile, dtype=bf16)
    vmem = lambda a: pltpu.VMEM(a.shape, a.dtype)
    normed = pltpu.VMEM((count + edge_rows, width), bf16)
    leave_scratch = [pltpu.VMEM((2, size, inner), bf16), pltpu.VMEM(state_s.shape, bf16), dma((2,)), dma((seqs,))]
    back_scratch = [
        pltpu.VMEM((2, size + states, inner), bf16),
        pltpu.VMEM((GROUP, states, tile), f32),
        pltpu.VMEM((GROUP, states, tile), f32),
        pltpu.VMEM((GROUP, states, tile), f32),
        pltpu.VMEM((GROUP, states, tile), f32),
        pltpu.VMEM((states, inner), f32),
        vmem(acts),
        vmem(acts),
        vmem(proj_s),
        pltpu.VMEM((rows + 16, WIDE), f32),
        pltpu.VMEM((count + edge_rows, inner), bf16),
        normed,
        vmem(low_s),
        dma((2,)),
    ]
    tok_s, halo_s, din_s = like(count, width), like(edge_rows, width), like(width, 2 * inner, dtype=bf16)
    dout_s, dsmall_s = like(inner, width, dtype=bf16), like(inner, tile, dtype=bf16)
    drouter_s, dskip_s, dgain_s = like(width, tile), like(1, inner), like(1, width)
    wide = inner // WIDE
    if fast:
        in_s, out_s = like(width, 2 * inner, dtype=bf16), like(inner, width, dtype=bf16)
        tail_s, halo_b = like(inner, 2 * tile, dtype=bf16), like(edge_rows, width, dtype=bf16)
        (in_full, out_full, tail_full, halo, ext, z, u, dt, y, gated, hist, proj, dsum, vec, gain, router, hid, moe_in,
         gate, sent) = pl.pallas_call(
            partial(forward_kernel, dims, share, low_share, experts, capacity, room, batch, seq),
            out_shape=[in_s, out_s, tail_s, halo_b, ext_s, acts, acts, acts, acts, low_s, hist_s, proj_s, dsum_s, vec_s,
                       gain_s, router_s, hid_s, moe_s, gate_s, rows_s],
            in_specs=[VM] * 16 + [HBM],
            out_specs=[HBM] * 11 + [VM] * 9,
            scratch_shapes=[
                vmem(in_s), vmem(out_s), vmem(tail_s), vmem(halo_b), vmem(ext_s), vmem(acts), vmem(acts), vmem(acts),
                vmem(acts), vmem(low_s), vmem(state_s), vmem(state_s), normed, *leave_scratch,
                pltpu.VMEM((share, 2 * tile), bf16),
                pltpu.VMEM((room, share), f32),
                pltpu.VMEM((8, low_share), f32),
                vmem(halo_b),
                dma((3, n_sends(seq // 2))),
                dma((3, devices)),
                dma((3, seqs)),
                dma((2 * wide + 12,)),
                *relay_scratch(seqs, states, inner),
            ],
            compiler_params=pltpu.CompilerParams(
                collective_id=3, has_side_effects=True, vmem_limit_bytes=58 << 20),
            name="forward",
        )(tok, cot, routes, slot_index, state_proj, step_proj, router_proj.T, *lines, norm_gain[None], moe_gain[None],
          in_proj, out_proj, tokens)
    else:
        vec = tail_full[:, tile : tile + room].T.astype(f32)
        router = tail_full[:, tile:].reshape(devices, share, tile)[:, :low_share].reshape(width, tile)
        gain = router[:, room + experts : room + experts + 2].T.astype(f32)
        ext, z, u, dt, proj, end, dsum = pl.pallas_call(
            partial(enter_kernel, dims),
            out_shape=[ext_s, acts, acts, acts, proj_s, state_s, dsum_s],
            in_specs=[VM] * 6,
            out_specs=[VM] * 7,
            scratch_shapes=[normed],
            compiler_params=params(),
            name="enter",
        )(tok, halo, in_full, tail_full[:, :tile], vec, gain)
        rates = -jnp.exp(vec[:states])
        before = chain_states(seq, True, dsum, rates, end)
        hist, y, hid, gated, moe_in, gate, sent = pl.pallas_call(
            partial(leave_kernel, dims, capacity, room),
            out_shape=[hist_s, acts, hid_s, low_s, moe_s, gate_s, rows_s],
            in_specs=[VM] * 13,
            out_specs=[HBM] + [VM] * 6,
            scratch_shapes=leave_scratch,
            compiler_params=params(),
            name="leave",
        )(tok, cot, before, dt, u, z, proj, vec, out_full, gain, router, routes, slot_index)

    back, d_up, d_down = moe_rows(
        batch, seq, sent.reshape(experts, capacity, 2 * width), expert_up[0], expert_down[0])
    back = back.reshape(total, 2 * width)

    if fast:
        own = [(share, width), (low_share, inner), (low_share, inner), (share, 2 * tile)]
        block_out, d_tok, from_next, s_in, s_out, s_tail = pl.pallas_call(
            partial(backward_kernel, dims, share, low_share, experts, capacity, room, batch, seq),
            out_shape=[moe_s, tok_s, halo_s, like(low_share, 2 * inner), like(*own[0]), like(*own[3])],
            in_specs=[VM] * 12 + [HBM] * 12,
            out_specs=[VM] * 2 + [HBM] + [VM] * 3,
            scratch_shapes=[
                vmem(low_s), vmem(out_s), vmem(acts), vmem(acts), vmem(acts), vmem(acts), vmem(ext_s), vmem(in_s),
                vmem(tail_s), vmem(tok), vmem(halo_b), vmem(acts), vmem(low_s), vmem(tok_s), vmem(state_s),
                vmem(state_s), vmem(halo_s), vmem(dsmall_s), vmem(vec_s), vmem(dgain_s), vmem(dgain_s),
                vmem(drouter_s), vmem(dskip_s), vmem(halo_s), *back_scratch, dma((12,)), dma((3,)),
                *relay_scratch(seqs, states, inner), *reduce_scratch(devices, seq // 2, own),
            ],
            compiler_params=pltpu.CompilerParams(
                collective_id=4, has_side_effects=True, vmem_limit_bytes=62 << 20),
            name="backward",
        )(back, cot, hid, moe_in, gate, vec, gain, router, routes, slot_index, dsum, proj,
          gated, out_full, z, y, u, dt, ext, in_full, tail_full, tok, halo, hist)
    else:
        block_out, ghid, gy, gz, d_out, d_router, d_skip, d_moe, adj = pl.pallas_call(
            partial(return_kernel, dims, capacity, room),
            out_shape=[moe_s, tok_s, acts, low_s, dout_s, drouter_s, dskip_s, dgain_s, state_s],
            in_specs=[VM] * 17,
            out_specs=[VM] * 9,
            compiler_params=params(),
            name="back_experts",
        )(back, cot, hid, moe_in, gate, gated, y, u, z, dt, proj, vec, out_full, gain, router, routes, slot_index)
        later = chain_states(seq, False, dsum, rates, adj)
        d_tok, d_halo, d_in, d_small, d_vec, d_norm = pl.pallas_call(
            partial(back_kernel, dims),
            out_shape=[tok_s, halo_s, din_s, dsmall_s, vec_s, dgain_s],
            in_specs=[VM] * 3 + [HBM] + [VM] * 11,
            out_specs=[VM] * 6,
            scratch_shapes=back_scratch,
            compiler_params=params(),
            name="back_mixer",
        )(tok, halo, ext, hist, later, gy, gz, ghid, u, dt, proj, in_full, tail_full, vec, gain)

    skip_row = states + taps + 2
    if fast:
        shapes = [
            s_in.shape, (taps, share), (1, share), (share, rank + 2 * states), (rank, share), (1, share),
            (states, share), (1, share), s_out.shape, (1, low_share), (1, low_share), (experts, low_share),
        ]
        block_out, d_tok = block_out.reshape(tokens.shape), d_tok.reshape(tokens.shape)
        block_out, d_tok, *sums, d_up, d_down = pl.pallas_call(
            partial(finish_kernel, dims, low_share, experts),
            out_shape=[like(*tokens.shape, dtype=bf16), like(*tokens.shape)] + [like(*a) for a in shapes]
            + [like(*d_up.shape), like(*d_down.shape)],
            in_specs=[VM] * 4 + [HBM] * 4,
            out_specs=[HBM] * 2 + [VM] * 12 + [HBM] * 2,
            scratch_shapes=[vmem(block_out), vmem(d_tok), vmem(d_up), vmem(d_down), dma((20,))],
            compiler_params=params(),
            name="finish",
        )(s_tail, from_next.reshape(seqs, 8, width), s_in, s_out, block_out, d_tok, d_up, d_down)
        for i in (2, 5, 7, 9, 10):
            sums[i] = sums[i][0]
        sums[11] = sums[11].T
        return (block_out, d_tok, *sums, d_up[None], d_down[None])
    d_model = d_router.at[:, room + experts : room + experts + 2].set(jnp.concatenate([d_norm, d_moe]).T)
    d_model = jnp.pad(
        d_model.reshape(devices, low_share, tile)[:, :, room:], ((0, 0), (0, share - low_share), (0, 0))
    ).reshape(inner, tile - room)
    d_vec = d_vec.at[skip_row].set(d_skip[0])
    d_tail = jnp.concatenate([d_small, d_vec.T.astype(bf16), d_model.astype(bf16)], axis=1)
    s_in, s_out, s_tail = (
        lax.psum_scatter(a.astype(f32), both, scatter_dimension=0, tiled=True) for a in (d_in, d_out, d_tail)
    )
    from_next = lax.ppermute(
        d_halo.reshape(seqs, 8, width)[:, 8 - taps + 1 :], "seq", [(i + 1, i) for i in range(seq - 1)]
    )
    d_tok = d_tok.reshape(tokens.shape).at[:, rows - taps + 1 :].add(from_next)
    s_vec = s_tail[:, tile : tile + room].T
    s_model = s_tail[:low_share, tile + room :]
    return (
        block_out.reshape(tokens.shape),
        d_tok,
        s_in,
        s_vec[states : states + taps],
        s_vec[states + taps],
        s_tail[:, : rank + 2 * states],
        s_tail[:, rank + 2 * states : tile].T,
        s_vec[states + taps + 1],
        s_vec[:states],
        s_vec[states + taps + 2],
        s_out,
        s_model[:, experts],
        s_model[:, experts + 1],
        s_model[:, :experts],
        d_up[None],
        d_down[None],
    )


def solution(mesh):
    in_specs = (
        P("batch", "seq", None),
        P(("batch", "seq"), None),
        P(None, ("batch", "seq")),
        P(("batch", "seq")),
        P(("batch", "seq"), None),
        P(None, ("batch", "seq")),
        P(("batch", "seq")),
        P(None, ("batch", "seq")),
        P(("batch", "seq")),
        P(("batch", "seq"), None),
        P(("batch", "seq")),
        P(("batch", "seq")),
        P(("batch", "seq"), None),
        P("seq", None, "batch"),
        P("seq", "batch", None),
        P("batch", "seq"),
        P("batch", "seq"),
        P("batch", "seq", None),
    )
    out_specs = (
        P("batch", "seq", None),
        P("batch", "seq", None),
        P(("batch", "seq"), None),
        P(None, ("batch", "seq")),
        P(("batch", "seq")),
        P(("batch", "seq"), None),
        P(None, ("batch", "seq")),
        P(("batch", "seq")),
        P(None, ("batch", "seq")),
        P(("batch", "seq")),
        P(("batch", "seq"), None),
        P(("batch", "seq")),
        P(("batch", "seq")),
        P(("batch", "seq"), None),
        P("seq", None, "batch"),
        P("seq", "batch", None),
    )
    return jax.shard_map(body, mesh=mesh, in_specs=in_specs, out_specs=out_specs, check_vma=False)
```

```python
from functools import partial
import functools
import math

import jax
import jax.numpy as jnp
from jax import lax
from jax.experimental import pallas as pl
from jax.experimental.pallas import tpu as pltpu
from jax.sharding import PartitionSpec as P

epsilon = 1e-05
MESH = pl.DeviceIdType.MESH
HBM = pl.BlockSpec(memory_space=pl.ANY)
VM = pl.BlockSpec(memory_space=pltpu.VMEM)
bf16, f32 = jnp.bfloat16, jnp.float32


class Place:
    def __init__(self, batch, seq, ydim=2):
        self.batch, self.seq, self.Y = batch, seq, ydim
        self.Z = seq // ydim
        b, s = lax.axis_index("batch"), lax.axis_index("seq")
        self.x, self.c = b // 2, b % 2
        self.z, self.y = s // ydim, s % ydim

    def at(self, x=None, c=None, y=None, z=None):
        pick = lambda v, own: own if v is None else v
        x, c, y, z = pick(x, self.x), pick(c, self.c), pick(y, self.y), pick(z, self.z)
        return (x * 2 + c, z * self.Y + y)

    def index(self, dev):
        return dev[0] * self.seq + dev[1]


def greet(devices):
    barrier = pltpu.get_barrier_semaphore()
    count = 0
    for pred, dev in devices:
        if pred is None:
            pl.semaphore_signal(barrier, inc=1, device_id=dev, device_id_type=MESH)
            count = count + 1
        else:
            @pl.when(pred)
            def _(dev=dev):
                pl.semaphore_signal(barrier, inc=1, device_id=dev, device_id_type=MESH)
            count = count + jnp.where(pred, 1, 0)
    pl.semaphore_wait(barrier, count)


TILE = 128


def spot(rows, at, width):
    return (lanes((rows, width)) == subs((rows, width)) + at).astype(bf16)


class Gatherer:
    def __init__(self, batch, seq, ins, outs, send_sem, recv_sem):
        self.ins, self.outs, self.send_sem, self.recv_sem = ins, outs, send_sem, recv_sem
        self.me = me = Place(batch, seq)
        self.Z, self.z = me.Z, me.z
        self.sib = me.at(c=1 - me.c)
        self.up_ok, self.down_ok = me.z < me.Z - 1, me.z > 0
        self.up, self.down = me.at(z=me.z + 1), me.at(z=me.z - 1)
        self.nx, self.ny = me.at(x=1 - me.x), me.at(y=1 - me.y)
        first = me.c == 0
        pick = lambda a, b: tuple(jnp.where(first, p, q) for p, q in zip(a, b))
        self.second_dev, self.third_dev = pick(self.ny, self.nx), pick(self.nx, self.ny)
        ox, oy = 1 - me.x, 1 - me.y
        self.second_at = (jnp.where(first, me.x, ox), jnp.where(first, oy, me.y))
        self.third_at = (jnp.where(first, ox, me.x), jnp.where(first, me.y, oy))
        self.across_at = (ox, oy)
        self.own = me.index(me.at())
        self.sends = [[] for _ in ins]

    def peers(self):
        return [(None, self.sib), (None, self.nx), (None, self.ny), (self.up_ok, self.up), (self.down_ok, self.down)]

    def part(self, a, index):
        rows = self.ins[a].shape[0]
        return self.outs[a].at[pl.ds(pl.multiple_of(index * rows, 8), rows)]

    def send(self, a, pred, src, index, dev):
        copy = pltpu.make_async_remote_copy(
            src_ref=src, dst_ref=self.part(a, index), send_sem=self.send_sem.at[a, len(self.sends[a])],
            recv_sem=self.recv_sem.at[a, index], device_id=dev, device_id_type=MESH)
        self.sends[a].append((pred, copy))
        if pred is None:
            copy.start()
        else:
            pl.when(pred)(copy.start)

    def give(self, a):
        for pred, dev in self.targets():
            self.send(a, pred, self.ins[a], self.own, dev)

    def targets(self):
        return [(self.up_ok, self.up), (self.down_ok, self.down), (None, self.second_dev), (None, self.third_dev),
                (None, self.sib)]

    def arrive(self, a, pred, index, targets):
        part = self.part(a, index)
        copy = pltpu.make_async_remote_copy(
            src_ref=part, dst_ref=part, send_sem=self.send_sem.at[a, 0], recv_sem=self.recv_sem.at[a, index],
            device_id=self.sib, device_id_type=MESH)
        if pred is None:
            copy.wait_recv()
        else:
            pl.when(pred)(copy.wait_recv)
        for extra, dev in targets:
            p = pred if extra is None else (extra if pred is None else jnp.logical_and(pred, extra))
            self.send(a, p, part, index, dev)

    def offsets(self, k):
        return [(None, 0)] if k == 0 else [(self.z >= k, -k), (self.z + k < self.Z, k)]

    def hop(self, arrays, h):
        me, z = self.me, self.z
        to_second, to_third, to_sib = (None, self.second_dev), (None, self.third_dev), (None, self.sib)
        for k, at, targets in (
            (h, (me.x, me.y), None), (h - 1, self.second_at, [to_third, to_sib]), (h - 2, self.third_at, [to_sib]),
            (h - 3, self.across_at, [to_sib]),
        ):
            if not 0 <= k < self.Z or (targets is None and k == 0):
                continue
            for pred, off in self.offsets(k):
                onward = targets
                if targets is None:
                    onward = [(self.up_ok, self.up) if off < 0 else (self.down_ok, self.down), to_second, to_third, to_sib]
                for a in arrays:
                    self.arrive(a, pred, me.index(me.at(x=at[0], y=at[1], z=z + off)), onward)

    def rest(self, arrays):
        me = self.me
        for h in range(self.Z):
            for xx in (0, 1):
                for yy in (0, 1):
                    for pred, off in self.offsets(h):
                        for a in arrays:
                            self.arrive(a, pred, me.index(me.at(x=xx, y=yy, c=1 - me.c, z=self.z + off)), [])

    def settle(self):
        for sends in self.sends:
            for pred, copy in sends:
                if pred is None:
                    copy.wait_send()
                else:
                    pl.when(pred)(copy.wait_send)


def n_sends(Z):
    return 5 + (Z - 1) * 8 + (2 * Z - 1) * 2 + (2 * Z - 1) * 2


def pack_weights(tail, vecs, feats, state_ref, step_ref, router_ref, lines, gains):
    share, low_share, experts = state_ref.shape[0], router_ref.shape[1], router_ref.shape[0]
    rank, room, wide = step_ref.shape[0], vecs.shape[0], tail.shape[1]
    vecs[...] = jnp.zeros_like(vecs)
    at = 0
    for ref in lines:
        vecs[at : at + ref.shape[0]] = ref[...].astype(f32)
        at += ref.shape[0]
    feats[...] = jnp.zeros_like(feats)
    for i, ref in enumerate(gains):
        feats[i : i + 1] = ref[...].astype(f32)
    by_channel = (
        dot(state_ref[...], spot(state_ref.shape[1], 0, wide))
        + dot_tn(step_ref[...], spot(rank, TILE - rank, wide))
        + dot_tn(vecs[...].astype(bf16), spot(room, TILE, wide))
    )
    by_feature = dot_tn(router_ref[...], spot(experts, TILE + room, wide)) + dot_tn(
        feats[...].astype(bf16), spot(feats.shape[0], TILE + room + experts, wide))
    by_feature = jnp.concatenate([by_feature, jnp.zeros((share - low_share, wide), f32)])
    tail[...] = (by_channel + by_feature).astype(bf16)


class Reducer:
    def __init__(self, batch, seq, items, sib_bufs, far_bufs, near_bufs, line_bufs, sems):
        self.items, self.sib_bufs, self.far_bufs, self.near_bufs, self.line_bufs = (
            items, sib_bufs, far_bufs, near_bufs, line_bufs)
        (self.sib_send, self.sib_recv, self.far_send, self.far_recv, self.near_send, self.near_recv,
         self.line_send, self.line_recv) = sems
        self.me = me = Place(batch, seq)
        self.Z, self.z = me.Z, me.z
        self.sib = me.at(c=1 - me.c)
        self.nx, self.ny = me.at(x=1 - me.x), me.at(y=1 - me.y)
        pick = lambda a, b: tuple(jnp.where(me.c == 0, p, q) for p, q in zip(a, b))
        self.near, self.far = pick(self.ny, self.nx), pick(self.nx, self.ny)
        self.mine, self.others = self.groups(me.c), self.groups(1 - me.c)

    def peers(self):
        column = [(None, self.me.at(z=self.turn(k))) for k in range(self.Z - 1)]
        return [(None, self.sib), (None, self.nx), (None, self.ny)] + column

    def groups(self, c):
        me = self.me
        ox, oy = 1 - me.x, 1 - me.y
        pick = lambda a, b: jnp.where(c == 0, a, b)
        return [(ox, oy), (pick(ox, me.x), pick(me.y, oy)), (pick(me.x, ox), pick(oy, me.y)), (me.x, me.y)]

    def slot(self, xy, zz):
        return (xy[0] * 2 + xy[1]) * self.Z + zz

    def turn(self, k):
        above = self.Z - 1 - self.z
        return jnp.where(k < above, self.Z - 1 - k, jnp.where(k < self.Z - 1, k - above, self.z))

    def item(self, a, c, xy, zz):
        return self.items[a].at[self.me.index((xy[0] * 2 + c, zz * self.me.Y + xy[1]))]

    def copy(self, src, dst, send, recv, dev):
        return pltpu.make_async_remote_copy(
            src_ref=src, dst_ref=dst, send_sem=send, recv_sem=recv, device_id=dev, device_id_type=MESH)

    def to_sib(self, a, xy, k):
        t = self.turn(k)
        s = self.slot(xy, t)
        return self.copy(self.item(a, 1 - self.me.c, xy, t), self.sib_bufs[a].at[s],
                         self.sib_send.at[a, s], self.sib_recv.at[a, s], self.sib)

    def give(self, a, columns):
        for k in range(self.Z):
            for xy in columns:
                self.to_sib(a, xy, k).start()

    def to_far(self, a, g, k):
        t = self.turn(k)
        fs = g * self.Z + t
        return self.copy(self.item(a, self.me.c, self.mine[g], t), self.far_bufs[a].at[fs],
                         self.far_send.at[a, fs], self.far_recv.at[a, fs], self.far)

    def to_near(self, a, k):
        t = self.turn(k)
        return self.copy(self.item(a, self.me.c, self.mine[2], t), self.near_bufs[a].at[t],
                         self.near_send.at[a, t], self.near_recv.at[a, t], self.near)

    def step(self, a, g, k):
        t = self.turn(k)
        s = self.slot(self.mine[g], t)
        item = self.item(a, self.me.c, self.mine[g], t)
        take = lambda ref, recv: self.copy(ref, ref, self.sib_send.at[a, 0], recv, self.sib).wait_recv()
        parts = [self.sib_bufs[a].at[s]]
        take(parts[0], self.sib_recv.at[a, s])
        if g >= 2:
            fs = (g - 2) * self.Z + t
            parts.append(self.far_bufs[a].at[fs])
            take(parts[-1], self.far_recv.at[a, fs])
        if g == 3:
            parts.append(self.near_bufs[a].at[t])
            take(parts[-1], self.near_recv.at[a, t])
        total = item[...].astype(f32)
        for part in parts:
            total = total + part[...].astype(f32)
        item[...] = total.astype(bf16)
        if g < 2:
            self.to_far(a, g, k).start()
        elif g == 2:
            self.to_near(a, k).start()
        else:
            pl.when(k < self.Z - 1)(lambda: self.onward(a, k).start())

    def onward(self, a, k):
        t = self.turn(k)
        return self.copy(self.item(a, self.me.c, self.mine[3], t), self.line_bufs[a].at[self.z],
                         self.line_send.at[a, k], self.line_recv.at[a, self.z], self.me.at(z=t))

    def result(self, a, out_ref):
        total = self.item(a, self.me.c, self.mine[3], self.z)[...].astype(f32)
        for k in range(self.Z - 1):
            t = self.turn(k)
            ref = self.line_bufs[a].at[t]
            self.copy(ref, ref, self.sib_send.at[a, 0], self.line_recv.at[a, t], self.sib).wait_recv()
            total = total + ref[...].astype(f32)
        out_ref[...] = total

    def settle(self, a):
        def one(k, carry):
            for xy in self.others:
                self.to_sib(a, xy, k).wait_send()
            for g in range(2):
                self.to_far(a, g, k).wait_send()
            self.to_near(a, k).wait_send()

            @pl.when(k < self.Z - 1)
            def _():
                self.onward(a, k).wait_send()
            return carry
        lax.fori_loop(0, self.Z, one, 0)


def reduce_scratch(count, Z, shapes):
    half, n, dma = count // 2, len(shapes), pltpu.SemaphoreType.DMA
    bufs = [pltpu.VMEM(lead + s, bf16) for lead in ((count,), (half,), (2 * Z,), (Z,), (Z,)) for s in shapes]
    return bufs + [dma((n, half)), dma((n, half)), dma((n, 2 * Z)), dma((n, 2 * Z)), dma((n, Z)), dma((n, Z)),
                   dma((n, Z)), dma((n, Z))]


def pack_tail(tail, low_share, experts, skip_row, dsmall_ref, dvec_ref, dskip_ref, drouter_ref, dnorm_ref, dmoe_ref):
    blocks, share = tail.shape[:2]
    room, width = dvec_ref.shape[0], drouter_ref.shape[0]
    vec = jnp.where(subs(dvec_ref.shape) == skip_row, dskip_ref[...], dvec_ref[...])
    line = subs((8, width))
    gains = jnp.where(line == 0, dnorm_ref[...], jnp.where(line == 1, dmoe_ref[...], 0.0))
    model = drouter_ref[...] + dot_tn(gains.astype(bf16), spot(8, room + experts, TILE))
    model = jnp.concatenate(
        [model.reshape(blocks, low_share, TILE), jnp.zeros((blocks, share - low_share, TILE), f32)], axis=1)
    right = dot_tn(vec.astype(bf16), spot(room, 0, TILE)).reshape(blocks, share, TILE) + model
    tail[:, :, 0:TILE] = dsmall_ref[...].reshape(blocks, share, TILE)
    tail[:, :, TILE:] = right.astype(bf16)


def finish_kernel(dims, low_share, experts, tail_ref, halo_ref, in_ref, out_ref, block_hbm, tok_hbm, up_hbm, down_hbm,
                  block_out, tok_out, din, dconv, dbias, dstate, dstep, dstep_bias, ddecay, dskip, dout, dnorm, dmoe,
                  drouter, dup, ddown, block, tok, up, down, up_wide, down_wide, sems):
    seqs, rows, inner, states, rank, taps = dims
    moves = Moves(sems)
    routes, widened = [], {}
    for i in range(4):
        for src, at, wide, dst in ((up_hbm, up, up_wide, dup), (down_hbm, down, down_wide, ddown)):
            n = src.shape[0] // 4
            piece = pl.ds(i * n, n)
            routes.append((len(routes), src.at[piece], at.at[piece], dst.at[piece]))
            widened[routes[-1][0]] = wide.at[piece]
    routes.append(("tok", tok_hbm, tok, tok_out))
    routes.append(("block", block_hbm, block, block_out))
    for name, src, at, _ in routes:
        moves.start(name, src, at)
    din[...] = in_ref[...]
    dout[...] = out_ref[...]
    tail = tail_ref[...]
    wide = tail.shape[1]
    eye = (lanes((wide, wide)) == subs((wide, wide))).astype(bf16)
    high = tail.astype(bf16)
    turned = dot_nt(eye, high) + dot_nt(eye, (tail - high.astype(f32)).astype(bf16))
    dstate[...] = tail[:, : rank + 2 * states]
    dstep[...] = turned[TILE - rank : TILE]
    ddecay[...] = turned[TILE : TILE + states]
    dconv[...] = turned[TILE + states : TILE + states + taps]
    at = TILE + states + taps
    dbias[...] = turned[at : at + 1]
    dstep_bias[...] = turned[at + 1 : at + 2]
    dskip[...] = turned[at + 2 : at + 3]
    at = TILE + -(-(states + taps + 3) // 8) * 8
    drouter[...] = turned[at : at + experts, :low_share]
    at += experts
    dnorm[...] = turned[at : at + 1, :low_share]
    dmoe[...] = turned[at + 1 : at + 2, :low_share]
    for name, _, at, dst in routes:
        moves.wait(name)
        if name == "tok":
            tok[:, rows - 8 :] = tok[:, rows - 8 :] + halo_ref[...]
        if name in widened:
            widened[name][...] = at[...].astype(f32)
            at = widened[name]
        moves.start("out", at, dst)
    moves.wait_all()


def tuned(batch, seq):
    return batch == 4 and seq == 8


def chain_kernel(seq, forward, dsum_ref, rates_ref, end_ref, out_ref, held, outgoing, send_sem, recv_sem):
    s = lax.axis_index("seq")
    b = lax.axis_index("batch")
    step = 1 if forward else -1
    has_before = s > 0 if forward else s < seq - 1
    has_after = s < seq - 1 if forward else s > 0
    before, after = (b, s - step), (b, s + step)
    barrier = pltpu.get_barrier_semaphore()
    for pred, dev in ((has_before, before), (has_after, after)):
        @pl.when(pred)
        def _(dev=dev):
            pl.semaphore_signal(barrier, inc=1, device_id=dev, device_id_type=MESH)
    pl.semaphore_wait(barrier, jnp.where(has_before, 1, 0) + jnp.where(has_after, 1, 0))
    count = end_ref.shape[0]

    def copy(i):
        return pltpu.make_async_remote_copy(
            src_ref=outgoing.at[i], dst_ref=held.at[i], send_sem=send_sem.at[i],
            recv_sem=recv_sem.at[i], device_id=after, device_id_type=MESH)

    for i in range(count):
        @pl.when(has_before)
        def _(i=i):
            copy(i).wait_recv()
            out_ref[i] = held[i].astype(jnp.float32)
            decay = jnp.exp(rates_ref[...] * dsum_ref[i])
            outgoing[i] = (end_ref[i] + decay * out_ref[i]).astype(jnp.bfloat16)

        @pl.when(jnp.logical_not(has_before))
        def _(i=i):
            out_ref[i] = jnp.zeros_like(out_ref[i])
            outgoing[i] = end_ref[i].astype(jnp.bfloat16)

        @pl.when(has_after)
        def _(i=i):
            copy(i).start()
    for i in range(count):
        @pl.when(has_after)
        def _(i=i):
            copy(i).wait_send()


def chain_states(seq, forward, dsum, rates, end):
    vm = pl.BlockSpec(memory_space=pltpu.VMEM)
    return pl.pallas_call(
        functools.partial(chain_kernel, seq, forward),
        out_shape=jax.ShapeDtypeStruct(end.shape, jnp.float32),
        in_specs=[vm] * 3,
        out_specs=vm,
        scratch_shapes=[
            pltpu.VMEM(end.shape, jnp.bfloat16),
            pltpu.VMEM(end.shape, jnp.bfloat16),
            pltpu.SemaphoreType.DMA((end.shape[0],)),
            pltpu.SemaphoreType.DMA((end.shape[0],)),
        ],
        compiler_params=pltpu.CompilerParams(
            collective_id=5 if forward else 6, has_side_effects=True),
        name="chain_forward" if forward else "chain_backward",
    )(dsum, rates, end)


class Relay:
    def __init__(self, seq, forward, states, dsum_ref, vec_ref, end_ref, out_ref, mine, theirs, their_sum, held,
                 outgoing, pair_send, pair_recv, line_send, line_recv):
        me = Place(4, seq)
        y, z, last = me.y, me.z, me.Z - 1
        step = 1 if forward else -1
        self.first = y == (0 if forward else 1)
        self.has_before = z > 0 if forward else z < last
        self.has_after = z < last if forward else z > 0
        self.pair, self.before, self.after = me.at(y=1 - y), me.at(z=z - step), me.at(z=z + step)
        self.states, self.vec_ref, self.end_ref, self.out_ref = states, vec_ref, end_ref, out_ref
        self.mine, self.theirs, self.dsum_ref, self.their_sum = mine, theirs, dsum_ref, their_sum
        self.held, self.outgoing = held, outgoing
        self.pair_send, self.pair_recv, self.line_send, self.line_recv = pair_send, pair_recv, line_send, line_recv
        self.count = end_ref.shape[0]

    def peers(self):
        return [(None, self.pair), (self.has_before, self.before), (self.has_after, self.after)]

    def swaps(self, i):
        both = ((self.mine.at[i], self.theirs.at[i]), (self.dsum_ref.at[i], self.their_sum.at[i]))
        return [
            pltpu.make_async_remote_copy(
                src_ref=src, dst_ref=dst, send_sem=self.pair_send.at[i, k], recv_sem=self.pair_recv.at[i, k],
                device_id=self.pair, device_id_type=MESH)
            for k, (src, dst) in enumerate(both)
        ]

    def onward(self, i):
        return pltpu.make_async_remote_copy(
            src_ref=self.outgoing.at[i], dst_ref=self.held.at[i], send_sem=self.line_send.at[i],
            recv_sem=self.line_recv.at[i], device_id=self.after, device_id_type=MESH)

    def start(self, i):
        self.mine[i] = self.end_ref[i].astype(bf16)
        for cp in self.swaps(i):
            cp.start()

    def finish(self, i):
        rates = -jnp.exp(self.vec_ref[0 : self.states])
        for cp in self.swaps(i):
            cp.wait_recv()
        pick = lambda a, b: (jnp.where(self.first, a, b), jnp.where(self.first, b, a))
        early, late = pick(self.end_ref[i], self.theirs[i].astype(f32))
        early_sum, late_sum = pick(self.dsum_ref[i], self.their_sum[i])
        both = late + jnp.exp(rates * late_sum) * early

        @pl.when(self.has_before)
        def _():
            self.onward(i).wait_recv()
            arrived = self.held[i].astype(f32)
            self.outgoing[i] = (both + jnp.exp(rates * (early_sum + late_sum)) * arrived).astype(bf16)

        @pl.when(jnp.logical_not(self.has_before))
        def _():
            self.outgoing[i] = both.astype(bf16)

        @pl.when(self.has_after)
        def _():
            self.onward(i).start()

        @pl.when(self.has_before)
        def _():
            arrived = self.held[i].astype(f32)
            self.out_ref[i] = jnp.where(self.first, arrived, early + jnp.exp(rates * early_sum) * arrived)

        @pl.when(jnp.logical_not(self.has_before))
        def _():
            self.out_ref[i] = jnp.where(self.first, jnp.zeros_like(early), early)

    def settle(self):
        for i in range(self.count):
            for cp in self.swaps(i):
                cp.wait_send()
            pl.when(self.has_after)(self.onward(i).wait_send)


def relay_scratch(seqs, states, inner):
    n, state = seqs, (seqs, states, inner)
    dma = pltpu.SemaphoreType.DMA
    return [
        pltpu.VMEM(state, bf16),
        pltpu.VMEM(state, bf16),
        pltpu.VMEM((seqs, 1, inner), f32),
        pltpu.VMEM(state, bf16),
        pltpu.VMEM(state, bf16),
        dma((n, 2)),
        dma((n, 2)),
        dma((n,)),
        dma((n,)),
    ]


def dot(a, b):
    return jnp.dot(a, b, preferred_element_type=jnp.float32)


def dot_nt(a, b):
    return lax.dot_general(a, b, (((1,), (1,)), ((), ())), preferred_element_type=jnp.float32)


def dot_tn(a, b):
    return lax.dot_general(a, b, (((0,), (0,)), ((), ())), preferred_element_type=jnp.float32)


def sigmoid(v):
    return 1.0 / (1.0 + jnp.exp(-v))


def lanes(shape):
    return lax.broadcasted_iota(jnp.int32, shape, 1)


def subs(shape):
    return lax.broadcasted_iota(jnp.int32, shape, 0)


def column(row, base, states):
    shape = (states, row.shape[1])
    only = jnp.where(lanes(shape) == subs(shape) + base, jnp.broadcast_to(row, shape), 0.0)
    return jnp.broadcast_to(jnp.sum(only, axis=1, keepdims=True), shape)


def row_sums(parts):
    row = subs(parts[0].shape)
    four, two, one = row < 4, (row // 2) % 2 == 0, row % 2 == 0
    turn = lambda v, by: pltpu.roll(v, by, axis=0)
    a = [
        jnp.where(four, parts[j], parts[j + 4]) + turn(jnp.where(four, parts[j + 4], parts[j]), 4)
        for j in range(4)
    ]
    b = [jnp.where(two, a[j] + turn(a[j], 6), a[j + 2] + turn(a[j + 2], 2)) for j in range(2)]
    return jnp.where(one, b[0] + turn(b[0], 7), b[1] + turn(b[1], 1))


def fold(v):
    return sum(v[i : i + 8] for i in range(8, v.shape[0], 8)) + v[:8]


WIDE = 256
GROUP = 16
LOG2E = math.log2(math.e)


def conv_sum(ext_ref, s, cols, vec_ref, states, taps, rows):
    first = ext_ref.shape[1] - rows - taps + 1
    total = vec_ref[states + taps : states + taps + 1, cols]
    for k in range(taps):
        total = total + vec_ref[states + k : states + k + 1, cols] * ext_ref[s, first + k : first + k + rows, cols]
    return total


def normalize(x):
    return lax.rsqrt(jnp.mean(x * x, axis=-1, keepdims=True) + epsilon)


class Quiet:
    def __getattr__(self, name):
        return lambda *args: None


QUIET = Quiet()


class Hooks(Quiet):
    def __init__(self, **steps):
        self.__dict__.update(steps)


def unpack(tail_ref, share, low_share, room, experts, vec_ref, gain_ref, router_ref):
    right = tail_ref[:, TILE : 2 * TILE]
    vec_ref[...] = dot_nt(spot(room, 0, TILE), right)
    blocks = right.shape[0] // share
    model = right.astype(f32).reshape(blocks, share, TILE)[:, :low_share].reshape(blocks * low_share, TILE).astype(bf16)
    router_ref[...] = model
    gain_ref[...] = dot_nt(spot(gain_ref.shape[0], room + experts, TILE), model)


def enter_packed(dims, share, low_share, experts, tok_ref, halo_ref, win_ref, tail_ref,
                 ext_ref, z_ref, u_ref, dt_ref, proj_ref, end_ref, dsum_ref, vec_ref, gain_ref, router_ref, xn,
                 hooks=QUIET):
    unpack(tail_ref, share, low_share, vec_ref.shape[0], experts, vec_ref, gain_ref, router_ref)
    enter_kernel(dims, tok_ref, halo_ref, win_ref, tail_ref.at[:, 0:TILE], vec_ref, gain_ref,
                 ext_ref, z_ref, u_ref, dt_ref, proj_ref, end_ref, dsum_ref, xn, hooks)


def as_column(ref):
    seqs, rows = ref.shape
    diagonal = lanes((rows, rows)) == subs((rows, rows))
    spread = [
        jnp.where(diagonal, jnp.broadcast_to(ref[s : s + 1].astype(f32), (rows, rows)), 0.0) for s in range(seqs)
    ]
    return jnp.concatenate([jnp.sum(v, axis=1, keepdims=True) for v in spread]).astype(jnp.int32)


def enter_kernel(dims, tok_ref, halo_ref, win_ref, small_ref, vec_ref, gain_ref,
                 ext_ref, z_ref, u_ref, dt_ref, proj_ref, end_ref, dsum_ref, xn, hooks=QUIET):
    seqs, rows, inner, states, rank, taps = dims
    count = seqs * rows
    for ref, at in ((tok_ref, 0), (halo_ref, count)):
        x = ref[...].astype(jnp.float32)
        xn[at : at + x.shape[0]] = (x * normalize(x) * gain_ref[0:1]).astype(jnp.bfloat16)
    proj = jnp.zeros((count, small_ref.shape[1]), jnp.float32)
    for j in range(inner // WIDE):
        cols = slice(j * WIDE, (j + 1) * WIDE)
        hooks.weights(j)
        part = dot(xn[...], win_ref[:, cols])
        z_ref[:, cols] = dot(xn[:count], win_ref[:, inner + j * WIDE : inner + (j + 1) * WIDE])
        for s in range(seqs):
            ext_ref[s, 0:8, cols] = part[count + 8 * s : count + 8 * s + 8]
            ext_ref[s, 8:, cols] = part[s * rows : (s + 1) * rows]
            pre = conv_sum(ext_ref, s, cols, vec_ref, states, taps, rows)
            u_ref[s * rows : (s + 1) * rows, cols] = pre * sigmoid(pre)
        proj = proj + dot(u_ref[:, cols].astype(jnp.bfloat16), small_ref[cols, :])
    proj_ref[...] = proj
    low = rank_lanes(proj, rank, states)
    for j in range(inner // WIDE):
        cols = slice(j * WIDE, (j + 1) * WIDE)
        pre = dot_nt(low, small_ref[cols, :]) + vec_ref[states + taps + 1 : states + taps + 2, cols]
        dt = jnp.maximum(pre, 0.0) + jnp.log1p(jnp.exp(-jnp.abs(pre)))
        dt_ref[:, cols] = dt
        for s in range(seqs):
            dsum_ref[s, 0:1, cols] = jnp.sum(dt[s * rows : (s + 1) * rows], axis=0, keepdims=True)
    hooks.projected()
    a2 = -jnp.exp(vec_ref[0:states]) * LOG2E
    blocks = inner // 128
    for s in range(seqs):
        def eight(i, hs):
            hs = list(hs)
            at = pl.multiple_of(s * rows + i * 8, 8)
            small = proj_ref[pl.ds(at, 8), :]
            bs = [column(small[j : j + 1], rank, states) for j in range(8)]
            for k in range(blocks):
                sl = slice(k * 128, (k + 1) * 128)
                d8 = dt_ref[pl.ds(at, 8), sl]
                w8 = d8 * u_ref[pl.ds(at, 8), sl]
                for j in range(8):
                    hs[k] = jnp.exp2(d8[j : j + 1] * a2[:, sl]) * hs[k] + bs[j] * w8[j : j + 1]
            return tuple(hs)
        zero = jnp.zeros((states, 128), jnp.float32)
        hs = lax.fori_loop(0, rows // 8, eight, (zero,) * blocks)
        for k in range(blocks):
            end_ref[s, :, k * 128 : (k + 1) * 128] = hs[k]
        hooks.scanned(s)


def rank_lanes(proj, rank, states):
    at = rank + 2 * states
    moved = pltpu.roll(proj, at, axis=1)
    return jnp.where(lanes(proj.shape) >= at, moved, 0.0).astype(jnp.bfloat16)


def leave_kernel(dims, capacity, room, tok_ref, cot_ref, h0_ref, dt_ref, u_ref, z_ref, proj_ref, vec_ref, out_ref,
                 gain_ref, router_ref, route_ref, slot_ref,
                 hist_ref, y_ref, hid_ref, gated_ref, moe_ref, gate_ref, rows_ref,
                 hbuf, hcur, sem, sem0, hooks=QUIET):
    seqs, rows, inner, states, rank, taps = dims
    count = seqs * rows
    a2 = -jnp.exp(vec_ref[0:states]) * LOG2E
    blocks = inner // 128
    groups = rows // GROUP
    size = GROUP * states
    firsts = []
    for s in range(seqs):
        hcur[s] = h0_ref[s].astype(jnp.bfloat16)
        cp = pltpu.make_async_copy(hcur.at[s], hist_ref.at[s, pl.ds(0, states)], sem0.at[s])
        cp.start()
        firsts.append(cp)

    def out_copy(s, g, slot):
        at = pl.multiple_of(states + g * size, states)
        return pltpu.make_async_copy(hbuf.at[slot], hist_ref.at[s, pl.ds(at, size)], sem.at[slot])

    for s in range(seqs):
        def group(g, hs):
            hs = list(hs)
            slot = g % 2

            @pl.when(g >= 2)
            def _():
                out_copy(s, g - 2, slot).wait()
            for half in range(GROUP // 8):
                at = pl.multiple_of(s * rows + g * GROUP + half * 8, 8)
                small = proj_ref[pl.ds(at, 8), :]
                bs = [column(small[j : j + 1], rank, states) for j in range(8)]
                cs = [column(small[j : j + 1], rank + states, states) for j in range(8)]
                for k in range(blocks):
                    sl = slice(k * 128, (k + 1) * 128)
                    d8 = dt_ref[pl.ds(at, 8), sl]
                    w8 = d8 * u_ref[pl.ds(at, 8), sl]
                    parts = []
                    for j in range(8):
                        t = half * 8 + j
                        hs[k] = jnp.exp2(d8[j : j + 1] * a2[:, sl]) * hs[k] + bs[j] * w8[j : j + 1]
                        hbuf[slot, t * states : (t + 1) * states, sl] = hs[k].astype(jnp.bfloat16)
                        parts.append(fold(cs[j] * hs[k]))
                    y_ref[pl.ds(at, 8), sl] = row_sums(parts)
            out_copy(s, g, slot).start()
            return tuple(hs)
        hs = tuple(h0_ref[s, :, k * 128 : (k + 1) * 128] for k in range(blocks))
        lax.fori_loop(0, groups, group, hs)
        hooks.half(s)
        for g in (groups - 2, groups - 1):
            out_copy(s, g, g % 2).wait()
    for cp in firsts:
        cp.wait()
    hooks.out_proj()
    hid = tok_ref[...].astype(jnp.float32)
    for j in range(inner // WIDE):
        cols = slice(j * WIDE, (j + 1) * WIDE)
        y = y_ref[:, cols] + vec_ref[states + taps + 2 : states + taps + 3, cols] * u_ref[:, cols]
        y_ref[:, cols] = y
        z = z_ref[:, cols]
        gated = (y * (z * sigmoid(z))).astype(jnp.bfloat16)
        gated_ref[:, cols] = gated
        hid = hid + dot(gated, out_ref[cols, :])
    hooks.mixed()
    hid_ref[...] = hid
    moe_in = (hid * normalize(hid) * gain_ref[1:2]).astype(jnp.bfloat16)
    moe_ref[...] = moe_in
    logits = dot(moe_in, router_ref[...])
    route, slot = as_column(route_ref), as_column(slot_ref)
    chosen = lanes(logits.shape) == route + room
    gate = sigmoid(jnp.sum(jnp.where(chosen, logits, 0.0), axis=1, keepdims=True))
    gate_ref[...] = gate
    kept = (slot < capacity).astype(jnp.float32)
    grad_rows = (cot_ref[...].astype(jnp.float32) * (gate * kept)).astype(jnp.bfloat16)
    total = rows_ref.shape[0]
    place = jnp.where(slot_ref[...] < capacity, route_ref[...] * capacity + slot_ref[...], -1)
    place = jnp.concatenate([place[s : s + 1] for s in range(seqs)], axis=1)
    pick = (subs((total, count)) == place).astype(jnp.bfloat16)
    width = moe_in.shape[1]
    rows_ref[:, :width] = dot(pick, moe_in).astype(jnp.bfloat16)
    rows_ref[:, width:] = dot(pick, grad_rows).astype(jnp.bfloat16)


def erf(x):
    x = jnp.clip(x, -4.0, 4.0)
    x2 = x * x
    top = (-2.72614225801306e-10, 2.77068142495902e-08, -2.10102402082508e-06, -5.69250639462346e-05,
           -7.34990630326855e-04, -2.95459980854025e-03, -1.60960333262415e-02)
    low = (-1.45660718464996e-05, -2.13374055278905e-04, -1.68282697438203e-03, -7.37332916720468e-03,
           -1.42647390514189e-02)
    p = jnp.full_like(x2, top[0])
    for c in top[1:]:
        p = p * x2 + c
    q = jnp.full_like(x2, low[0])
    for c in low[1:]:
        q = q * x2 + c
    return x * p / q


def expert_kernel(rows_ref, up_ref, down_ref, part_ref, dup_ref, ddown_ref):
    width = up_ref.shape[0]
    x, g = rows_ref[:, :width], rows_ref[:, width:]
    hidden = dot(x, up_ref[...])
    half = 0.5 * (1.0 + erf(hidden * math.sqrt(0.5)))
    act = (hidden * half).astype(jnp.bfloat16)
    slope = half + hidden * (jnp.exp(-0.5 * hidden * hidden) * (1.0 / math.sqrt(2.0 * math.pi)))
    part_ref[:, :width] = dot(act, down_ref[...]).astype(jnp.bfloat16)
    grad_hidden = (dot_nt(g, down_ref[...]) * slope).astype(jnp.bfloat16)
    part_ref[:, width:] = dot_nt(grad_hidden, up_ref[...]).astype(jnp.bfloat16)
    ddown, dup = dot_tn(act, g), dot_tn(x, grad_hidden)

    @pl.when(pl.program_id(0) == 0)
    def _():
        dup_ref[...] = dup
        ddown_ref[...] = ddown

    @pl.when(pl.program_id(0) > 0)
    def _():
        dup_ref[...] += dup
        ddown_ref[...] += ddown


def return_kernel(dims, capacity, room, ret_ref, cot_ref, hid_ref, moe_ref, gate_ref, gated_ref, y_ref, u_ref, z_ref, dt_ref,
                  proj_ref, vec_ref, out_ref, gain_ref, router_ref, route_ref, slot_ref,
                  block_ref, ghid_ref, gy_ref, gz_ref, dout_ref, drouter_ref, dskip_ref, dgain_ref, adj_ref,
                  hooks=QUIET):
    seqs, rows, inner, states, rank, taps = dims
    count = seqs * rows
    total, width = ret_ref.shape[0], hid_ref.shape[1]
    route, slot = as_column(route_ref), as_column(slot_ref)
    place = jnp.where(slot < capacity, route * capacity + slot, -1)
    pick = (lanes((count, total)) == place).astype(jnp.bfloat16)
    result = dot(pick, ret_ref[:, :width])
    hid, gate = hid_ref[...], gate_ref[...]
    block_ref[...] = (hid + gate * result).astype(jnp.bfloat16)
    cot = cot_ref[...].astype(jnp.float32)
    grad_gate = jnp.sum(cot * result, axis=1, keepdims=True)
    wide = (count, router_ref.shape[1])
    grad_logits = jnp.where(lanes(wide) == route + room, grad_gate * gate * (1.0 - gate), 0.0).astype(jnp.bfloat16)
    grad_in = dot(pick, ret_ref[:, width:]) + dot_nt(grad_logits, router_ref[...])
    drouter_ref[...] = dot_tn(moe_ref[...], grad_logits)
    r2 = normalize(hid)
    dgain_ref[...] = jnp.sum(grad_in * (hid * r2), axis=0, keepdims=True)
    scaled = grad_in * gain_ref[1:2]
    grad_hid = cot + r2 * scaled - hid * (r2 * r2 * r2) * jnp.mean(scaled * hid, axis=1, keepdims=True)
    ghid_ref[...] = grad_hid
    branch = grad_hid.astype(jnp.bfloat16)
    hooks.activations()
    for j in range(inner // WIDE):
        cols = slice(j * WIDE, (j + 1) * WIDE)
        if dout_ref is not None:
            dout_ref[cols, :] = dot_tn(gated_ref[:, cols], branch).astype(jnp.bfloat16)
        grad = dot_nt(branch, out_ref[cols, :])
        z = z_ref[:, cols]
        sig = sigmoid(z)
        gy = grad * (z * sig)
        gy_ref[:, cols] = gy
        gz_ref[:, cols] = (grad * y_ref[:, cols] * (sig + z * sig * (1.0 - sig))).astype(jnp.bfloat16)
        dskip_ref[:, cols] = jnp.sum(gy * u_ref[:, cols], axis=0, keepdims=True)
    hooks.gradients()
    a2 = -jnp.exp(vec_ref[0:states]) * LOG2E
    blocks = inner // 128
    for s in range(seqs):
        def eight(i, ms):
            ms = list(ms)
            at = pl.multiple_of((s + 1) * rows - 8 - i * 8, 8)
            small = proj_ref[pl.ds(at, 8), :]
            cs = [column(small[j : j + 1], rank + states, states) for j in range(8)]
            for k in range(blocks):
                sl = slice(k * 128, (k + 1) * 128)
                d8, g8 = dt_ref[pl.ds(at, 8), sl], gy_ref[pl.ds(at, 8), sl]
                for j in reversed(range(8)):
                    ms[k] = jnp.exp2(d8[j : j + 1] * a2[:, sl]) * (ms[k] + cs[j] * g8[j : j + 1])
            return tuple(ms)
        zero = jnp.zeros((states, 128), jnp.float32)
        ms = lax.fori_loop(0, rows // 8, eight, (zero,) * blocks)
        for k in range(blocks):
            adj_ref[s, :, k * 128 : (k + 1) * 128] = ms[k]
        hooks.scanned(s)


def back_kernel(dims, tok_ref, halo_ref, ext_ref, hist_ref, later_ref, gy_ref, gz_ref, ghid_ref, u_ref, dt_ref,
                proj_ref, win_ref, small_ref, vec_ref, gain_ref,
                dtok_ref, dhalo_ref, din_ref, dsmall_ref, dvec_ref, dgain_ref,
                hbuf, ccol, bcol, gbsum, gcsum, adj, gdt, gu, gproj, gpad, gm, xn, gpre, sem, hooks=QUIET, in_grads=None):
    small_ref = small_ref.at[:, 0:TILE]
    seqs, rows, inner, states, rank, taps = dims
    count = seqs * rows
    groups = rows // GROUP
    size = GROUP * states
    steps = seqs * groups

    def fetch(i, slot):
        s, g = i // groups, groups - 1 - i % groups
        at = pl.multiple_of(g * size, size)
        return pltpu.make_async_copy(hist_ref.at[s, pl.ds(at, size + states)], hbuf.at[slot], sem.at[slot])

    fetch(0, 0).start()
    dvec_ref[...] = jnp.zeros_like(dvec_ref)
    strip = 512

    def group(i, carry):
        slot = i % 2
        s, g = i // groups, groups - 1 - i % groups

        @pl.when(i + 1 < steps)
        def _():
            fetch(i + 1, 1 - slot).start()

        @pl.when(g == groups - 1)
        def _():
            adj[...] = later_ref[s]
        at = pl.multiple_of(s * rows + g * GROUP, GROUP)
        small = proj_ref[pl.ds(at, GROUP), :]
        for t in range(GROUP):
            ccol[t] = column(small[t : t + 1], rank + states, states)
            bcol[t] = column(small[t : t + 1], rank, states)
            gbsum[t] = jnp.zeros((states, 128), f32)
            gcsum[t] = jnp.zeros((states, 128), f32)
        fetch(i, slot).wait()
        hooks.group(i)
        for c0 in range(0, inner, strip):
            sls = [slice(c0 + k, c0 + k + 128) for k in range(0, strip, 128)]
            scaled = [-jnp.exp(vec_ref[0:states, sl]) * LOG2E for sl in sls]
            m = [adj[:, sl] for sl in sls]
            dd = [dvec_ref[0:states, sl] for sl in sls]
            now = [hbuf[slot, GROUP * states : (GROUP + 1) * states, sl].astype(f32) for sl in sls]
            for half in reversed(range(GROUP // 8)):
                a8 = pl.multiple_of(at + half * 8, 8)
                d8 = [dt_ref[pl.ds(a8, 8), sl] for sl in sls]
                g8 = [gy_ref[pl.ds(a8, 8), sl] for sl in sls]
                u8 = [u_ref[pl.ds(a8, 8), sl] for sl in sls]
                w8 = [d * u for d, u in zip(d8, u8)]
                r1, r2 = [[None] * 8 for _ in sls], [[None] * 8 for _ in sls]
                for j in reversed(range(8)):
                    t = half * 8 + j
                    gb = gc = 0.0
                    for k, sl in enumerate(sls):
                        d, gy = d8[k][j : j + 1], g8[k][j : j + 1]
                        a = m[k] + ccol[t] * gy
                        m[k] = jnp.exp2(d * scaled[k]) * a
                        gb = gb + a * w8[k][j : j + 1]
                        gc = gc + gy * now[k]
                        now[k] = hbuf[slot, t * states : (t + 1) * states, sl].astype(f32)
                        p = m[k] * now[k] * scaled[k]
                        dd[k] = dd[k] + p * d
                        r1[k][j], r2[k][j] = fold(p), fold(a * bcol[t])
                    gbsum[t] += gb
                    gcsum[t] += gc
                for k, sl in enumerate(sls):
                    w1, w2 = row_sums(r1[k]), row_sums(r2[k])
                    gdt[pl.ds(a8, 8), sl] = w1 * (1.0 / LOG2E) + u8[k] * w2
                    gu[pl.ds(a8, 8), sl] = d8[k] * w2
            for k, sl in enumerate(sls):
                adj[:, sl] = m[k]
                dvec_ref[0:states, sl] = dd[k]
        square = (states, small.shape[1])
        where, entry = lanes(square), subs(square)
        for half in range(GROUP // 8):
            parts = []
            for t in range(half * 8, half * 8 + 8):
                gb = jnp.broadcast_to(jnp.sum(gbsum[t], axis=1, keepdims=True), square)
                gc = jnp.broadcast_to(jnp.sum(gcsum[t], axis=1, keepdims=True), square)
                put = jnp.where(where == entry + rank, gb, jnp.where(where == entry + rank + states, gc, 0.0))
                parts.append(fold(put))
            gproj[pl.ds(pl.multiple_of(at + half * 8, 8), 8), :] = row_sums(parts)
        return carry
    lax.fori_loop(0, steps, group, 0)
    dvec_ref[0:states] = dvec_ref[0:states] * (1.0 / LOG2E)
    hooks.rest()

    low = rank_lanes(proj_ref[...], rank, states)
    at = rank + 2 * states
    row = states + taps
    grad_rank = jnp.zeros(proj_ref.shape, jnp.float32)
    for j in range(inner // WIDE):
        cols = slice(j * WIDE, (j + 1) * WIDE)
        pre = dot_nt(low, small_ref[cols, :]) + vec_ref[row + 1 : row + 2, cols]
        grad_pre = gdt[:, cols] * sigmoid(pre)
        dvec_ref[row + 1 : row + 2, cols] = jnp.sum(grad_pre, axis=0, keepdims=True)
        grad_pre = grad_pre.astype(jnp.bfloat16)
        gpre[:, cols] = grad_pre
        grad_rank = grad_rank + dot(grad_pre, small_ref[cols, :])
    where = lanes(grad_rank.shape)
    grad_rank = pltpu.roll(grad_rank, small_ref.shape[1] - at, axis=1)
    grad_proj = jnp.where(where < rank, grad_rank, jnp.where(where < at, gproj[...], 0.0)).astype(jnp.bfloat16)
    for ref, to in ((tok_ref, 0), (halo_ref, count)):
        x = ref[...].astype(jnp.float32)
        xn[to : to + x.shape[0]] = (x * normalize(x) * gain_ref[0:1]).astype(jnp.bfloat16)
    grad_normed = jnp.zeros((gm.shape[0], xn.shape[1]), jnp.float32)
    first = ext_ref.shape[1] - rows - taps + 1
    for j in range(inner // WIDE):
        cols = slice(j * WIDE, (j + 1) * WIDE)
        dsmall_ref[cols, :] = (
            dot_tn(u_ref[:, cols].astype(jnp.bfloat16), grad_proj) + dot_tn(gpre[:, cols], low)
        ).astype(jnp.bfloat16)
        grad_u = dot_nt(grad_proj, small_ref[cols, :]) + gy_ref[:, cols] * vec_ref[row + 2 : row + 3, cols] + gu[:, cols]
        taps_sum = [0.0] * taps
        bias_sum = 0.0
        heads = []
        for s in range(seqs):
            pre = conv_sum(ext_ref, s, cols, vec_ref, states, taps, rows)
            sig = sigmoid(pre)
            grad_conv = grad_u[s * rows : (s + 1) * rows] * (sig + pre * sig * (1.0 - sig))
            bias_sum = bias_sum + jnp.sum(grad_conv, axis=0, keepdims=True)
            for k in range(taps):
                taps_sum[k] = taps_sum[k] + jnp.sum(
                    grad_conv * ext_ref[s, first + k : first + k + rows, cols], axis=0, keepdims=True)
            gpad[0:8] = jnp.zeros((8, WIDE), jnp.float32)
            gpad[8 : 8 + rows] = grad_conv
            gpad[8 + rows :] = jnp.zeros((8, WIDE), jnp.float32)
            grad = 0.0
            for k in range(taps):
                grad = grad + vec_ref[states + k : states + k + 1, cols] * gpad[taps - 1 - k : taps + 7 - k + rows]
            heads.append(grad[0:8])
            gm[s * rows : (s + 1) * rows, cols] = grad[8:].astype(jnp.bfloat16)
        gm[count:, cols] = jnp.concatenate(heads).astype(jnp.bfloat16)
        dvec_ref[row : row + 1, cols] = bias_sum
        for k in range(taps):
            dvec_ref[states + k : states + k + 1, cols] = taps_sum[k]
    if in_grads is None:
        for j in range(inner // WIDE):
            cols, zcols = (slice(at + j * WIDE, at + (j + 1) * WIDE) for at in (0, inner))
            din_ref[:, cols] = dot_tn(xn[...], gm[:, cols]).astype(jnp.bfloat16)
            din_ref[:, zcols] = dot_tn(xn[:count], gz_ref[:, cols]).astype(jnp.bfloat16)
    else:
        in_grads()
    for j in range(inner // WIDE):
        cols, zcols = (slice(at + j * WIDE, at + (j + 1) * WIDE) for at in (0, inner))
        gz = jnp.concatenate([gz_ref[:, cols], jnp.zeros((gm.shape[0] - count, WIDE), jnp.bfloat16)])
        grad_normed = grad_normed + dot_nt(gm[:, cols], win_ref[:, cols]) + dot_nt(gz, win_ref[:, zcols])
    gain_sum = 0.0
    for ref, to, base, out in ((tok_ref, 0, ghid_ref, dtok_ref), (halo_ref, count, None, dhalo_ref)):
        x = ref[...].astype(jnp.float32)
        r1 = normalize(x)
        grad = grad_normed[to : to + x.shape[0]]
        gain_sum = gain_sum + jnp.sum(grad * (x * r1), axis=0, keepdims=True)
        grad = grad * gain_ref[0:1]
        grad = r1 * grad - x * (r1 * r1 * r1) * jnp.mean(grad * x, axis=1, keepdims=True)
        out[...] = grad if base is None else grad + base[...]
    dgain_ref[...] = gain_sum


def like(*shape, dtype=f32):
    return jax.ShapeDtypeStruct(shape, dtype)


def params(mib=56):
    return pltpu.CompilerParams(vmem_limit_bytes=mib << 20)


def moe_kernel(seq, rows_ref, up_ref, down_ref,
               back_ref, land_ref, dup_ref, ddown_ref,
               xbuf, part, act, ghid, hid, gact, far_buf, own_sum, up2_ref, down2_ref, dup2, ddown2, dup3, ddown3, dup_sum, ddown_sum,
               local_sem, disp_sem, pass_sem, recv_sem, load_sem, far_send, far_recv,
               final_send, final_recv, final_local, swap_send, swap_recv):
    me = Place(4, seq)
    b, s = me.at()
    y, z, Z, x = me.y, me.z, me.Z, me.x
    cap, wide = rows_ref.shape[1], rows_ref.shape[2]
    width = wide // 2
    share = up_ref.shape[1]
    two = 2 * cap
    block = 2 * two
    sib, nx = me.at(c=1 - me.c), me.at(x=1 - x)
    greet([(None, sib), (None, nx)] + [(None, (b, (s + k) % seq)) for k in range(1, seq)])

    def remote(src, dst, send, recv, dev):
        return pltpu.make_async_remote_copy(
            src_ref=src, dst_ref=dst, send_sem=send, recv_sem=recv, device_id=dev, device_id_type=MESH)

    def slab(xx, ss):
        return land_ref.at[xx, pl.ds(pl.multiple_of(ss * cap, 8), cap)]

    def there(k, j):
        return ((z + k) % Z) * 2 + j

    def arrived(xx, ss):
        remote(slab(xx, ss), slab(xx, ss), disp_sem.at[0], recv_sem.at[xx, ss], nx).wait_recv()

    def hand(ss):
        return remote(slab(x, ss), slab(x, ss), pass_sem.at[ss], recv_sem.at[x, ss], nx)

    def load(k, xx):
        zz = (z + k) % Z
        return pltpu.make_async_copy(
            land_ref.at[xx, pl.ds(pl.multiple_of(zz * two, 8), two)],
            xbuf.at[k, pl.ds(pl.multiple_of(xx * two, 16), two)], load_sem.at[k, xx])

    def dispatch(k, j):
        to = ((z + Z - k) % Z) * 2 + j
        return remote(rows_ref.at[to], slab(x, s), disp_sem.at[2 * k + j], recv_sem.at[x, s], (b, to))

    dispatch(0, 1 - y).start()
    own = remote(rows_ref.at[s], slab(x, s), pass_sem.at[s], recv_sem.at[x, s], nx)
    own.start()
    local = pltpu.make_async_copy(rows_ref.at[s], slab(x, s), local_sem)
    local.start()
    for j in range(2):
        dispatch(1, j).start()

    def swap(i, src, dst):
        return remote(src, dst, swap_send.at[i], swap_recv.at[i], sib)

    weights = [swap(0, up_ref, up2_ref), swap(1, down_ref, down2_ref)]
    for cp in weights:
        cp.start()
    ups, downs = (up_ref, up2_ref), (down_ref, down2_ref)

    def compute(k):
        for i in range(2):
            for n in range(0, share, WIDE):
                to = slice(i * share + n, i * share + n + WIDE)
                hid[:, to] = dot(xbuf[k, :, :width], ups[i][:, n : n + WIDE])
                gact[:, to] = dot_nt(xbuf[k, :, width:], downs[i][n : n + WIDE, :])

        def sixteen(r, carry):
            at = pl.ds(pl.multiple_of(r * 16, 16), 16)
            to = pl.ds(pl.multiple_of(k * block + r * 16, 16), 16)
            h = hid[at, :]
            half = 0.5 * (1.0 + erf(h * math.sqrt(0.5)))
            act[to, :] = (h * half).astype(bf16)
            slope = half + h * (jnp.exp(-0.5 * h * h) * (1.0 / math.sqrt(2.0 * math.pi)))
            ghid[to, :] = (gact[at, :] * slope).astype(bf16)
            return carry
        lax.fori_loop(0, block // 16, sixteen, 0)
        mine = pl.ds(pl.multiple_of(k * block, 16), block)
        for n in range(0, width, WIDE):
            cols = slice(n, n + WIDE)
            part[k, :, cols] = (
                dot(act[mine, :share], down_ref[:, cols]) + dot(act[mine, share:], down2_ref[:, cols])
            ).astype(bf16)
            part[k, :, width + n : width + n + WIDE] = (
                dot_nt(ghid[mine, :share], up_ref[cols, :]) + dot_nt(ghid[mine, share:], up2_ref[cols, :])
            ).astype(bf16)

    def of_chip(k, xx):
        return part.at[k, pl.ds(pl.multiple_of(xx * two, 16), two)]

    def to_far(k):
        return remote(of_chip(k, 1 - x), far_buf.at[k], far_send.at[k], far_recv.at[k], nx)

    def to_home(k, j):
        return remote(own_sum.at[k, j], back_ref.at[s], final_send.at[k, j], final_recv.at[s], (b, there(k, j)))

    def keep_home():
        return pltpu.make_async_copy(own_sum.at[0, y], back_ref.at[s], final_local)

    def own_stage(k):
        @pl.when(k == 0)
        def _():
            arrived(x, z * 2 + 1 - y)
            hand(z * 2 + 1 - y).start()
            local.wait()

        @pl.when(k > 0)
        def _():
            for j in range(2):
                arrived(x, there(k, j))
                hand(there(k, j)).start()

        @pl.when(k < Z - 2)
        def _():
            for j in range(2):
                dispatch(k + 2, j).start()
        load(k, x).start()

    def compute_stage(k):
        for j in range(2):
            arrived(1 - x, there(k, j))
        load(k, 1 - x).start()
        for xx in range(2):
            load(k, xx).wait()

        @pl.when(k == 0)
        def _():
            for cp in weights:
                cp.wait_recv()
        compute(k)
        to_far(k).start()

    def home_stage(k):
        to_far(k).wait_recv()
        total = of_chip(k, x)[...].astype(f32) + far_buf[k].astype(f32)
        for j in range(2):
            own_sum[k, j] = total[j * cap : (j + 1) * cap].astype(bf16)

        @pl.when(k > 0)
        def _():
            for j in range(2):
                to_home(k, j).start()

        @pl.when(k == 0)
        def _():
            keep_home().start()
            to_home(0, 1 - y).start()

    everything = (Z * block, width)
    stages = ((own_stage, 0), (home_stage, 2), (compute_stage, 1))

    def step(t, carry):
        for stage, lag in stages:
            k = t - lag
            pl.when(jnp.logical_and(k >= 0, k < Z))(functools.partial(stage, k))
        return carry
    lax.fori_loop(0, Z + 2, step, 0)
    x_all = lambda: xbuf[:, :, :width].reshape(everything)
    g_all = lambda: xbuf[:, :, width:].reshape(everything)
    grads = [swap(2, dup2, dup3), swap(3, ddown2, ddown3)]
    for n in range(0, share, WIDE):
        dup2[:, n : n + WIDE] = dot_tn(x_all(), ghid[:, share + n : share + n + WIDE]).astype(bf16)
    grads[0].start()
    for n in range(0, share, WIDE):
        ddown2[n : n + WIDE, :] = dot_tn(act[:, share + n : share + n + WIDE], g_all()).astype(bf16)
    grads[1].start()
    for n in range(0, share, WIDE):
        dup_sum[:, n : n + WIDE] = dot_tn(x_all(), ghid[:, n : n + WIDE])
        ddown_sum[n : n + WIDE, :] = dot_tn(act[:, n : n + WIDE], g_all())
    grads[0].wait_recv()
    dup_ref[...] = (dup_sum[...] + dup3[...].astype(f32)).astype(bf16)
    grads[1].wait_recv()
    ddown_ref[...] = (ddown_sum[...] + ddown3[...].astype(f32)).astype(bf16)
    for cp in weights + grads:
        cp.wait_send()

    for k in range(1, seq):
        e = (s + k) % seq
        remote(back_ref.at[e], back_ref.at[e], disp_sem.at[0], final_recv.at[e], sib).wait_recv()
    keep_home().wait()
    dispatch(0, 1 - y).wait_send()
    own.wait_send()
    hand(z * 2 + 1 - y).wait_send()
    to_home(0, 1 - y).wait_send()

    def settle(k, carry):
        to_far(k).wait_send()

        @pl.when(k > 0)
        def _():
            for j in range(2):
                dispatch(k, j).wait_send()
                to_home(k, j).wait_send()
                hand(there(k, j)).wait_send()
        return carry
    lax.fori_loop(0, Z, settle, 0)


def moe_rows(batch, seq, sent, up, down):
    width, hidden_share = up.shape
    capacity, wide = sent.shape[1:]
    block = seq * capacity
    if tuned(batch, seq):
        Z, block = seq // 2, 4 * capacity
        dma = pltpu.SemaphoreType.DMA
        quarter = [pltpu.VMEM((width, hidden_share), bf16), pltpu.VMEM((hidden_share, width), bf16)]
        out = pl.pallas_call(
            functools.partial(moe_kernel, seq),
            out_shape=[
                like(seq, capacity, wide, dtype=bf16),
                like(2, seq * capacity, wide, dtype=bf16),
                like(width, hidden_share, dtype=bf16),
                like(hidden_share, width, dtype=bf16),
            ],
            in_specs=[VM] * 3,
            out_specs=[HBM, HBM] + [VM] * 2,
            scratch_shapes=[
                pltpu.VMEM((Z, block, wide), bf16),
                pltpu.VMEM((Z, block, wide), bf16),
                pltpu.VMEM((Z * block, 2 * hidden_share), bf16),
                pltpu.VMEM((Z * block, 2 * hidden_share), bf16),
                pltpu.VMEM((block, 2 * hidden_share), f32),
                pltpu.VMEM((block, 2 * hidden_share), f32),
                pltpu.VMEM((Z, 2 * capacity, wide), bf16),
                pltpu.VMEM((Z, 2, capacity, wide), bf16),
                *quarter,
                *quarter,
                *quarter,
                pltpu.VMEM((width, hidden_share), f32),
                pltpu.VMEM((hidden_share, width), f32),
                dma,
                dma((2 * Z,)),
                dma((seq,)),
                dma((2, seq)),
                dma((Z, 2)),
                dma((Z,)),
                dma((Z,)),
                dma((Z, 2)),
                dma((seq,)),
                dma,
                dma((4,)),
                dma((4,)),
            ],
            compiler_params=pltpu.CompilerParams(
                collective_id=2, has_side_effects=True, vmem_limit_bytes=56 << 20),
            name="experts",
        )(sent, up, down)
        return out[0], out[2], out[3]
    mine = lax.all_to_all(sent, "seq", split_axis=0, concat_axis=0, tiled=True)
    rows = lax.all_gather(mine, "batch", axis=0).reshape(batch * block, wide)
    part, d_up, d_down = pl.pallas_call(
        expert_kernel,
        out_shape=[
            like(batch * block, wide, dtype=bf16),
            like(width, hidden_share),
            like(hidden_share, width),
        ],
        grid=(batch,),
        in_specs=[
            pl.BlockSpec((block, wide), lambda i: (i, 0)),
            pl.BlockSpec((width, hidden_share), lambda i: (0, 0)),
            pl.BlockSpec((hidden_share, width), lambda i: (0, 0)),
        ],
        out_specs=[
            pl.BlockSpec((block, wide), lambda i: (i, 0)),
            pl.BlockSpec((width, hidden_share), lambda i: (0, 0)),
            pl.BlockSpec((hidden_share, width), lambda i: (0, 0)),
        ],
        compiler_params=params(),
        name="experts",
    )(rows, up, down)
    part = part.reshape((batch,) + sent.shape)
    mine = lax.psum_scatter(part, "batch", scatter_dimension=0, tiled=False)
    return lax.all_to_all(mine, "seq", split_axis=0, concat_axis=0, tiled=True), d_up, d_down


class Moves:
    def __init__(self, sems):
        self.sems, self.used, self.named = sems, 0, {}

    def start(self, name, src, dst):
        cp = pltpu.make_async_copy(src, dst, self.sems.at[self.used])
        self.used += 1
        cp.start()
        self.named.setdefault(name, []).append(cp)

    def wait(self, *names):
        for name in names:
            for cp in self.named.pop(name):
                cp.wait()

    def wait_all(self):
        self.wait(*list(self.named))


def forward_kernel(dims, share, low_share, experts, capacity, room, batch, seq,
                   tok_ref, cot_ref, route_ref, slot_ref, state_ref, step_ref, router_in, *refs):
    seqs, rows, inner = dims[:3]
    lines, gains, refs = refs[:5], refs[5:7], refs[7:]
    (win_in, out_in, tok_hbm,
     win_hbm, out_hbm, tail_hbm, halo_hbm, ext_hbm, z_hbm, u_hbm, dt_hbm, y_hbm, gated_hbm, hist_ref,
     proj_ref, dsum_ref, vec_ref, gain_ref, router_ref, hid_ref, moe_ref, gate_ref, rows_ref,
     win, out, tail_all, halo, ext, z, u, dt, y, gated, end, start, xn, hbuf, hcur, sem, sem0,
     tail, vecs, feats, zeros, send_sem, recv_sem, edge_sem, sems) = refs[:48]
    relay_refs = refs[48:]
    moves = Moves(sems)
    gather = Gatherer(batch, seq, (win_in, tail, out_in), (win_hbm, tail_hbm, out_hbm), send_sem, recv_sem)
    WIN, TAIL, OUT = range(3)
    relay = Relay(seq, True, dims[3], dsum_ref, vec_ref, end, start, *relay_refs)
    b, s = gather.me.at()
    has_before, has_after = s > 0, s < seq - 1
    greet(gather.peers() + [(has_before, (b, s - 1)), (has_after, (b, s + 1))])

    gather.give(WIN)
    edges = [
        pltpu.make_async_remote_copy(
            src_ref=tok_hbm.at[i, pl.ds(rows - 8, 8)], dst_ref=halo_hbm.at[pl.ds(8 * i, 8)],
            send_sem=edge_sem.at[0, i], recv_sem=edge_sem.at[1, i], device_id=(b, s + 1), device_id_type=MESH)
        for i in range(seqs)
    ]
    none = pltpu.make_async_copy(zeros, halo_hbm, edge_sem.at[2, 0])
    zeros[...] = jnp.zeros_like(zeros)

    @pl.when(has_after)
    def _():
        for cp in edges:
            cp.start()
    pl.when(jnp.logical_not(has_before))(none.start)
    pack_weights(tail, vecs, feats, state_ref, step_ref, router_in, lines, gains)
    gather.give(TAIL)
    moves.start("own", win_in, gather.part(WIN, gather.own))
    moves.start("own", tail, gather.part(TAIL, gather.own))
    moves.start("own out", out_in, gather.part(OUT, gather.own))
    for h in range(1, gather.Z + 3):
        gather.hop((WIN, TAIL), h)
    gather.give(OUT)
    gather.rest((WIN, TAIL))

    @pl.when(has_before)
    def _():
        for cp in edges:
            cp.wait_recv()
    pl.when(jnp.logical_not(has_before))(none.wait)
    moves.wait("own")
    moves.start("head", halo_hbm, halo)
    moves.start("head", tail_hbm, tail_all)
    for j in range(inner // WIDE):
        for base in (0, inner):
            cols = pl.ds(base + j * WIDE, WIDE)
            moves.start(("win", j), win_hbm.at[:, cols], win.at[:, cols])
    moves.wait("head")

    def weights(j):
        moves.wait(("win", j))
        if j in (2, 5):
            gather.hop((OUT,), 1 + j // 5)

    def projected():
        for name, src, dst in (("ext", ext, ext_hbm), ("z", z, z_hbm), ("u", u, u_hbm), ("dt", dt, dt_hbm)):
            moves.start(name, src, dst)
        gather.hop((OUT,), 3)

    def scanned(i):
        relay.start(i)
        gather.hop((OUT,), 4 + i)

    enter_packed(dims, share, low_share, experts, tok_ref, halo, win, tail_all, ext, z, u, dt, proj_ref, end,
                 dsum_ref, vec_ref, gain_ref, router_ref, xn,
                 hooks=Hooks(weights=weights, projected=projected, scanned=scanned))
    for i in range(relay.count):
        relay.finish(i)
    for h in range(4 + relay.count, gather.Z + 3):
        gather.hop((OUT,), h)

    def half(i):
        if i == 0:
            gather.rest((OUT,))
            moves.wait("own out")
            moves.start("out", out_hbm, out)

    def mixed():
        moves.start("y", y, y_hbm)
        moves.start("gated", gated, gated_hbm)

    leave_kernel(dims, capacity, room, tok_ref, cot_ref, start, dt, u, z, proj_ref, vec_ref, out, gain_ref, router_ref,
                 route_ref, slot_ref, hist_ref, y, hid_ref, gated, moe_ref, gate_ref, rows_ref, hbuf, hcur, sem, sem0,
                 hooks=Hooks(out_proj=lambda: moves.wait("out"), mixed=mixed, half=half))
    relay.settle()
    gather.settle()

    @pl.when(has_after)
    def _():
        for cp in edges:
            cp.wait_send()
    moves.wait_all()


def backward_kernel(dims, share, low_share, experts, capacity, room, batch, seq,
                    ret_ref, cot_ref, hid_ref, moe_ref, gate_ref, vec_ref, gain_ref, router_ref, route_ref, slot_ref,
                    dsum_ref, proj_ref, gated_hbm, out_hbm, z_hbm, y_hbm, u_hbm, dt_hbm, ext_hbm, win_hbm, tail_hbm,
                    tok_hbm, halo_hbm, hist_ref,
                    block_ref, dtok_ref, next_ref, in_out, out_out, tail_out,
                    gated, out, z, y, u, dt, ext, win, tail, tok, halo, gy, gz, ghid, adj, later,
                    dhalo, dsmall, dvec, dnorm, dmoe, drouter, dskip, blank,
                    hbuf, ccol, bcol, gbsum, gcsum, carry, gdt, gu, gproj, gpad, gm, xn, gpre, sem, sems, edge_sem,
                    *more):
    seqs, rows, inner, states, rank, taps = dims
    count, devices = seqs * rows, batch * seq
    relay_refs, more = more[:9], more[9:]
    moves = Moves(sems)
    for name, src, dst in (
        ("gated", gated_hbm, gated), ("out", out_hbm, out), ("z", z_hbm, z), ("y", y_hbm, y), ("u", u_hbm, u),
        ("dt", dt_hbm, dt), ("ext", ext_hbm, ext), ("win", win_hbm, win), ("tail", tail_hbm, tail),
        ("tok", tok_hbm, tok), ("halo", halo_hbm, halo),
    ):
        moves.start(name, src, dst)
    relay = Relay(seq, False, states, dsum_ref, vec_ref, adj, later, *relay_refs)
    reducer = Reducer(batch, seq, *(more[4 * i : 4 * i + 4] for i in range(5)), more[20:])
    OUT, GATE, IN, REST = range(4)
    b, s = reducer.me.at()
    has_before, has_after = s > 0, s < seq - 1
    greet(reducer.peers() + [(has_before, (b, s - 1)), (has_after, (b, s + 1))])
    me = reducer.me

    return_kernel(dims, capacity, room, ret_ref, cot_ref, hid_ref, moe_ref, gate_ref, gated, y, u, z, dt, proj_ref,
                  vec_ref, out, gain_ref, router_ref, route_ref, slot_ref,
                  block_ref, ghid, gy, gz, None, drouter, dskip, dmoe, adj,
                  hooks=Hooks(activations=lambda: moves.wait("gated", "out", "z", "y", "u"),
                              gradients=lambda: moves.wait("dt"), scanned=relay.start))

    def in_grads(a, grads, n, xx):
        half, cut, wide = devices // 2, low_share * devices // 2, 2 * WIDE
        at = pl.ds(pl.multiple_of(xx * cut, 128), cut)
        for c0 in range(0, inner, wide):
            part = dot_tn(xn[0:n, at], grads[:, c0 : c0 + wide]).reshape(half, low_share, wide)
            reducer.items[a][pl.ds(xx * half, half), :, c0 : c0 + wide] = part.astype(bf16)
        reducer.give(a, [(xx, 1 - me.y), (xx, me.y)])

    branch = ghid[...].astype(bf16)
    cut = 8 * share
    for q in range(devices // 8):
        part = dot_tn(gated[:, q * cut : (q + 1) * cut], branch)
        reducer.items[OUT][q * 8 : (q + 1) * 8] = part.astype(bf16).reshape(8, share, part.shape[1])
    reducer.give(OUT, reducer.others)
    relay.finish(0)
    moves.wait("tok")
    x = tok[...].astype(f32)
    xn[0:count] = (x * normalize(x) * gain_ref[0:1]).astype(bf16)
    for xx in (1 - me.x, me.x):
        in_grads(GATE, gz, count, xx)
    for i in range(1, relay.count):
        relay.finish(i)

    def group(i):
        for g in range(4):
            @pl.when(i // reducer.Z == g)
            def _(g=g):
                for a in (OUT, GATE):
                    reducer.step(a, g, i % reducer.Z)

    def late_grads():
        for xx in (1 - me.x, me.x):
            in_grads(IN, gm, count + 8 * seqs, xx)

    back_kernel(dims, tok, halo, ext, hist_ref, later, gy, gz, ghid, u, dt, proj_ref, win, tail, vec_ref, gain_ref,
                dtok_ref, dhalo, None, dsmall, dvec, dnorm,
                hbuf, ccol, bcol, gbsum, gcsum, carry, gdt, gu, gproj, gpad, gm, xn, gpre, sem,
                hooks=Hooks(rest=lambda: moves.wait("ext", "win", "tail", "halo"), group=group),
                in_grads=late_grads)
    edge = reducer.copy(dhalo, next_ref, edge_sem.at[0], edge_sem.at[1], (b, s - 1))
    none = pltpu.make_async_copy(blank, next_ref, edge_sem.at[2])
    blank[...] = jnp.zeros_like(blank)
    pl.when(has_before)(edge.start)
    pl.when(jnp.logical_not(has_after))(none.start)
    pack_tail(reducer.items[REST], low_share, experts, states + taps + 2, dsmall, dvec, dskip, drouter, dnorm, dmoe)
    reducer.give(REST, reducer.others)
    for t in range(reducer.Z + 2):
        for g, k in ((0, t), (1, t), (2, t - 1), (3, t - 2)):
            if 0 <= k < reducer.Z:
                for a in (IN, REST):
                    reducer.step(a, g, k)
    for a, ref in ((OUT, out_out), (GATE, in_out.at[:, inner:]), (IN, in_out.at[:, :inner]), (REST, tail_out)):
        reducer.result(a, ref)
    relay.settle()
    for a in (OUT, GATE, IN, REST):
        reducer.settle(a)
    pl.when(has_after)(edge.wait_recv)
    pl.when(has_before)(edge.wait_send)
    pl.when(jnp.logical_not(has_after))(none.wait)


def body(
    tokens,
    in_proj,
    conv_weight,
    conv_bias,
    state_proj,
    step_proj,
    step_bias,
    decay_log,
    skip_gain,
    out_proj,
    norm_gain,
    moe_gain,
    router_proj,
    expert_up,
    expert_down,
    routes,
    slot_index,
    cotangent,
):
    batch, seq = lax.axis_size("batch"), lax.axis_size("seq")
    both = ("batch", "seq")
    seqs, rows, width = tokens.shape
    count = seqs * rows
    devices = batch * seq
    taps, share = conv_weight.shape
    inner = share * devices
    states, rank = decay_log.shape[0], step_proj.shape[0]
    low_share = norm_gain.shape[0]
    experts = router_proj.shape[1]
    capacity = max(2, 5 * count // (4 * experts))
    dims = (seqs, rows, inner, states, rank, taps)
    tile = 128

    lines = (decay_log, conv_weight, conv_bias[None], step_bias[None], skip_gain[None])
    used = sum(a.shape[0] for a in lines)
    room = -(-used // 8) * 8
    fast = tuned(batch, seq)
    if not fast:
        features = jnp.concatenate([router_proj, norm_gain[:, None], moe_gain[:, None]], axis=1)
        tail = jnp.concatenate(
            [
                state_proj,
                step_proj.T,
                jnp.pad(jnp.concatenate(lines), ((0, room - used), (0, 0))).T,
                jnp.pad(features, ((0, share - low_share), (0, tile - room - features.shape[1]))),
            ],
            axis=1,
        )
        halo = lax.ppermute(tokens[:, rows - taps + 1 :], "seq", [(i, i + 1) for i in range(seq - 1)])
        halo = jnp.pad(halo, ((0, 0), (8 - taps + 1, 0), (0, 0))).reshape(seqs * 8, width)
        in_full, out_full, tail_full = (
            lax.all_gather(a, both, axis=0, tiled=True) for a in (in_proj, out_proj, tail)
        )
    tok, cot = tokens.reshape(count, width), cotangent.reshape(count, width)
    size = GROUP * states
    total = experts * capacity
    edge_rows = seqs * 8
    dma = pltpu.SemaphoreType.DMA
    acts = like(count, inner)
    ext_s, state_s, dsum_s = like(seqs, rows + 8, inner), like(seqs, states, inner), like(seqs, 1, inner)
    proj_s, low_s, vec_s = like(count, tile), like(count, inner, dtype=bf16), like(room, inner)
    hist_s = like(seqs, (rows + 1) * states, inner, dtype=bf16)
    hid_s, moe_s, gate_s = like(count, width), like(count, width, dtype=bf16), like(count, 1)
    rows_s = like(total, 2 * width, dtype=bf16)
    gain_s, router_s = like(8, width), like(width, tile, dtype=bf16)
    vmem = lambda a: pltpu.VMEM(a.shape, a.dtype)
    normed = pltpu.VMEM((count + edge_rows, width), bf16)
    leave_scratch = [pltpu.VMEM((2, size, inner), bf16), pltpu.VMEM(state_s.shape, bf16), dma((2,)), dma((seqs,))]
    back_scratch = [
        pltpu.VMEM((2, size + states, inner), bf16),
        pltpu.VMEM((GROUP, states, tile), f32),
        pltpu.VMEM((GROUP, states, tile), f32),
        pltpu.VMEM((GROUP, states, tile), f32),
        pltpu.VMEM((GROUP, states, tile), f32),
        pltpu.VMEM((states, inner), f32),
        vmem(acts),
        vmem(acts),
        vmem(proj_s),
        pltpu.VMEM((rows + 16, WIDE), f32),
        pltpu.VMEM((count + edge_rows, inner), bf16),
        normed,
        vmem(low_s),
        dma((2,)),
    ]
    tok_s, halo_s, din_s = like(count, width), like(edge_rows, width), like(width, 2 * inner, dtype=bf16)
    dout_s, dsmall_s = like(inner, width, dtype=bf16), like(inner, tile, dtype=bf16)
    drouter_s, dskip_s, dgain_s = like(width, tile), like(1, inner), like(1, width)
    wide = inner // WIDE
    if fast:
        in_s, out_s = like(width, 2 * inner, dtype=bf16), like(inner, width, dtype=bf16)
        tail_s, halo_b = like(inner, 2 * tile, dtype=bf16), like(edge_rows, width, dtype=bf16)
        (in_full, out_full, tail_full, halo, ext, z, u, dt, y, gated, hist, proj, dsum, vec, gain, router, hid, moe_in,
         gate, sent) = pl.pallas_call(
            partial(forward_kernel, dims, share, low_share, experts, capacity, room, batch, seq),
            out_shape=[in_s, out_s, tail_s, halo_b, ext_s, acts, acts, acts, acts, low_s, hist_s, proj_s, dsum_s, vec_s,
                       gain_s, router_s, hid_s, moe_s, gate_s, rows_s],
            in_specs=[VM] * 16 + [HBM],
            out_specs=[HBM] * 11 + [VM] * 9,
            scratch_shapes=[
                vmem(in_s), vmem(out_s), vmem(tail_s), vmem(halo_b), vmem(ext_s), vmem(acts), vmem(acts), vmem(acts),
                vmem(acts), vmem(low_s), vmem(state_s), vmem(state_s), normed, *leave_scratch,
                pltpu.VMEM((share, 2 * tile), bf16),
                pltpu.VMEM((room, share), f32),
                pltpu.VMEM((8, low_share), f32),
                vmem(halo_b),
                dma((3, n_sends(seq // 2))),
                dma((3, devices)),
                dma((3, seqs)),
                dma((2 * wide + 12,)),
                *relay_scratch(seqs, states, inner),
            ],
            compiler_params=pltpu.CompilerParams(
                collective_id=3, has_side_effects=True, vmem_limit_bytes=58 << 20),
            name="forward",
        )(tok, cot, routes, slot_index, state_proj, step_proj, router_proj.T, *lines, norm_gain[None], moe_gain[None],
          in_proj, out_proj, tokens)
    else:
        vec = tail_full[:, tile : tile + room].T.astype(f32)
        router = tail_full[:, tile:].reshape(devices, share, tile)[:, :low_share].reshape(width, tile)
        gain = router[:, room + experts : room + experts + 2].T.astype(f32)
        ext, z, u, dt, proj, end, dsum = pl.pallas_call(
            partial(enter_kernel, dims),
            out_shape=[ext_s, acts, acts, acts, proj_s, state_s, dsum_s],
            in_specs=[VM] * 6,
            out_specs=[VM] * 7,
            scratch_shapes=[normed],
            compiler_params=params(),
            name="enter",
        )(tok, halo, in_full, tail_full[:, :tile], vec, gain)
        rates = -jnp.exp(vec[:states])
        before = chain_states(seq, True, dsum, rates, end)
        hist, y, hid, gated, moe_in, gate, sent = pl.pallas_call(
            partial(leave_kernel, dims, capacity, room),
            out_shape=[hist_s, acts, hid_s, low_s, moe_s, gate_s, rows_s],
            in_specs=[VM] * 13,
            out_specs=[HBM] + [VM] * 6,
            scratch_shapes=leave_scratch,
            compiler_params=params(),
            name="leave",
        )(tok, cot, before, dt, u, z, proj, vec, out_full, gain, router, routes, slot_index)

    back, d_up, d_down = moe_rows(
        batch, seq, sent.reshape(experts, capacity, 2 * width), expert_up[0], expert_down[0])
    back = back.reshape(total, 2 * width)

    if fast:
        own = [(share, width), (low_share, inner), (low_share, inner), (share, 2 * tile)]
        block_out, d_tok, from_next, s_in, s_out, s_tail = pl.pallas_call(
            partial(backward_kernel, dims, share, low_share, experts, capacity, room, batch, seq),
            out_shape=[moe_s, tok_s, halo_s, like(low_share, 2 * inner), like(*own[0]), like(*own[3])],
            in_specs=[VM] * 12 + [HBM] * 12,
            out_specs=[VM] * 2 + [HBM] + [VM] * 3,
            scratch_shapes=[
                vmem(low_s), vmem(out_s), vmem(acts), vmem(acts), vmem(acts), vmem(acts), vmem(ext_s), vmem(in_s),
                vmem(tail_s), vmem(tok), vmem(halo_b), vmem(acts), vmem(low_s), vmem(tok_s), vmem(state_s),
                vmem(state_s), vmem(halo_s), vmem(dsmall_s), vmem(vec_s), vmem(dgain_s), vmem(dgain_s),
                vmem(drouter_s), vmem(dskip_s), vmem(halo_s), *back_scratch, dma((12,)), dma((3,)),
                *relay_scratch(seqs, states, inner), *reduce_scratch(devices, seq // 2, own),
            ],
            compiler_params=pltpu.CompilerParams(
                collective_id=4, has_side_effects=True, vmem_limit_bytes=62 << 20),
            name="backward",
        )(back, cot, hid, moe_in, gate, vec, gain, router, routes, slot_index, dsum, proj,
          gated, out_full, z, y, u, dt, ext, in_full, tail_full, tok, halo, hist)
    else:
        block_out, ghid, gy, gz, d_out, d_router, d_skip, d_moe, adj = pl.pallas_call(
            partial(return_kernel, dims, capacity, room),
            out_shape=[moe_s, tok_s, acts, low_s, dout_s, drouter_s, dskip_s, dgain_s, state_s],
            in_specs=[VM] * 17,
            out_specs=[VM] * 9,
            compiler_params=params(),
            name="back_experts",
        )(back, cot, hid, moe_in, gate, gated, y, u, z, dt, proj, vec, out_full, gain, router, routes, slot_index)
        later = chain_states(seq, False, dsum, rates, adj)
        d_tok, d_halo, d_in, d_small, d_vec, d_norm = pl.pallas_call(
            partial(back_kernel, dims),
            out_shape=[tok_s, halo_s, din_s, dsmall_s, vec_s, dgain_s],
            in_specs=[VM] * 3 + [HBM] + [VM] * 11,
            out_specs=[VM] * 6,
            scratch_shapes=back_scratch,
            compiler_params=params(),
            name="back_mixer",
        )(tok, halo, ext, hist, later, gy, gz, ghid, u, dt, proj, in_full, tail_full, vec, gain)

    skip_row = states + taps + 2
    if fast:
        shapes = [
            s_in.shape, (taps, share), (1, share), (share, rank + 2 * states), (rank, share), (1, share),
            (states, share), (1, share), s_out.shape, (1, low_share), (1, low_share), (experts, low_share),
        ]
        block_out, d_tok = block_out.reshape(tokens.shape), d_tok.reshape(tokens.shape)
        block_out, d_tok, *sums, d_up, d_down = pl.pallas_call(
            partial(finish_kernel, dims, low_share, experts),
            out_shape=[like(*tokens.shape, dtype=bf16), like(*tokens.shape)] + [like(*a) for a in shapes]
            + [like(*d_up.shape), like(*d_down.shape)],
            in_specs=[VM] * 4 + [HBM] * 4,
            out_specs=[HBM] * 2 + [VM] * 12 + [HBM] * 2,
            scratch_shapes=[
                vmem(block_out), vmem(d_tok), vmem(d_up), vmem(d_down), vmem(like(*d_up.shape)), vmem(like(*d_down.shape)),
                dma((20,)),
            ],
            compiler_params=params(),
            name="finish",
        )(s_tail, from_next.reshape(seqs, 8, width), s_in, s_out, block_out, d_tok, d_up, d_down)
        for i in (2, 5, 7, 9, 10):
            sums[i] = sums[i][0]
        sums[11] = sums[11].T
        return (block_out, d_tok, *sums, d_up[None], d_down[None])
    d_model = d_router.at[:, room + experts : room + experts + 2].set(jnp.concatenate([d_norm, d_moe]).T)
    d_model = jnp.pad(
        d_model.reshape(devices, low_share, tile)[:, :, room:], ((0, 0), (0, share - low_share), (0, 0))
    ).reshape(inner, tile - room)
    d_vec = d_vec.at[skip_row].set(d_skip[0])
    d_tail = jnp.concatenate([d_small, d_vec.T.astype(bf16), d_model.astype(bf16)], axis=1)
    s_in, s_out, s_tail = (
        lax.psum_scatter(a.astype(f32), both, scatter_dimension=0, tiled=True) for a in (d_in, d_out, d_tail)
    )
    from_next = lax.ppermute(
        d_halo.reshape(seqs, 8, width)[:, 8 - taps + 1 :], "seq", [(i + 1, i) for i in range(seq - 1)]
    )
    d_tok = d_tok.reshape(tokens.shape).at[:, rows - taps + 1 :].add(from_next)
    s_vec = s_tail[:, tile : tile + room].T
    s_model = s_tail[:low_share, tile + room :]
    return (
        block_out.reshape(tokens.shape),
        d_tok,
        s_in,
        s_vec[states : states + taps],
        s_vec[states + taps],
        s_tail[:, : rank + 2 * states],
        s_tail[:, rank + 2 * states : tile].T,
        s_vec[states + taps + 1],
        s_vec[:states],
        s_vec[states + taps + 2],
        s_out,
        s_model[:, experts],
        s_model[:, experts + 1],
        s_model[:, :experts],
        d_up[None],
        d_down[None],
    )


def solution(mesh):
    in_specs = (
        P("batch", "seq", None),
        P(("batch", "seq"), None),
        P(None, ("batch", "seq")),
        P(("batch", "seq")),
        P(("batch", "seq"), None),
        P(None, ("batch", "seq")),
        P(("batch", "seq")),
        P(None, ("batch", "seq")),
        P(("batch", "seq")),
        P(("batch", "seq"), None),
        P(("batch", "seq")),
        P(("batch", "seq")),
        P(("batch", "seq"), None),
        P("seq", None, "batch"),
        P("seq", "batch", None),
        P("batch", "seq"),
        P("batch", "seq"),
        P("batch", "seq", None),
    )
    out_specs = (
        P("batch", "seq", None),
        P("batch", "seq", None),
        P(("batch", "seq"), None),
        P(None, ("batch", "seq")),
        P(("batch", "seq")),
        P(("batch", "seq"), None),
        P(None, ("batch", "seq")),
        P(("batch", "seq")),
        P(None, ("batch", "seq")),
        P(("batch", "seq")),
        P(("batch", "seq"), None),
        P(("batch", "seq")),
        P(("batch", "seq")),
        P(("batch", "seq"), None),
        P("seq", None, "batch"),
        P("seq", "batch", None),
    )
    return jax.shard_map(body, mesh=mesh, in_specs=in_specs, out_specs=out_specs, check_vma=False)
```
